32 devices in a mesh: dp: 8 (over z, x), ctx: 4 (over y, core).
Axes of the slice: x: 2, y: 2, z: 4, core: 2. Of those that a mesh axis runs over, the one named last changes fastest.
Arguments:
- hidden: bfloat16 [8, 1024, 768], P('dp', 'ctx'), may hold values from -6 to 6
- teacher: bfloat16 [8, 1024, 768], P('dp', 'ctx'), may hold values from -12 to 12
- lengths: int32 [8], P('dp'), may hold values from 256 to 1024, as said below
- w_qkv: bfloat16 [768, 2304], P('dp'), may hold values from -0.21875 to 0.21875
- w_out: bfloat16 [768, 768], P('dp'), may hold values from -0.375 to 0.375
- w_up: bfloat16 [768, 3072], P('dp'), may hold values from -0.375 to 0.375
- w_down: bfloat16 [3072, 768], P('dp'), may hold values from -0.1875 to 0.1875
- norm_gain: bfloat16 [768, 3], P('dp'), may hold values from 0.099609375 to 1.8984375
- norm_shift: bfloat16 [768, 3], P('dp'), may hold values from -3 to 3
- proj_bias: bfloat16 [768, 4], P('dp'), may hold values from -3 to 3
- mid_gain: bfloat16 [3072], P('dp'), may hold values from 0.099609375 to 1.8984375
- mid_shift: bfloat16 [3072], P('dp'), may hold values from -3 to 3
- up_bias: bfloat16 [3072], P('dp'), may hold values from -3 to 3
Outputs:
- layer_output: bfloat16 [8, 1024, 768], P('dp', 'ctx')
- loss: float32 [], replicated
- hidden_grad: float32 [8, 1024, 768], P('dp', 'ctx')
- qkv_grad: float32 [768, 2304], P('dp')
- out_grad: float32 [768, 768], P('dp')
- up_grad: float32 [768, 3072], P('dp')
- down_grad: float32 [3072, 768], P('dp')
- gain_grad: float32 [768, 3], P('dp')
- shift_grad: float32 [768, 3], P('dp')
- bias_grad: float32 [768, 4], P('dp')
- mid_gain_grad: float32 [3072], P('dp')
- mid_shift_grad: float32 [3072], P('dp')
- up_bias_grad: float32 [3072], P('dp')
The draws below stay inside these ranges and needn't reach their ends.
Inputs may be any that keep to these rules, and one draw needn't show every extreme that they name: Sequence s has valid tokens at positions 0 to lengths[s] - 1 and padding after them; some sequence has exactly 1024 and some exactly 256 valid tokens.
All inputs are finite; a program needn't handle non-finite values.
Results may differ from the reference program's by a relative error of at most 0.013.
Values may be sent and summed in bfloat16 or wider, within the bound.
No kernel may reach another device: no remote copies, remote signals or barrier semaphores. Data moves between devices by JAX's collectives and lax.ppermute only.
A program may use at most 192 MiB of HBM per device.

```python
import math
import jax
import jax.numpy as jnp
from jax import lax

D = 768
HEADS = 12
HEAD_DIM = 64
FF = 3072
SEQS = 8
LENGTH = 1024


def draw_lengths(key, part):
    key_draw, key_long, key_short = jax.random.split(key, 3)
    shortest = LENGTH // 4
    lengths_drawn = jax.random.randint(key_draw, (SEQS,), shortest, LENGTH + 1)
    longest_at = jax.random.randint(key_long, (), 0, SEQS)
    offset = jax.random.randint(key_short, (), 1, SEQS)
    shortest_at = (longest_at + offset) % SEQS
    slot_index = jnp.arange(SEQS)
    lengths_drawn = jnp.where(slot_index == longest_at, LENGTH, lengths_drawn)
    lengths_drawn = jnp.where(slot_index == shortest_at, shortest, lengths_drawn)
    return lengths_drawn.astype(jnp.int32)


def draw_teacher(key, part):
    spots = jnp.arange(SEQS, dtype=jnp.float32) / max(SEQS - 1, 1)
    base = jnp.clip(jax.random.normal(key, (SEQS, LENGTH, D), jnp.float32), -6.0, 6.0)
    rising = 0.6 + 1.2 * spots
    return (base * rising[:, None, None]).astype(jnp.bfloat16)


def steps_of(rng, dims, cuts, least, high):
    level, own = 1.0, jax.random.fold_in(rng, 6)
    for dim, shards_of in cuts:
        steps = jnp.exp(jax.random.uniform(jax.random.fold_in(own, dim), (shards_of,), jnp.float32, least / len(cuts), high / len(cuts)))
        level = level * jnp.repeat(steps, dims[dim] // shards_of).reshape([-1 if axis == dim else 1 for axis in range(len(dims))])
    return level


def bell_draw(own_key, shape, width, limit, shards=(), kind=jnp.bfloat16):
    entries = width * jax.random.normal(own_key, shape, jnp.float32)
    if shards:
        entries = entries * steps_of(own_key, shape, shards, -0.22, 0.18)
    return jnp.clip(entries, -limit, limit).astype(kind)


def setup_inputs(seed: int = 0) -> dict:
    streams_of = jax.random.split(jax.random.key(seed), 14)
    return {
        "hidden": bell_draw(streams_of[0], (SEQS, LENGTH, D), 1.0, 6.0, ((0, 8), (1, 4))),
        "teacher": draw_teacher(jax.random.fold_in(streams_of[13], 71), 0),
        "lengths": draw_lengths(jax.random.fold_in(streams_of[13], 71), 0),
        "w_qkv": bell_draw(streams_of[3], (D, 3 * D), D ** -0.5, 0.21875, ((0, 8),)),
        "w_out": bell_draw(streams_of[4], (D, D), (D // 3) ** -0.5, 0.375, ((0, 8),)),
        "w_up": bell_draw(streams_of[5], (D, FF), (D // 3) ** -0.5, 0.375, ((0, 8),)),
        "w_down": bell_draw(streams_of[6], (FF, D), (FF // 3) ** -0.5, 0.1875, ((0, 8),)),
        "norm_gain": jnp.clip(1.0 + 0.18 * jax.random.normal(streams_of[7], (D, 3), jnp.float32), 0.099609375, 1.8984375).astype(jnp.bfloat16),
        "norm_shift": bell_draw(streams_of[8], (D, 3), 0.5, 3.0, ((0, 8),)),
        "proj_bias": bell_draw(streams_of[9], (D, 4), 0.5, 3.0, ((0, 8),)),
        "mid_gain": jnp.clip(1.0 + 0.18 * jax.random.normal(streams_of[10], (FF,), jnp.float32), 0.099609375, 1.8984375).astype(jnp.bfloat16),
        "mid_shift": bell_draw(streams_of[11], (FF,), 0.5, 3.0, ((0, 8),)),
        "up_bias": bell_draw(streams_of[12], (FF,), 0.5, 3.0, ((0, 8),)),
    }


@jax.custom_vjp
def low(v):
    return lax.optimization_barrier(v.astype(jnp.bfloat16)).astype(jnp.float32)

@jax.custom_vjp
def low_back(v):
    return v

def low_keep(v):
    return (low(v), None)

def low_pass(kept, grad):
    return (grad,)

def back_keep(v):
    return (v, None)

def back_low(kept, grad):
    return (low(grad),)
low.defvjp(low_keep, low_pass)
low_back.defvjp(back_keep, back_low)
EPSILON = 1e-05
NEGATIVE = -1e+30
HIGHEST = lax.Precision.HIGHEST

def layer_norm(values, gain_vec, shift_vec):
    average = lax.optimization_barrier(jnp.mean(values, axis=-1, keepdims=True))
    centred = values - average
    variance = lax.optimization_barrier(jnp.mean(centred * centred, axis=-1, keepdims=True))
    return centred * lax.rsqrt(variance + EPSILON) * gain_vec + shift_vec

def attend(query_rows, key_rows, value_rows, seq_length):
    total_len = query_rows.shape[0]
    block_len = min(512, total_len)
    key_pos = jnp.arange(total_len, dtype=jnp.int32)
    score_scale = 1.0 / math.sqrt(HEAD_DIM)

    def one_block(block_start):
        query_block = lax.dynamic_slice_in_dim(query_rows, block_start, block_len, 0)
        scores = jnp.einsum('qhd,khd->hqk', query_block, key_rows, precision=HIGHEST) * score_scale
        scores = low_back(scores)
        query_pos = block_start + jnp.arange(block_len, dtype=jnp.int32)
        allowed = (key_pos[None, :] <= query_pos[:, None]) & (key_pos[None, :] < seq_length)
        scores = jnp.where(allowed[None], scores, NEGATIVE)
        top_score = lax.optimization_barrier(jnp.max(scores, axis=-1, keepdims=True))
        exponent_vals = jnp.exp(scores - top_score)
        weights = exponent_vals / lax.optimization_barrier(jnp.sum(exponent_vals, axis=-1, keepdims=True))
        return jnp.einsum('hqk,khd->qhd', low(weights), value_rows, precision=HIGHEST)
    starts = jnp.arange(total_len // block_len, dtype=jnp.int32) * block_len
    blocks = lax.map(jax.checkpoint(one_block), starts)
    return blocks.reshape(total_len, HEADS * HEAD_DIM)

def layer(hidden_seq, params, seq_length, teacher_seq):
    w_qkv, w_out, w_up, w_down, norm_gain, norm_shift, proj_bias, mid_gain, mid_shift, up_bias = params
    model_width = hidden_seq.shape[1]
    positions = jnp.arange(hidden_seq.shape[0], dtype=jnp.int32)
    valid_mask = (positions < seq_length).astype(jnp.float32)[:, None]
    normed = low(layer_norm(hidden_seq, norm_gain[:, 0], norm_shift[:, 0]))
    projected = jnp.dot(normed, w_qkv, precision=HIGHEST)
    query_rows = low(low_back(projected[:, :model_width] + proj_bias[:, 0]))
    key_rows = low(low_back(projected[:, model_width:2 * model_width]))
    value_rows = low(low_back(projected[:, 2 * model_width:] + proj_bias[:, 1]))
    head_shape = (hidden_seq.shape[0], HEADS, HEAD_DIM)
    attended = low_back(attend(query_rows.reshape(head_shape), key_rows.reshape(head_shape), value_rows.reshape(head_shape), seq_length))
    mixed = low(layer_norm(attended, norm_gain[:, 1], norm_shift[:, 1]))
    residual = hidden_seq + low_back(jnp.dot(mixed, w_out, precision=HIGHEST) + proj_bias[:, 2])
    ffn_in = low(layer_norm(residual, norm_gain[:, 2], norm_shift[:, 2]))
    up_proj = low_back(jnp.dot(ffn_in, w_up, precision=HIGHEST) + up_bias)
    activated = low(layer_norm(jax.nn.gelu(up_proj, approximate=False), mid_gain, mid_shift))
    result = residual + low_back(jnp.dot(activated, w_down, precision=HIGHEST) + proj_bias[:, 3])
    error_rows = (result - teacher_seq) * valid_mask
    return (0.5 * jnp.sum(error_rows * error_rows), (result, valid_mask))

def reference(hidden, teacher, lengths, w_qkv, w_out, w_up, w_down, norm_gain, norm_shift, proj_bias, mid_gain, mid_shift, up_bias):
    params = tuple((array.astype(jnp.float32) for array in (w_qkv, w_out, w_up, w_down, norm_gain, norm_shift, proj_bias, mid_gain, mid_shift, up_bias)))
    zero_grads = tuple((jnp.zeros_like(array) for array in params))

    def one_sequence(running, items):
        grad_sums, loss_sum = running
        hidden_seq, teacher_seq, seq_length = items

        def objective(hidden_in, param_in):
            return layer(hidden_in, param_in, seq_length, teacher_seq.astype(jnp.float32))
        seq_loss, pullback, aux_pair = jax.vjp(objective, hidden_seq.astype(jnp.float32), params, has_aux=True)
        result, valid_mask = aux_pair
        hidden_grad, param_grads = pullback(jnp.ones((), jnp.float32))
        grad_sums = tuple((acc_sum + piece for acc_sum, piece in zip(grad_sums, param_grads)))
        layer_output = (result * valid_mask).astype(jnp.bfloat16)
        return ((grad_sums, loss_sum + seq_loss), (layer_output, hidden_grad))
    (grad_sums, loss_sum), (layer_output, hidden_grad) = lax.scan(one_sequence, (zero_grads, jnp.zeros((), jnp.float32)), (hidden, teacher, lengths))
    valid_total = jnp.sum(lengths).astype(jnp.float32)
    loss = loss_sum / (valid_total * hidden.shape[2])
    return (layer_output, loss, hidden_grad, grad_sums[0], grad_sums[1], grad_sums[2], grad_sums[3], grad_sums[4], grad_sums[5], grad_sums[6], grad_sums[7], grad_sums[8], grad_sums[9])
```

```python
import math

import jax
import jax.numpy as jnp
from jax import lax
from jax.experimental import pallas as pl
from jax.experimental.pallas import tpu as pltpu
from jax.sharding import PartitionSpec as P

HEADS = 12
HEAD_DIM = 64


EPSILON = 1e-05
NEGATIVE = -1e30


def passed_along(value, axis, steps):
    count = lax.axis_size(axis)
    pairs = [(source, (source + steps) % count) for source in range(count)]
    return lax.ppermute(value, axis, pairs)


def passed_along_2(block, axis, distance):
    devices = range(lax.axis_size(axis))
    route = [(i - distance, i) for i in devices if i - distance in devices]
    return lax.ppermute(block, axis, route)


def layer_norm(values, gain_vec, shift_vec):
    average = jnp.mean(values, axis=-1, keepdims=True)
    centred = values - average
    variance = jnp.mean(centred * centred, axis=-1, keepdims=True)
    return centred * lax.rsqrt(variance + EPSILON) * gain_vec + shift_vec


def mid_norm(up_proj, gain_vec, shift_vec):
    return layer_norm(jax.nn.gelu(up_proj, approximate=False), gain_vec, shift_vec)


def split_heads(values):
    return values.reshape(values.shape[0], values.shape[1], HEADS, HEAD_DIM)


def key_mask(query_pos, key_start, key_count, lengths):
    key_pos = key_start + jnp.arange(key_count, dtype=jnp.int32)
    causal = key_pos[None, :] <= query_pos[:, None]
    inside = key_pos[None, :] < lengths[:, None]
    return causal[None, :, :] & inside[:, None, :]


def fold_keys(running, pieces, key_start, heads_q, query_pos, lengths):
    row_max, row_total, weighted = running
    key_piece, value_piece = pieces
    key_count = key_piece.shape[1]
    score_scale = 1.0 / math.sqrt(HEAD_DIM)
    scores = (
        jnp.einsum(
            "sqhd,skhd->shqk", heads_q, split_heads(key_piece), preferred_element_type=jnp.float32
        )
        * score_scale
    )
    allowed = key_mask(query_pos, key_start, key_count, lengths)[:, None]
    scores = jnp.where(allowed, scores, NEGATIVE)
    fresh_max = jnp.maximum(row_max, jnp.max(scores, axis=-1))
    exponent_vals = jnp.exp(scores - fresh_max[..., None])
    row_total = jnp.sum(exponent_vals, axis=-1)
    update = jnp.einsum(
        "shqk,skhd->sqhd",
        exponent_vals.astype(jnp.bfloat16),
        split_heads(value_piece),
        preferred_element_type=jnp.float32,
    )
    weighted = update
    return (fresh_max, row_total, weighted)


def grad_keys(
    heads_q, heads_do, log_total, dterm, key_piece, value_piece, key_start, query_pos, lengths
):
    seq_count, key_count = (key_piece.shape[0], key_piece.shape[1])
    heads_k = split_heads(key_piece)
    heads_v = split_heads(value_piece)
    score_scale = 1.0 / math.sqrt(HEAD_DIM)
    scores = (
        jnp.einsum("sqhd,skhd->shqk", heads_q, heads_k, preferred_element_type=jnp.float32)
        * score_scale
    )
    allowed = key_mask(query_pos, key_start, key_count, lengths)[:, None]
    probability = jnp.where(allowed, jnp.exp(scores - log_total[..., None]), 0.0)
    dprob = jnp.einsum("sqhd,skhd->shqk", heads_do, heads_v, preferred_element_type=jnp.float32)
    dscores = (probability * (dprob - dterm[..., None])).astype(jnp.bfloat16)
    dq_part = (
        jnp.einsum("shqk,skhd->sqhd", dscores, heads_k, preferred_element_type=jnp.float32)
        * score_scale
    )
    dk_part = (
        jnp.einsum("shqk,sqhd->skhd", dscores, heads_q, preferred_element_type=jnp.float32)
        * score_scale
    )
    dv_part = jnp.einsum(
        "shqk,sqhd->skhd",
        probability.astype(jnp.bfloat16),
        heads_do,
        preferred_element_type=jnp.float32,
    )
    return (
        dq_part,
        dk_part.reshape(seq_count, key_count, -1),
        dv_part.reshape(seq_count, key_count, -1),
    )


def shards(
    hidden,
    teacher,
    lengths,
    w_qkv,
    w_out,
    w_up,
    w_down,
    norm_gain,
    norm_shift,
    proj_bias,
    mid_gain,
    mid_shift,
    up_bias,
):
    (
        full_qkv,
        full_out,
        full_up,
        full_down,
        gain_full,
        shift_full,
        bias_full,
        mid_gain_full,
        mid_shift_full,
        up_bias_full,
    ) = (
        lax.all_gather(w_qkv, "dp", axis=0, tiled=True),
        lax.all_gather(w_out, "dp", axis=0, tiled=True),
        lax.all_gather(w_up, "dp", axis=0, tiled=True),
        lax.all_gather(w_down, "dp", axis=0, tiled=True),
        lax.all_gather(norm_gain, "dp", axis=0, tiled=True),
        lax.all_gather(norm_shift, "dp", axis=0, tiled=True),
        lax.all_gather(proj_bias, "dp", axis=0, tiled=True),
        lax.all_gather(mid_gain, "dp", axis=0, tiled=True),
        lax.all_gather(mid_shift, "dp", axis=0, tiled=True),
        lax.all_gather(up_bias, "dp", axis=0, tiled=True),
    )
    gain_f = gain_full.astype(jnp.float32)
    shift_f = shift_full.astype(jnp.float32)
    bias_f = bias_full.astype(jnp.float32)
    mid_gain_f = mid_gain_full.astype(jnp.float32)
    mid_shift_f = mid_shift_full.astype(jnp.float32)
    up_bias_f = up_bias_full.astype(jnp.float32)
    seq_count, local_rows, model_width = hidden.shape
    token_rows = seq_count * local_rows
    seq_shape = (seq_count, local_rows, model_width)
    ctx_place = lax.axis_index("ctx")
    ctx_parts = lax.axis_size("ctx")
    query_pos = ctx_place * local_rows + jnp.arange(local_rows, dtype=jnp.int32)
    last_query = ctx_place * local_rows + local_rows - 1
    valid_mask = (query_pos[None, :] < lengths[:, None]).astype(jnp.float32)
    valid_rows = valid_mask.reshape(token_rows, 1)
    hidden_rows = hidden.reshape(token_rows, model_width).astype(jnp.float32)
    normed, pull_in = jax.vjp(layer_norm, hidden_rows, gain_f[:, 0], shift_f[:, 0])
    normed_low = normed.astype(jnp.bfloat16)
    projected = jnp.dot(normed_low, full_qkv, preferred_element_type=jnp.float32)
    query_low = (projected[:, :model_width] + bias_f[:, 0]).astype(jnp.bfloat16).reshape(seq_shape)
    key_low = projected[:, model_width : 2 * model_width].astype(jnp.bfloat16).reshape(seq_shape)
    value_low = (
        (projected[:, 2 * model_width :] + bias_f[:, 1]).astype(jnp.bfloat16).reshape(seq_shape)
    )
    heads_q = split_heads(query_low)
    start_state = (
        jnp.full((seq_count, HEADS, local_rows), NEGATIVE, jnp.float32),
        jnp.zeros((seq_count, HEADS, local_rows), jnp.float32),
        jnp.zeros((seq_count, local_rows, HEADS, HEAD_DIM), jnp.float32),
    )
    pieces = (
        lax.all_gather(key_low, "ctx", axis=1, tiled=True),
        lax.all_gather(value_low, "ctx", axis=1, tiled=True),
    )
    key_start = jnp.int32(0)
    row_max, row_total, weighted = lax.cond(
        key_start <= last_query,
        lambda: fold_keys(start_state, pieces, key_start, heads_q, query_pos, lengths),
        lambda: start_state,
    )
    attended = weighted / jnp.transpose(row_total, (0, 2, 1))[..., None]
    log_total = row_max + jnp.log(row_total)
    attended_rows = attended.reshape(token_rows, model_width)
    mixed, pull_mix = jax.vjp(layer_norm, attended_rows, gain_f[:, 1], shift_f[:, 1])
    mixed_low = mixed.astype(jnp.bfloat16)
    residual = (
        hidden_rows
        + jnp.dot(mixed_low, full_out, preferred_element_type=jnp.float32)
        + bias_f[:, 2]
    )
    ffn_in, pull_ffn = jax.vjp(layer_norm, residual, gain_f[:, 2], shift_f[:, 2])
    ffn_low = ffn_in.astype(jnp.bfloat16)
    up_proj = jnp.dot(ffn_low, full_up, preferred_element_type=jnp.float32) + up_bias_f
    activated, pull_mid = jax.vjp(mid_norm, up_proj, mid_gain_f, mid_shift_f)
    act_low = activated.astype(jnp.bfloat16)
    result = (
        residual + jnp.dot(act_low, full_down, preferred_element_type=jnp.float32) + bias_f[:, 3]
    )
    layer_output = (result * valid_rows).astype(jnp.bfloat16).reshape(hidden.shape)
    error_rows = (
        result - teacher.reshape(token_rows, model_width).astype(jnp.float32)
    ) * valid_rows
    loss_total, valid_total = lax.psum(
        (0.5 * jnp.sum(error_rows * error_rows), jnp.sum(valid_mask)), ("dp", "ctx")
    )
    loss = loss_total / (valid_total * model_width)
    down_low = error_rows.astype(jnp.bfloat16)
    bias_down_grad = jnp.sum(down_low.astype(jnp.float32), axis=0)
    down_grad = jnp.einsum("rf,rd->fd", act_low, down_low, preferred_element_type=jnp.float32)
    d_act = jnp.einsum("rd,fd->rf", down_low, full_down, preferred_element_type=jnp.float32)
    d_up, mid_gain_grad, mid_shift_grad = pull_mid(d_act)
    up_low = d_up.astype(jnp.bfloat16)
    up_bias_grad = jnp.sum(up_low.astype(jnp.float32), axis=0)
    up_grad = jnp.einsum("rd,rf->df", ffn_low, up_low, preferred_element_type=jnp.float32)
    d_ffn = jnp.einsum("rf,df->rd", up_low, full_up, preferred_element_type=jnp.float32)
    d_res_norm, gain_two, shift_two = pull_ffn(d_ffn)
    d_residual = error_rows + d_res_norm
    branch_low = d_residual.astype(jnp.bfloat16)
    bias_out_grad = jnp.sum(branch_low.astype(jnp.float32), axis=0)
    out_grad = jnp.einsum("rd,re->de", mixed_low, branch_low, preferred_element_type=jnp.float32)
    d_mixed = jnp.einsum("re,de->rd", branch_low, full_out, preferred_element_type=jnp.float32)
    d_att, gain_one, shift_one = pull_mix(d_mixed)
    heads_do = split_heads(d_att.astype(jnp.bfloat16).reshape(seq_shape))
    dterm = jnp.einsum("sqhd,sqhd->shq", heads_do.astype(jnp.float32), attended)

    def grad_step(key_piece, value_piece, key_start):
        return grad_keys(
            heads_q,
            heads_do,
            log_total,
            dterm,
            key_piece,
            value_piece,
            key_start,
            query_pos,
            lengths,
        )

    dq_zero = jnp.zeros((seq_count, local_rows, HEADS, HEAD_DIM), jnp.float32)
    own_zero = jnp.zeros(seq_shape, jnp.float32)

    def pass_step(step_index, running):
        key_cur, value_cur, dk_run, dv_run, dq_sum = running
        owner = (ctx_place - step_index) % ctx_parts
        dq_part, dk_part, dv_part = lax.cond(
            owner <= ctx_place,
            lambda: grad_step(key_cur, value_cur, owner * local_rows),
            lambda: (dq_zero, own_zero, own_zero),
        )
        dk_run, dv_run = (
            passed_along((dk_run + dk_part).astype(jnp.bfloat16), "ctx", 1).astype(jnp.float32),
            passed_along((dv_run + dv_part).astype(jnp.bfloat16), "ctx", 1).astype(jnp.float32),
        )
        key_cur, value_cur = passed_along_2((key_cur, value_cur), "ctx", 1)
        return (key_cur, value_cur, dk_run, dv_run, dq_sum + dq_part)

    key_end, value_end, dk_own, dv_own, dq_sum = lax.fori_loop(
        0, ctx_parts, pass_step, (key_low, value_low, own_zero, own_zero, dq_zero)
    )
    dq_low = dq_sum.reshape(token_rows, model_width).astype(jnp.bfloat16)
    dk_low = dk_own.reshape(token_rows, model_width).astype(jnp.bfloat16)
    dv_low = dv_own.reshape(token_rows, model_width).astype(jnp.bfloat16)
    dqkv_low = jnp.concatenate([dq_low, dk_low, dv_low], axis=1)
    bias_q_grad = jnp.sum(dq_low.astype(jnp.float32), axis=0)
    bias_v_grad = jnp.sum(dv_low.astype(jnp.float32), axis=0)
    qkv_grad = jnp.einsum("rd,re->de", normed_low, dqkv_low, preferred_element_type=jnp.float32)
    d_normed = jnp.einsum("re,de->rd", dqkv_low, full_qkv, preferred_element_type=jnp.float32)
    d_in_norm, gain_zero, shift_zero = pull_in(d_normed)
    hidden_grad = (d_residual + d_in_norm).reshape(hidden.shape)
    gain_grad = jnp.stack([gain_zero, gain_one, gain_two], axis=1)
    shift_grad = jnp.stack([shift_zero, shift_one, shift_two], axis=1)
    bias_grad = jnp.stack([bias_q_grad, bias_v_grad, bias_out_grad, bias_down_grad], axis=1)
    shares = (
        lax.psum_scatter(
            qkv_grad.astype(jnp.bfloat16), "dp", scatter_dimension=0, tiled=True
        ).astype(jnp.float32),
        lax.psum_scatter(
            out_grad.astype(jnp.bfloat16), "dp", scatter_dimension=0, tiled=True
        ).astype(jnp.float32),
        lax.psum_scatter(
            up_grad.astype(jnp.bfloat16), "dp", scatter_dimension=0, tiled=True
        ).astype(jnp.float32),
        lax.psum_scatter(
            down_grad.astype(jnp.bfloat16), "dp", scatter_dimension=0, tiled=True
        ).astype(jnp.float32),
        lax.psum_scatter(
            gain_grad.astype(jnp.bfloat16), "dp", scatter_dimension=0, tiled=True
        ).astype(jnp.float32),
        lax.psum_scatter(
            shift_grad.astype(jnp.bfloat16), "dp", scatter_dimension=0, tiled=True
        ).astype(jnp.float32),
        lax.psum_scatter(
            bias_grad.astype(jnp.bfloat16), "dp", scatter_dimension=0, tiled=True
        ).astype(jnp.float32),
        lax.psum_scatter(
            mid_gain_grad.astype(jnp.bfloat16), "dp", scatter_dimension=0, tiled=True
        ).astype(jnp.float32),
        lax.psum_scatter(
            mid_shift_grad.astype(jnp.bfloat16), "dp", scatter_dimension=0, tiled=True
        ).astype(jnp.float32),
        lax.psum_scatter(
            up_bias_grad.astype(jnp.bfloat16), "dp", scatter_dimension=0, tiled=True
        ).astype(jnp.float32),
    )
    summed = (
        lax.psum(shares[0].astype(jnp.bfloat16), "ctx").astype(jnp.float32),
        lax.psum(shares[1].astype(jnp.bfloat16), "ctx").astype(jnp.float32),
        lax.psum(shares[2].astype(jnp.bfloat16), "ctx").astype(jnp.float32),
        lax.psum(shares[3].astype(jnp.bfloat16), "ctx").astype(jnp.float32),
        lax.psum(shares[4].astype(jnp.bfloat16), "ctx").astype(jnp.float32),
        lax.psum(shares[5].astype(jnp.bfloat16), "ctx").astype(jnp.float32),
        lax.psum(shares[6].astype(jnp.bfloat16), "ctx").astype(jnp.float32),
        lax.psum(shares[7].astype(jnp.bfloat16), "ctx").astype(jnp.float32),
        lax.psum(shares[8].astype(jnp.bfloat16), "ctx").astype(jnp.float32),
        lax.psum(shares[9].astype(jnp.bfloat16), "ctx").astype(jnp.float32),
    )
    return (
        layer_output,
        loss,
        hidden_grad,
        summed[0],
        summed[1],
        summed[2],
        summed[3],
        summed[4],
        summed[5],
        summed[6],
        summed[7],
        summed[8],
        summed[9],
    )


AXES = ("dp", "ctx")


def swap(value, mask):
    count = lax.axis_size("dp") * lax.axis_size("ctx")
    return lax.ppermute(value, AXES, [(i, i ^ mask) for i in range(count)])


def gathered_dp(piece):
    column = jnp.stack([piece] + [swap(piece, 8 * step) for step in (1, 2, 3)])
    return jnp.stack([column, swap(column, 4)])


def wide(value):
    return value.astype(jnp.float32)


def narrow(value):
    return value.astype(jnp.bfloat16)


def scattered_dp(slots):
    kept = wide(slots[0]) + wide(swap(slots[1], 4))
    send = narrow(kept)
    return kept[0] + sum(wide(swap(send[step], 8 * step)) for step in (1, 2, 3))


def halves(value):
    high = narrow(value)
    return high, narrow(value - wide(high))


def by_block(slots, dp_at):
    flat = slots.reshape((8,) + slots.shape[2:])
    place = [((b & 1) ^ (dp_at & 1)) * 4 + ((b >> 1) ^ (dp_at >> 1)) for b in range(8)]
    return jnp.stack([lax.dynamic_index_in_dim(flat, at, 0, keepdims=False) for at in place])


def to_slots(blocks, dp_at):
    order = [2 * ((s & 3) ^ (dp_at >> 1)) + ((s >> 2) ^ (dp_at & 1)) for s in range(8)]
    flat = jnp.stack([lax.dynamic_index_in_dim(blocks, at, 0, keepdims=False) for at in order])
    return flat.reshape((2, 4) + blocks.shape[1:])


def by_ctx(tiles, ctx_at):
    stack = jnp.stack(tiles)
    return [lax.dynamic_index_in_dim(stack, ctx_at ^ j, 0, keepdims=False) for j in range(4)]


def attention_mask(length):
    pos = jnp.arange(1024, dtype=jnp.int32)
    return (pos[None, :] <= pos[:, None]) & (pos[None, :] < length)


def dots(spec, a, b):
    return jnp.einsum(spec, a, b, preferred_element_type=jnp.float32)


def fast(
    hidden, teacher, lengths, w_qkv, w_out, w_up, w_down, norm_gain, norm_shift, proj_bias,
    mid_gain, mid_shift, up_bias,
):
    dp_at, ctx_at = lax.axis_index("dp"), lax.axis_index("ctx")
    length = lengths[0]
    own = hidden[0]
    rows, width = own.shape
    pick = lambda at: lax.dynamic_slice(w_qkv, (0, at), (96, 192))
    piece = jnp.concatenate(
        [pick(768 * part + 192 * ctx_at) for part in range(3)]
        + [norm_gain, norm_shift, proj_bias, jnp.zeros((96, 54), jnp.bfloat16)], axis=1)
    h_y = swap(own, 2)
    h_c = swap(own, 1)
    h_yc = swap(h_y, 1)
    q_slots = gathered_dp(piece)
    mid_rows = jnp.concatenate([mid_gain, mid_shift, up_bias, jnp.zeros((13 * 384,), jnp.bfloat16)]).reshape(8, 768)
    piece_a = jnp.concatenate([
        lax.dynamic_slice(w_up, (0, 768 * ctx_at), (96, 768)),
        lax.dynamic_slice(w_out, (48 * (ctx_at & 1), 0), (48, 768)), mid_rows])
    a_slots = gathered_dp(piece_a)
    down4 = w_down.reshape(4, 96, 768)
    piece_b = jnp.stack([lax.dynamic_index_in_dim(down4, ctx_at ^ t, 0, keepdims=False) for t in (0, 2)])
    b_slots = gathered_dp(piece_b)

    w_all = by_block(q_slots, dp_at).reshape(768, 640)
    vecs = wide(w_all[:, 576:586]).T
    w_q3 = w_all[:, :576]
    hid_all = jnp.concatenate(by_ctx([own, h_c, h_y, h_yc], ctx_at))
    normed, pull_in = jax.vjp(layer_norm, wide(hid_all), vecs[0], vecs[3])
    normed_low = narrow(normed)
    projected = jnp.dot(normed_low, w_q3, preferred_element_type=jnp.float32)
    bias_q = lax.dynamic_slice(vecs[6], (192 * ctx_at,), (192,))
    bias_v = lax.dynamic_slice(vecs[7], (192 * ctx_at,), (192,))
    q = narrow(projected[:, :192] + bias_q).reshape(1024, 3, 64)
    k = narrow(projected[:, 192:384]).reshape(1024, 3, 64)
    v = narrow(projected[:, 384:] + bias_v).reshape(1024, 3, 64)
    allowed = attention_mask(length)
    scores = jnp.where(allowed, dots("qhd,khd->hqk", q, k) * 0.125, NEGATIVE)
    prob = jax.nn.softmax(scores, axis=-1)
    att = dots("hqk,khd->qhd", narrow(prob), v).reshape(4, 256, 192)
    att_slots = by_ctx([att[j] for j in range(4)], ctx_at)
    att_slots = [narrow(t) for t in att_slots]
    got = [att_slots[0]] + [swap(att_slots[r], r) for r in (1, 2, 3)]
    attended = wide(jnp.concatenate(by_ctx(got, ctx_at), axis=1))
    out_own = a_slots[:, :, 96:144]
    out_other = swap(out_own, 1)
    core = ctx_at & 1
    first = jnp.where(core == 0, out_own, out_other)
    second = jnp.where(core == 0, out_other, out_own)
    full_out = by_block(jnp.concatenate([first, second], axis=2), dp_at).reshape(768, 768)
    mixed, pull_mix = jax.vjp(layer_norm, attended, vecs[1], vecs[4])
    mixed_low = narrow(mixed)
    own_f = wide(own)
    residual = own_f + jnp.dot(mixed_low, full_out, preferred_element_type=jnp.float32) + vecs[8]
    ffn_in, pull_ffn = jax.vjp(layer_norm, residual, vecs[2], vecs[5])
    ffn_low = narrow(ffn_in)
    up_0 = a_slots[:, :, :96]
    up_2 = swap(up_0, 2)
    up_1, up_3 = swap(up_0, 1), swap(up_2, 1)
    down_0, down_2 = b_slots[:, :, 0], b_slots[:, :, 1]
    down_1, down_3 = swap(down_0, 1), swap(down_2, 1)
    full_up = jnp.concatenate(
        [by_block(t, dp_at).reshape(768, 768) for t in by_ctx([up_0, up_1, up_2, up_3], ctx_at)], axis=1)
    full_down = jnp.stack(
        [by_block(t, dp_at) for t in by_ctx([down_0, down_1, down_2, down_3], ctx_at)], axis=1).reshape(3072, 768)
    mids = by_block(a_slots[:, :, 144:152], dp_at).reshape(8, 16, 384)
    mid_gain_f, mid_shift_f, up_bias_f = (wide(mids[:, i].reshape(3072)) for i in range(3))
    up_proj = jnp.dot(ffn_low, full_up, preferred_element_type=jnp.float32) + up_bias_f
    activated, pull_mid = jax.vjp(mid_norm, up_proj, mid_gain_f, mid_shift_f)
    act_low = narrow(activated)
    result = residual + jnp.dot(act_low, full_down, preferred_element_type=jnp.float32) + vecs[9]
    pos = ctx_at * rows + jnp.arange(rows, dtype=jnp.int32)
    valid = (pos < length).astype(jnp.float32)[:, None]
    layer_output = narrow(result * valid)[None]
    error = (result - wide(teacher[0])) * valid
    loss_part = 0.5 * jnp.sum(error * error)
    valid_part = jnp.sum(valid)
    down_low = narrow(error)
    bias_down = jnp.sum(wide(down_low), axis=0)
    down_grad = narrow(dots("rf,rd->fd", act_low, down_low))
    d_act = dots("rd,fd->rf", down_low, full_down)
    d_up, mid_gain_grad, mid_shift_grad = pull_mid(d_act)
    up_low = narrow(d_up)
    up_bias_grad = jnp.sum(wide(up_low), axis=0)
    up_grad = narrow(dots("rd,rf->df", ffn_low, up_low))
    d_ffn = dots("rf,df->rd", up_low, full_up)
    d_res, gain_two, shift_two = pull_ffn(d_ffn)
    d_residual = error + d_res
    branch_low = narrow(d_residual)
    bias_out = jnp.sum(wide(branch_low), axis=0)
    out_grad = narrow(dots("rd,re->de", mixed_low, branch_low))
    d_mixed = dots("re,de->rd", branch_low, full_out)
    d_att, gain_one, shift_one = pull_mix(d_mixed)
    do_low = narrow(d_att)
    do_tiles = by_ctx([do_low[:, 192 * j:192 * j + 192] for j in range(4)], ctx_at)
    do_got = [do_tiles[0]] + [swap(do_tiles[r], r) for r in (1, 2, 3)]
    do = jnp.concatenate(by_ctx(do_got, ctx_at)).reshape(1024, 3, 64)
    dterm = jnp.einsum("qhd,qhd->hq", wide(do), att.reshape(1024, 3, 64))
    dprob = dots("qhd,khd->hqk", do, v)
    dscore = narrow(prob * (dprob - dterm[..., None]))
    dq = narrow(dots("hqk,khd->qhd", dscore, k) * 0.125).reshape(1024, 192)
    dk = narrow(dots("hqk,qhd->khd", dscore, q) * 0.125).reshape(1024, 192)
    dv = narrow(dots("hqk,qhd->khd", narrow(prob), do)).reshape(1024, 192)
    dqkv = jnp.concatenate([dq, dk, dv], axis=1)
    sums = jnp.sum(wide(dqkv), axis=0)
    qkv_grad = dots("rd,re->de", normed_low, dqkv)
    d_normed = dots("re,de->rd", dqkv, w_q3)
    _, gain_zero, shift_zero = pull_in(d_normed)
    dn = by_ctx([t for t in d_normed.reshape(4, 256, 768)], ctx_at)
    dn_0 = dn[0] + wide(swap(narrow(dn[1]), 1))
    dn_2 = dn[2] + wide(swap(narrow(dn[3]), 1))
    d_own = dn_0 + wide(swap(narrow(dn_2), 2))
    _, pull_own = jax.vjp(lambda t: layer_norm(t, vecs[0], vecs[3]), own_f)
    hidden_grad = (d_residual + pull_own(d_own)[0])[None]
    place = jnp.zeros((768,), jnp.float32)
    bias_q_grad = lax.dynamic_update_slice(place, sums[:192], (192 * ctx_at,))
    bias_v_grad = lax.dynamic_update_slice(place, sums[384:], (192 * ctx_at,))
    small = jnp.stack([gain_zero, gain_one, gain_two, shift_zero, shift_one, shift_two,
                       bias_q_grad, bias_v_grad, bias_out, bias_down])
    small = small.reshape(10, 8, 96).transpose(1, 0, 2).reshape(8, 960)
    mid_small = jnp.stack([mid_gain_grad, mid_shift_grad, up_bias_grad]).reshape(3, 8, 384).transpose(1, 0, 2).reshape(8, 1152)
    loss_hi, loss_lo = halves(loss_part)
    scal = jnp.broadcast_to(jnp.stack([wide(loss_hi), wide(loss_lo), valid_part]), (8, 3))
    extra = jnp.concatenate([mid_small, small, scal, jnp.zeros((8, 8 * 576 - 2115), jnp.float32)], axis=1).reshape(8, 8, 576)
    packed = jnp.concatenate([qkv_grad.reshape(8, 96, 576), extra], axis=1)
    q_share = narrow(scattered_dp(to_slots(narrow(packed), dp_at)))
    up_tiles = by_ctx([to_slots(up_grad[:, 768 * j:768 * j + 768].reshape(8, 96, 768), dp_at) for j in range(4)], ctx_at)
    down_t = down_grad.reshape(8, 4, 96, 768)
    down_tiles = by_ctx([to_slots(down_t[:, j], dp_at) for j in range(4)], ctx_at)

    def ctx_sum(tiles):
        near = wide(tiles[0]) + wide(swap(tiles[1], 1))
        far = wide(tiles[2]) + wide(swap(tiles[3], 1))
        return narrow(near + wide(swap(narrow(far), 2)))

    up_share = narrow(scattered_dp(ctx_sum(up_tiles)))
    down_share = narrow(scattered_dp(ctx_sum(down_tiles)))
    out_b = out_grad.reshape(8, 2, 48, 768)
    out_slots = to_slots(lax.dynamic_index_in_dim(out_b, core, 1, keepdims=False), dp_at)
    out_sent = to_slots(lax.dynamic_index_in_dim(out_b, 1 - core, 1, keepdims=False), dp_at)
    out_pair = narrow(wide(out_slots) + wide(swap(out_sent, 1)))
    out_share = narrow(scattered_dp(out_pair))
    out_share = narrow(wide(out_share) + wide(swap(out_share, 2)))

    def ctx_all(share):
        far = swap(share, 2)
        return by_ctx([share, swap(share, 1), far, swap(far, 1)], ctx_at)

    q_all = ctx_all(q_share)
    grad_qkv = wide(jnp.concatenate([q_all[j][:96, 192 * p:192 * p + 192] for p in range(3) for j in range(4)], axis=1))
    rest = sum(wide(t[96:]) for t in q_all).reshape(8 * 576)
    mid_gain_out, mid_shift_out, up_bias_out = (rest[384 * i:384 * i + 384] for i in range(3))
    vec_out = rest[1152:2112].reshape(10, 96)
    loss = (rest[2112] + rest[2113]) / (rest[2114] * width)
    grad_up = wide(jnp.concatenate(ctx_all(up_share), axis=1))
    grad_down = wide(jnp.concatenate(ctx_all(down_share), axis=0))
    out_far = swap(out_share, 1)
    grad_out = wide(jnp.where(core == 0, jnp.concatenate([out_share, out_far]), jnp.concatenate([out_far, out_share])))
    return (layer_output, loss, hidden_grad, grad_qkv, grad_out, grad_up, grad_down,
            vec_out[:3].T, vec_out[3:6].T, vec_out[6:].T, mid_gain_out, mid_shift_out, up_bias_out)


def solution(mesh):
    step = fast if (mesh.shape["dp"], mesh.shape["ctx"]) == (8, 4) else shards
    placed = (
        P("dp", "ctx", None),
        P("dp", "ctx", None),
        P("dp"),
        P("dp", None),
        P("dp", None),
        P("dp", None),
        P("dp", None),
        P("dp", None),
        P("dp", None),
        P("dp", None),
        P("dp"),
        P("dp"),
        P("dp"),
    )
    return jax.shard_map(
        step,
        mesh=mesh,
        in_specs=placed,
        out_specs=(
            P("dp", "ctx", None),
            P(),
            P("dp", "ctx", None),
            P("dp", None),
            P("dp", None),
            P("dp", None),
            P("dp", None),
            P("dp", None),
            P("dp", None),
            P("dp", None),
            P("dp"),
            P("dp"),
            P("dp"),
        ),
        check_vma=False,
    )
```

```python
import math

import jax
import jax.numpy as jnp
from jax import lax
from jax.experimental import pallas as pl
from jax.experimental.pallas import tpu as pltpu
from jax.sharding import PartitionSpec as P

HEADS = 12
HEAD_DIM = 64


EPSILON = 1e-05
NEGATIVE = -1e30


def passed_along(value, axis, steps):
    count = lax.axis_size(axis)
    pairs = [(source, (source + steps) % count) for source in range(count)]
    return lax.ppermute(value, axis, pairs)


def passed_along_2(block, axis, distance):
    devices = range(lax.axis_size(axis))
    route = [(i - distance, i) for i in devices if i - distance in devices]
    return lax.ppermute(block, axis, route)


def layer_norm(values, gain_vec, shift_vec):
    average = jnp.mean(values, axis=-1, keepdims=True)
    centred = values - average
    variance = jnp.mean(centred * centred, axis=-1, keepdims=True)
    return centred * lax.rsqrt(variance + EPSILON) * gain_vec + shift_vec


def mid_norm(up_proj, gain_vec, shift_vec):
    return layer_norm(jax.nn.gelu(up_proj, approximate=False), gain_vec, shift_vec)


def split_heads(values):
    return values.reshape(values.shape[0], values.shape[1], HEADS, HEAD_DIM)


def key_mask(query_pos, key_start, key_count, lengths):
    key_pos = key_start + jnp.arange(key_count, dtype=jnp.int32)
    causal = key_pos[None, :] <= query_pos[:, None]
    inside = key_pos[None, :] < lengths[:, None]
    return causal[None, :, :] & inside[:, None, :]


def fold_keys(running, pieces, key_start, heads_q, query_pos, lengths):
    row_max, row_total, weighted = running
    key_piece, value_piece = pieces
    key_count = key_piece.shape[1]
    score_scale = 1.0 / math.sqrt(HEAD_DIM)
    scores = (
        jnp.einsum(
            "sqhd,skhd->shqk", heads_q, split_heads(key_piece), preferred_element_type=jnp.float32
        )
        * score_scale
    )
    allowed = key_mask(query_pos, key_start, key_count, lengths)[:, None]
    scores = jnp.where(allowed, scores, NEGATIVE)
    fresh_max = jnp.maximum(row_max, jnp.max(scores, axis=-1))
    exponent_vals = jnp.exp(scores - fresh_max[..., None])
    row_total = jnp.sum(exponent_vals, axis=-1)
    update = jnp.einsum(
        "shqk,skhd->sqhd",
        exponent_vals.astype(jnp.bfloat16),
        split_heads(value_piece),
        preferred_element_type=jnp.float32,
    )
    weighted = update
    return (fresh_max, row_total, weighted)


def grad_keys(
    heads_q, heads_do, log_total, dterm, key_piece, value_piece, key_start, query_pos, lengths
):
    seq_count, key_count = (key_piece.shape[0], key_piece.shape[1])
    heads_k = split_heads(key_piece)
    heads_v = split_heads(value_piece)
    score_scale = 1.0 / math.sqrt(HEAD_DIM)
    scores = (
        jnp.einsum("sqhd,skhd->shqk", heads_q, heads_k, preferred_element_type=jnp.float32)
        * score_scale
    )
    allowed = key_mask(query_pos, key_start, key_count, lengths)[:, None]
    probability = jnp.where(allowed, jnp.exp(scores - log_total[..., None]), 0.0)
    dprob = jnp.einsum("sqhd,skhd->shqk", heads_do, heads_v, preferred_element_type=jnp.float32)
    dscores = (probability * (dprob - dterm[..., None])).astype(jnp.bfloat16)
    dq_part = (
        jnp.einsum("shqk,skhd->sqhd", dscores, heads_k, preferred_element_type=jnp.float32)
        * score_scale
    )
    dk_part = (
        jnp.einsum("shqk,sqhd->skhd", dscores, heads_q, preferred_element_type=jnp.float32)
        * score_scale
    )
    dv_part = jnp.einsum(
        "shqk,sqhd->skhd",
        probability.astype(jnp.bfloat16),
        heads_do,
        preferred_element_type=jnp.float32,
    )
    return (
        dq_part,
        dk_part.reshape(seq_count, key_count, -1),
        dv_part.reshape(seq_count, key_count, -1),
    )


def shards(
    hidden,
    teacher,
    lengths,
    w_qkv,
    w_out,
    w_up,
    w_down,
    norm_gain,
    norm_shift,
    proj_bias,
    mid_gain,
    mid_shift,
    up_bias,
):
    (
        full_qkv,
        full_out,
        full_up,
        full_down,
        gain_full,
        shift_full,
        bias_full,
        mid_gain_full,
        mid_shift_full,
        up_bias_full,
    ) = (
        lax.all_gather(w_qkv, "dp", axis=0, tiled=True),
        lax.all_gather(w_out, "dp", axis=0, tiled=True),
        lax.all_gather(w_up, "dp", axis=0, tiled=True),
        lax.all_gather(w_down, "dp", axis=0, tiled=True),
        lax.all_gather(norm_gain, "dp", axis=0, tiled=True),
        lax.all_gather(norm_shift, "dp", axis=0, tiled=True),
        lax.all_gather(proj_bias, "dp", axis=0, tiled=True),
        lax.all_gather(mid_gain, "dp", axis=0, tiled=True),
        lax.all_gather(mid_shift, "dp", axis=0, tiled=True),
        lax.all_gather(up_bias, "dp", axis=0, tiled=True),
    )
    gain_f = gain_full.astype(jnp.float32)
    shift_f = shift_full.astype(jnp.float32)
    bias_f = bias_full.astype(jnp.float32)
    mid_gain_f = mid_gain_full.astype(jnp.float32)
    mid_shift_f = mid_shift_full.astype(jnp.float32)
    up_bias_f = up_bias_full.astype(jnp.float32)
    seq_count, local_rows, model_width = hidden.shape
    token_rows = seq_count * local_rows
    seq_shape = (seq_count, local_rows, model_width)
    ctx_place = lax.axis_index("ctx")
    ctx_parts = lax.axis_size("ctx")
    query_pos = ctx_place * local_rows + jnp.arange(local_rows, dtype=jnp.int32)
    last_query = ctx_place * local_rows + local_rows - 1
    valid_mask = (query_pos[None, :] < lengths[:, None]).astype(jnp.float32)
    valid_rows = valid_mask.reshape(token_rows, 1)
    hidden_rows = hidden.reshape(token_rows, model_width).astype(jnp.float32)
    normed, pull_in = jax.vjp(layer_norm, hidden_rows, gain_f[:, 0], shift_f[:, 0])
    normed_low = normed.astype(jnp.bfloat16)
    projected = jnp.dot(normed_low, full_qkv, preferred_element_type=jnp.float32)
    query_low = (projected[:, :model_width] + bias_f[:, 0]).astype(jnp.bfloat16).reshape(seq_shape)
    key_low = projected[:, model_width : 2 * model_width].astype(jnp.bfloat16).reshape(seq_shape)
    value_low = (
        (projected[:, 2 * model_width :] + bias_f[:, 1]).astype(jnp.bfloat16).reshape(seq_shape)
    )
    heads_q = split_heads(query_low)
    start_state = (
        jnp.full((seq_count, HEADS, local_rows), NEGATIVE, jnp.float32),
        jnp.zeros((seq_count, HEADS, local_rows), jnp.float32),
        jnp.zeros((seq_count, local_rows, HEADS, HEAD_DIM), jnp.float32),
    )
    pieces = (
        lax.all_gather(key_low, "ctx", axis=1, tiled=True),
        lax.all_gather(value_low, "ctx", axis=1, tiled=True),
    )
    key_start = jnp.int32(0)
    row_max, row_total, weighted = lax.cond(
        key_start <= last_query,
        lambda: fold_keys(start_state, pieces, key_start, heads_q, query_pos, lengths),
        lambda: start_state,
    )
    attended = weighted / jnp.transpose(row_total, (0, 2, 1))[..., None]
    log_total = row_max + jnp.log(row_total)
    attended_rows = attended.reshape(token_rows, model_width)
    mixed, pull_mix = jax.vjp(layer_norm, attended_rows, gain_f[:, 1], shift_f[:, 1])
    mixed_low = mixed.astype(jnp.bfloat16)
    residual = (
        hidden_rows
        + jnp.dot(mixed_low, full_out, preferred_element_type=jnp.float32)
        + bias_f[:, 2]
    )
    ffn_in, pull_ffn = jax.vjp(layer_norm, residual, gain_f[:, 2], shift_f[:, 2])
    ffn_low = ffn_in.astype(jnp.bfloat16)
    up_proj = jnp.dot(ffn_low, full_up, preferred_element_type=jnp.float32) + up_bias_f
    activated, pull_mid = jax.vjp(mid_norm, up_proj, mid_gain_f, mid_shift_f)
    act_low = activated.astype(jnp.bfloat16)
    result = (
        residual + jnp.dot(act_low, full_down, preferred_element_type=jnp.float32) + bias_f[:, 3]
    )
    layer_output = (result * valid_rows).astype(jnp.bfloat16).reshape(hidden.shape)
    error_rows = (
        result - teacher.reshape(token_rows, model_width).astype(jnp.float32)
    ) * valid_rows
    loss_total, valid_total = lax.psum(
        (0.5 * jnp.sum(error_rows * error_rows), jnp.sum(valid_mask)), ("dp", "ctx")
    )
    loss = loss_total / (valid_total * model_width)
    down_low = error_rows.astype(jnp.bfloat16)
    bias_down_grad = jnp.sum(down_low.astype(jnp.float32), axis=0)
    down_grad = jnp.einsum("rf,rd->fd", act_low, down_low, preferred_element_type=jnp.float32)
    d_act = jnp.einsum("rd,fd->rf", down_low, full_down, preferred_element_type=jnp.float32)
    d_up, mid_gain_grad, mid_shift_grad = pull_mid(d_act)
    up_low = d_up.astype(jnp.bfloat16)
    up_bias_grad = jnp.sum(up_low.astype(jnp.float32), axis=0)
    up_grad = jnp.einsum("rd,rf->df", ffn_low, up_low, preferred_element_type=jnp.float32)
    d_ffn = jnp.einsum("rf,df->rd", up_low, full_up, preferred_element_type=jnp.float32)
    d_res_norm, gain_two, shift_two = pull_ffn(d_ffn)
    d_residual = error_rows + d_res_norm
    branch_low = d_residual.astype(jnp.bfloat16)
    bias_out_grad = jnp.sum(branch_low.astype(jnp.float32), axis=0)
    out_grad = jnp.einsum("rd,re->de", mixed_low, branch_low, preferred_element_type=jnp.float32)
    d_mixed = jnp.einsum("re,de->rd", branch_low, full_out, preferred_element_type=jnp.float32)
    d_att, gain_one, shift_one = pull_mix(d_mixed)
    heads_do = split_heads(d_att.astype(jnp.bfloat16).reshape(seq_shape))
    dterm = jnp.einsum("sqhd,sqhd->shq", heads_do.astype(jnp.float32), attended)

    def grad_step(key_piece, value_piece, key_start):
        return grad_keys(
            heads_q,
            heads_do,
            log_total,
            dterm,
            key_piece,
            value_piece,
            key_start,
            query_pos,
            lengths,
        )

    dq_zero = jnp.zeros((seq_count, local_rows, HEADS, HEAD_DIM), jnp.float32)
    own_zero = jnp.zeros(seq_shape, jnp.float32)

    def pass_step(step_index, running):
        key_cur, value_cur, dk_run, dv_run, dq_sum = running
        owner = (ctx_place - step_index) % ctx_parts
        dq_part, dk_part, dv_part = lax.cond(
            owner <= ctx_place,
            lambda: grad_step(key_cur, value_cur, owner * local_rows),
            lambda: (dq_zero, own_zero, own_zero),
        )
        dk_run, dv_run = (
            passed_along((dk_run + dk_part).astype(jnp.bfloat16), "ctx", 1).astype(jnp.float32),
            passed_along((dv_run + dv_part).astype(jnp.bfloat16), "ctx", 1).astype(jnp.float32),
        )
        key_cur, value_cur = passed_along_2((key_cur, value_cur), "ctx", 1)
        return (key_cur, value_cur, dk_run, dv_run, dq_sum + dq_part)

    key_end, value_end, dk_own, dv_own, dq_sum = lax.fori_loop(
        0, ctx_parts, pass_step, (key_low, value_low, own_zero, own_zero, dq_zero)
    )
    dq_low = dq_sum.reshape(token_rows, model_width).astype(jnp.bfloat16)
    dk_low = dk_own.reshape(token_rows, model_width).astype(jnp.bfloat16)
    dv_low = dv_own.reshape(token_rows, model_width).astype(jnp.bfloat16)
    dqkv_low = jnp.concatenate([dq_low, dk_low, dv_low], axis=1)
    bias_q_grad = jnp.sum(dq_low.astype(jnp.float32), axis=0)
    bias_v_grad = jnp.sum(dv_low.astype(jnp.float32), axis=0)
    qkv_grad = jnp.einsum("rd,re->de", normed_low, dqkv_low, preferred_element_type=jnp.float32)
    d_normed = jnp.einsum("re,de->rd", dqkv_low, full_qkv, preferred_element_type=jnp.float32)
    d_in_norm, gain_zero, shift_zero = pull_in(d_normed)
    hidden_grad = (d_residual + d_in_norm).reshape(hidden.shape)
    gain_grad = jnp.stack([gain_zero, gain_one, gain_two], axis=1)
    shift_grad = jnp.stack([shift_zero, shift_one, shift_two], axis=1)
    bias_grad = jnp.stack([bias_q_grad, bias_v_grad, bias_out_grad, bias_down_grad], axis=1)
    shares = (
        lax.psum_scatter(
            qkv_grad.astype(jnp.bfloat16), "dp", scatter_dimension=0, tiled=True
        ).astype(jnp.float32),
        lax.psum_scatter(
            out_grad.astype(jnp.bfloat16), "dp", scatter_dimension=0, tiled=True
        ).astype(jnp.float32),
        lax.psum_scatter(
            up_grad.astype(jnp.bfloat16), "dp", scatter_dimension=0, tiled=True
        ).astype(jnp.float32),
        lax.psum_scatter(
            down_grad.astype(jnp.bfloat16), "dp", scatter_dimension=0, tiled=True
        ).astype(jnp.float32),
        lax.psum_scatter(
            gain_grad.astype(jnp.bfloat16), "dp", scatter_dimension=0, tiled=True
        ).astype(jnp.float32),
        lax.psum_scatter(
            shift_grad.astype(jnp.bfloat16), "dp", scatter_dimension=0, tiled=True
        ).astype(jnp.float32),
        lax.psum_scatter(
            bias_grad.astype(jnp.bfloat16), "dp", scatter_dimension=0, tiled=True
        ).astype(jnp.float32),
        lax.psum_scatter(
            mid_gain_grad.astype(jnp.bfloat16), "dp", scatter_dimension=0, tiled=True
        ).astype(jnp.float32),
        lax.psum_scatter(
            mid_shift_grad.astype(jnp.bfloat16), "dp", scatter_dimension=0, tiled=True
        ).astype(jnp.float32),
        lax.psum_scatter(
            up_bias_grad.astype(jnp.bfloat16), "dp", scatter_dimension=0, tiled=True
        ).astype(jnp.float32),
    )
    summed = (
        lax.psum(shares[0].astype(jnp.bfloat16), "ctx").astype(jnp.float32),
        lax.psum(shares[1].astype(jnp.bfloat16), "ctx").astype(jnp.float32),
        lax.psum(shares[2].astype(jnp.bfloat16), "ctx").astype(jnp.float32),
        lax.psum(shares[3].astype(jnp.bfloat16), "ctx").astype(jnp.float32),
        lax.psum(shares[4].astype(jnp.bfloat16), "ctx").astype(jnp.float32),
        lax.psum(shares[5].astype(jnp.bfloat16), "ctx").astype(jnp.float32),
        lax.psum(shares[6].astype(jnp.bfloat16), "ctx").astype(jnp.float32),
        lax.psum(shares[7].astype(jnp.bfloat16), "ctx").astype(jnp.float32),
        lax.psum(shares[8].astype(jnp.bfloat16), "ctx").astype(jnp.float32),
        lax.psum(shares[9].astype(jnp.bfloat16), "ctx").astype(jnp.float32),
    )
    return (
        layer_output,
        loss,
        hidden_grad,
        summed[0],
        summed[1],
        summed[2],
        summed[3],
        summed[4],
        summed[5],
        summed[6],
        summed[7],
        summed[8],
        summed[9],
    )


AXES = ("dp", "ctx")


def swap(value, mask):
    count = lax.axis_size("dp") * lax.axis_size("ctx")
    return lax.ppermute(value, AXES, [(i, i ^ mask) for i in range(count)])


def near_of(piece):
    return jnp.stack([piece] + [swap(piece, 8 * step) for step in (1, 2, 3)])


def wide(value):
    return value.astype(jnp.float32)


def narrow(value):
    return value.astype(jnp.bfloat16)


def shared_dp(keep, send):
    kept = wide(keep) + wide(swap(send, 4))
    sent = narrow(kept)
    return kept[0] + sum(wide(swap(sent[step], 8 * step)) for step in (1, 2, 3))


def by_ctx(tiles, ctx_at):
    stack = jnp.stack(tiles)
    return [lax.dynamic_index_in_dim(stack, ctx_at ^ j, 0, keepdims=False) for j in range(4)]


VMEM_BYTES = 56 * 1024 * 1024


def whole(shape):
    return pl.BlockSpec(tuple(shape), lambda i: (0,) * len(shape), pipeline_mode=pl.Buffered(1))


def call(body, ins, outs, scratch=(), flops=0, moved=0):
    pairs = [v if isinstance(v, tuple) else (v, whole(v.shape)) for v in ins[1:]]
    return pl.pallas_call(
        body,
        grid=(1,),
        in_specs=[pl.BlockSpec(memory_space=pltpu.SMEM)] + [spec for _, spec in pairs],
        out_specs=[whole(shape) for shape, _ in outs],
        out_shape=[jax.ShapeDtypeStruct(shape, dtype) for shape, dtype in outs],
        scratch_shapes=[pltpu.VMEM(shape, dtype) for shape, dtype in scratch],
        compiler_params=pltpu.CompilerParams(vmem_limit_bytes=VMEM_BYTES),
        cost_estimate=pl.CostEstimate(flops=flops, bytes_accessed=moved, transcendentals=0),
    )(ins[0], *[v for v, _ in pairs])


BF, F32 = jnp.bfloat16, jnp.float32


def contract(a, b, da, db):
    return lax.dot_general(a, b, (((da,), (db,)), ((), ())), preferred_element_type=F32)


def block_of(sc, xr, zr):
    return 2 * ((sc[0] >> 1) ^ zr) + ((sc[0] & 1) ^ xr)


def slot_of(sc, block):
    return ((block & 1) ^ (sc[0] & 1)) * 4 + ((block >> 1) ^ (sc[0] >> 1))


def lay(sc, scr, near, far, rows, stride, offset=0):
    for xr, ref in ((0, near), (1, far)):
        for zr in range(4):
            at = pl.multiple_of(stride * block_of(sc, xr, zr) + offset, 16)
            scr[pl.ds(at, rows), :] = ref[zr]


def moments(value):
    average = jnp.mean(value, axis=-1, keepdims=True)
    centred = value - average
    scale = lax.rsqrt(jnp.mean(centred * centred, axis=-1, keepdims=True) + EPSILON)
    return centred * scale, scale


def norm_back(grad, hat, scale):
    return scale * (grad - jnp.mean(grad, axis=-1, keepdims=True) - hat * jnp.mean(grad * hat, axis=-1, keepdims=True))


def mine(ctx_at, row):
    out = row[:, :192]
    for j in range(1, 4):
        out = jnp.where(ctx_at == j, row[:, 192 * j:192 * j + 192], out)
    return out


def pack_body(sc, w, gain, shift, bias, out, scr):
    scr[...] = jnp.zeros((16, 128), F32)
    scr[0:3, :96] = gain[...].astype(F32)
    scr[3:6, :96] = shift[...].astype(F32)
    scr[6:10, :96] = bias[...].astype(F32)
    small = scr[...].T[:96].astype(BF)
    for j in range(4):
        @pl.when(sc[1] == j)
        def _():
            cols = [w[:, 768 * part + 192 * j:768 * part + 192 * j + 192] for part in range(3)]
            out[...] = jnp.concatenate(cols + [small, jnp.zeros((96, 48), BF)], axis=1)


def attend_body(sc, h0, h1, h2, h3, wa, wb, a0, a1, a2, a3, q_o, k_o, v_o, lse_o, ot_o, n_o, vec_o, w_scr):
    ctx_at, length = sc[1], sc[2]
    lay(sc, w_scr, wa, wb, 96, 96)
    vec = w_scr[:, 512:640].astype(F32).T[64:80]
    vec_o[...] = vec
    bias_q, bias_v = mine(ctx_at, vec[6:7]), mine(ctx_at, vec[7:8])
    for r, ref in enumerate((h0, h1, h2, h3)):
        rows = pl.ds(pl.multiple_of((ctx_at ^ r) * 256, 256), 256)
        hat, _ = moments(ref[...].astype(F32))
        normed = (hat * vec[0:1] + vec[3:4]).astype(BF)
        n_o[rows, :] = normed
        p = jnp.dot(normed, w_scr[...], preferred_element_type=F32)
        for h in range(3):
            q_o[h, rows, :] = ((p[:, 64 * h:64 * h + 64] + bias_q[:, 64 * h:64 * h + 64]) * 0.125).astype(BF)
            k_o[h, rows, :] = p[:, 192 + 64 * h:256 + 64 * h].astype(BF)
            v_o[h, rows, :] = (p[:, 384 + 64 * h:448 + 64 * h] + bias_v[:, 64 * h:64 * h + 64]).astype(BF)

    def head(h, carry):
        for i in range(4):
            n = 256 * (i + 1)
            scores = contract(k_o[h, :n, :], q_o[h, 256 * i:256 * i + 256, :], 1, 1)
            limit = jnp.minimum(256 * i + lax.broadcasted_iota(jnp.int32, (1, 256), 1), length - 1)
            scores = jnp.where(lax.broadcasted_iota(jnp.int32, (n, 256), 0) <= limit, scores, NEGATIVE)
            top = jnp.max(scores, axis=0, keepdims=True)
            grown = jnp.exp(scores - top)
            total = jnp.sum(grown, axis=0, keepdims=True)
            out = contract(v_o[h, :n, :], grown.astype(BF), 0, 0) / total
            ot_o[i, pl.ds(pl.multiple_of(64 * h, 64), 64), :] = out
            lse_o[h, i:i + 1, :] = top + jnp.log(total)
        return carry

    lax.fori_loop(0, 3, head, 0)
    for r, ref in enumerate((a0, a1, a2, a3)):
        ref[...] = ot_o[ctx_at ^ r].T.astype(BF)


def attend(sc, hids, wa, wb):
    rows = (256, 192)
    return call(
        attend_body, [sc, *hids, wa, wb],
        [(rows, BF)] * 4 + [((3, 1024, 64), BF)] * 3
        + [((3, 8, 256), F32), ((4, 192, 256), F32), ((1024, 768), BF), ((16, 768), F32)],
        [((768, 640), BF)], flops=2 * 10 ** 9, moved=8 * 10 ** 6)


def attend_back_body(sc, d0, d1, d2, d3, q_i, k_i, v_i, lse_i, ot_i, n_i, h0, h1, h2, h3, wa, wb, vec_i, side_e, side_d, mids,
                     n0, n1, n2, n3, keep, send, w_scr, do_scr, dq_s, dk_s, dv_s, dk_acc, dv_acc, all_scr, g_scr):
    ctx_at, length = sc[1], sc[2]
    lay(sc, w_scr, wa, wb, 96, 96)
    for r, ref in enumerate((d0, d1, d2, d3)):
        rows = pl.ds(pl.multiple_of((ctx_at ^ r) * 256, 256), 256)
        value = ref[...]
        for h in range(3):
            do_scr[h, rows, :] = value[:, 64 * h:64 * h + 64]

    def head(h, carry):
        for i in (3, 2, 1, 0):
            n = 256 * (i + 1)
            mine_rows = slice(256 * i, 256 * i + 256)
            q, do, k = q_i[h, mine_rows, :], do_scr[h, mine_rows, :], k_i[h, :n, :]
            out = ot_i[i, pl.ds(pl.multiple_of(64 * h, 64), 64), :]
            dterm = jnp.sum(do.astype(F32).T * out, axis=0, keepdims=True)
            limit = jnp.minimum(256 * i + lax.broadcasted_iota(jnp.int32, (1, 256), 1), length - 1)
            prob = jnp.exp(contract(k, q, 1, 1) - lse_i[h, i:i + 1, :])
            prob = jnp.where(lax.broadcasted_iota(jnp.int32, (n, 256), 0) <= limit, prob, 0.0)
            dscore = (prob * (contract(v_i[h, :n, :], do, 1, 1) - dterm)).astype(BF)
            dv = jnp.dot(prob.astype(BF), do, preferred_element_type=F32)
            dk = jnp.dot(dscore, q, preferred_element_type=F32)
            if i == 3:
                dv_acc[...] = dv
                dk_acc[...] = dk
            else:
                dv_acc[:n, :] += dv
                dk_acc[:n, :] += dk
            dq_s[h, mine_rows, :] = (contract(k, dscore, 0, 0) * 0.125).T.astype(BF)
        dk_s[h] = dk_acc[...].astype(BF)
        dv_s[h] = dv_acc[...].astype(BF)
        return carry

    lax.fori_loop(0, 3, head, 0)
    for i in range(4):
        rows = slice(256 * i, 256 * i + 256)
        all_scr[rows, :] = jnp.concatenate([s[h, rows, :] for s in (dq_s, dk_s, dv_s) for h in range(3)], axis=1)
    sums = jnp.sum(all_scr[...].astype(F32), axis=0, keepdims=True)
    bias_q = jnp.concatenate([jnp.where(ctx_at == j, sums[:, :192], 0.0) for j in range(4)], axis=1)
    bias_v = jnp.concatenate([jnp.where(ctx_at == j, sums[:, 384:], 0.0) for j in range(4)], axis=1)
    gain_sum, shift_sum = jnp.zeros((1, 768), F32), jnp.zeros((1, 768), F32)
    for r, (ref, out) in enumerate(((h0, n0), (h1, n1), (h2, n2), (h3, n3))):
        rows = pl.ds(pl.multiple_of((ctx_at ^ r) * 256, 256), 256)
        grad = contract(all_scr[rows, :], w_scr[:, :576], 1, 1)
        hat, _ = moments(ref[...].astype(F32))
        gain_sum += jnp.sum(grad * hat, axis=0, keepdims=True)
        shift_sum += jnp.sum(grad, axis=0, keepdims=True)
        out[...] = grad.astype(BF)
    rows16 = jnp.concatenate(
        [gain_sum, side_e[0:2], shift_sum, side_e[2:4], bias_q, bias_v, side_e[4:5], side_d[0:2], jnp.zeros((5, 768), F32)], axis=0)
    w_grad = contract(n_i[...], all_scr[...], 0, 0)
    for b in range(8):
        at = slot_of(sc, b)
        extra = jnp.concatenate([mids[:, 384 * b:384 * b + 384], rows16[:, 96 * b:96 * b + 96], jnp.zeros((16, 96), F32)], axis=1)
        g_scr[at, :96, :] = w_grad[96 * b:96 * b + 96].astype(BF)
        g_scr[at, 96:112, :] = extra.astype(BF)
    keep[...] = g_scr[:4]
    send[...] = g_scr[4:]


def attend_back(sc, douts, saved, hids, wa, wb, side_e, side_d, mids):
    q, k, v, lse, ot, normed, vec = saved
    return call(
        attend_back_body, [sc, *douts, q, k, v, lse, ot, normed, *hids, wa, wb, vec, side_e, side_d, mids],
        [((256, 768), BF)] * 4 + [((4, 112, 576), BF)] * 2,
        [((768, 640), BF), ((3, 1024, 64), BF), ((3, 1024, 64), BF), ((3, 1024, 64), BF), ((3, 1024, 64), BF),
         ((1024, 64), F32), ((1024, 64), F32), ((1024, 576), BF), ((8, 112, 576), BF)],
        flops=4 * 10 ** 9, moved=12 * 10 ** 6)


def part(rows, at):
    return pl.BlockSpec((4, rows, 768), lambda i: (0, at, 0), pipeline_mode=pl.Buffered(1))


def lay_out(sc, scr, own_near, own_far, other_near, other_far):
    core = sc[1] & 1
    lay(sc, scr, own_near, own_far, 48, 96, 48 * core)
    lay(sc, scr, other_near, other_far, 48, 96, 48 * (1 - core))


def lay_down(sc, scr, own_near, own_far, other_near, other_far):
    for c, refs in ((0, (own_near, own_far)), (1, (other_near, other_far))):
        for y in (0, 1):
            offset = 96 * (sc[1] ^ (2 * y + c))
            for xr in (0, 1):
                for zr in range(4):
                    at = pl.multiple_of(384 * block_of(sc, xr, zr) + offset, 32)
                    scr[pl.ds(at, 96), :] = refs[xr][zr, y]


def join_heads(sc, scr, pieces):
    for r, ref in enumerate(pieces):
        scr[r] = ref[...]
    return jnp.concatenate([scr[sc[1] ^ j] for j in range(4)], axis=1).astype(F32)


def mid_body(sc, g0, g1, g2, g3, own, vec, on, of, tn, tf, mixed_o, resid_o, ffn_o, w_scr, a_scr):
    lay_out(sc, w_scr, on, of, tn, tf)
    hat, _ = moments(join_heads(sc, a_scr, (g0, g1, g2, g3)))
    mixed = (hat * vec[1:2] + vec[4:5]).astype(BF)
    mixed_o[...] = mixed
    resid = own[...].astype(F32) + jnp.dot(mixed, w_scr[...], preferred_element_type=F32) + vec[8:9]
    resid_o[...] = resid
    hat, _ = moments(resid)
    ffn_o[...] = (hat * vec[2:3] + vec[5:6]).astype(BF)


def up_body(sc, ffn, w0n, w0f, w1n, w1f, w2n, w2f, w3n, w3f, mn, mf, act_o, hat_o, slope_o, scale_o, nat_o,
            w_scr, g_scr, m_scr):
    for xr, ref in ((0, mn), (1, mf)):
        for zr in range(4):
            m_scr[block_of(sc, xr, zr)] = ref[zr].astype(F32)
    flat = [m_scr[b] for b in range(8)]
    for j in range(4):
        two = flat[2 * j:2 * j + 2]
        nat_o[j, 0:1, :] = jnp.concatenate([m[0:1, :384] for m in two], axis=1)
        nat_o[j, 1:2, :] = jnp.concatenate([m[0:1, 384:] for m in two], axis=1)
        nat_o[j, 2:3, :] = jnp.concatenate([m[1:2, :384] for m in two], axis=1)
        nat_o[j, 3:8, :] = jnp.zeros((5, 768), F32)
    value = ffn[...]
    total = jnp.zeros((256, 1), F32)
    for t, (near, far) in enumerate(((w0n, w0f), (w1n, w1f), (w2n, w2f), (w3n, w3f))):
        j = sc[1] ^ t
        lay(sc, w_scr.at[t % 2], near, far, 96, 96)
        up = jnp.dot(value, w_scr[t % 2], preferred_element_type=F32) + nat_o[j, 2:3, :]
        chance = 0.5 * (1.0 + lax.erf(up * math.sqrt(0.5)))
        slope_o[j] = (chance + up * jnp.exp(-0.5 * up * up) * (1.0 / math.sqrt(2.0 * math.pi))).astype(BF)
        gelu = up * chance
        g_scr[j] = gelu
        total += jnp.sum(gelu, axis=-1, keepdims=True)
    average = total * (1.0 / 3072)
    square = jnp.zeros((256, 1), F32)
    for j in range(4):
        centred = g_scr[j] - average
        square += jnp.sum(centred * centred, axis=-1, keepdims=True)
    scale = lax.rsqrt(square * (1.0 / 3072) + EPSILON)
    scale_o[...] = scale
    for j in range(4):
        hat = (g_scr[j] - average) * scale
        hat_o[j] = hat.astype(BF)
        act_o[j] = (hat * nat_o[j, 0:1, :] + nat_o[j, 1:2, :]).astype(BF)


def down_body(sc, act, resid, teacher, vec, on, of, tn, tf, out_o, err_o, low_o, side_o, w_scr):
    lay_down(sc, w_scr, on, of, tn, tf)
    result = resid[...] + vec[9:10]
    for j in range(4):
        result += jnp.dot(act[j], w_scr[768 * j:768 * j + 768, :], preferred_element_type=F32)
    pos = sc[1] * 256 + lax.broadcasted_iota(jnp.int32, (256, 1), 0)
    valid = jnp.where(pos < sc[2], 1.0, 0.0)
    out_o[...] = (result * valid).astype(BF)
    error = (result - teacher[...].astype(F32)) * valid
    err_o[...] = error
    low = error.astype(BF)
    low_o[...] = low
    side_o[0:1, :] = jnp.sum(low.astype(F32), axis=0, keepdims=True)
    loss = 0.5 * jnp.sum(jnp.sum(error * error, axis=0, keepdims=True), axis=1, keepdims=True)
    count = jnp.sum(valid, axis=0, keepdims=True)
    high = loss.astype(BF).astype(F32)
    lane = lax.broadcasted_iota(jnp.int32, (1, 768), 1) % 96
    side_o[1:2, :] = jnp.where(lane == 0, high, jnp.where(lane == 1, loss - high, jnp.where(lane == 2, count, 0.0)))
    side_o[2:8, :] = jnp.zeros((6, 768), F32)


def down_grad_body(sc, act, low, keep, send, g_scr):
    value = low[...]
    for j in range(4):
        grad = contract(act[j], value, 0, 0).astype(BF)
        for half in (0, 1):
            at = slot_of(sc, 2 * j + half)
            for q in range(4):
                g_scr[sc[1] ^ q, at] = grad[384 * half + 96 * q:384 * half + 96 * q + 96]
    for y in (0, 1):
        keep[y] = g_scr[2 * y]
        send[y] = g_scr[2 * y + 1]


def ffn_back_body(sc, low, err, resid, hat_i, slope, scale, nat, don, dof, dtn, dtf,
                  w0n, w0f, w1n, w1f, w2n, w2f, w3n, w3f, on, of, tn, tf, vec, g0, g1, g2, g3,
                  up_o, branch_o, dres_o, p0, p1, p2, p3, side_o, mids_o, wd_scr, w_scr, dh_scr, a_scr):
    lay_down(sc, wd_scr, don, dof, dtn, dtf)
    value = low[...]
    first, second = jnp.zeros((256, 1), F32), jnp.zeros((256, 1), F32)
    for j in range(4):
        grad = contract(value, wd_scr[768 * j:768 * j + 768, :], 1, 1)
        hat = hat_i[j].astype(F32)
        cols = slice(768 * j, 768 * j + 768)
        mids_o[0:1, cols] = jnp.sum(grad * hat, axis=0, keepdims=True)
        mids_o[1:2, cols] = jnp.sum(grad, axis=0, keepdims=True)
        grad = grad * nat[j, 0:1, :]
        dh_scr[j] = grad
        first += jnp.sum(grad, axis=-1, keepdims=True)
        second += jnp.sum(grad * hat, axis=-1, keepdims=True)
    first, second = first * (1.0 / 3072), second * (1.0 / 3072)
    for j in range(4):
        hat = hat_i[j].astype(F32)
        grad = (scale[...] * (dh_scr[j] - first - hat * second) * slope[j].astype(F32)).astype(BF)
        up_o[j] = grad
        mids_o[2:3, 768 * j:768 * j + 768] = jnp.sum(grad.astype(F32), axis=0, keepdims=True)
    mids_o[3:16, :] = jnp.zeros((13, 3072), F32)
    grad = jnp.zeros((256, 768), F32)
    for t, (near, far) in enumerate(((w0n, w0f), (w1n, w1f), (w2n, w2f), (w3n, w3f))):
        lay(sc, w_scr.at[t % 2], near, far, 96, 96)
        grad += contract(up_o[sc[1] ^ t], w_scr[t % 2], 1, 1)
    hat, factor = moments(resid[...])
    side_o[1:2, :] = jnp.sum(grad * hat, axis=0, keepdims=True)
    side_o[3:4, :] = jnp.sum(grad, axis=0, keepdims=True)
    dres = err[...] + norm_back(grad * vec[2:3], hat, factor)
    dres_o[...] = dres
    branch = dres.astype(BF)
    branch_o[...] = branch
    side_o[4:5, :] = jnp.sum(branch.astype(F32), axis=0, keepdims=True)
    lay_out(sc, w_scr.at[0], on, of, tn, tf)
    grad = contract(branch, w_scr[0], 1, 1)
    hat, factor = moments(join_heads(sc, a_scr, (g0, g1, g2, g3)))
    side_o[0:1, :] = jnp.sum(grad * hat, axis=0, keepdims=True)
    side_o[2:3, :] = jnp.sum(grad, axis=0, keepdims=True)
    side_o[5:8, :] = jnp.zeros((3, 768), F32)
    grad = norm_back(grad * vec[1:2], hat, factor).astype(BF)
    for j in range(4):
        a_scr[j] = grad[:, 192 * j:192 * j + 192]
    for r, ref in enumerate((p0, p1, p2, p3)):
        ref[...] = a_scr[sc[1] ^ r]


def up_grad_body(sc, ffn, up, mixed, branch, keep, send, out_keep, out_send, g_scr, o_scr):
    value = ffn[...]
    for j in range(4):
        grad = contract(value, up[j], 0, 0).astype(BF)
        for b in range(8):
            g_scr[sc[1] ^ j, slot_of(sc, b)] = grad[96 * b:96 * b + 96]
    for y in (0, 1):
        keep[y] = g_scr[2 * y]
        send[y] = g_scr[2 * y + 1]
    grad = contract(mixed[...], branch[...], 0, 0).astype(BF)
    for b in range(8):
        for c in (0, 1):
            o_scr[(sc[1] & 1) ^ c, slot_of(sc, b)] = grad[96 * b + 48 * c:96 * b + 48 * c + 48]
    out_keep[...] = o_scr[0]
    out_send[...] = o_scr[1]


def both(value):
    return tuple(swap(v, 1) for v in value)


def fast(
    hidden, teacher, lengths, w_qkv, w_out, w_up, w_down, norm_gain, norm_shift, proj_bias,
    mid_gain, mid_shift, up_bias,
):
    dp_at, ctx_at = lax.axis_index("dp"), lax.axis_index("ctx")
    core = ctx_at & 1
    sc = jnp.stack([dp_at, ctx_at, lengths[0]]).astype(jnp.int32)
    own = hidden[0]
    tall = (256, 768)
    h_y = swap(own, 2)
    h_c = swap(own, 1)
    piece = call(pack_body, [sc, w_qkv, norm_gain.T, norm_shift.T, proj_bias.T], [((96, 640), BF)], [((16, 128), F32)])[0]
    q_near = near_of(piece)
    q_far = swap(q_near, 4)
    h_yc = swap(h_y, 1)
    mid_rows = jnp.concatenate([mid_gain, mid_shift, up_bias, jnp.zeros((13 * 384,), BF)]).reshape(8, 768)
    piece_a = jnp.concatenate([
        lax.dynamic_slice(w_up, (0, 768 * ctx_at), (96, 768)),
        lax.dynamic_slice(w_out, (48 * core, 0), (48, 768)), mid_rows])
    a_near = near_of(piece_a)
    a_far = swap(a_near, 4)
    down4 = w_down.reshape(4, 96, 768)
    piece_b = jnp.stack([lax.dynamic_index_in_dim(down4, ctx_at ^ t, 0, keepdims=False) for t in (0, 2)])
    b_near = near_of(piece_b)
    b_far = swap(b_near, 4)

    hids = [own, h_c, h_y, h_yc]
    *att, q, k, v, lse, ot, normed, vec = attend(sc, hids, q_near, q_far)
    got = [att[0]] + [swap(att[r], r) for r in (1, 2, 3)]
    a_own = (a_near, a_far)
    a_other = both(a_own)
    outs = [(t, part(48, 2)) for t in a_own + a_other]
    mixed, resid, ffn = call(
        mid_body, [sc, *got, own, vec, *outs], [(tall, BF), (tall, F32), (tall, BF)],
        [((768, 768), BF), ((4, 256, 192), BF)], flops=3 * 10 ** 8, moved=3 * 10 ** 6)
    y_own = tuple(swap(t[:, :96], 2) for t in a_own)
    y_other = both(y_own)
    ups = [(t, part(96, 0)) for t in a_own + a_other] + [*y_own, *y_other]
    four = (4, 256, 768)
    act, hat, slope, scale, nat = call(
        up_body, [sc, ffn, *ups] + [(t, part(8, 18)) for t in a_own],
        [(four, BF), (four, BF), (four, BF), ((256, 1), F32), ((4, 8, 768), F32)],
        [((2, 768, 768), BF), (four, F32), ((8, 8, 768), F32)], flops=12 * 10 ** 8, moved=10 ** 7)
    downs = (b_near, b_far) + both((b_near, b_far))
    out, err, low, side_d = call(
        down_body, [sc, act, resid, teacher[0], vec, *downs],
        [(tall, BF), (tall, F32), (tall, BF), ((8, 768), F32)], [((3072, 768), BF)], flops=12 * 10 ** 8, moved=8 * 10 ** 6)
    halves_of = ((2, 8, 96, 768), BF)
    down_keep, down_send = call(
        down_grad_body, [sc, act, low], [halves_of] * 2, [((4, 8, 96, 768), BF)], flops=12 * 10 ** 8, moved=7 * 10 ** 6)
    *pieces, side_e, mids = call(
        ffn_back_body, [sc, low, err, resid, hat, slope, scale, nat, *downs, *ups, *outs, vec, *got],
        [(four, BF), (tall, BF), (tall, F32)] + [((256, 192), BF)] * 4 + [((8, 768), F32), ((16, 3072), F32)],
        [((3072, 768), BF), ((2, 768, 768), BF), (four, F32), ((4, 256, 192), BF)], flops=27 * 10 ** 8, moved=2 * 10 ** 7)
    up_low, branch, d_res, *d_att = pieces
    up_keep, up_send, out_keep, out_send = call(
        up_grad_body, [sc, ffn, up_low, mixed, branch], [halves_of] * 2 + [((8, 48, 768), BF)] * 2,
        [((4, 8, 96, 768), BF), ((2, 8, 48, 768), BF)], flops=15 * 10 ** 8, moved=8 * 10 ** 6)
    d_got = [d_att[0]] + [swap(d_att[r], r) for r in (1, 2, 3)]
    *dn, q_keep, q_send = attend_back(sc, d_got, (q, k, v, lse, ot, normed, vec), hids, q_near, q_far, side_e, side_d, mids)
    dn_0 = wide(dn[0]) + wide(swap(dn[1], 1))
    dn_2 = wide(dn[2]) + wide(swap(dn[3], 1))
    d_own = dn_0 + wide(swap(narrow(dn_2), 2))
    _, pull_own = jax.vjp(lambda t: layer_norm(t, vec[0], vec[3]), wide(own))
    hidden_grad = (d_res + pull_own(d_own)[0])[None]
    q_share = narrow(shared_dp(q_keep, q_send))

    def ctx_sum(keep, send):
        pair = wide(keep) + wide(swap(send, 1))
        total = pair[0] + wide(swap(narrow(pair[1]), 2))
        return narrow(total[:4]), narrow(total[4:])

    down_share = narrow(shared_dp(*ctx_sum(down_keep, down_send)))
    up_share = narrow(shared_dp(*ctx_sum(up_keep, up_send)))
    out_pair = wide(out_keep) + wide(swap(out_send, 1))
    out_share = narrow(shared_dp(narrow(out_pair[:4]), narrow(out_pair[4:])))
    out_share = narrow(wide(out_share) + wide(swap(out_share, 2)))

    def ctx_all(share):
        far = swap(share, 2)
        return by_ctx([share, swap(share, 1), far, swap(far, 1)], ctx_at)

    q_all = ctx_all(q_share)
    grad_qkv = wide(jnp.concatenate([q_all[j][:96, 192 * p:192 * p + 192] for p in range(3) for j in range(4)], axis=1))
    rest = sum(wide(t[96:]) for t in q_all)
    mid_gain_out, mid_shift_out, up_bias_out = (rest[i, :384] for i in range(3))
    vec_out = rest[:10, 384:480]
    loss = (rest[10, 384] + rest[10, 385]) / (rest[10, 386] * hidden.shape[2])
    grad_up = wide(jnp.concatenate(ctx_all(up_share), axis=1))
    grad_down = wide(jnp.concatenate(ctx_all(down_share), axis=0))
    out_far = swap(out_share, 1)
    grad_out = wide(jnp.where(core == 0, jnp.concatenate([out_share, out_far]), jnp.concatenate([out_far, out_share])))
    return (out[None], loss, hidden_grad, grad_qkv, grad_out, grad_up, grad_down,
            vec_out[:3].T, vec_out[3:6].T, vec_out[6:].T, mid_gain_out, mid_shift_out, up_bias_out)


def solution(mesh):
    step = fast if (mesh.shape["dp"], mesh.shape["ctx"]) == (8, 4) else shards
    placed = (
        P("dp", "ctx", None),
        P("dp", "ctx", None),
        P("dp"),
        P("dp", None),
        P("dp", None),
        P("dp", None),
        P("dp", None),
        P("dp", None),
        P("dp", None),
        P("dp", None),
        P("dp"),
        P("dp"),
        P("dp"),
    )
    return jax.shard_map(
        step,
        mesh=mesh,
        in_specs=placed,
        out_specs=(
            P("dp", "ctx", None),
            P(),
            P("dp", "ctx", None),
            P("dp", None),
            P("dp", None),
            P("dp", None),
            P("dp", None),
            P("dp", None),
            P("dp", None),
            P("dp", None),
            P("dp"),
            P("dp"),
            P("dp"),
        ),
        check_vma=False,
    )
```

```python
import math

import jax
import jax.numpy as jnp
from jax import lax
from jax.experimental import pallas as pl
from jax.experimental.pallas import tpu as pltpu
from jax.sharding import PartitionSpec as P

HEADS = 12
HEAD_DIM = 64


EPSILON = 1e-05
NEGATIVE = -1e30


def passed_along(value, axis, steps):
    count = lax.axis_size(axis)
    pairs = [(source, (source + steps) % count) for source in range(count)]
    return lax.ppermute(value, axis, pairs)


def passed_along_2(block, axis, distance):
    devices = range(lax.axis_size(axis))
    route = [(i - distance, i) for i in devices if i - distance in devices]
    return lax.ppermute(block, axis, route)


def layer_norm(values, gain_vec, shift_vec):
    average = jnp.mean(values, axis=-1, keepdims=True)
    centred = values - average
    variance = jnp.mean(centred * centred, axis=-1, keepdims=True)
    return centred * lax.rsqrt(variance + EPSILON) * gain_vec + shift_vec


def mid_norm(up_proj, gain_vec, shift_vec):
    return layer_norm(jax.nn.gelu(up_proj, approximate=False), gain_vec, shift_vec)


def split_heads(values):
    return values.reshape(values.shape[0], values.shape[1], HEADS, HEAD_DIM)


def key_mask(query_pos, key_start, key_count, lengths):
    key_pos = key_start + jnp.arange(key_count, dtype=jnp.int32)
    causal = key_pos[None, :] <= query_pos[:, None]
    inside = key_pos[None, :] < lengths[:, None]
    return causal[None, :, :] & inside[:, None, :]


def fold_keys(running, pieces, key_start, heads_q, query_pos, lengths):
    row_max, row_total, weighted = running
    key_piece, value_piece = pieces
    key_count = key_piece.shape[1]
    score_scale = 1.0 / math.sqrt(HEAD_DIM)
    scores = (
        jnp.einsum(
            "sqhd,skhd->shqk", heads_q, split_heads(key_piece), preferred_element_type=jnp.float32
        )
        * score_scale
    )
    allowed = key_mask(query_pos, key_start, key_count, lengths)[:, None]
    scores = jnp.where(allowed, scores, NEGATIVE)
    fresh_max = jnp.maximum(row_max, jnp.max(scores, axis=-1))
    exponent_vals = jnp.exp(scores - fresh_max[..., None])
    row_total = jnp.sum(exponent_vals, axis=-1)
    update = jnp.einsum(
        "shqk,skhd->sqhd",
        exponent_vals.astype(jnp.bfloat16),
        split_heads(value_piece),
        preferred_element_type=jnp.float32,
    )
    weighted = update
    return (fresh_max, row_total, weighted)


def grad_keys(
    heads_q, heads_do, log_total, dterm, key_piece, value_piece, key_start, query_pos, lengths
):
    seq_count, key_count = (key_piece.shape[0], key_piece.shape[1])
    heads_k = split_heads(key_piece)
    heads_v = split_heads(value_piece)
    score_scale = 1.0 / math.sqrt(HEAD_DIM)
    scores = (
        jnp.einsum("sqhd,skhd->shqk", heads_q, heads_k, preferred_element_type=jnp.float32)
        * score_scale
    )
    allowed = key_mask(query_pos, key_start, key_count, lengths)[:, None]
    probability = jnp.where(allowed, jnp.exp(scores - log_total[..., None]), 0.0)
    dprob = jnp.einsum("sqhd,skhd->shqk", heads_do, heads_v, preferred_element_type=jnp.float32)
    dscores = (probability * (dprob - dterm[..., None])).astype(jnp.bfloat16)
    dq_part = (
        jnp.einsum("shqk,skhd->sqhd", dscores, heads_k, preferred_element_type=jnp.float32)
        * score_scale
    )
    dk_part = (
        jnp.einsum("shqk,sqhd->skhd", dscores, heads_q, preferred_element_type=jnp.float32)
        * score_scale
    )
    dv_part = jnp.einsum(
        "shqk,sqhd->skhd",
        probability.astype(jnp.bfloat16),
        heads_do,
        preferred_element_type=jnp.float32,
    )
    return (
        dq_part,
        dk_part.reshape(seq_count, key_count, -1),
        dv_part.reshape(seq_count, key_count, -1),
    )


def shards(
    hidden,
    teacher,
    lengths,
    w_qkv,
    w_out,
    w_up,
    w_down,
    norm_gain,
    norm_shift,
    proj_bias,
    mid_gain,
    mid_shift,
    up_bias,
):
    (
        full_qkv,
        full_out,
        full_up,
        full_down,
        gain_full,
        shift_full,
        bias_full,
        mid_gain_full,
        mid_shift_full,
        up_bias_full,
    ) = (
        lax.all_gather(w_qkv, "dp", axis=0, tiled=True),
        lax.all_gather(w_out, "dp", axis=0, tiled=True),
        lax.all_gather(w_up, "dp", axis=0, tiled=True),
        lax.all_gather(w_down, "dp", axis=0, tiled=True),
        lax.all_gather(norm_gain, "dp", axis=0, tiled=True),
        lax.all_gather(norm_shift, "dp", axis=0, tiled=True),
        lax.all_gather(proj_bias, "dp", axis=0, tiled=True),
        lax.all_gather(mid_gain, "dp", axis=0, tiled=True),
        lax.all_gather(mid_shift, "dp", axis=0, tiled=True),
        lax.all_gather(up_bias, "dp", axis=0, tiled=True),
    )
    gain_f = gain_full.astype(jnp.float32)
    shift_f = shift_full.astype(jnp.float32)
    bias_f = bias_full.astype(jnp.float32)
    mid_gain_f = mid_gain_full.astype(jnp.float32)
    mid_shift_f = mid_shift_full.astype(jnp.float32)
    up_bias_f = up_bias_full.astype(jnp.float32)
    seq_count, local_rows, model_width = hidden.shape
    token_rows = seq_count * local_rows
    seq_shape = (seq_count, local_rows, model_width)
    ctx_place = lax.axis_index("ctx")
    ctx_parts = lax.axis_size("ctx")
    query_pos = ctx_place * local_rows + jnp.arange(local_rows, dtype=jnp.int32)
    last_query = ctx_place * local_rows + local_rows - 1
    valid_mask = (query_pos[None, :] < lengths[:, None]).astype(jnp.float32)
    valid_rows = valid_mask.reshape(token_rows, 1)
    hidden_rows = hidden.reshape(token_rows, model_width).astype(jnp.float32)
    normed, pull_in = jax.vjp(layer_norm, hidden_rows, gain_f[:, 0], shift_f[:, 0])
    normed_low = normed.astype(jnp.bfloat16)
    projected = jnp.dot(normed_low, full_qkv, preferred_element_type=jnp.float32)
    query_low = (projected[:, :model_width] + bias_f[:, 0]).astype(jnp.bfloat16).reshape(seq_shape)
    key_low = projected[:, model_width : 2 * model_width].astype(jnp.bfloat16).reshape(seq_shape)
    value_low = (
        (projected[:, 2 * model_width :] + bias_f[:, 1]).astype(jnp.bfloat16).reshape(seq_shape)
    )
    heads_q = split_heads(query_low)
    start_state = (
        jnp.full((seq_count, HEADS, local_rows), NEGATIVE, jnp.float32),
        jnp.zeros((seq_count, HEADS, local_rows), jnp.float32),
        jnp.zeros((seq_count, local_rows, HEADS, HEAD_DIM), jnp.float32),
    )
    pieces = (
        lax.all_gather(key_low, "ctx", axis=1, tiled=True),
        lax.all_gather(value_low, "ctx", axis=1, tiled=True),
    )
    key_start = jnp.int32(0)
    row_max, row_total, weighted = lax.cond(
        key_start <= last_query,
        lambda: fold_keys(start_state, pieces, key_start, heads_q, query_pos, lengths),
        lambda: start_state,
    )
    attended = weighted / jnp.transpose(row_total, (0, 2, 1))[..., None]
    log_total = row_max + jnp.log(row_total)
    attended_rows = attended.reshape(token_rows, model_width)
    mixed, pull_mix = jax.vjp(layer_norm, attended_rows, gain_f[:, 1], shift_f[:, 1])
    mixed_low = mixed.astype(jnp.bfloat16)
    residual = (
        hidden_rows
        + jnp.dot(mixed_low, full_out, preferred_element_type=jnp.float32)
        + bias_f[:, 2]
    )
    ffn_in, pull_ffn = jax.vjp(layer_norm, residual, gain_f[:, 2], shift_f[:, 2])
    ffn_low = ffn_in.astype(jnp.bfloat16)
    up_proj = jnp.dot(ffn_low, full_up, preferred_element_type=jnp.float32) + up_bias_f
    activated, pull_mid = jax.vjp(mid_norm, up_proj, mid_gain_f, mid_shift_f)
    act_low = activated.astype(jnp.bfloat16)
    result = (
        residual + jnp.dot(act_low, full_down, preferred_element_type=jnp.float32) + bias_f[:, 3]
    )
    layer_output = (result * valid_rows).astype(jnp.bfloat16).reshape(hidden.shape)
    error_rows = (
        result - teacher.reshape(token_rows, model_width).astype(jnp.float32)
    ) * valid_rows
    loss_total, valid_total = lax.psum(
        (0.5 * jnp.sum(error_rows * error_rows), jnp.sum(valid_mask)), ("dp", "ctx")
    )
    loss = loss_total / (valid_total * model_width)
    down_low = error_rows.astype(jnp.bfloat16)
    bias_down_grad = jnp.sum(down_low.astype(jnp.float32), axis=0)
    down_grad = jnp.einsum("rf,rd->fd", act_low, down_low, preferred_element_type=jnp.float32)
    d_act = jnp.einsum("rd,fd->rf", down_low, full_down, preferred_element_type=jnp.float32)
    d_up, mid_gain_grad, mid_shift_grad = pull_mid(d_act)
    up_low = d_up.astype(jnp.bfloat16)
    up_bias_grad = jnp.sum(up_low.astype(jnp.float32), axis=0)
    up_grad = jnp.einsum("rd,rf->df", ffn_low, up_low, preferred_element_type=jnp.float32)
    d_ffn = jnp.einsum("rf,df->rd", up_low, full_up, preferred_element_type=jnp.float32)
    d_res_norm, gain_two, shift_two = pull_ffn(d_ffn)
    d_residual = error_rows + d_res_norm
    branch_low = d_residual.astype(jnp.bfloat16)
    bias_out_grad = jnp.sum(branch_low.astype(jnp.float32), axis=0)
    out_grad = jnp.einsum("rd,re->de", mixed_low, branch_low, preferred_element_type=jnp.float32)
    d_mixed = jnp.einsum("re,de->rd", branch_low, full_out, preferred_element_type=jnp.float32)
    d_att, gain_one, shift_one = pull_mix(d_mixed)
    heads_do = split_heads(d_att.astype(jnp.bfloat16).reshape(seq_shape))
    dterm = jnp.einsum("sqhd,sqhd->shq", heads_do.astype(jnp.float32), attended)

    def grad_step(key_piece, value_piece, key_start):
        return grad_keys(
            heads_q,
            heads_do,
            log_total,
            dterm,
            key_piece,
            value_piece,
            key_start,
            query_pos,
            lengths,
        )

    dq_zero = jnp.zeros((seq_count, local_rows, HEADS, HEAD_DIM), jnp.float32)
    own_zero = jnp.zeros(seq_shape, jnp.float32)

    def pass_step(step_index, running):
        key_cur, value_cur, dk_run, dv_run, dq_sum = running
        owner = (ctx_place - step_index) % ctx_parts
        dq_part, dk_part, dv_part = lax.cond(
            owner <= ctx_place,
            lambda: grad_step(key_cur, value_cur, owner * local_rows),
            lambda: (dq_zero, own_zero, own_zero),
        )
        dk_run, dv_run = (
            passed_along((dk_run + dk_part).astype(jnp.bfloat16), "ctx", 1).astype(jnp.float32),
            passed_along((dv_run + dv_part).astype(jnp.bfloat16), "ctx", 1).astype(jnp.float32),
        )
        key_cur, value_cur = passed_along_2((key_cur, value_cur), "ctx", 1)
        return (key_cur, value_cur, dk_run, dv_run, dq_sum + dq_part)

    key_end, value_end, dk_own, dv_own, dq_sum = lax.fori_loop(
        0, ctx_parts, pass_step, (key_low, value_low, own_zero, own_zero, dq_zero)
    )
    dq_low = dq_sum.reshape(token_rows, model_width).astype(jnp.bfloat16)
    dk_low = dk_own.reshape(token_rows, model_width).astype(jnp.bfloat16)
    dv_low = dv_own.reshape(token_rows, model_width).astype(jnp.bfloat16)
    dqkv_low = jnp.concatenate([dq_low, dk_low, dv_low], axis=1)
    bias_q_grad = jnp.sum(dq_low.astype(jnp.float32), axis=0)
    bias_v_grad = jnp.sum(dv_low.astype(jnp.float32), axis=0)
    qkv_grad = jnp.einsum("rd,re->de", normed_low, dqkv_low, preferred_element_type=jnp.float32)
    d_normed = jnp.einsum("re,de->rd", dqkv_low, full_qkv, preferred_element_type=jnp.float32)
    d_in_norm, gain_zero, shift_zero = pull_in(d_normed)
    hidden_grad = (d_residual + d_in_norm).reshape(hidden.shape)
    gain_grad = jnp.stack([gain_zero, gain_one, gain_two], axis=1)
    shift_grad = jnp.stack([shift_zero, shift_one, shift_two], axis=1)
    bias_grad = jnp.stack([bias_q_grad, bias_v_grad, bias_out_grad, bias_down_grad], axis=1)
    shares = (
        lax.psum_scatter(
            qkv_grad.astype(jnp.bfloat16), "dp", scatter_dimension=0, tiled=True
        ).astype(jnp.float32),
        lax.psum_scatter(
            out_grad.astype(jnp.bfloat16), "dp", scatter_dimension=0, tiled=True
        ).astype(jnp.float32),
        lax.psum_scatter(
            up_grad.astype(jnp.bfloat16), "dp", scatter_dimension=0, tiled=True
        ).astype(jnp.float32),
        lax.psum_scatter(
            down_grad.astype(jnp.bfloat16), "dp", scatter_dimension=0, tiled=True
        ).astype(jnp.float32),
        lax.psum_scatter(
            gain_grad.astype(jnp.bfloat16), "dp", scatter_dimension=0, tiled=True
        ).astype(jnp.float32),
        lax.psum_scatter(
            shift_grad.astype(jnp.bfloat16), "dp", scatter_dimension=0, tiled=True
        ).astype(jnp.float32),
        lax.psum_scatter(
            bias_grad.astype(jnp.bfloat16), "dp", scatter_dimension=0, tiled=True
        ).astype(jnp.float32),
        lax.psum_scatter(
            mid_gain_grad.astype(jnp.bfloat16), "dp", scatter_dimension=0, tiled=True
        ).astype(jnp.float32),
        lax.psum_scatter(
            mid_shift_grad.astype(jnp.bfloat16), "dp", scatter_dimension=0, tiled=True
        ).astype(jnp.float32),
        lax.psum_scatter(
            up_bias_grad.astype(jnp.bfloat16), "dp", scatter_dimension=0, tiled=True
        ).astype(jnp.float32),
    )
    summed = (
        lax.psum(shares[0].astype(jnp.bfloat16), "ctx").astype(jnp.float32),
        lax.psum(shares[1].astype(jnp.bfloat16), "ctx").astype(jnp.float32),
        lax.psum(shares[2].astype(jnp.bfloat16), "ctx").astype(jnp.float32),
        lax.psum(shares[3].astype(jnp.bfloat16), "ctx").astype(jnp.float32),
        lax.psum(shares[4].astype(jnp.bfloat16), "ctx").astype(jnp.float32),
        lax.psum(shares[5].astype(jnp.bfloat16), "ctx").astype(jnp.float32),
        lax.psum(shares[6].astype(jnp.bfloat16), "ctx").astype(jnp.float32),
        lax.psum(shares[7].astype(jnp.bfloat16), "ctx").astype(jnp.float32),
        lax.psum(shares[8].astype(jnp.bfloat16), "ctx").astype(jnp.float32),
        lax.psum(shares[9].astype(jnp.bfloat16), "ctx").astype(jnp.float32),
    )
    return (
        layer_output,
        loss,
        hidden_grad,
        summed[0],
        summed[1],
        summed[2],
        summed[3],
        summed[4],
        summed[5],
        summed[6],
        summed[7],
        summed[8],
        summed[9],
    )


AXES = ("dp", "ctx")


def swap(value, mask):
    count = lax.axis_size("dp") * lax.axis_size("ctx")
    return lax.ppermute(value, AXES, [(i, i ^ mask) for i in range(count)])


def along_z(piece):
    return [swap(piece, 8 * step) for step in (1, 2, 3)]


def wide(value):
    return value.astype(jnp.float32)


def narrow(value):
    return value.astype(jnp.bfloat16)


def by_ctx(tiles, ctx_at):
    stack = jnp.stack(tiles)
    return [lax.dynamic_index_in_dim(stack, ctx_at ^ j, 0, keepdims=False) for j in range(4)]


VMEM_BYTES = 56 * 1024 * 1024


def whole(shape):
    return pl.BlockSpec(tuple(shape), lambda i: (0,) * len(shape), pipeline_mode=pl.Buffered(1))


def padded(shape, dtype):
    lead = math.prod(shape[:-2])
    size = jnp.dtype(dtype).itemsize
    rows = -(-shape[-2] // (32 // size)) * (32 // size) if len(shape) > 1 else 8
    return lead * rows * (-(-shape[-1] // 128) * 128) * size


def call(body, ins, outs, scratch=(), us=1, deps=(), room=6):
    pairs = [v if isinstance(v, tuple) else (v, whole(v.shape)) for v in ins[1:]]
    held = sum(padded(spec.block_shape, v.dtype) for v, spec in pairs)
    held += sum(padded(shape, dtype) for shape, dtype in (*outs, *scratch))
    count = len(pairs)

    def kernel(sc, *refs):
        body(sc, *refs[:count], *refs[count + len(deps):])

    return pl.pallas_call(
        kernel,
        grid=(1,),
        in_specs=[pl.BlockSpec(memory_space=pltpu.SMEM)] + [spec for _, spec in pairs]
        + [pl.BlockSpec(memory_space=pl.ANY)] * len(deps),
        out_specs=[whole(shape) for shape, _ in outs],
        out_shape=[jax.ShapeDtypeStruct(shape, dtype) for shape, dtype in outs],
        scratch_shapes=[pltpu.VMEM(shape, dtype) for shape, dtype in scratch],
        compiler_params=pltpu.CompilerParams(vmem_limit_bytes=held + room * 1024 * 1024),
        cost_estimate=pl.CostEstimate(flops=int(us * 2e7), bytes_accessed=0, transcendentals=0),
        name=body.__name__,
    )(ins[0], *[v for v, _ in pairs], *deps)


def after(value, *deps):
    return lax.optimization_barrier((value, *deps))[0]


BF, F32 = jnp.bfloat16, jnp.float32


def contract(a, b, da, db):
    return lax.dot_general(a, b, (((da,), (db,)), ((), ())), preferred_element_type=F32)


def block_of(sc, xr, zr):
    return 2 * ((sc[0] >> 1) ^ zr) + ((sc[0] & 1) ^ xr)


def slot_of(sc, block):
    return ((block & 1) ^ (sc[0] & 1)) * 4 + ((block >> 1) ^ (sc[0] >> 1))


def lay(sc, scr, near, far, rows, stride, offset=0):
    for xr, ref in ((0, near), (1, far)):
        for zr in range(4):
            at = pl.multiple_of(stride * block_of(sc, xr, zr) + offset, 16)
            scr[pl.ds(at, rows), :] = ref[zr]


def moments(value):
    average = jnp.mean(value, axis=-1, keepdims=True)
    centred = value - average
    scale = lax.rsqrt(jnp.mean(centred * centred, axis=-1, keepdims=True) + EPSILON)
    return centred * scale, scale


def norm_back(grad, hat, scale):
    return scale * (grad - jnp.mean(grad, axis=-1, keepdims=True) - hat * jnp.mean(grad * hat, axis=-1, keepdims=True))


def mine(ctx_at, row):
    out = row[:, :192]
    for j in range(1, 4):
        out = jnp.where(ctx_at == j, row[:, 192 * j:192 * j + 192], out)
    return out


def pack_body(sc, w, gain, shift, bias, out, scr):
    scr[...] = jnp.zeros((16, 128), F32)
    scr[0:3, :96] = gain[...].astype(F32)
    scr[3:6, :96] = shift[...].astype(F32)
    scr[6:10, :96] = bias[...].astype(F32)
    small = scr[...].T[:96].astype(BF)
    for j in range(4):
        @pl.when(sc[1] == j)
        def _():
            cols = [w[:, 768 * part + 192 * j:768 * part + 192 * j + 192] for part in range(3)]
            out[...] = jnp.concatenate(cols + [small, jnp.zeros((96, 48), BF)], axis=1)


def attend_body(sc, h0, h1, h2, h3, wa, wb, a0, a1, a2, a3, q_o, k_o, v_o, lse_o, ot_o, n_o, vec_o, w_scr):
    ctx_at, length = sc[1], sc[2]
    lay(sc, w_scr, wa, wb, 96, 96)
    vec = w_scr[:, 512:640].astype(F32).T[64:80]
    vec_o[...] = vec
    bias_q, bias_v = mine(ctx_at, vec[6:7]), mine(ctx_at, vec[7:8])
    for r, ref in enumerate((h0, h1, h2, h3)):
        rows = pl.ds(pl.multiple_of((ctx_at ^ r) * 256, 256), 256)
        hat, _ = moments(ref[...].astype(F32))
        normed = (hat * vec[0:1] + vec[3:4]).astype(BF)
        n_o[rows, :] = normed
        p = jnp.dot(normed, w_scr[...], preferred_element_type=F32)
        for h in range(3):
            q_o[h, rows, :] = ((p[:, 64 * h:64 * h + 64] + bias_q[:, 64 * h:64 * h + 64]) * 0.125).astype(BF)
            k_o[h, rows, :] = p[:, 192 + 64 * h:256 + 64 * h].astype(BF)
            v_o[h, rows, :] = (p[:, 384 + 64 * h:448 + 64 * h] + bias_v[:, 64 * h:64 * h + 64]).astype(BF)

    def head(h, carry):
        for i in range(4):
            n = 256 * (i + 1)
            scores = contract(k_o[h, :n, :], q_o[h, 256 * i:256 * i + 256, :], 1, 1)
            limit = jnp.minimum(256 * i + lax.broadcasted_iota(jnp.int32, (1, 256), 1), length - 1)
            scores = jnp.where(lax.broadcasted_iota(jnp.int32, (n, 256), 0) <= limit, scores, NEGATIVE)
            top = jnp.max(scores, axis=0, keepdims=True)
            grown = jnp.exp(scores - top)
            total = jnp.sum(grown, axis=0, keepdims=True)
            out = contract(v_o[h, :n, :], grown.astype(BF), 0, 0) / total
            ot_o[i, pl.ds(pl.multiple_of(64 * h, 64), 64), :] = out
            lse_o[h, i:i + 1, :] = top + jnp.log(total)
        return carry

    lax.fori_loop(0, 3, head, 0)
    for r, ref in enumerate((a0, a1, a2, a3)):
        ref[...] = ot_o[ctx_at ^ r].T.astype(BF)


def attend(sc, hids, wa, wb, deps):
    rows = (256, 192)
    return call(
        attend_body, [sc, *hids, wa, wb],
        [(rows, BF)] * 4 + [((3, 1024, 64), BF)] * 3
        + [((3, 8, 256), F32), ((4, 192, 256), F32), ((1024, 768), BF), ((16, 768), F32)],
        [((768, 640), BF)], us=13, deps=deps)


def attend_back_body(sc, d0, d1, d2, d3, q_i, k_i, v_i, lse_i, ot_i, n_i, h0, h1, h2, h3, wa, wb, vec_i, side_e, side_d, mids,
                     n0, n2, n13, keep, send, w_scr, do_scr, dq_s, dk_s, dv_s, dk_acc, dv_acc, all_scr, g_scr):
    ctx_at, length = sc[1], sc[2]
    lay(sc, w_scr, wa, wb, 96, 96)
    for r, ref in enumerate((d0, d1, d2, d3)):
        rows = pl.ds(pl.multiple_of((ctx_at ^ r) * 256, 256), 256)
        value = ref[...]
        for h in range(3):
            do_scr[h, rows, :] = value[:, 64 * h:64 * h + 64]

    def head(h, carry):
        for i in (3, 2, 1, 0):
            n = 256 * (i + 1)
            mine_rows = slice(256 * i, 256 * i + 256)
            q, do, k = q_i[h, mine_rows, :], do_scr[h, mine_rows, :], k_i[h, :n, :]
            out = ot_i[i, pl.ds(pl.multiple_of(64 * h, 64), 64), :]
            dterm = jnp.sum(do.astype(F32).T * out, axis=0, keepdims=True)
            limit = jnp.minimum(256 * i + lax.broadcasted_iota(jnp.int32, (1, 256), 1), length - 1)
            prob = jnp.exp(contract(k, q, 1, 1) - lse_i[h, i:i + 1, :])
            prob = jnp.where(lax.broadcasted_iota(jnp.int32, (n, 256), 0) <= limit, prob, 0.0)
            dscore = (prob * (contract(v_i[h, :n, :], do, 1, 1) - dterm)).astype(BF)
            dv = jnp.dot(prob.astype(BF), do, preferred_element_type=F32)
            dk = jnp.dot(dscore, q, preferred_element_type=F32)
            if i == 3:
                dv_acc[...] = dv
                dk_acc[...] = dk
            else:
                dv_acc[:n, :] += dv
                dk_acc[:n, :] += dk
            dq_s[h, mine_rows, :] = (contract(k, dscore, 0, 0) * 0.125).T.astype(BF)
        dk_s[h] = dk_acc[...].astype(BF)
        dv_s[h] = dv_acc[...].astype(BF)
        return carry

    lax.fori_loop(0, 3, head, 0)
    for i in range(4):
        rows = slice(256 * i, 256 * i + 256)
        all_scr[rows, :] = jnp.concatenate([s[h, rows, :] for s in (dq_s, dk_s, dv_s) for h in range(3)], axis=1)
    sums = jnp.sum(all_scr[...].astype(F32), axis=0, keepdims=True)
    bias_q = jnp.concatenate([jnp.where(ctx_at == j, sums[:, :192], 0.0) for j in range(4)], axis=1)
    bias_v = jnp.concatenate([jnp.where(ctx_at == j, sums[:, 384:], 0.0) for j in range(4)], axis=1)
    gain_sum, shift_sum = jnp.zeros((1, 768), F32), jnp.zeros((1, 768), F32)
    for r, (ref, out) in enumerate(((h0, n0), (h1, n13.at[0]), (h2, n2), (h3, n13.at[1]))):
        rows = pl.ds(pl.multiple_of((ctx_at ^ r) * 256, 256), 256)
        grad = contract(all_scr[rows, :], w_scr[:, :576], 1, 1)
        hat, _ = moments(ref[...].astype(F32))
        gain_sum += jnp.sum(grad * hat, axis=0, keepdims=True)
        shift_sum += jnp.sum(grad, axis=0, keepdims=True)
        out[...] = grad.astype(BF)
    rows16 = jnp.concatenate(
        [gain_sum, side_e[0:2], shift_sum, side_e[2:4], bias_q, bias_v, side_e[4:5], side_d[0:2], jnp.zeros((5, 768), F32)], axis=0)
    w_grad = contract(n_i[...], all_scr[...], 0, 0)
    for b in range(8):
        at = slot_of(sc, b)
        extra = jnp.concatenate([mids[:, 384 * b:384 * b + 384], rows16[:, 96 * b:96 * b + 96], jnp.zeros((16, 96), F32)], axis=1)
        g_scr[at, :96, :] = w_grad[96 * b:96 * b + 96].astype(BF)
        g_scr[at, 96:112, :] = extra.astype(BF)
    keep[...] = g_scr[:4]
    send[...] = g_scr[4:]


def attend_back(sc, douts, saved, hids, wa, wb, side_e, side_d, mids, deps):
    q, k, v, lse, ot, normed, vec = saved
    return call(
        attend_back_body, [sc, *douts, q, k, v, lse, ot, normed, *hids, wa, wb, vec, side_e, side_d, mids],
        [((256, 768), BF)] * 2 + [((2, 256, 768), BF)] + [((4, 112, 576), BF)] * 2,
        [((768, 640), BF), ((3, 1024, 64), BF), ((3, 1024, 64), BF), ((3, 1024, 64), BF), ((3, 1024, 64), BF),
         ((1024, 64), F32), ((1024, 64), F32), ((1024, 576), BF), ((8, 112, 576), BF)],
        us=12, deps=deps)


def part(rows, at):
    return pl.BlockSpec((4, rows, 768), lambda i: (0, at, 0), pipeline_mode=pl.Buffered(1))


def lay_out(sc, scr, own_near, own_far, other_near, other_far):
    core = sc[1] & 1
    lay(sc, scr, own_near, own_far, 48, 96, 48 * core)
    lay(sc, scr, other_near, other_far, 48, 96, 48 * (1 - core))


def lay_down(sc, scr, refs):
    for c in (0, 1):
        for xr in (0, 1):
            for y in (0, 1):
                lay_one(sc, scr, refs[4 * c + 2 * xr + y], xr, 96 * (sc[1] ^ (2 * y + c)))


def lay_one(sc, scr, ref, xr, offset):
    for zr in range(4):
        scr[pl.ds(pl.multiple_of(384 * block_of(sc, xr, zr) + offset, 32), 96), :] = ref[zr]


def join_heads(sc, scr, pieces):
    for r, ref in enumerate(pieces):
        scr[r] = ref[...]
    return jnp.concatenate([scr[sc[1] ^ j] for j in range(4)], axis=1).astype(F32)


def mid_body(sc, g0, g1, g2, g3, own, vec, on, of, tn, tf, mixed_o, resid_o, ffn_o, w_scr, a_scr):
    lay_out(sc, w_scr, on, of, tn, tf)
    hat, _ = moments(join_heads(sc, a_scr, (g0, g1, g2, g3)))
    mixed = (hat * vec[1:2] + vec[4:5]).astype(BF)
    mixed_o[...] = mixed
    resid = own[...].astype(F32) + jnp.dot(mixed, w_scr[...], preferred_element_type=F32) + vec[8:9]
    resid_o[...] = resid
    hat, _ = moments(resid)
    ffn_o[...] = (hat * vec[2:3] + vec[5:6]).astype(BF)


def up_body(sc, ffn, w0n, w0f, w1n, w1f, w2n, w2f, w3n, w3f, mn, mf, act_o, hat_o, slope_o, scale_o, nat_o,
            w_scr, g_scr, m_scr):
    for xr, ref in ((0, mn), (1, mf)):
        for zr in range(4):
            m_scr[block_of(sc, xr, zr)] = ref[zr].astype(F32)
    flat = [m_scr[b] for b in range(8)]
    for j in range(4):
        two = flat[2 * j:2 * j + 2]
        nat_o[j, 0:1, :] = jnp.concatenate([m[0:1, :384] for m in two], axis=1)
        nat_o[j, 1:2, :] = jnp.concatenate([m[0:1, 384:] for m in two], axis=1)
        nat_o[j, 2:3, :] = jnp.concatenate([m[1:2, :384] for m in two], axis=1)
        nat_o[j, 3:8, :] = jnp.zeros((5, 768), F32)
    value = ffn[...]
    total = jnp.zeros((256, 1), F32)
    for t, (near, far) in enumerate(((w0n, w0f), (w1n, w1f), (w2n, w2f), (w3n, w3f))):
        j = sc[1] ^ t
        lay(sc, w_scr.at[t], near, far, 96, 96)
        up = jnp.dot(value, w_scr[t], preferred_element_type=F32) + nat_o[j, 2:3, :]
        chance = 0.5 * (1.0 + lax.erf(up * math.sqrt(0.5)))
        slope_o[j] = (chance + up * jnp.exp(-0.5 * up * up) * (1.0 / math.sqrt(2.0 * math.pi))).astype(BF)
        gelu = up * chance
        g_scr[j] = gelu
        total += jnp.sum(gelu, axis=-1, keepdims=True)
    average = total * (1.0 / 3072)
    square = jnp.zeros((256, 1), F32)
    for j in range(4):
        centred = g_scr[j] - average
        square += jnp.sum(centred * centred, axis=-1, keepdims=True)
    scale = lax.rsqrt(square * (1.0 / 3072) + EPSILON)
    scale_o[...] = scale
    for j in range(4):
        hat = (g_scr[j] - average) * scale
        hat_o[j] = hat.astype(BF)
        act_o[j] = (hat * nat_o[j, 0:1, :] + nat_o[j, 1:2, :]).astype(BF)


def down_body(sc, act, resid, teacher, vec, e0, e1, e2, e3, e4, e5, e6, e7, out_o, err_o, low_o, side_o, w_scr):
    lay_down(sc, w_scr, (e0, e1, e2, e3, e4, e5, e6, e7))
    result = resid[...] + vec[9:10]
    for j in range(4):
        result += jnp.dot(act[j], w_scr[768 * j:768 * j + 768, :], preferred_element_type=F32)
    pos = sc[1] * 256 + lax.broadcasted_iota(jnp.int32, (256, 1), 0)
    valid = jnp.where(pos < sc[2], 1.0, 0.0)
    out_o[...] = (result * valid).astype(BF)
    error = (result - teacher[...].astype(F32)) * valid
    err_o[...] = error
    low = error.astype(BF)
    low_o[...] = low
    side_o[0:1, :] = jnp.sum(low.astype(F32), axis=0, keepdims=True)
    loss = 0.5 * jnp.sum(jnp.sum(error * error, axis=0, keepdims=True), axis=1, keepdims=True)
    count = jnp.sum(valid, axis=0, keepdims=True)
    high = loss.astype(BF).astype(F32)
    lane = lax.broadcasted_iota(jnp.int32, (1, 768), 1) % 96
    side_o[1:2, :] = jnp.where(lane == 0, high, jnp.where(lane == 1, loss - high, jnp.where(lane == 2, count, 0.0)))
    side_o[2:8, :] = jnp.zeros((6, 768), F32)


def down_grad_body(sc, act, low, keep, send, g_scr):
    value = low[...]
    for j in range(4):
        grad = contract(act[j], value, 0, 0).astype(BF)
        for half in (0, 1):
            at = slot_of(sc, 2 * j + half)
            for q in range(4):
                g_scr[sc[1] ^ q, at] = grad[384 * half + 96 * q:384 * half + 96 * q + 96]
    for y in (0, 1):
        keep[y] = g_scr[2 * y]
        send[y] = g_scr[2 * y + 1]


def act_back_body(sc, low, hat_i, slope, scale, nat, e0, e1, e2, e3, e4, e5, e6, e7, up_o, mids_o, wd_scr, dh_scr):
    lay_down(sc, wd_scr, (e0, e1, e2, e3, e4, e5, e6, e7))
    value = low[...]
    first, second = jnp.zeros((256, 1), F32), jnp.zeros((256, 1), F32)
    for j in range(4):
        grad = contract(value, wd_scr[768 * j:768 * j + 768, :], 1, 1)
        hat = hat_i[j].astype(F32)
        cols = slice(768 * j, 768 * j + 768)
        mids_o[0:1, cols] = jnp.sum(grad * hat, axis=0, keepdims=True)
        mids_o[1:2, cols] = jnp.sum(grad, axis=0, keepdims=True)
        grad = grad * nat[j, 0:1, :]
        dh_scr[j] = grad
        first += jnp.sum(grad, axis=-1, keepdims=True)
        second += jnp.sum(grad * hat, axis=-1, keepdims=True)
    first, second = first * (1.0 / 3072), second * (1.0 / 3072)
    for j in range(4):
        hat = hat_i[j].astype(F32)
        grad = (scale[...] * (dh_scr[j] - first - hat * second) * slope[j].astype(F32)).astype(BF)
        up_o[j] = grad
        mids_o[2:3, 768 * j:768 * j + 768] = jnp.sum(grad.astype(F32), axis=0, keepdims=True)
    mids_o[3:16, :] = jnp.zeros((13, 3072), F32)


def ffn_back_body(sc, up_i, err, resid, w0n, w0f, w1n, w1f, w2n, w2f, w3n, w3f, on, of, tn, tf, vec, g0, g1, g2, g3,
                  branch_o, dres_o, p0, p1, p2, p3, side_o, w_scr, o_scr, a_scr, b_scr):
    grad = jnp.zeros((256, 768), F32)
    for t, (near, far) in enumerate(((w0n, w0f), (w1n, w1f), (w2n, w2f), (w3n, w3f))):
        lay(sc, w_scr.at[t], near, far, 96, 96)
        grad += contract(up_i[sc[1] ^ t], w_scr[t], 1, 1)
    hat, factor = moments(resid[...])
    side_o[1:2, :] = jnp.sum(grad * hat, axis=0, keepdims=True)
    side_o[3:4, :] = jnp.sum(grad, axis=0, keepdims=True)
    dres = err[...] + norm_back(grad * vec[2:3], hat, factor)
    dres_o[...] = dres
    branch = dres.astype(BF)
    branch_o[...] = branch
    side_o[4:5, :] = jnp.sum(branch.astype(F32), axis=0, keepdims=True)
    lay_out(sc, o_scr, on, of, tn, tf)
    grad = contract(branch, o_scr[...], 1, 1)
    hat, factor = moments(join_heads(sc, a_scr, (g0, g1, g2, g3)))
    side_o[0:1, :] = jnp.sum(grad * hat, axis=0, keepdims=True)
    side_o[2:3, :] = jnp.sum(grad, axis=0, keepdims=True)
    side_o[5:8, :] = jnp.zeros((3, 768), F32)
    grad = norm_back(grad * vec[1:2], hat, factor).astype(BF)
    for j in range(4):
        b_scr[j] = grad[:, 192 * j:192 * j + 192]
    for r, ref in enumerate((p0, p1, p2, p3)):
        ref[...] = b_scr[sc[1] ^ r]


def up_grad_body(sc, ffn, up, keep, send, g_scr):
    value = ffn[...]
    for j in range(4):
        grad = contract(value, up[j], 0, 0).astype(BF)
        for b in range(8):
            g_scr[sc[1] ^ j, slot_of(sc, b)] = grad[96 * b:96 * b + 96]
    for y in (0, 1):
        keep[y] = g_scr[2 * y]
        send[y] = g_scr[2 * y + 1]


def out_grad_body(sc, mixed, branch, out_keep, out_send, o_scr):
    grad = contract(mixed[...], branch[...], 0, 0).astype(BF)
    for b in range(8):
        for c in (0, 1):
            o_scr[(sc[1] & 1) ^ c, slot_of(sc, b)] = grad[96 * b + 48 * c:96 * b + 48 * c + 48]
    out_keep[...] = o_scr[0]
    out_send[...] = o_scr[1]


def added(a, b):
    return a.astype(F32) + b.astype(F32)


def pair_body(sc, keep, got, near0, near1, far0, far1):
    for y, near, far in ((0, near0, far0), (1, near1, far1)):
        near[...] = added(keep[y, :4], got[y, :4]).astype(BF)
        far[...] = added(keep[y, 4:], got[y, 4:]).astype(BF)


def slots_body(sc, near, got, own, s1, s2, s3):
    own[...] = added(near[0], got[0])
    for at, out in ((1, s1), (2, s2), (3, s3)):
        out[...] = added(near[at], got[at]).astype(BF)


def join_far_body(sc, mine, got, out_keep, out_got, far):
    far[:, :96, :] = added(mine[...], got[...]).astype(BF)
    far[:, 96:, :] = added(out_keep[...], out_got[...]).astype(BF)


def join_near_body(sc, mine, y_got, out_keep, out_got, x_got, own, s1, s2, s3):
    for at, out in ((0, own), (1, s1), (2, s2), (3, s3)):
        kind = out.dtype
        out[:96, :] = (added(mine[at], y_got[at]) + x_got[at, :96, :].astype(F32)).astype(kind)
        out[96:, :] = (added(out_keep[at], out_got[at]) + x_got[at, 96:, :].astype(F32)).astype(kind)


def fast(
    hidden, teacher, lengths, w_qkv, w_out, w_up, w_down, norm_gain, norm_shift, proj_bias,
    mid_gain, mid_shift, up_bias,
):
    dp_at, ctx_at = lax.axis_index("dp"), lax.axis_index("ctx")
    core = ctx_at & 1
    sc = jnp.stack([dp_at, ctx_at, lengths[0]]).astype(jnp.int32)
    own = hidden[0]
    tall = (256, 768)
    barrier = lax.optimization_barrier
    h_y, h_c = swap(own, 2), swap(own, 1)
    piece = call(pack_body, [sc, w_qkv, norm_gain.T, norm_shift.T, proj_bias.T], [((96, 640), BF)], [((16, 128), F32)])[0]
    q_cols = along_z(piece)
    mid_rows = jnp.concatenate([mid_gain, mid_shift, up_bias, jnp.zeros((13 * 384,), BF)]).reshape(8, 768)
    piece_a = jnp.concatenate([
        lax.dynamic_slice(w_up, (0, 768 * ctx_at), (96, 768)), lax.dynamic_slice(w_out, (48 * core, 0), (48, 768)), mid_rows])
    down4 = w_down.reshape(4, 96, 768)
    piece_b, piece_c = (lax.dynamic_index_in_dim(down4, ctx_at ^ t, 0, keepdims=False) for t in (0, 2))
    q_cols, piece_a, h_y = barrier((q_cols, piece_a, h_y))
    q_near = jnp.stack([piece] + q_cols)
    q_far = swap(q_near, 4)
    h_yc = swap(h_y, 1)
    a_cols = along_z(piece_a)
    a_cols, q_far, piece_b, h_c, h_yc = barrier((a_cols, q_far, piece_b, h_c, h_yc))
    a_near = jnp.stack([piece_a] + a_cols)
    a_far = swap(a_near, 4)
    y_near = swap(a_near[:, :96], 2)
    a_near_o = swap(a_near, 1)
    b_cols = along_z(piece_b)
    hids = [own, h_c, h_y, h_yc]
    *att, q, k, v, lse, ot, normed, vec = attend(sc, hids, q_near, q_far, (a_near,))
    b_cols, piece_c, att = barrier((b_cols, piece_c, att))
    c_cols = along_z(piece_c)
    b_near = jnp.stack([piece_b] + b_cols)
    a_far, y_near, b_near, att = barrier((a_far, y_near, b_near, att))
    b_far, b_near_o = swap(b_near, 4), swap(b_near, 1)
    got = [att[0]] + [swap(att[r], r) for r in (1, 2, 3)]
    y_far = swap(a_far[:, :96], 2)
    a_far_o, y_near_o = swap(a_far, 1), swap(y_near, 1)
    outs = [(t, part(48, 2)) for t in (a_near, a_far, a_near_o, a_far_o)]
    mixed, resid, ffn = call(
        mid_body, [sc, *got, own, vec, *outs], [(tall, BF), (tall, F32), (tall, BF)],
        [((768, 768), BF), ((4, 256, 192), BF)], us=3)
    c_cols, b_far, mixed = barrier((c_cols, b_far, mixed))
    c_near = jnp.stack([piece_c] + c_cols)
    c_far, c_near_o = swap(c_near, 4), swap(c_near, 1)
    b_far_o, y_far_o = swap(b_far, 1), swap(y_far, 1)
    ups = [(t, part(96, 0)) for t in (a_near, a_far, a_near_o, a_far_o)] + [y_near, y_far, y_near_o, y_far_o]
    four = (4, 256, 768)
    act, hat, slope, scale, nat = call(
        up_body, [sc, ffn, *ups] + [(t, part(8, 18)) for t in (a_near, a_far)],
        [(four, BF), (four, BF), (four, BF), ((256, 1), F32), ((4, 8, 768), F32)],
        [((4, 768, 768), BF), (four, F32), ((8, 8, 768), F32)], us=5, deps=(c_near,))
    c_far_o = swap(c_far, 1)
    downs = [b_near, c_near, b_far, c_far, b_near_o, c_near_o, b_far_o, c_far_o]
    out, err, low, side_d = call(
        down_body, [sc, act, resid, teacher[0], vec, *downs],
        [(tall, BF), (tall, F32), (tall, BF), ((8, 768), F32)], [((3072, 768), BF)], us=5)
    halves_of = ((2, 8, 96, 768), BF)
    down_keep, down_send = call(
        down_grad_body, [sc, act, low], [halves_of] * 2, [((4, 8, 96, 768), BF)], us=3)
    down_got = swap(down_send, 1)
    up_low, mids = call(
        act_back_body, [sc, low, hat, slope, scale, nat, *downs], [(four, BF), ((16, 3072), F32)],
        [((3072, 768), BF), (four, F32)], us=5, deps=(down_keep,))
    slots = ((4, 96, 768), BF)
    d_near0, d_near1, d_far0, d_far1 = call(pair_body, [sc, down_keep, down_got], [slots] * 4, us=2, deps=(mids,))
    d_got0 = swap(d_far0, 4)
    up_keep, up_send = call(up_grad_body, [sc, ffn, up_low], [halves_of] * 2, [((4, 8, 96, 768), BF)], us=3, deps=(d_near0,))
    up_got = swap(up_send, 1)
    branch, d_res, *d_att, side_e = call(
        ffn_back_body, [sc, up_low, err, resid, *ups, *outs, vec, *got],
        [(tall, BF), (tall, F32)] + [((256, 192), BF)] * 4 + [((8, 768), F32)],
        [((4, 768, 768), BF), ((768, 768), BF), ((4, 256, 192), BF), ((4, 256, 192), BF)], us=6, deps=(up_keep,))
    u_near0, u_near1, u_far0, u_far1 = call(pair_body, [sc, up_keep, up_got], [slots] * 4, us=2, deps=(side_e,))
    d_got = [d_att[0]] + [swap(d_att[r], r) for r in (1, 2, 3)]
    out_keep, out_send = call(
        out_grad_body, [sc, mixed, branch], [((8, 48, 768), BF)] * 2, [((2, 8, 48, 768), BF)], us=1, deps=(u_near0,))
    out_got = swap(out_send, 1)
    own_part, sent = ((96, 768), F32), ((96, 768), BF)
    d_own0, *d_z0 = call(slots_body, [sc, d_near0, d_got0], [own_part] + [sent] * 3, us=1, deps=(out_keep,))

    def along_z_back(parts):
        return [swap(parts[step - 1], 8 * step) for step in (1, 2, 3)]

    d_z0, d_far1, u_far1, d_got, out_got = barrier((d_z0, d_far1, u_far1, d_got, out_got))
    d_z0 = along_z_back(d_z0)
    d_got1 = swap(d_far1, 4)
    uy_far = swap(u_far1, 2)
    dn_0, dn_2, dn_13, q_keep, q_send = attend_back(
        sc, d_got, (q, k, v, lse, ot, normed, vec), hids, q_near, q_far, side_e, side_d, mids, (d_own0, out_got))
    d_z0, d_got1, uy_far, u_near1, dn_0, dn_2, dn_13, q_keep, q_send = barrier(
        (d_z0, d_got1, uy_far, u_near1, dn_0, dn_2, dn_13, q_keep, q_send))
    near, far = (pl.BlockSpec((4, 48, 768), lambda i, at=at: (at, 0, 0), pipeline_mode=pl.Buffered(1)) for at in (0, 1))
    u_x = call(join_far_body, [sc, u_far0, uy_far, (out_keep, far), (out_got, far)], [((4, 144, 768), BF)], us=1)[0]
    ux_got = swap(u_x, 4)
    uy_near = swap(u_near1, 2)
    d_own1, *d_z1 = call(slots_body, [sc, d_near1, d_got1], [own_part] + [sent] * 3, us=1, deps=(u_x,))
    d_z1 = along_z_back(d_z1)
    ux_got, uy_near, d_z1, q_send, dn_13 = barrier((ux_got, uy_near, d_z1, q_send, dn_13))
    q_got = swap(q_send, 4)
    u_own, *u_z = call(
        join_near_body, [sc, u_near0, uy_near, (out_keep, near), (out_got, near), ux_got],
        [((144, 768), F32)] + [((144, 768), BF)] * 3, us=1)
    u_z = along_z_back(u_z)
    dn_got = swap(dn_13, 1)

    def total(own_sum, parts):
        return narrow(own_sum + sum(wide(t) for t in parts))

    q_got, u_z, dn_got, d_z0, d_z1 = barrier((q_got, u_z, dn_got, d_z0, d_z1))
    q_own, *q_z = call(slots_body, [sc, q_keep, q_got], [((112, 576), F32)] + [((112, 576), BF)] * 3, us=1)
    q_z = along_z_back(q_z)
    dn_2 = swap(narrow(wide(dn_2) + wide(dn_got[1])), 2)
    sums = jnp.concatenate([total(u_own, u_z), total(d_own0, d_z0), total(d_own1, d_z1)])
    sums_y = swap(sums, 2)
    q_z, dn_2, sums_y = barrier((q_z, dn_2, sums_y))
    q_sum = total(q_own, q_z)
    q_two = jnp.stack([q_sum, swap(q_sum, 2)])
    q_more = swap(q_two, 1)
    q_all = by_ctx([q_two[0], q_more[0], q_two[1], q_more[1]], ctx_at)
    d_own = wide(dn_0) + wide(dn_got[0]) + wide(dn_2)
    _, pull_own = jax.vjp(lambda t: layer_norm(t, vec[0], vec[3]), wide(own))
    hidden_grad = (d_res + pull_own(d_own)[0])[None]
    five = jnp.concatenate([
        sums[:96], sums_y[:96], narrow(wide(sums[96:144]) + wide(sums_y[96:144])),
        narrow(wide(sums[144:240]) + wide(sums_y[240:])), narrow(wide(sums[240:]) + wide(sums_y[144:240]))])
    more = swap(five, 1)
    grad_qkv = wide(jnp.concatenate([q_all[j][:96, 192 * p:192 * p + 192] for p in range(3) for j in range(4)], axis=1))
    rest = sum(wide(t[96:]) for t in q_all)
    mid_gain_out, mid_shift_out, up_bias_out = (rest[i, :384] for i in range(3))
    vec_out = rest[:10, 384:480]
    loss = (rest[10, 384] + rest[10, 385]) / (rest[10, 386] * hidden.shape[2])
    grad_up = wide(jnp.concatenate(by_ctx([five[:96], more[:96], five[96:192], more[96:192]], ctx_at), axis=1))
    out_mine, out_far = five[192:240], more[192:240]
    grad_out = wide(jnp.where(core == 0, jnp.concatenate([out_mine, out_far]), jnp.concatenate([out_far, out_mine])))
    grad_down = wide(jnp.concatenate(by_ctx([five[240:336], more[240:336], five[336:], more[336:]], ctx_at), axis=0))
    return (out[None], loss, hidden_grad, grad_qkv, grad_out, grad_up, grad_down,
            vec_out[:3].T, vec_out[3:6].T, vec_out[6:].T, mid_gain_out, mid_shift_out, up_bias_out)


def solution(mesh):
    step = fast if (mesh.shape["dp"], mesh.shape["ctx"]) == (8, 4) else shards
    placed = (
        P("dp", "ctx", None),
        P("dp", "ctx", None),
        P("dp"),
        P("dp", None),
        P("dp", None),
        P("dp", None),
        P("dp", None),
        P("dp", None),
        P("dp", None),
        P("dp", None),
        P("dp"),
        P("dp"),
        P("dp"),
    )
    return jax.shard_map(
        step,
        mesh=mesh,
        in_specs=placed,
        out_specs=(
            P("dp", "ctx", None),
            P(),
            P("dp", "ctx", None),
            P("dp", None),
            P("dp", None),
            P("dp", None),
            P("dp", None),
            P("dp", None),
            P("dp", None),
            P("dp", None),
            P("dp"),
            P("dp"),
            P("dp"),
        ),
        check_vma=False,
    )
```

```python
import math

import jax
import jax.numpy as jnp
from jax import lax
from jax.experimental import pallas as pl
from jax.experimental.pallas import tpu as pltpu
from jax.sharding import PartitionSpec as P

HEADS = 12
HEAD_DIM = 64


EPSILON = 1e-05
NEGATIVE = -1e30


def passed_along(value, axis, steps):
    count = lax.axis_size(axis)
    pairs = [(source, (source + steps) % count) for source in range(count)]
    return lax.ppermute(value, axis, pairs)


def passed_along_2(block, axis, distance):
    devices = range(lax.axis_size(axis))
    route = [(i - distance, i) for i in devices if i - distance in devices]
    return lax.ppermute(block, axis, route)


def layer_norm(values, gain_vec, shift_vec):
    average = jnp.mean(values, axis=-1, keepdims=True)
    centred = values - average
    variance = jnp.mean(centred * centred, axis=-1, keepdims=True)
    return centred * lax.rsqrt(variance + EPSILON) * gain_vec + shift_vec


def mid_norm(up_proj, gain_vec, shift_vec):
    return layer_norm(jax.nn.gelu(up_proj, approximate=False), gain_vec, shift_vec)


def split_heads(values):
    return values.reshape(values.shape[0], values.shape[1], HEADS, HEAD_DIM)


def key_mask(query_pos, key_start, key_count, lengths):
    key_pos = key_start + jnp.arange(key_count, dtype=jnp.int32)
    causal = key_pos[None, :] <= query_pos[:, None]
    inside = key_pos[None, :] < lengths[:, None]
    return causal[None, :, :] & inside[:, None, :]


def fold_keys(running, pieces, key_start, heads_q, query_pos, lengths):
    row_max, row_total, weighted = running
    key_piece, value_piece = pieces
    key_count = key_piece.shape[1]
    score_scale = 1.0 / math.sqrt(HEAD_DIM)
    scores = (
        jnp.einsum(
            "sqhd,skhd->shqk", heads_q, split_heads(key_piece), preferred_element_type=jnp.float32
        )
        * score_scale
    )
    allowed = key_mask(query_pos, key_start, key_count, lengths)[:, None]
    scores = jnp.where(allowed, scores, NEGATIVE)
    fresh_max = jnp.maximum(row_max, jnp.max(scores, axis=-1))
    exponent_vals = jnp.exp(scores - fresh_max[..., None])
    row_total = jnp.sum(exponent_vals, axis=-1)
    update = jnp.einsum(
        "shqk,skhd->sqhd",
        exponent_vals.astype(jnp.bfloat16),
        split_heads(value_piece),
        preferred_element_type=jnp.float32,
    )
    weighted = update
    return (fresh_max, row_total, weighted)


def grad_keys(
    heads_q, heads_do, log_total, dterm, key_piece, value_piece, key_start, query_pos, lengths
):
    seq_count, key_count = (key_piece.shape[0], key_piece.shape[1])
    heads_k = split_heads(key_piece)
    heads_v = split_heads(value_piece)
    score_scale = 1.0 / math.sqrt(HEAD_DIM)
    scores = (
        jnp.einsum("sqhd,skhd->shqk", heads_q, heads_k, preferred_element_type=jnp.float32)
        * score_scale
    )
    allowed = key_mask(query_pos, key_start, key_count, lengths)[:, None]
    probability = jnp.where(allowed, jnp.exp(scores - log_total[..., None]), 0.0)
    dprob = jnp.einsum("sqhd,skhd->shqk", heads_do, heads_v, preferred_element_type=jnp.float32)
    dscores = (probability * (dprob - dterm[..., None])).astype(jnp.bfloat16)
    dq_part = (
        jnp.einsum("shqk,skhd->sqhd", dscores, heads_k, preferred_element_type=jnp.float32)
        * score_scale
    )
    dk_part = (
        jnp.einsum("shqk,sqhd->skhd", dscores, heads_q, preferred_element_type=jnp.float32)
        * score_scale
    )
    dv_part = jnp.einsum(
        "shqk,sqhd->skhd",
        probability.astype(jnp.bfloat16),
        heads_do,
        preferred_element_type=jnp.float32,
    )
    return (
        dq_part,
        dk_part.reshape(seq_count, key_count, -1),
        dv_part.reshape(seq_count, key_count, -1),
    )


def shards(
    hidden,
    teacher,
    lengths,
    w_qkv,
    w_out,
    w_up,
    w_down,
    norm_gain,
    norm_shift,
    proj_bias,
    mid_gain,
    mid_shift,
    up_bias,
):
    (
        full_qkv,
        full_out,
        full_up,
        full_down,
        gain_full,
        shift_full,
        bias_full,
        mid_gain_full,
        mid_shift_full,
        up_bias_full,
    ) = (
        lax.all_gather(w_qkv, "dp", axis=0, tiled=True),
        lax.all_gather(w_out, "dp", axis=0, tiled=True),
        lax.all_gather(w_up, "dp", axis=0, tiled=True),
        lax.all_gather(w_down, "dp", axis=0, tiled=True),
        lax.all_gather(norm_gain, "dp", axis=0, tiled=True),
        lax.all_gather(norm_shift, "dp", axis=0, tiled=True),
        lax.all_gather(proj_bias, "dp", axis=0, tiled=True),
        lax.all_gather(mid_gain, "dp", axis=0, tiled=True),
        lax.all_gather(mid_shift, "dp", axis=0, tiled=True),
        lax.all_gather(up_bias, "dp", axis=0, tiled=True),
    )
    gain_f = gain_full.astype(jnp.float32)
    shift_f = shift_full.astype(jnp.float32)
    bias_f = bias_full.astype(jnp.float32)
    mid_gain_f = mid_gain_full.astype(jnp.float32)
    mid_shift_f = mid_shift_full.astype(jnp.float32)
    up_bias_f = up_bias_full.astype(jnp.float32)
    seq_count, local_rows, model_width = hidden.shape
    token_rows = seq_count * local_rows
    seq_shape = (seq_count, local_rows, model_width)
    ctx_place = lax.axis_index("ctx")
    ctx_parts = lax.axis_size("ctx")
    query_pos = ctx_place * local_rows + jnp.arange(local_rows, dtype=jnp.int32)
    last_query = ctx_place * local_rows + local_rows - 1
    valid_mask = (query_pos[None, :] < lengths[:, None]).astype(jnp.float32)
    valid_rows = valid_mask.reshape(token_rows, 1)
    hidden_rows = hidden.reshape(token_rows, model_width).astype(jnp.float32)
    normed, pull_in = jax.vjp(layer_norm, hidden_rows, gain_f[:, 0], shift_f[:, 0])
    normed_low = normed.astype(jnp.bfloat16)
    projected = jnp.dot(normed_low, full_qkv, preferred_element_type=jnp.float32)
    query_low = (projected[:, :model_width] + bias_f[:, 0]).astype(jnp.bfloat16).reshape(seq_shape)
    key_low = projected[:, model_width : 2 * model_width].astype(jnp.bfloat16).reshape(seq_shape)
    value_low = (
        (projected[:, 2 * model_width :] + bias_f[:, 1]).astype(jnp.bfloat16).reshape(seq_shape)
    )
    heads_q = split_heads(query_low)
    start_state = (
        jnp.full((seq_count, HEADS, local_rows), NEGATIVE, jnp.float32),
        jnp.zeros((seq_count, HEADS, local_rows), jnp.float32),
        jnp.zeros((seq_count, local_rows, HEADS, HEAD_DIM), jnp.float32),
    )
    pieces = (
        lax.all_gather(key_low, "ctx", axis=1, tiled=True),
        lax.all_gather(value_low, "ctx", axis=1, tiled=True),
    )
    key_start = jnp.int32(0)
    row_max, row_total, weighted = lax.cond(
        key_start <= last_query,
        lambda: fold_keys(start_state, pieces, key_start, heads_q, query_pos, lengths),
        lambda: start_state,
    )
    attended = weighted / jnp.transpose(row_total, (0, 2, 1))[..., None]
    log_total = row_max + jnp.log(row_total)
    attended_rows = attended.reshape(token_rows, model_width)
    mixed, pull_mix = jax.vjp(layer_norm, attended_rows, gain_f[:, 1], shift_f[:, 1])
    mixed_low = mixed.astype(jnp.bfloat16)
    residual = (
        hidden_rows
        + jnp.dot(mixed_low, full_out, preferred_element_type=jnp.float32)
        + bias_f[:, 2]
    )
    ffn_in, pull_ffn = jax.vjp(layer_norm, residual, gain_f[:, 2], shift_f[:, 2])
    ffn_low = ffn_in.astype(jnp.bfloat16)
    up_proj = jnp.dot(ffn_low, full_up, preferred_element_type=jnp.float32) + up_bias_f
    activated, pull_mid = jax.vjp(mid_norm, up_proj, mid_gain_f, mid_shift_f)
    act_low = activated.astype(jnp.bfloat16)
    result = (
        residual + jnp.dot(act_low, full_down, preferred_element_type=jnp.float32) + bias_f[:, 3]
    )
    layer_output = (result * valid_rows).astype(jnp.bfloat16).reshape(hidden.shape)
    error_rows = (
        result - teacher.reshape(token_rows, model_width).astype(jnp.float32)
    ) * valid_rows
    loss_total, valid_total = lax.psum(
        (0.5 * jnp.sum(error_rows * error_rows), jnp.sum(valid_mask)), ("dp", "ctx")
    )
    loss = loss_total / (valid_total * model_width)
    down_low = error_rows.astype(jnp.bfloat16)
    bias_down_grad = jnp.sum(down_low.astype(jnp.float32), axis=0)
    down_grad = jnp.einsum("rf,rd->fd", act_low, down_low, preferred_element_type=jnp.float32)
    d_act = jnp.einsum("rd,fd->rf", down_low, full_down, preferred_element_type=jnp.float32)
    d_up, mid_gain_grad, mid_shift_grad = pull_mid(d_act)
    up_low = d_up.astype(jnp.bfloat16)
    up_bias_grad = jnp.sum(up_low.astype(jnp.float32), axis=0)
    up_grad = jnp.einsum("rd,rf->df", ffn_low, up_low, preferred_element_type=jnp.float32)
    d_ffn = jnp.einsum("rf,df->rd", up_low, full_up, preferred_element_type=jnp.float32)
    d_res_norm, gain_two, shift_two = pull_ffn(d_ffn)
    d_residual = error_rows + d_res_norm
    branch_low = d_residual.astype(jnp.bfloat16)
    bias_out_grad = jnp.sum(branch_low.astype(jnp.float32), axis=0)
    out_grad = jnp.einsum("rd,re->de", mixed_low, branch_low, preferred_element_type=jnp.float32)
    d_mixed = jnp.einsum("re,de->rd", branch_low, full_out, preferred_element_type=jnp.float32)
    d_att, gain_one, shift_one = pull_mix(d_mixed)
    heads_do = split_heads(d_att.astype(jnp.bfloat16).reshape(seq_shape))
    dterm = jnp.einsum("sqhd,sqhd->shq", heads_do.astype(jnp.float32), attended)

    def grad_step(key_piece, value_piece, key_start):
        return grad_keys(
            heads_q,
            heads_do,
            log_total,
            dterm,
            key_piece,
            value_piece,
            key_start,
            query_pos,
            lengths,
        )

    dq_zero = jnp.zeros((seq_count, local_rows, HEADS, HEAD_DIM), jnp.float32)
    own_zero = jnp.zeros(seq_shape, jnp.float32)

    def pass_step(step_index, running):
        key_cur, value_cur, dk_run, dv_run, dq_sum = running
        owner = (ctx_place - step_index) % ctx_parts
        dq_part, dk_part, dv_part = lax.cond(
            owner <= ctx_place,
            lambda: grad_step(key_cur, value_cur, owner * local_rows),
            lambda: (dq_zero, own_zero, own_zero),
        )
        dk_run, dv_run = (
            passed_along((dk_run + dk_part).astype(jnp.bfloat16), "ctx", 1).astype(jnp.float32),
            passed_along((dv_run + dv_part).astype(jnp.bfloat16), "ctx", 1).astype(jnp.float32),
        )
        key_cur, value_cur = passed_along_2((key_cur, value_cur), "ctx", 1)
        return (key_cur, value_cur, dk_run, dv_run, dq_sum + dq_part)

    key_end, value_end, dk_own, dv_own, dq_sum = lax.fori_loop(
        0, ctx_parts, pass_step, (key_low, value_low, own_zero, own_zero, dq_zero)
    )
    dq_low = dq_sum.reshape(token_rows, model_width).astype(jnp.bfloat16)
    dk_low = dk_own.reshape(token_rows, model_width).astype(jnp.bfloat16)
    dv_low = dv_own.reshape(token_rows, model_width).astype(jnp.bfloat16)
    dqkv_low = jnp.concatenate([dq_low, dk_low, dv_low], axis=1)
    bias_q_grad = jnp.sum(dq_low.astype(jnp.float32), axis=0)
    bias_v_grad = jnp.sum(dv_low.astype(jnp.float32), axis=0)
    qkv_grad = jnp.einsum("rd,re->de", normed_low, dqkv_low, preferred_element_type=jnp.float32)
    d_normed = jnp.einsum("re,de->rd", dqkv_low, full_qkv, preferred_element_type=jnp.float32)
    d_in_norm, gain_zero, shift_zero = pull_in(d_normed)
    hidden_grad = (d_residual + d_in_norm).reshape(hidden.shape)
    gain_grad = jnp.stack([gain_zero, gain_one, gain_two], axis=1)
    shift_grad = jnp.stack([shift_zero, shift_one, shift_two], axis=1)
    bias_grad = jnp.stack([bias_q_grad, bias_v_grad, bias_out_grad, bias_down_grad], axis=1)
    shares = (
        lax.psum_scatter(
            qkv_grad.astype(jnp.bfloat16), "dp", scatter_dimension=0, tiled=True
        ).astype(jnp.float32),
        lax.psum_scatter(
            out_grad.astype(jnp.bfloat16), "dp", scatter_dimension=0, tiled=True
        ).astype(jnp.float32),
        lax.psum_scatter(
            up_grad.astype(jnp.bfloat16), "dp", scatter_dimension=0, tiled=True
        ).astype(jnp.float32),
        lax.psum_scatter(
            down_grad.astype(jnp.bfloat16), "dp", scatter_dimension=0, tiled=True
        ).astype(jnp.float32),
        lax.psum_scatter(
            gain_grad.astype(jnp.bfloat16), "dp", scatter_dimension=0, tiled=True
        ).astype(jnp.float32),
        lax.psum_scatter(
            shift_grad.astype(jnp.bfloat16), "dp", scatter_dimension=0, tiled=True
        ).astype(jnp.float32),
        lax.psum_scatter(
            bias_grad.astype(jnp.bfloat16), "dp", scatter_dimension=0, tiled=True
        ).astype(jnp.float32),
        lax.psum_scatter(
            mid_gain_grad.astype(jnp.bfloat16), "dp", scatter_dimension=0, tiled=True
        ).astype(jnp.float32),
        lax.psum_scatter(
            mid_shift_grad.astype(jnp.bfloat16), "dp", scatter_dimension=0, tiled=True
        ).astype(jnp.float32),
        lax.psum_scatter(
            up_bias_grad.astype(jnp.bfloat16), "dp", scatter_dimension=0, tiled=True
        ).astype(jnp.float32),
    )
    summed = (
        lax.psum(shares[0].astype(jnp.bfloat16), "ctx").astype(jnp.float32),
        lax.psum(shares[1].astype(jnp.bfloat16), "ctx").astype(jnp.float32),
        lax.psum(shares[2].astype(jnp.bfloat16), "ctx").astype(jnp.float32),
        lax.psum(shares[3].astype(jnp.bfloat16), "ctx").astype(jnp.float32),
        lax.psum(shares[4].astype(jnp.bfloat16), "ctx").astype(jnp.float32),
        lax.psum(shares[5].astype(jnp.bfloat16), "ctx").astype(jnp.float32),
        lax.psum(shares[6].astype(jnp.bfloat16), "ctx").astype(jnp.float32),
        lax.psum(shares[7].astype(jnp.bfloat16), "ctx").astype(jnp.float32),
        lax.psum(shares[8].astype(jnp.bfloat16), "ctx").astype(jnp.float32),
        lax.psum(shares[9].astype(jnp.bfloat16), "ctx").astype(jnp.float32),
    )
    return (
        layer_output,
        loss,
        hidden_grad,
        summed[0],
        summed[1],
        summed[2],
        summed[3],
        summed[4],
        summed[5],
        summed[6],
        summed[7],
        summed[8],
        summed[9],
    )


AXES = ("dp", "ctx")


def swap(value, mask):
    count = lax.axis_size("dp") * lax.axis_size("ctx")
    return lax.ppermute(value, AXES, [(i, i ^ mask) for i in range(count)])


def along_z(piece):
    return [swap(piece, 8 * step) for step in (1, 2, 3)]


def wide(value):
    return value.astype(jnp.float32)


def narrow(value):
    return value.astype(jnp.bfloat16)


VMEM_BYTES = 56 * 1024 * 1024


def whole(shape):
    return pl.BlockSpec(tuple(shape), lambda i: (0,) * len(shape), pipeline_mode=pl.Buffered(1))


def padded(shape, dtype):
    lead = math.prod(shape[:-2])
    size = jnp.dtype(dtype).itemsize
    rows = -(-shape[-2] // (32 // size)) * (32 // size) if len(shape) > 1 else 8
    return lead * rows * (-(-shape[-1] // 128) * 128) * size


def call(body, ins, outs, scratch=(), us=1, deps=(), room=6):
    pairs = [v if isinstance(v, tuple) else (v, whole(v.shape)) for v in ins[1:]]
    held = sum(padded(spec.block_shape, v.dtype) for v, spec in pairs)
    held += sum(padded(shape, dtype) for shape, dtype in (*outs, *scratch))
    count = len(pairs)

    def kernel(sc, *refs):
        body(sc, *refs[:count], *refs[count + len(deps):])

    return pl.pallas_call(
        kernel,
        grid=(1,),
        in_specs=[pl.BlockSpec(memory_space=pltpu.SMEM)] + [spec for _, spec in pairs]
        + [pl.BlockSpec(memory_space=pl.ANY)] * len(deps),
        out_specs=[whole(shape) for shape, _ in outs],
        out_shape=[jax.ShapeDtypeStruct(shape, dtype) for shape, dtype in outs],
        scratch_shapes=[pltpu.VMEM(shape, dtype) for shape, dtype in scratch],
        compiler_params=pltpu.CompilerParams(vmem_limit_bytes=held + room * 1024 * 1024),
        cost_estimate=pl.CostEstimate(flops=int(us * 2e7), bytes_accessed=0, transcendentals=0),
        name=body.__name__,
    )(ins[0], *[v for v, _ in pairs], *deps)


def after(value, *deps):
    return lax.optimization_barrier((value, *deps))[0]


BF, F32 = jnp.bfloat16, jnp.float32


def contract(a, b, da, db):
    return lax.dot_general(a, b, (((da,), (db,)), ((), ())), preferred_element_type=F32)


def block_of(sc, xr, zr):
    return 2 * ((sc[0] >> 1) ^ zr) + ((sc[0] & 1) ^ xr)


def slot_of(sc, block):
    return ((block & 1) ^ (sc[0] & 1)) * 4 + ((block >> 1) ^ (sc[0] >> 1))


def lay(sc, scr, near, far, rows, stride, offset=0):
    for xr, ref in ((0, near), (1, far)):
        for zr in range(4):
            at = pl.multiple_of(stride * block_of(sc, xr, zr) + offset, 16)
            scr[pl.ds(at, rows), :] = ref[zr]


def moments(value):
    average = jnp.mean(value, axis=-1, keepdims=True)
    centred = value - average
    scale = lax.rsqrt(jnp.mean(centred * centred, axis=-1, keepdims=True) + EPSILON)
    return centred * scale, scale


def norm_back(grad, hat, scale):
    return scale * (grad - jnp.mean(grad, axis=-1, keepdims=True) - hat * jnp.mean(grad * hat, axis=-1, keepdims=True))


def mine(ctx_at, row):
    out = row[:, :192]
    for j in range(1, 4):
        out = jnp.where(ctx_at == j, row[:, 192 * j:192 * j + 192], out)
    return out


def pack_body(sc, w, gain, shift, bias, out, scr):
    scr[...] = jnp.zeros((16, 128), F32)
    scr[0:3, :96] = gain[...].astype(F32)
    scr[3:6, :96] = shift[...].astype(F32)
    scr[6:10, :96] = bias[...].astype(F32)
    small = scr[...].T[:96].astype(BF)
    for j in range(4):
        @pl.when(sc[1] == j)
        def _():
            cols = [w[:, 768 * part + 192 * j:768 * part + 192 * j + 192] for part in range(3)]
            out[...] = jnp.concatenate(cols + [small, jnp.zeros((96, 48), BF)], axis=1)


def attend_body(sc, h0, h1, h2, h3, wa, wb, a0, a1, a2, a3, q_o, k_o, v_o, lse_o, ot_o, n_o, vec_o, w_scr):
    ctx_at, length = sc[1], sc[2]
    lay(sc, w_scr, wa, wb, 96, 96)
    vec = w_scr[:, 512:640].astype(F32).T[64:80]
    vec_o[...] = vec
    bias_q, bias_v = mine(ctx_at, vec[6:7]), mine(ctx_at, vec[7:8])
    for r, ref in enumerate((h0, h1, h2, h3)):
        rows = pl.ds(pl.multiple_of((ctx_at ^ r) * 256, 256), 256)
        hat, _ = moments(ref[...].astype(F32))
        normed = (hat * vec[0:1] + vec[3:4]).astype(BF)
        n_o[rows, :] = normed
        p = jnp.dot(normed, w_scr[...], preferred_element_type=F32)
        for h in range(3):
            q_o[h, rows, :] = ((p[:, 64 * h:64 * h + 64] + bias_q[:, 64 * h:64 * h + 64]) * 0.125).astype(BF)
            k_o[h, rows, :] = p[:, 192 + 64 * h:256 + 64 * h].astype(BF)
            v_o[h, rows, :] = (p[:, 384 + 64 * h:448 + 64 * h] + bias_v[:, 64 * h:64 * h + 64]).astype(BF)

    def head(h, carry):
        for i in range(4):
            n = 256 * (i + 1)
            scores = contract(k_o[h, :n, :], q_o[h, 256 * i:256 * i + 256, :], 1, 1)
            limit = jnp.minimum(256 * i + lax.broadcasted_iota(jnp.int32, (1, 256), 1), length - 1)
            scores = jnp.where(lax.broadcasted_iota(jnp.int32, (n, 256), 0) <= limit, scores, NEGATIVE)
            top = jnp.max(scores, axis=0, keepdims=True)
            grown = jnp.exp(scores - top)
            total = jnp.sum(grown, axis=0, keepdims=True)
            out = contract(v_o[h, :n, :], grown.astype(BF), 0, 0) / total
            ot_o[i, pl.ds(pl.multiple_of(64 * h, 64), 64), :] = out
            lse_o[h, i:i + 1, :] = top + jnp.log(total)
        return carry

    lax.fori_loop(0, 3, head, 0)
    for r, ref in enumerate((a0, a1, a2, a3)):
        ref[...] = ot_o[ctx_at ^ r].T.astype(BF)


def attend(sc, hids, wa, wb, deps):
    rows = (256, 192)
    return call(
        attend_body, [sc, *hids, wa, wb],
        [(rows, BF)] * 4 + [((3, 1024, 64), BF)] * 3
        + [((3, 8, 256), F32), ((4, 192, 256), F32), ((1024, 768), BF), ((16, 768), F32)],
        [((768, 640), BF)], us=13, deps=deps)


def attend_back_body(sc, d0, d1, d2, d3, q_i, k_i, v_i, lse_i, ot_i, n_i, h0, h1, h2, h3, wa, wb, vec_i, side_e, side_d, mids,
                     n0, n1, n23, keep, send, w_scr, do_scr, dq_s, dk_s, dv_s, dk_acc, dv_acc, all_scr, g_scr):
    ctx_at, length = sc[1], sc[2]
    lay(sc, w_scr, wa, wb, 96, 96)
    for r, ref in enumerate((d0, d1, d2, d3)):
        rows = pl.ds(pl.multiple_of((ctx_at ^ r) * 256, 256), 256)
        value = ref[...]
        for h in range(3):
            do_scr[h, rows, :] = value[:, 64 * h:64 * h + 64]

    def head(h, carry):
        for i in (3, 2, 1, 0):
            n = 256 * (i + 1)
            mine_rows = slice(256 * i, 256 * i + 256)
            q, do, k = q_i[h, mine_rows, :], do_scr[h, mine_rows, :], k_i[h, :n, :]
            out = ot_i[i, pl.ds(pl.multiple_of(64 * h, 64), 64), :]
            dterm = jnp.sum(do.astype(F32).T * out, axis=0, keepdims=True)
            limit = jnp.minimum(256 * i + lax.broadcasted_iota(jnp.int32, (1, 256), 1), length - 1)
            prob = jnp.exp(contract(k, q, 1, 1) - lse_i[h, i:i + 1, :])
            prob = jnp.where(lax.broadcasted_iota(jnp.int32, (n, 256), 0) <= limit, prob, 0.0)
            dscore = (prob * (contract(v_i[h, :n, :], do, 1, 1) - dterm)).astype(BF)
            dv = jnp.dot(prob.astype(BF), do, preferred_element_type=F32)
            dk = jnp.dot(dscore, q, preferred_element_type=F32)
            if i == 3:
                dv_acc[...] = dv
                dk_acc[...] = dk
            else:
                dv_acc[:n, :] += dv
                dk_acc[:n, :] += dk
            dq_s[h, mine_rows, :] = (contract(k, dscore, 0, 0) * 0.125).T.astype(BF)
        dk_s[h] = dk_acc[...].astype(BF)
        dv_s[h] = dv_acc[...].astype(BF)
        return carry

    lax.fori_loop(0, 3, head, 0)
    for i in range(4):
        rows = slice(256 * i, 256 * i + 256)
        all_scr[rows, :] = jnp.concatenate([s[h, rows, :] for s in (dq_s, dk_s, dv_s) for h in range(3)], axis=1)
    sums = jnp.sum(all_scr[...].astype(F32), axis=0, keepdims=True)
    bias_q = jnp.concatenate([jnp.where(ctx_at == j, sums[:, :192], 0.0) for j in range(4)], axis=1)
    bias_v = jnp.concatenate([jnp.where(ctx_at == j, sums[:, 384:], 0.0) for j in range(4)], axis=1)
    gain_sum, shift_sum = jnp.zeros((1, 768), F32), jnp.zeros((1, 768), F32)
    for r, (ref, out) in enumerate(((h0, n0), (h1, n1), (h2, n23.at[0]), (h3, n23.at[1]))):
        rows = pl.ds(pl.multiple_of((ctx_at ^ r) * 256, 256), 256)
        grad = contract(all_scr[rows, :], w_scr[:, :576], 1, 1)
        hat, _ = moments(ref[...].astype(F32))
        gain_sum += jnp.sum(grad * hat, axis=0, keepdims=True)
        shift_sum += jnp.sum(grad, axis=0, keepdims=True)
        out[...] = grad.astype(BF)
    rows16 = jnp.concatenate(
        [gain_sum, side_e[0:2], shift_sum, side_e[2:4], bias_q, bias_v, side_e[4:5], side_d[0:2], jnp.zeros((5, 768), F32)], axis=0)
    w_grad = contract(n_i[...], all_scr[...], 0, 0)
    for b in range(8):
        at = slot_of(sc, b)
        extra = jnp.concatenate([mids[:, 384 * b:384 * b + 384], rows16[:, 96 * b:96 * b + 96], jnp.zeros((16, 96), F32)], axis=1)
        g_scr[at, :96, :] = w_grad[96 * b:96 * b + 96].astype(BF)
        g_scr[at, 96:112, :] = extra.astype(BF)
    keep[...] = g_scr[:4]
    send[...] = g_scr[4:]


def attend_back(sc, douts, saved, hids, wa, wb, side_e, side_d, mids, deps):
    q, k, v, lse, ot, normed, vec = saved
    return call(
        attend_back_body, [sc, *douts, q, k, v, lse, ot, normed, *hids, wa, wb, vec, side_e, side_d, mids],
        [((256, 768), BF)] * 2 + [((2, 256, 768), BF)] + [((4, 112, 576), BF)] * 2,
        [((768, 640), BF), ((3, 1024, 64), BF), ((3, 1024, 64), BF), ((3, 1024, 64), BF), ((3, 1024, 64), BF),
         ((1024, 64), F32), ((1024, 64), F32), ((1024, 576), BF), ((8, 112, 576), BF)],
        us=12, deps=deps)


def part(rows, at):
    return pl.BlockSpec((4, rows, 768), lambda i: (0, at, 0), pipeline_mode=pl.Buffered(1))


def lay_out(sc, scr, own_near, own_far, other_near, other_far):
    core = sc[1] & 1
    lay(sc, scr, own_near, own_far, 48, 96, 48 * core)
    lay(sc, scr, other_near, other_far, 48, 96, 48 * (1 - core))


def lay_down(sc, scr, refs):
    for c in (0, 1):
        for xr in (0, 1):
            for y in (0, 1):
                lay_one(sc, scr, refs[4 * c + 2 * xr + y], xr, 96 * (sc[1] ^ (2 * y + c)))


def lay_one(sc, scr, ref, xr, offset):
    for zr in range(4):
        scr[pl.ds(pl.multiple_of(384 * block_of(sc, xr, zr) + offset, 32), 96), :] = ref[zr]


def join_heads(sc, scr, pieces):
    for r, ref in enumerate(pieces):
        scr[r] = ref[...]
    return jnp.concatenate([scr[sc[1] ^ j] for j in range(4)], axis=1).astype(F32)


def mid_body(sc, g0, g1, g2, g3, own, vec, on, of, tn, tf, mixed_o, resid_o, ffn_o, w_scr, a_scr):
    lay_out(sc, w_scr, on, of, tn, tf)
    hat, _ = moments(join_heads(sc, a_scr, (g0, g1, g2, g3)))
    mixed = (hat * vec[1:2] + vec[4:5]).astype(BF)
    mixed_o[...] = mixed
    resid = own[...].astype(F32) + jnp.dot(mixed, w_scr[...], preferred_element_type=F32) + vec[8:9]
    resid_o[...] = resid
    hat, _ = moments(resid)
    ffn_o[...] = (hat * vec[2:3] + vec[5:6]).astype(BF)


def up_body(sc, ffn, w0n, w0f, w1n, w1f, w2n, w2f, w3n, w3f, mn, mf, act_o, hat_o, slope_o, scale_o, nat_o,
            w_scr, g_scr, m_scr):
    for xr, ref in ((0, mn), (1, mf)):
        for zr in range(4):
            m_scr[block_of(sc, xr, zr)] = ref[zr].astype(F32)
    flat = [m_scr[b] for b in range(8)]
    for j in range(4):
        two = flat[2 * j:2 * j + 2]
        nat_o[j, 0:1, :] = jnp.concatenate([m[0:1, :384] for m in two], axis=1)
        nat_o[j, 1:2, :] = jnp.concatenate([m[0:1, 384:] for m in two], axis=1)
        nat_o[j, 2:3, :] = jnp.concatenate([m[1:2, :384] for m in two], axis=1)
        nat_o[j, 3:8, :] = jnp.zeros((5, 768), F32)
    value = ffn[...]
    total = jnp.zeros((256, 1), F32)
    for t, (near, far) in enumerate(((w0n, w0f), (w1n, w1f), (w2n, w2f), (w3n, w3f))):
        j = sc[1] ^ t
        lay(sc, w_scr.at[t], near, far, 96, 96)
        up = jnp.dot(value, w_scr[t], preferred_element_type=F32) + nat_o[j, 2:3, :]
        chance = 0.5 * (1.0 + lax.erf(up * math.sqrt(0.5)))
        slope_o[j] = (chance + up * jnp.exp(-0.5 * up * up) * (1.0 / math.sqrt(2.0 * math.pi))).astype(BF)
        gelu = up * chance
        g_scr[j] = gelu
        total += jnp.sum(gelu, axis=-1, keepdims=True)
    average = total * (1.0 / 3072)
    square = jnp.zeros((256, 1), F32)
    for j in range(4):
        centred = g_scr[j] - average
        square += jnp.sum(centred * centred, axis=-1, keepdims=True)
    scale = lax.rsqrt(square * (1.0 / 3072) + EPSILON)
    scale_o[...] = scale
    for j in range(4):
        hat = (g_scr[j] - average) * scale
        hat_o[j] = hat.astype(BF)
        act_o[j] = (hat * nat_o[j, 0:1, :] + nat_o[j, 1:2, :]).astype(BF)


def down_body(sc, act, resid, teacher, vec, e0, e1, e2, e3, e4, e5, e6, e7, out_o, err_o, low_o, side_o, w_scr):
    lay_down(sc, w_scr, (e0, e1, e2, e3, e4, e5, e6, e7))
    result = resid[...] + vec[9:10]
    for j in range(4):
        result += jnp.dot(act[j], w_scr[768 * j:768 * j + 768, :], preferred_element_type=F32)
    pos = sc[1] * 256 + lax.broadcasted_iota(jnp.int32, (256, 1), 0)
    valid = jnp.where(pos < sc[2], 1.0, 0.0)
    out_o[...] = (result * valid).astype(BF)
    error = (result - teacher[...].astype(F32)) * valid
    err_o[...] = error
    low = error.astype(BF)
    low_o[...] = low
    side_o[0:1, :] = jnp.sum(low.astype(F32), axis=0, keepdims=True)
    loss = 0.5 * jnp.sum(jnp.sum(error * error, axis=0, keepdims=True), axis=1, keepdims=True)
    count = jnp.sum(valid, axis=0, keepdims=True)
    high = loss.astype(BF).astype(F32)
    lane = lax.broadcasted_iota(jnp.int32, (1, 768), 1) % 96
    side_o[1:2, :] = jnp.where(lane == 0, high, jnp.where(lane == 1, loss - high, jnp.where(lane == 2, count, 0.0)))
    side_o[2:8, :] = jnp.zeros((6, 768), F32)


def down_grad_body(sc, act, low, keep, send, g_scr):
    value = low[...]
    for j in range(4):
        grad = contract(act[j], value, 0, 0).astype(BF)
        for half in (0, 1):
            at = slot_of(sc, 2 * j + half)
            for q in range(4):
                g_scr[sc[1] ^ q, at] = grad[384 * half + 96 * q:384 * half + 96 * q + 96]
    for y in (0, 1):
        keep[y] = g_scr[2 * y]
        send[y] = g_scr[2 * y + 1]


def act_back_body(sc, low, hat_i, slope, scale, nat, e0, e1, e2, e3, e4, e5, e6, e7, up_o, mids_o, wd_scr, dh_scr):
    lay_down(sc, wd_scr, (e0, e1, e2, e3, e4, e5, e6, e7))
    value = low[...]
    first, second = jnp.zeros((256, 1), F32), jnp.zeros((256, 1), F32)
    for j in range(4):
        grad = contract(value, wd_scr[768 * j:768 * j + 768, :], 1, 1)
        hat = hat_i[j].astype(F32)
        cols = slice(768 * j, 768 * j + 768)
        mids_o[0:1, cols] = jnp.sum(grad * hat, axis=0, keepdims=True)
        mids_o[1:2, cols] = jnp.sum(grad, axis=0, keepdims=True)
        grad = grad * nat[j, 0:1, :]
        dh_scr[j] = grad
        first += jnp.sum(grad, axis=-1, keepdims=True)
        second += jnp.sum(grad * hat, axis=-1, keepdims=True)
    first, second = first * (1.0 / 3072), second * (1.0 / 3072)
    for j in range(4):
        hat = hat_i[j].astype(F32)
        grad = (scale[...] * (dh_scr[j] - first - hat * second) * slope[j].astype(F32)).astype(BF)
        up_o[j] = grad
        mids_o[2:3, 768 * j:768 * j + 768] = jnp.sum(grad.astype(F32), axis=0, keepdims=True)
    mids_o[3:16, :] = jnp.zeros((13, 3072), F32)


def ffn_back_body(sc, up_i, err, resid, w0n, w0f, w1n, w1f, w2n, w2f, w3n, w3f, on, of, tn, tf, vec, g0, g1, g2, g3,
                  branch_o, dres_o, p0, p1, p2, p3, side_o, w_scr, o_scr, a_scr, b_scr):
    grad = jnp.zeros((256, 768), F32)
    for t, (near, far) in enumerate(((w0n, w0f), (w1n, w1f), (w2n, w2f), (w3n, w3f))):
        lay(sc, w_scr.at[t], near, far, 96, 96)
        grad += contract(up_i[sc[1] ^ t], w_scr[t], 1, 1)
    hat, factor = moments(resid[...])
    side_o[1:2, :] = jnp.sum(grad * hat, axis=0, keepdims=True)
    side_o[3:4, :] = jnp.sum(grad, axis=0, keepdims=True)
    dres = err[...] + norm_back(grad * vec[2:3], hat, factor)
    dres_o[...] = dres
    branch = dres.astype(BF)
    branch_o[...] = branch
    side_o[4:5, :] = jnp.sum(branch.astype(F32), axis=0, keepdims=True)
    lay_out(sc, o_scr, on, of, tn, tf)
    grad = contract(branch, o_scr[...], 1, 1)
    hat, factor = moments(join_heads(sc, a_scr, (g0, g1, g2, g3)))
    side_o[0:1, :] = jnp.sum(grad * hat, axis=0, keepdims=True)
    side_o[2:3, :] = jnp.sum(grad, axis=0, keepdims=True)
    side_o[5:8, :] = jnp.zeros((3, 768), F32)
    grad = norm_back(grad * vec[1:2], hat, factor).astype(BF)
    for j in range(4):
        b_scr[j] = grad[:, 192 * j:192 * j + 192]
    for r, ref in enumerate((p0, p1, p2, p3)):
        ref[...] = b_scr[sc[1] ^ r]


def up_grad_body(sc, ffn, up, keep, send, g_scr):
    value = ffn[...]
    for j in range(4):
        grad = contract(value, up[j], 0, 0).astype(BF)
        for b in range(8):
            g_scr[sc[1] ^ j, slot_of(sc, b)] = grad[96 * b:96 * b + 96]
    for y in (0, 1):
        keep[y] = g_scr[2 * y]
        send[y] = g_scr[2 * y + 1]


def out_grad_body(sc, mixed, branch, out_keep, out_send, o_scr):
    grad = contract(mixed[...], branch[...], 0, 0).astype(BF)
    for b in range(8):
        for c in (0, 1):
            o_scr[(sc[1] & 1) ^ c, slot_of(sc, b)] = grad[96 * b + 48 * c:96 * b + 48 * c + 48]
    out_keep[...] = o_scr[0]
    out_send[...] = o_scr[1]


def added(a, b):
    return a.astype(F32) + b.astype(F32)


def pair_body(sc, keep, got, near0, near1, far0, far1):
    for y, near, far in ((0, near0, far0), (1, near1, far1)):
        near[...] = added(keep[y, :4], got[y, :4]).astype(BF)
        far[...] = added(keep[y, 4:], got[y, 4:]).astype(BF)


def slots_body(sc, near, got, own, s1, s2, s3):
    own[...] = added(near[0], got[0])
    for at, out in ((1, s1), (2, s2), (3, s3)):
        out[...] = added(near[at], got[at]).astype(BF)


def join_far_body(sc, mine, got, out_keep, out_got, far):
    far[:, :96, :] = added(mine[...], got[...]).astype(BF)
    far[:, 96:, :] = added(out_keep[...], out_got[...]).astype(BF)


def join_near_body(sc, mine, y_got, out_keep, out_got, x_got, own, s1, s2, s3):
    for at, out in ((0, own), (1, s1), (2, s2), (3, s3)):
        kind = out.dtype
        out[:96, :] = (added(mine[at], y_got[at]) + x_got[at, :96, :].astype(F32)).astype(kind)
        out[96:, :] = (added(out_keep[at], out_got[at]) + x_got[at, 96:, :].astype(F32)).astype(kind)


def total_of(own, parts):
    return (own[...] + sum(p[...].astype(F32) for p in parts)).astype(BF)


def sums_body(sc, u0, u1, u2, u3, d0, d1, d2, d3, e0, e1, e2, e3, out):
    out[0:144, :] = total_of(u0, (u1, u2, u3))
    out[144:240, :] = total_of(d0, (d1, d2, d3))
    out[240:336, :] = total_of(e0, (e1, e2, e3))


def fold_body(sc, own, other, out):
    out[0:96, :] = own[0:96, :]
    out[96:192, :] = other[0:96, :]
    out[192:240, :] = added(own[96:144, :], other[96:144, :]).astype(BF)
    out[240:336, :] = added(own[144:240, :], other[240:336, :]).astype(BF)
    out[336:432, :] = added(own[240:336, :], other[144:240, :]).astype(BF)


def add_body(sc, a, b, out):
    out[...] = added(a[...], b[0]).astype(BF)


def spread_body(sc, mine, other, up_o, out_o, down_o, scr):
    core = sc[1] & 1
    for t, (ref, at) in enumerate(((mine, 0), (other, 0), (mine, 96), (other, 96))):
        scr[sc[1] ^ t] = ref[at:at + 96, :].astype(F32)
        rows = pl.multiple_of(96 * (sc[1] ^ t), 32)
        down_o[pl.ds(rows, 96), :] = ref[240 + at:336 + at, :].astype(F32)
    for j in range(4):
        up_o[:, 768 * j:768 * j + 768] = scr[j]
    out_o[pl.ds(pl.multiple_of(48 * core, 16), 48), :] = mine[192:240, :].astype(F32)
    out_o[pl.ds(pl.multiple_of(48 * (1 - core), 16), 48), :] = other[192:240, :].astype(F32)


def spread_qkv_body(sc, t0, t1, t2, t3, grad_o, gain_o, shift_o, bias_o, mid_o, loss_o, scr):
    rest = jnp.zeros((16, 576), F32)
    for r, ref in enumerate((t0, t1, t2, t3)):
        scr[sc[1] ^ r] = ref[:96, :]
        rest += ref[96:112, :].astype(F32)
    for p in range(3):
        cols = [scr[j, :, 192 * p:192 * p + 192] for j in range(4)]
        grad_o[:, 768 * p:768 * p + 768] = jnp.concatenate(cols, axis=1).astype(F32)
    gain_o[...] = rest[0:3, 384:480]
    shift_o[...] = rest[3:6, 384:480]
    bias_o[...] = rest[6:10, 384:480]
    mid_o[...] = rest[0:8, :384]
    row = rest[10:11, 384:480]
    lane = lax.broadcasted_iota(jnp.int32, (1, 96), 1)
    error = jnp.sum(jnp.where(lane < 2, row, 0.0), axis=1, keepdims=True)
    count = jnp.sum(jnp.where(lane == 2, row, 0.0), axis=1, keepdims=True)
    loss_o[...] = error / (count * 768.0)


def hidden_body(sc, a, b, c, own, vec, d_res, out):
    grad = (added(a[...], b[0]) + c[...].astype(F32)) * vec[0:1]
    hat, factor = moments(own[...].astype(F32))
    out[...] = d_res[...] + norm_back(grad, hat, factor)


def total_body(sc, own, s1, s2, s3, out):
    out[...] = total_of(own, (s1, s2, s3))


def fast(
    hidden, teacher, lengths, w_qkv, w_out, w_up, w_down, norm_gain, norm_shift, proj_bias,
    mid_gain, mid_shift, up_bias,
):
    dp_at, ctx_at = lax.axis_index("dp"), lax.axis_index("ctx")
    core = ctx_at & 1
    sc = jnp.stack([dp_at, ctx_at, lengths[0]]).astype(jnp.int32)
    own = hidden[0]
    tall = (256, 768)
    barrier = lax.optimization_barrier
    h_y, h_c = swap(own, 2), swap(own, 1)
    piece = call(pack_body, [sc, w_qkv, norm_gain.T, norm_shift.T, proj_bias.T], [((96, 640), BF)], [((16, 128), F32)])[0]
    q_cols = along_z(piece)
    mid_rows = jnp.concatenate([mid_gain, mid_shift, up_bias, jnp.zeros((13 * 384,), BF)]).reshape(8, 768)
    piece_a = jnp.concatenate([
        lax.dynamic_slice(w_up, (0, 768 * ctx_at), (96, 768)), lax.dynamic_slice(w_out, (48 * core, 0), (48, 768)), mid_rows])
    down4 = w_down.reshape(4, 96, 768)
    piece_b, piece_c = (lax.dynamic_index_in_dim(down4, ctx_at ^ t, 0, keepdims=False) for t in (0, 2))
    q_cols, piece_a, h_y = barrier((q_cols, piece_a, h_y))
    q_near = jnp.stack([piece] + q_cols)
    q_far = swap(q_near, 4)
    h_yc = swap(h_y, 1)
    a_cols = along_z(piece_a)
    a_cols, q_far, piece_b, h_c, h_yc = barrier((a_cols, q_far, piece_b, h_c, h_yc))
    a_near = jnp.stack([piece_a] + a_cols)
    a_far = swap(a_near, 4)
    y_near = swap(a_near[:, :96], 2)
    a_near_o = swap(a_near, 1)
    b_cols = along_z(piece_b)
    hids = [own, h_c, h_y, h_yc]
    *att, q, k, v, lse, ot, normed, vec = attend(sc, hids, q_near, q_far, (a_near,))
    b_cols, piece_c, att = barrier((b_cols, piece_c, att))
    c_cols = along_z(piece_c)
    b_near = jnp.stack([piece_b] + b_cols)
    a_far, y_near, b_near, att = barrier((a_far, y_near, b_near, att))
    b_far, b_near_o = swap(b_near, 4), swap(b_near, 1)
    got = [att[0]] + [swap(att[r], r) for r in (1, 2, 3)]
    y_far = swap(a_far[:, :96], 2)
    a_far_o, y_near_o = swap(a_far, 1), swap(y_near, 1)
    outs = [(t, part(48, 2)) for t in (a_near, a_far, a_near_o, a_far_o)]
    mixed, resid, ffn = call(
        mid_body, [sc, *got, own, vec, *outs], [(tall, BF), (tall, F32), (tall, BF)],
        [((768, 768), BF), ((4, 256, 192), BF)], us=3)
    c_cols, b_far, mixed = barrier((c_cols, b_far, mixed))
    c_near = jnp.stack([piece_c] + c_cols)
    c_far, c_near_o = swap(c_near, 4), swap(c_near, 1)
    b_far_o, y_far_o = swap(b_far, 1), swap(y_far, 1)
    ups = [(t, part(96, 0)) for t in (a_near, a_far, a_near_o, a_far_o)] + [y_near, y_far, y_near_o, y_far_o]
    four = (4, 256, 768)
    act, hat, slope, scale, nat = call(
        up_body, [sc, ffn, *ups] + [(t, part(8, 18)) for t in (a_near, a_far)],
        [(four, BF), (four, BF), (four, BF), ((256, 1), F32), ((4, 8, 768), F32)],
        [((4, 768, 768), BF), (four, F32), ((8, 8, 768), F32)], us=5, deps=(c_near,))
    c_far_o = swap(c_far, 1)
    downs = [b_near, c_near, b_far, c_far, b_near_o, c_near_o, b_far_o, c_far_o]
    out, err, low, side_d = call(
        down_body, [sc, act, resid, teacher[0], vec, *downs],
        [(tall, BF), (tall, F32), (tall, BF), ((8, 768), F32)], [((3072, 768), BF)], us=5)
    halves_of = ((2, 8, 96, 768), BF)
    down_keep, down_send = call(
        down_grad_body, [sc, act, low], [halves_of] * 2, [((4, 8, 96, 768), BF)], us=3)
    down_got = swap(down_send, 1)
    up_low, mids = call(
        act_back_body, [sc, low, hat, slope, scale, nat, *downs], [(four, BF), ((16, 3072), F32)],
        [((3072, 768), BF), (four, F32)], us=5, deps=(down_keep,))
    slots = ((4, 96, 768), BF)
    d_near0, d_near1, d_far0, d_far1 = call(pair_body, [sc, down_keep, down_got], [slots] * 4, us=2, deps=(mids,))
    d_far0, up_low = barrier((d_far0, up_low))
    d_got0 = swap(d_far0, 4)
    up_keep, up_send = call(up_grad_body, [sc, ffn, up_low], [halves_of] * 2, [((4, 8, 96, 768), BF)], us=3, deps=(d_near0,))
    up_got = swap(up_send, 1)
    branch, d_res, *d_att, side_e = call(
        ffn_back_body, [sc, up_low, err, resid, *ups, *outs, vec, *got],
        [(tall, BF), (tall, F32)] + [((256, 192), BF)] * 4 + [((8, 768), F32)],
        [((4, 768, 768), BF), ((768, 768), BF), ((4, 256, 192), BF), ((4, 256, 192), BF)], us=6, deps=(up_keep,))
    u_near0, u_near1, u_far0, u_far1 = call(pair_body, [sc, up_keep, up_got], [slots] * 4, us=2, deps=(side_e,))
    d_got = [d_att[0]] + [swap(d_att[r], r) for r in (1, 2, 3)]
    out_keep, out_send = call(
        out_grad_body, [sc, mixed, branch], [((8, 48, 768), BF)] * 2, [((2, 8, 48, 768), BF)], us=1, deps=(u_near0,))
    out_got = swap(out_send, 1)
    own_part, sent = ((96, 768), F32), ((96, 768), BF)
    d_own0, *d_z0 = call(slots_body, [sc, d_near0, d_got0], [own_part] + [sent] * 3, us=1, deps=(out_keep,))

    def along_z_back(parts):
        return [swap(parts[step - 1], 8 * step) for step in (1, 2, 3)]

    d_z0, d_far1, u_far1, d_got, out_got = barrier((d_z0, d_far1, u_far1, d_got, out_got))
    d_z0 = along_z_back(d_z0)
    d_got1 = swap(d_far1, 4)
    uy_far = swap(u_far1, 2)
    dn_0, dn_1, dn_23, q_keep, q_send = attend_back(
        sc, d_got, (q, k, v, lse, ot, normed, vec), hids, q_near, q_far, side_e, side_d, mids, (d_own0, out_got))
    d_z0, d_got1, uy_far, u_near1, dn_0, dn_1, dn_23, q_keep, q_send = barrier(
        (d_z0, d_got1, uy_far, u_near1, dn_0, dn_1, dn_23, q_keep, q_send))
    near, far = (pl.BlockSpec((4, 48, 768), lambda i, at=at: (at, 0, 0), pipeline_mode=pl.Buffered(1)) for at in (0, 1))
    u_x = call(join_far_body, [sc, u_far0, uy_far, (out_keep, far), (out_got, far)], [((4, 144, 768), BF)], us=1)[0]
    ux_got = swap(u_x, 4)
    uy_near = swap(u_near1, 2)
    d_own1, *d_z1 = call(slots_body, [sc, d_near1, d_got1], [own_part] + [sent] * 3, us=1, deps=(u_x,))
    d_z1 = along_z_back(d_z1)
    ux_got, uy_near, d_z1, q_send, dn_23 = barrier((ux_got, uy_near, d_z1, q_send, dn_23))
    u_own, *u_z = call(
        join_near_body, [sc, u_near0, uy_near, (out_keep, near), (out_got, near), ux_got],
        [((144, 768), F32)] + [((144, 768), BF)] * 3, us=1)
    u_z = along_z_back(u_z)
    q_got = swap(q_send, 4)
    dn_y = swap(dn_23, 2)
    q_got, first, dn_y = barrier((q_got, u_z[0], dn_y))
    q_own, *q_z = call(slots_body, [sc, q_keep, q_got], [((112, 576), F32)] + [((112, 576), BF)] * 3, us=1)
    q_z = along_z_back(q_z)
    one = [pl.BlockSpec((1, 256, 768), lambda i, at=at: (at, 0, 0), pipeline_mode=pl.Buffered(1)) for at in (0, 1)]
    dn_1 = call(add_body, [sc, dn_1, (dn_y, one[1])], [(tall, BF)], us=1, deps=(q_own,))[0]
    dn_c = swap(dn_1, 1)
    sums = call(
        sums_body, [sc, u_own, first, *u_z[1:], d_own0, *d_z0, d_own1, *d_z1], [((336, 768), BF)], us=1, deps=(dn_1,))[0]
    sums_y = swap(sums, 2)
    hidden_grad = call(hidden_body, [sc, dn_0, (dn_y, one[0]), dn_c, own, vec, d_res], [(tall, F32)], us=1, deps=(sums,))[0]
    q_sum = call(total_body, [sc, q_own, *q_z], [((112, 576), BF)], us=1, deps=(hidden_grad,))[0]
    q_y, q_c = swap(q_sum, 2), swap(q_sum, 1)
    five = call(fold_body, [sc, sums, sums_y], [((432, 768), BF)], us=1, deps=(q_sum,))[0]
    more = swap(five, 1)
    q_yc = swap(q_y, 1)
    grad_up, grad_out, grad_down = call(
        spread_body, [sc, five, more], [((96, 3072), F32), ((96, 768), F32), ((384, 768), F32)], [((4, 96, 768), F32)],
        us=2)
    grad_qkv, gain, shift, bias, mid, loss = call(
        spread_qkv_body, [sc, q_sum, q_c, q_y, q_yc],
        [((96, 2304), F32), ((3, 96), F32), ((3, 96), F32), ((4, 96), F32), ((8, 384), F32), ((1, 1), F32)],
        [((4, 96, 576), BF)], us=2, deps=(grad_out,))
    return (out[None], loss[0, 0], hidden_grad[None], grad_qkv, grad_out, grad_up, grad_down,
            gain.T, shift.T, bias.T, mid[0], mid[1], mid[2])


def solution(mesh):
    step = fast if (mesh.shape["dp"], mesh.shape["ctx"]) == (8, 4) else shards
    placed = (
        P("dp", "ctx", None),
        P("dp", "ctx", None),
        P("dp"),
        P("dp", None),
        P("dp", None),
        P("dp", None),
        P("dp", None),
        P("dp", None),
        P("dp", None),
        P("dp", None),
        P("dp"),
        P("dp"),
        P("dp"),
    )
    return jax.shard_map(
        step,
        mesh=mesh,
        in_specs=placed,
        out_specs=(
            P("dp", "ctx", None),
            P(),
            P("dp", "ctx", None),
            P("dp", None),
            P("dp", None),
            P("dp", None),
            P("dp", None),
            P("dp", None),
            P("dp", None),
            P("dp", None),
            P("dp"),
            P("dp"),
            P("dp"),
        ),
        check_vma=False,
    )
```

```python
import math

import jax
import jax.numpy as jnp
from jax import lax
from jax.experimental import pallas as pl
from jax.experimental.pallas import tpu as pltpu
from jax.sharding import PartitionSpec as P

HEADS = 12
HEAD_DIM = 64


EPSILON = 1e-05
NEGATIVE = -1e30


def passed_along(value, axis, steps):
    count = lax.axis_size(axis)
    pairs = [(source, (source + steps) % count) for source in range(count)]
    return lax.ppermute(value, axis, pairs)


def passed_along_2(block, axis, distance):
    devices = range(lax.axis_size(axis))
    route = [(i - distance, i) for i in devices if i - distance in devices]
    return lax.ppermute(block, axis, route)


def layer_norm(values, gain_vec, shift_vec):
    average = jnp.mean(values, axis=-1, keepdims=True)
    centred = values - average
    variance = jnp.mean(centred * centred, axis=-1, keepdims=True)
    return centred * lax.rsqrt(variance + EPSILON) * gain_vec + shift_vec


def mid_norm(up_proj, gain_vec, shift_vec):
    return layer_norm(jax.nn.gelu(up_proj, approximate=False), gain_vec, shift_vec)


def split_heads(values):
    return values.reshape(values.shape[0], values.shape[1], HEADS, HEAD_DIM)


def key_mask(query_pos, key_start, key_count, lengths):
    key_pos = key_start + jnp.arange(key_count, dtype=jnp.int32)
    causal = key_pos[None, :] <= query_pos[:, None]
    inside = key_pos[None, :] < lengths[:, None]
    return causal[None, :, :] & inside[:, None, :]


def fold_keys(running, pieces, key_start, heads_q, query_pos, lengths):
    row_max, row_total, weighted = running
    key_piece, value_piece = pieces
    key_count = key_piece.shape[1]
    score_scale = 1.0 / math.sqrt(HEAD_DIM)
    scores = (
        jnp.einsum(
            "sqhd,skhd->shqk", heads_q, split_heads(key_piece), preferred_element_type=jnp.float32
        )
        * score_scale
    )
    allowed = key_mask(query_pos, key_start, key_count, lengths)[:, None]
    scores = jnp.where(allowed, scores, NEGATIVE)
    fresh_max = jnp.maximum(row_max, jnp.max(scores, axis=-1))
    exponent_vals = jnp.exp(scores - fresh_max[..., None])
    row_total = jnp.sum(exponent_vals, axis=-1)
    update = jnp.einsum(
        "shqk,skhd->sqhd",
        exponent_vals.astype(jnp.bfloat16),
        split_heads(value_piece),
        preferred_element_type=jnp.float32,
    )
    weighted = update
    return (fresh_max, row_total, weighted)


def grad_keys(
    heads_q, heads_do, log_total, dterm, key_piece, value_piece, key_start, query_pos, lengths
):
    seq_count, key_count = (key_piece.shape[0], key_piece.shape[1])
    heads_k = split_heads(key_piece)
    heads_v = split_heads(value_piece)
    score_scale = 1.0 / math.sqrt(HEAD_DIM)
    scores = (
        jnp.einsum("sqhd,skhd->shqk", heads_q, heads_k, preferred_element_type=jnp.float32)
        * score_scale
    )
    allowed = key_mask(query_pos, key_start, key_count, lengths)[:, None]
    probability = jnp.where(allowed, jnp.exp(scores - log_total[..., None]), 0.0)
    dprob = jnp.einsum("sqhd,skhd->shqk", heads_do, heads_v, preferred_element_type=jnp.float32)
    dscores = (probability * (dprob - dterm[..., None])).astype(jnp.bfloat16)
    dq_part = (
        jnp.einsum("shqk,skhd->sqhd", dscores, heads_k, preferred_element_type=jnp.float32)
        * score_scale
    )
    dk_part = (
        jnp.einsum("shqk,sqhd->skhd", dscores, heads_q, preferred_element_type=jnp.float32)
        * score_scale
    )
    dv_part = jnp.einsum(
        "shqk,sqhd->skhd",
        probability.astype(jnp.bfloat16),
        heads_do,
        preferred_element_type=jnp.float32,
    )
    return (
        dq_part,
        dk_part.reshape(seq_count, key_count, -1),
        dv_part.reshape(seq_count, key_count, -1),
    )


def shards(
    hidden,
    teacher,
    lengths,
    w_qkv,
    w_out,
    w_up,
    w_down,
    norm_gain,
    norm_shift,
    proj_bias,
    mid_gain,
    mid_shift,
    up_bias,
):
    (
        full_qkv,
        full_out,
        full_up,
        full_down,
        gain_full,
        shift_full,
        bias_full,
        mid_gain_full,
        mid_shift_full,
        up_bias_full,
    ) = (
        lax.all_gather(w_qkv, "dp", axis=0, tiled=True),
        lax.all_gather(w_out, "dp", axis=0, tiled=True),
        lax.all_gather(w_up, "dp", axis=0, tiled=True),
        lax.all_gather(w_down, "dp", axis=0, tiled=True),
        lax.all_gather(norm_gain, "dp", axis=0, tiled=True),
        lax.all_gather(norm_shift, "dp", axis=0, tiled=True),
        lax.all_gather(proj_bias, "dp", axis=0, tiled=True),
        lax.all_gather(mid_gain, "dp", axis=0, tiled=True),
        lax.all_gather(mid_shift, "dp", axis=0, tiled=True),
        lax.all_gather(up_bias, "dp", axis=0, tiled=True),
    )
    gain_f = gain_full.astype(jnp.float32)
    shift_f = shift_full.astype(jnp.float32)
    bias_f = bias_full.astype(jnp.float32)
    mid_gain_f = mid_gain_full.astype(jnp.float32)
    mid_shift_f = mid_shift_full.astype(jnp.float32)
    up_bias_f = up_bias_full.astype(jnp.float32)
    seq_count, local_rows, model_width = hidden.shape
    token_rows = seq_count * local_rows
    seq_shape = (seq_count, local_rows, model_width)
    ctx_place = lax.axis_index("ctx")
    ctx_parts = lax.axis_size("ctx")
    query_pos = ctx_place * local_rows + jnp.arange(local_rows, dtype=jnp.int32)
    last_query = ctx_place * local_rows + local_rows - 1
    valid_mask = (query_pos[None, :] < lengths[:, None]).astype(jnp.float32)
    valid_rows = valid_mask.reshape(token_rows, 1)
    hidden_rows = hidden.reshape(token_rows, model_width).astype(jnp.float32)
    normed, pull_in = jax.vjp(layer_norm, hidden_rows, gain_f[:, 0], shift_f[:, 0])
    normed_low = normed.astype(jnp.bfloat16)
    projected = jnp.dot(normed_low, full_qkv, preferred_element_type=jnp.float32)
    query_low = (projected[:, :model_width] + bias_f[:, 0]).astype(jnp.bfloat16).reshape(seq_shape)
    key_low = projected[:, model_width : 2 * model_width].astype(jnp.bfloat16).reshape(seq_shape)
    value_low = (
        (projected[:, 2 * model_width :] + bias_f[:, 1]).astype(jnp.bfloat16).reshape(seq_shape)
    )
    heads_q = split_heads(query_low)
    start_state = (
        jnp.full((seq_count, HEADS, local_rows), NEGATIVE, jnp.float32),
        jnp.zeros((seq_count, HEADS, local_rows), jnp.float32),
        jnp.zeros((seq_count, local_rows, HEADS, HEAD_DIM), jnp.float32),
    )
    pieces = (
        lax.all_gather(key_low, "ctx", axis=1, tiled=True),
        lax.all_gather(value_low, "ctx", axis=1, tiled=True),
    )
    key_start = jnp.int32(0)
    row_max, row_total, weighted = lax.cond(
        key_start <= last_query,
        lambda: fold_keys(start_state, pieces, key_start, heads_q, query_pos, lengths),
        lambda: start_state,
    )
    attended = weighted / jnp.transpose(row_total, (0, 2, 1))[..., None]
    log_total = row_max + jnp.log(row_total)
    attended_rows = attended.reshape(token_rows, model_width)
    mixed, pull_mix = jax.vjp(layer_norm, attended_rows, gain_f[:, 1], shift_f[:, 1])
    mixed_low = mixed.astype(jnp.bfloat16)
    residual = (
        hidden_rows
        + jnp.dot(mixed_low, full_out, preferred_element_type=jnp.float32)
        + bias_f[:, 2]
    )
    ffn_in, pull_ffn = jax.vjp(layer_norm, residual, gain_f[:, 2], shift_f[:, 2])
    ffn_low = ffn_in.astype(jnp.bfloat16)
    up_proj = jnp.dot(ffn_low, full_up, preferred_element_type=jnp.float32) + up_bias_f
    activated, pull_mid = jax.vjp(mid_norm, up_proj, mid_gain_f, mid_shift_f)
    act_low = activated.astype(jnp.bfloat16)
    result = (
        residual + jnp.dot(act_low, full_down, preferred_element_type=jnp.float32) + bias_f[:, 3]
    )
    layer_output = (result * valid_rows).astype(jnp.bfloat16).reshape(hidden.shape)
    error_rows = (
        result - teacher.reshape(token_rows, model_width).astype(jnp.float32)
    ) * valid_rows
    loss_total, valid_total = lax.psum(
        (0.5 * jnp.sum(error_rows * error_rows), jnp.sum(valid_mask)), ("dp", "ctx")
    )
    loss = loss_total / (valid_total * model_width)
    down_low = error_rows.astype(jnp.bfloat16)
    bias_down_grad = jnp.sum(down_low.astype(jnp.float32), axis=0)
    down_grad = jnp.einsum("rf,rd->fd", act_low, down_low, preferred_element_type=jnp.float32)
    d_act = jnp.einsum("rd,fd->rf", down_low, full_down, preferred_element_type=jnp.float32)
    d_up, mid_gain_grad, mid_shift_grad = pull_mid(d_act)
    up_low = d_up.astype(jnp.bfloat16)
    up_bias_grad = jnp.sum(up_low.astype(jnp.float32), axis=0)
    up_grad = jnp.einsum("rd,rf->df", ffn_low, up_low, preferred_element_type=jnp.float32)
    d_ffn = jnp.einsum("rf,df->rd", up_low, full_up, preferred_element_type=jnp.float32)
    d_res_norm, gain_two, shift_two = pull_ffn(d_ffn)
    d_residual = error_rows + d_res_norm
    branch_low = d_residual.astype(jnp.bfloat16)
    bias_out_grad = jnp.sum(branch_low.astype(jnp.float32), axis=0)
    out_grad = jnp.einsum("rd,re->de", mixed_low, branch_low, preferred_element_type=jnp.float32)
    d_mixed = jnp.einsum("re,de->rd", branch_low, full_out, preferred_element_type=jnp.float32)
    d_att, gain_one, shift_one = pull_mix(d_mixed)
    heads_do = split_heads(d_att.astype(jnp.bfloat16).reshape(seq_shape))
    dterm = jnp.einsum("sqhd,sqhd->shq", heads_do.astype(jnp.float32), attended)

    def grad_step(key_piece, value_piece, key_start):
        return grad_keys(
            heads_q,
            heads_do,
            log_total,
            dterm,
            key_piece,
            value_piece,
            key_start,
            query_pos,
            lengths,
        )

    dq_zero = jnp.zeros((seq_count, local_rows, HEADS, HEAD_DIM), jnp.float32)
    own_zero = jnp.zeros(seq_shape, jnp.float32)

    def pass_step(step_index, running):
        key_cur, value_cur, dk_run, dv_run, dq_sum = running
        owner = (ctx_place - step_index) % ctx_parts
        dq_part, dk_part, dv_part = lax.cond(
            owner <= ctx_place,
            lambda: grad_step(key_cur, value_cur, owner * local_rows),
            lambda: (dq_zero, own_zero, own_zero),
        )
        dk_run, dv_run = (
            passed_along((dk_run + dk_part).astype(jnp.bfloat16), "ctx", 1).astype(jnp.float32),
            passed_along((dv_run + dv_part).astype(jnp.bfloat16), "ctx", 1).astype(jnp.float32),
        )
        key_cur, value_cur = passed_along_2((key_cur, value_cur), "ctx", 1)
        return (key_cur, value_cur, dk_run, dv_run, dq_sum + dq_part)

    key_end, value_end, dk_own, dv_own, dq_sum = lax.fori_loop(
        0, ctx_parts, pass_step, (key_low, value_low, own_zero, own_zero, dq_zero)
    )
    dq_low = dq_sum.reshape(token_rows, model_width).astype(jnp.bfloat16)
    dk_low = dk_own.reshape(token_rows, model_width).astype(jnp.bfloat16)
    dv_low = dv_own.reshape(token_rows, model_width).astype(jnp.bfloat16)
    dqkv_low = jnp.concatenate([dq_low, dk_low, dv_low], axis=1)
    bias_q_grad = jnp.sum(dq_low.astype(jnp.float32), axis=0)
    bias_v_grad = jnp.sum(dv_low.astype(jnp.float32), axis=0)
    qkv_grad = jnp.einsum("rd,re->de", normed_low, dqkv_low, preferred_element_type=jnp.float32)
    d_normed = jnp.einsum("re,de->rd", dqkv_low, full_qkv, preferred_element_type=jnp.float32)
    d_in_norm, gain_zero, shift_zero = pull_in(d_normed)
    hidden_grad = (d_residual + d_in_norm).reshape(hidden.shape)
    gain_grad = jnp.stack([gain_zero, gain_one, gain_two], axis=1)
    shift_grad = jnp.stack([shift_zero, shift_one, shift_two], axis=1)
    bias_grad = jnp.stack([bias_q_grad, bias_v_grad, bias_out_grad, bias_down_grad], axis=1)
    shares = (
        lax.psum_scatter(
            qkv_grad.astype(jnp.bfloat16), "dp", scatter_dimension=0, tiled=True
        ).astype(jnp.float32),
        lax.psum_scatter(
            out_grad.astype(jnp.bfloat16), "dp", scatter_dimension=0, tiled=True
        ).astype(jnp.float32),
        lax.psum_scatter(
            up_grad.astype(jnp.bfloat16), "dp", scatter_dimension=0, tiled=True
        ).astype(jnp.float32),
        lax.psum_scatter(
            down_grad.astype(jnp.bfloat16), "dp", scatter_dimension=0, tiled=True
        ).astype(jnp.float32),
        lax.psum_scatter(
            gain_grad.astype(jnp.bfloat16), "dp", scatter_dimension=0, tiled=True
        ).astype(jnp.float32),
        lax.psum_scatter(
            shift_grad.astype(jnp.bfloat16), "dp", scatter_dimension=0, tiled=True
        ).astype(jnp.float32),
        lax.psum_scatter(
            bias_grad.astype(jnp.bfloat16), "dp", scatter_dimension=0, tiled=True
        ).astype(jnp.float32),
        lax.psum_scatter(
            mid_gain_grad.astype(jnp.bfloat16), "dp", scatter_dimension=0, tiled=True
        ).astype(jnp.float32),
        lax.psum_scatter(
            mid_shift_grad.astype(jnp.bfloat16), "dp", scatter_dimension=0, tiled=True
        ).astype(jnp.float32),
        lax.psum_scatter(
            up_bias_grad.astype(jnp.bfloat16), "dp", scatter_dimension=0, tiled=True
        ).astype(jnp.float32),
    )
    summed = (
        lax.psum(shares[0].astype(jnp.bfloat16), "ctx").astype(jnp.float32),
        lax.psum(shares[1].astype(jnp.bfloat16), "ctx").astype(jnp.float32),
        lax.psum(shares[2].astype(jnp.bfloat16), "ctx").astype(jnp.float32),
        lax.psum(shares[3].astype(jnp.bfloat16), "ctx").astype(jnp.float32),
        lax.psum(shares[4].astype(jnp.bfloat16), "ctx").astype(jnp.float32),
        lax.psum(shares[5].astype(jnp.bfloat16), "ctx").astype(jnp.float32),
        lax.psum(shares[6].astype(jnp.bfloat16), "ctx").astype(jnp.float32),
        lax.psum(shares[7].astype(jnp.bfloat16), "ctx").astype(jnp.float32),
        lax.psum(shares[8].astype(jnp.bfloat16), "ctx").astype(jnp.float32),
        lax.psum(shares[9].astype(jnp.bfloat16), "ctx").astype(jnp.float32),
    )
    return (
        layer_output,
        loss,
        hidden_grad,
        summed[0],
        summed[1],
        summed[2],
        summed[3],
        summed[4],
        summed[5],
        summed[6],
        summed[7],
        summed[8],
        summed[9],
    )


AXES = ("dp", "ctx")


def swap(value, mask):
    count = lax.axis_size("dp") * lax.axis_size("ctx")
    return lax.ppermute(value, AXES, [(i, i ^ mask) for i in range(count)])


def along_z(piece):
    return [swap(piece, 8 * step) for step in (1, 2, 3)]


def wide(value):
    return value.astype(jnp.float32)


def narrow(value):
    return value.astype(jnp.bfloat16)


VMEM_BYTES = 56 * 1024 * 1024


def whole(shape):
    return pl.BlockSpec(tuple(shape), lambda i: (0,) * len(shape), pipeline_mode=pl.Buffered(1))


def padded(shape, dtype):
    lead = math.prod(shape[:-2])
    size = jnp.dtype(dtype).itemsize
    rows = -(-shape[-2] // (32 // size)) * (32 // size) if len(shape) > 1 else 8
    return lead * rows * (-(-shape[-1] // 128) * 128) * size


def call(body, ins, outs, scratch=(), us=1, deps=(), room=6):
    pairs = [v if isinstance(v, tuple) else (v, whole(v.shape)) for v in ins[1:]]
    held = sum(padded(spec.block_shape, v.dtype) for v, spec in pairs)
    held += sum(padded(shape, dtype) for shape, dtype in (*outs, *scratch))
    count = len(pairs)

    def kernel(sc, *refs):
        body(sc, *refs[:count], *refs[count + len(deps):])

    return pl.pallas_call(
        kernel,
        grid=(1,),
        in_specs=[pl.BlockSpec(memory_space=pltpu.SMEM)] + [spec for _, spec in pairs]
        + [pl.BlockSpec(memory_space=pl.ANY)] * len(deps),
        out_specs=[whole(shape) for shape, _ in outs],
        out_shape=[jax.ShapeDtypeStruct(shape, dtype) for shape, dtype in outs],
        scratch_shapes=[pltpu.VMEM(shape, dtype) for shape, dtype in scratch],
        compiler_params=pltpu.CompilerParams(vmem_limit_bytes=held + room * 1024 * 1024),
        cost_estimate=pl.CostEstimate(flops=int(us * 2e7), bytes_accessed=0, transcendentals=0),
        name=body.__name__,
    )(ins[0], *[v for v, _ in pairs], *deps)


def after(value, *deps):
    return lax.optimization_barrier((value, *deps))[0]


BF, F32 = jnp.bfloat16, jnp.float32


def contract(a, b, da, db):
    return lax.dot_general(a, b, (((da,), (db,)), ((), ())), preferred_element_type=F32)


def block_of(sc, xr, zr):
    return 2 * ((sc[0] >> 1) ^ zr) + ((sc[0] & 1) ^ xr)


def slot_of(sc, block):
    return ((block & 1) ^ (sc[0] & 1)) * 4 + ((block >> 1) ^ (sc[0] >> 1))


def lay(sc, scr, near, far, rows, stride, offset=0):
    for xr, ref in ((0, near), (1, far)):
        for zr in range(4):
            at = pl.multiple_of(stride * block_of(sc, xr, zr) + offset, 16)
            scr[pl.ds(at, rows), :] = ref[zr]


def moments(value):
    average = jnp.mean(value, axis=-1, keepdims=True)
    centred = value - average
    scale = lax.rsqrt(jnp.mean(centred * centred, axis=-1, keepdims=True) + EPSILON)
    return centred * scale, scale


def norm_back(grad, hat, scale):
    return scale * (grad - jnp.mean(grad, axis=-1, keepdims=True) - hat * jnp.mean(grad * hat, axis=-1, keepdims=True))


def mine(ctx_at, row):
    out = row[:, :192]
    for j in range(1, 4):
        out = jnp.where(ctx_at == j, row[:, 192 * j:192 * j + 192], out)
    return out


def pack_body(sc, w, gain, shift, bias, out, scr):
    scr[...] = jnp.zeros((16, 128), F32)
    scr[0:3, :96] = gain[...].astype(F32)
    scr[3:6, :96] = shift[...].astype(F32)
    scr[6:10, :96] = bias[...].astype(F32)
    small = scr[...].T[:96].astype(BF)
    for j in range(4):
        @pl.when(sc[1] == j)
        def _():
            cols = [w[:, 768 * part + 192 * j:768 * part + 192 * j + 192] for part in range(3)]
            out[...] = jnp.concatenate(cols + [small, jnp.zeros((96, 48), BF)], axis=1)


def attend_body(sc, h0, h1, h2, h3, wa, wb, a0, a1, a23, q_o, k_o, v_o, lse_o, ot_o, n_o, vec_o, w_scr):
    ctx_at, length = sc[1], sc[2]
    lay(sc, w_scr, wa, wb, 96, 96)
    vec = w_scr[:, 512:640].astype(F32).T[64:80]
    vec_o[...] = vec
    bias_q, bias_v = mine(ctx_at, vec[6:7]), mine(ctx_at, vec[7:8])
    for r, ref in enumerate((h0, h1, h2, h3)):
        rows = pl.ds(pl.multiple_of((ctx_at ^ r) * 256, 256), 256)
        hat, _ = moments(ref[...].astype(F32))
        normed = (hat * vec[0:1] + vec[3:4]).astype(BF)
        n_o[rows, :] = normed
        p = jnp.dot(normed, w_scr[...], preferred_element_type=F32)
        for h in range(3):
            q_o[h, rows, :] = ((p[:, 64 * h:64 * h + 64] + bias_q[:, 64 * h:64 * h + 64]) * 0.125).astype(BF)
            k_o[h, rows, :] = p[:, 192 + 64 * h:256 + 64 * h].astype(BF)
            v_o[h, rows, :] = (p[:, 384 + 64 * h:448 + 64 * h] + bias_v[:, 64 * h:64 * h + 64]).astype(BF)

    def head(h, carry):
        for i in range(4):
            n = 256 * (i + 1)
            scores = contract(k_o[h, :n, :], q_o[h, 256 * i:256 * i + 256, :], 1, 1)
            limit = jnp.minimum(256 * i + lax.broadcasted_iota(jnp.int32, (1, 256), 1), length - 1)
            scores = jnp.where(lax.broadcasted_iota(jnp.int32, (n, 256), 0) <= limit, scores, NEGATIVE)
            top = jnp.max(scores, axis=0, keepdims=True)
            grown = jnp.exp(scores - top)
            total = jnp.sum(grown, axis=0, keepdims=True)
            out = contract(v_o[h, :n, :], grown.astype(BF), 0, 0) / total
            ot_o[i, pl.ds(pl.multiple_of(64 * h, 64), 64), :] = out
            lse_o[h, i:i + 1, :] = top + jnp.log(total)
        return carry

    lax.fori_loop(0, 3, head, 0)
    for r, ref in enumerate((a0, a1, a23.at[0], a23.at[1])):
        ref[...] = ot_o[ctx_at ^ r].T.astype(BF)


def attend(sc, hids, wa, wb, deps):
    rows = (256, 192)
    return call(
        attend_body, [sc, *hids, wa, wb],
        [(rows, BF)] * 2 + [((2, 256, 192), BF)] + [((3, 1024, 64), BF)] * 3
        + [((3, 8, 256), F32), ((4, 192, 256), F32), ((1024, 768), BF), ((16, 768), F32)],
        [((768, 640), BF)], us=13, deps=deps)


def attend_back_body(sc, d0, d1, d2, d3, q_i, k_i, v_i, lse_i, ot_i, n_i, h0, h1, h2, h3, wa, wb, vec_i, side_e, side_d, mids,
                     n0, n1, n23, keep, send, w_scr, do_scr, dq_s, dk_s, dv_s, dk_acc, dv_acc, all_scr, g_scr):
    ctx_at, length = sc[1], sc[2]
    lay(sc, w_scr, wa, wb, 96, 96)
    for r, ref in enumerate((d0, d1, d2, d3)):
        rows = pl.ds(pl.multiple_of((ctx_at ^ r) * 256, 256), 256)
        value = ref[...]
        for h in range(3):
            do_scr[h, rows, :] = value[:, 64 * h:64 * h + 64]

    def head(h, carry):
        for i in (3, 2, 1, 0):
            n = 256 * (i + 1)
            mine_rows = slice(256 * i, 256 * i + 256)
            q, do, k = q_i[h, mine_rows, :], do_scr[h, mine_rows, :], k_i[h, :n, :]
            out = ot_i[i, pl.ds(pl.multiple_of(64 * h, 64), 64), :]
            dterm = jnp.sum(do.astype(F32).T * out, axis=0, keepdims=True)
            limit = jnp.minimum(256 * i + lax.broadcasted_iota(jnp.int32, (1, 256), 1), length - 1)
            prob = jnp.exp(contract(k, q, 1, 1) - lse_i[h, i:i + 1, :])
            prob = jnp.where(lax.broadcasted_iota(jnp.int32, (n, 256), 0) <= limit, prob, 0.0)
            dscore = (prob * (contract(v_i[h, :n, :], do, 1, 1) - dterm)).astype(BF)
            dv = jnp.dot(prob.astype(BF), do, preferred_element_type=F32)
            dk = jnp.dot(dscore, q, preferred_element_type=F32)
            if i == 3:
                dv_acc[...] = dv
                dk_acc[...] = dk
            else:
                dv_acc[:n, :] += dv
                dk_acc[:n, :] += dk
            dq_s[h, mine_rows, :] = (contract(k, dscore, 0, 0) * 0.125).T.astype(BF)
        dk_s[h] = dk_acc[...].astype(BF)
        dv_s[h] = dv_acc[...].astype(BF)
        return carry

    lax.fori_loop(0, 3, head, 0)
    for i in range(4):
        rows = slice(256 * i, 256 * i + 256)
        all_scr[rows, :] = jnp.concatenate([s[h, rows, :] for s in (dq_s, dk_s, dv_s) for h in range(3)], axis=1)
    sums = jnp.sum(all_scr[...].astype(F32), axis=0, keepdims=True)
    bias_q = jnp.concatenate([jnp.where(ctx_at == j, sums[:, :192], 0.0) for j in range(4)], axis=1)
    bias_v = jnp.concatenate([jnp.where(ctx_at == j, sums[:, 384:], 0.0) for j in range(4)], axis=1)
    gain_sum, shift_sum = jnp.zeros((1, 768), F32), jnp.zeros((1, 768), F32)
    for r, (ref, out) in enumerate(((h0, n0), (h1, n1), (h2, n23.at[0]), (h3, n23.at[1]))):
        rows = pl.ds(pl.multiple_of((ctx_at ^ r) * 256, 256), 256)
        grad = contract(all_scr[rows, :], w_scr[:, :576], 1, 1)
        hat, _ = moments(ref[...].astype(F32))
        gain_sum += jnp.sum(grad * hat, axis=0, keepdims=True)
        shift_sum += jnp.sum(grad, axis=0, keepdims=True)
        out[...] = grad.astype(BF)
    rows16 = jnp.concatenate(
        [gain_sum, side_e[0:2], shift_sum, side_e[2:4], bias_q, bias_v, side_e[4:5], side_d[0:2], jnp.zeros((5, 768), F32)], axis=0)
    w_grad = contract(n_i[...], all_scr[...], 0, 0)
    for b in range(8):
        at = slot_of(sc, b)
        extra = jnp.concatenate([mids[:, 384 * b:384 * b + 384], rows16[:, 96 * b:96 * b + 96], jnp.zeros((16, 96), F32)], axis=1)
        g_scr[at, :96, :] = w_grad[96 * b:96 * b + 96].astype(BF)
        g_scr[at, 96:112, :] = extra.astype(BF)
    keep[...] = g_scr[:4]
    send[...] = g_scr[4:]


def attend_back(sc, douts, saved, hids, wa, wb, side_e, side_d, mids, deps):
    q, k, v, lse, ot, normed, vec = saved
    return call(
        attend_back_body, [sc, *douts, q, k, v, lse, ot, normed, *hids, wa, wb, vec, side_e, side_d, mids],
        [((256, 768), BF)] * 2 + [((2, 256, 768), BF)] + [((4, 112, 576), BF)] * 2,
        [((768, 640), BF), ((3, 1024, 64), BF), ((3, 1024, 64), BF), ((3, 1024, 64), BF), ((3, 1024, 64), BF),
         ((1024, 64), F32), ((1024, 64), F32), ((1024, 576), BF), ((8, 112, 576), BF)],
        us=12, deps=deps)


def part(rows, at):
    return pl.BlockSpec((4, rows, 768), lambda i: (0, at, 0), pipeline_mode=pl.Buffered(1))


def lay_out(sc, scr, own_near, own_far, other_near, other_far):
    core = sc[1] & 1
    lay(sc, scr, own_near, own_far, 48, 96, 48 * core)
    lay(sc, scr, other_near, other_far, 48, 96, 48 * (1 - core))


def lay_down(sc, scr, refs):
    for c in (0, 1):
        for xr in (0, 1):
            for y in (0, 1):
                lay_one(sc, scr, refs[4 * c + 2 * xr + y], xr, 96 * (sc[1] ^ (2 * y + c)))


def lay_one(sc, scr, ref, xr, offset):
    for zr in range(4):
        scr[pl.ds(pl.multiple_of(384 * block_of(sc, xr, zr) + offset, 32), 96), :] = ref[zr]


def join_heads(sc, scr, pieces):
    own, near, far = pieces
    for r, value in enumerate((own[...], near[0], far[0], near[1])):
        scr[r] = value
    return jnp.concatenate([scr[sc[1] ^ j] for j in range(4)], axis=1).astype(F32)


def mid_body(sc, g0, g1, g2, own, vec, on, of, tn, tf, mixed_o, resid_o, ffn_o, w_scr, a_scr):
    lay_out(sc, w_scr, on, of, tn, tf)
    hat, _ = moments(join_heads(sc, a_scr, (g0, g1, g2)))
    mixed = (hat * vec[1:2] + vec[4:5]).astype(BF)
    mixed_o[...] = mixed
    resid = own[...].astype(F32) + jnp.dot(mixed, w_scr[...], preferred_element_type=F32) + vec[8:9]
    resid_o[...] = resid
    hat, _ = moments(resid)
    ffn_o[...] = (hat * vec[2:3] + vec[5:6]).astype(BF)


def up_body(sc, ffn, w0n, w0f, w1n, w1f, w2n, w2f, w3n, w3f, mn, mf, act_o, hat_o, slope_o, scale_o, nat_o,
            w_scr, g_scr, m_scr):
    for xr, ref in ((0, mn), (1, mf)):
        for zr in range(4):
            m_scr[block_of(sc, xr, zr)] = ref[zr].astype(F32)
    flat = [m_scr[b] for b in range(8)]
    for j in range(4):
        two = flat[2 * j:2 * j + 2]
        nat_o[j, 0:1, :] = jnp.concatenate([m[0:1, :384] for m in two], axis=1)
        nat_o[j, 1:2, :] = jnp.concatenate([m[0:1, 384:] for m in two], axis=1)
        nat_o[j, 2:3, :] = jnp.concatenate([m[1:2, :384] for m in two], axis=1)
        nat_o[j, 3:8, :] = jnp.zeros((5, 768), F32)
    value = ffn[...]
    total = jnp.zeros((256, 1), F32)
    for t, (near, far) in enumerate(((w0n, w0f), (w1n, w1f), (w2n, w2f), (w3n, w3f))):
        j = sc[1] ^ t
        lay(sc, w_scr.at[t], near, far, 96, 96)
        up = jnp.dot(value, w_scr[t], preferred_element_type=F32) + nat_o[j, 2:3, :]
        chance = 0.5 * (1.0 + lax.erf(up * math.sqrt(0.5)))
        slope_o[j] = (chance + up * jnp.exp(-0.5 * up * up) * (1.0 / math.sqrt(2.0 * math.pi))).astype(BF)
        gelu = up * chance
        g_scr[j] = gelu
        total += jnp.sum(gelu, axis=-1, keepdims=True)
    average = total * (1.0 / 3072)
    square = jnp.zeros((256, 1), F32)
    for j in range(4):
        centred = g_scr[j] - average
        square += jnp.sum(centred * centred, axis=-1, keepdims=True)
    scale = lax.rsqrt(square * (1.0 / 3072) + EPSILON)
    scale_o[...] = scale
    for j in range(4):
        hat = (g_scr[j] - average) * scale
        hat_o[j] = hat.astype(BF)
        act_o[j] = (hat * nat_o[j, 0:1, :] + nat_o[j, 1:2, :]).astype(BF)


def down_body(sc, act, resid, teacher, vec, e0, e1, e2, e3, e4, e5, e6, e7, out_o, err_o, low_o, side_o, w_scr):
    lay_down(sc, w_scr, (e0, e1, e2, e3, e4, e5, e6, e7))
    result = resid[...] + vec[9:10]
    for j in range(4):
        result += jnp.dot(act[j], w_scr[768 * j:768 * j + 768, :], preferred_element_type=F32)
    pos = sc[1] * 256 + lax.broadcasted_iota(jnp.int32, (256, 1), 0)
    valid = jnp.where(pos < sc[2], 1.0, 0.0)
    out_o[...] = (result * valid).astype(BF)
    error = (result - teacher[...].astype(F32)) * valid
    err_o[...] = error
    low = error.astype(BF)
    low_o[...] = low
    side_o[0:1, :] = jnp.sum(low.astype(F32), axis=0, keepdims=True)
    loss = 0.5 * jnp.sum(jnp.sum(error * error, axis=0, keepdims=True), axis=1, keepdims=True)
    count = jnp.sum(valid, axis=0, keepdims=True)
    high = loss.astype(BF).astype(F32)
    lane = lax.broadcasted_iota(jnp.int32, (1, 768), 1) % 96
    side_o[1:2, :] = jnp.where(lane == 0, high, jnp.where(lane == 1, loss - high, jnp.where(lane == 2, count, 0.0)))
    side_o[2:8, :] = jnp.zeros((6, 768), F32)


def down_grad_body(sc, act, low, keep, send, g_scr):
    value = low[...]
    for j in range(4):
        grad = contract(act[j], value, 0, 0).astype(BF)
        for half in (0, 1):
            at = slot_of(sc, 2 * j + half)
            for q in range(4):
                g_scr[sc[1] ^ q, at] = grad[384 * half + 96 * q:384 * half + 96 * q + 96]
    for y in (0, 1):
        keep[y] = g_scr[2 * y]
        send[y] = g_scr[2 * y + 1]


def act_back_body(sc, low, hat_i, slope, scale, nat, e0, e1, e2, e3, e4, e5, e6, e7, up_o, mids_o, wd_scr, dh_scr):
    lay_down(sc, wd_scr, (e0, e1, e2, e3, e4, e5, e6, e7))
    value = low[...]
    first, second = jnp.zeros((256, 1), F32), jnp.zeros((256, 1), F32)
    for j in range(4):
        grad = contract(value, wd_scr[768 * j:768 * j + 768, :], 1, 1)
        hat = hat_i[j].astype(F32)
        cols = slice(768 * j, 768 * j + 768)
        mids_o[0:1, cols] = jnp.sum(grad * hat, axis=0, keepdims=True)
        mids_o[1:2, cols] = jnp.sum(grad, axis=0, keepdims=True)
        grad = grad * nat[j, 0:1, :]
        dh_scr[j] = grad
        first += jnp.sum(grad, axis=-1, keepdims=True)
        second += jnp.sum(grad * hat, axis=-1, keepdims=True)
    first, second = first * (1.0 / 3072), second * (1.0 / 3072)
    for j in range(4):
        hat = hat_i[j].astype(F32)
        grad = (scale[...] * (dh_scr[j] - first - hat * second) * slope[j].astype(F32)).astype(BF)
        up_o[j] = grad
        mids_o[2:3, 768 * j:768 * j + 768] = jnp.sum(grad.astype(F32), axis=0, keepdims=True)
    mids_o[3:16, :] = jnp.zeros((13, 3072), F32)


def ffn_back_body(sc, up_i, err, resid, w0n, w0f, w1n, w1f, w2n, w2f, w3n, w3f, on, of, tn, tf, vec, g0, g1, g2,
                  branch_o, dres_o, p0, p1, p2, p3, side_o, w_scr, o_scr, a_scr, b_scr):
    grad = jnp.zeros((256, 768), F32)
    for t, (near, far) in enumerate(((w0n, w0f), (w1n, w1f), (w2n, w2f), (w3n, w3f))):
        lay(sc, w_scr.at[t], near, far, 96, 96)
        grad += contract(up_i[sc[1] ^ t], w_scr[t], 1, 1)
    hat, factor = moments(resid[...])
    side_o[1:2, :] = jnp.sum(grad * hat, axis=0, keepdims=True)
    side_o[3:4, :] = jnp.sum(grad, axis=0, keepdims=True)
    dres = err[...] + norm_back(grad * vec[2:3], hat, factor)
    dres_o[...] = dres
    branch = dres.astype(BF)
    branch_o[...] = branch
    side_o[4:5, :] = jnp.sum(branch.astype(F32), axis=0, keepdims=True)
    lay_out(sc, o_scr, on, of, tn, tf)
    grad = contract(branch, o_scr[...], 1, 1)
    hat, factor = moments(join_heads(sc, a_scr, (g0, g1, g2)))
    side_o[0:1, :] = jnp.sum(grad * hat, axis=0, keepdims=True)
    side_o[2:3, :] = jnp.sum(grad, axis=0, keepdims=True)
    side_o[5:8, :] = jnp.zeros((3, 768), F32)
    grad = norm_back(grad * vec[1:2], hat, factor).astype(BF)
    for j in range(4):
        b_scr[j] = grad[:, 192 * j:192 * j + 192]
    for r, ref in enumerate((p0, p1, p2, p3)):
        ref[...] = b_scr[sc[1] ^ r]


def up_grad_body(sc, ffn, up, keep, send, g_scr):
    value = ffn[...]
    for j in range(4):
        grad = contract(value, up[j], 0, 0).astype(BF)
        for b in range(8):
            g_scr[sc[1] ^ j, slot_of(sc, b)] = grad[96 * b:96 * b + 96]
    for y in (0, 1):
        keep[y] = g_scr[2 * y]
        send[y] = g_scr[2 * y + 1]


def out_grad_body(sc, mixed, branch, out_keep, out_send, o_scr):
    grad = contract(mixed[...], branch[...], 0, 0).astype(BF)
    for b in range(8):
        for c in (0, 1):
            o_scr[(sc[1] & 1) ^ c, slot_of(sc, b)] = grad[96 * b + 48 * c:96 * b + 48 * c + 48]
    out_keep[...] = o_scr[0]
    out_send[...] = o_scr[1]


def added(a, b):
    return a.astype(F32) + b.astype(F32)


def pair_body(sc, keep, got, near0, near1, far0, far1):
    for y, near, far in ((0, near0, far0), (1, near1, far1)):
        near[...] = added(keep[y, :4], got[y, :4]).astype(BF)
        far[...] = added(keep[y, 4:], got[y, 4:]).astype(BF)


def slots_body(sc, near, got, own, s1, s2, s3):
    own[...] = added(near[0], got[0])
    for at, out in ((1, s1), (2, s2), (3, s3)):
        out[...] = added(near[at], got[at]).astype(BF)


def join_far_body(sc, mine, got, out_keep, out_got, far):
    far[:, :96, :] = added(mine[...], got[...]).astype(BF)
    far[:, 96:, :] = added(out_keep[...], out_got[...]).astype(BF)


def join_near_body(sc, mine, y_got, out_keep, out_got, x_got, own, s1, s2, s3):
    for at, out in ((0, own), (1, s1), (2, s2), (3, s3)):
        kind = out.dtype
        out[:96, :] = (added(mine[at], y_got[at]) + x_got[at, :96, :].astype(F32)).astype(kind)
        out[96:, :] = (added(out_keep[at], out_got[at]) + x_got[at, 96:, :].astype(F32)).astype(kind)


def total_of(own, parts):
    return (own[...] + sum(p[...].astype(F32) for p in parts)).astype(BF)


def middle_body(sc, q0, q1, q2, q3, dn, got, d0, d1, d2, d3, e0, e1, e2, e3, q_o, dn_o, early_o):
    q_o[...] = total_of(q0, (q1, q2, q3))
    dn_o[...] = added(dn[...], got[0]).astype(BF)
    early_o[0:96, :] = total_of(d0, (d1, d2, d3))
    early_o[96:192, :] = total_of(e0, (e1, e2, e3))


def fold_body(sc, own, other, early, early_got, out):
    out[0:96, :] = own[0:96, :]
    out[96:192, :] = other[0:96, :]
    out[192:240, :] = added(own[96:144, :], other[96:144, :]).astype(BF)
    out[240:336, :] = added(early[0:96, :], early_got[96:192, :]).astype(BF)
    out[336:432, :] = added(early[96:192, :], early_got[0:96, :]).astype(BF)


def spread_body(sc, mine, other, up_o, out_o, down_o, scr):
    core = sc[1] & 1
    for t, (ref, at) in enumerate(((mine, 0), (other, 0), (mine, 96), (other, 96))):
        scr[sc[1] ^ t] = ref[at:at + 96, :].astype(F32)
        rows = pl.multiple_of(96 * (sc[1] ^ t), 32)
        down_o[pl.ds(rows, 96), :] = ref[240 + at:336 + at, :].astype(F32)
    for j in range(4):
        up_o[:, 768 * j:768 * j + 768] = scr[j]
    out_o[pl.ds(pl.multiple_of(48 * core, 16), 48), :] = mine[192:240, :].astype(F32)
    out_o[pl.ds(pl.multiple_of(48 * (1 - core), 16), 48), :] = other[192:240, :].astype(F32)


def spread_qkv_body(sc, t0, t1, t2, t3, grad_o, gain_o, shift_o, bias_o, mid_o, loss_o, scr):
    rest = jnp.zeros((16, 576), F32)
    for r, ref in enumerate((t0, t1, t2, t3)):
        scr[sc[1] ^ r] = ref[:96, :]
        rest += ref[96:112, :].astype(F32)
    for p in range(3):
        cols = [scr[j, :, 192 * p:192 * p + 192] for j in range(4)]
        grad_o[:, 768 * p:768 * p + 768] = jnp.concatenate(cols, axis=1).astype(F32)
    gain_o[...] = rest[0:3, 384:480]
    shift_o[...] = rest[3:6, 384:480]
    bias_o[...] = rest[6:10, 384:480]
    mid_o[...] = rest[0:8, :384]
    row = rest[10:11, 384:480]
    lane = lax.broadcasted_iota(jnp.int32, (1, 96), 1)
    error = jnp.sum(jnp.where(lane < 2, row, 0.0), axis=1, keepdims=True)
    count = jnp.sum(jnp.where(lane == 2, row, 0.0), axis=1, keepdims=True)
    loss_o[...] = error / (count * 768.0)


def hidden_body(sc, a, b, c, own, vec, d_res, out):
    grad = (added(a[...], b[0]) + c[...].astype(F32)) * vec[0:1]
    hat, factor = moments(own[...].astype(F32))
    out[...] = d_res[...] + norm_back(grad, hat, factor)


def total_body(sc, own, s1, s2, s3, out):
    out[...] = total_of(own, (s1, s2, s3))


def fast(
    hidden, teacher, lengths, w_qkv, w_out, w_up, w_down, norm_gain, norm_shift, proj_bias,
    mid_gain, mid_shift, up_bias,
):
    dp_at, ctx_at = lax.axis_index("dp"), lax.axis_index("ctx")
    core = ctx_at & 1
    sc = jnp.stack([dp_at, ctx_at, lengths[0]]).astype(jnp.int32)
    own = hidden[0]
    tall = (256, 768)
    barrier = lax.optimization_barrier
    h_y, h_c = swap(own, 2), swap(own, 1)
    piece = call(pack_body, [sc, w_qkv, norm_gain.T, norm_shift.T, proj_bias.T], [((96, 640), BF)], [((16, 128), F32)])[0]
    q_cols = along_z(piece)
    mid_rows = jnp.concatenate([mid_gain, mid_shift, up_bias, jnp.zeros((13 * 384,), BF)]).reshape(8, 768)
    piece_a = jnp.concatenate([
        lax.dynamic_slice(w_up, (0, 768 * ctx_at), (96, 768)), lax.dynamic_slice(w_out, (48 * core, 0), (48, 768)), mid_rows])
    down4 = w_down.reshape(4, 96, 768)
    piece_b, piece_c = (lax.dynamic_index_in_dim(down4, ctx_at ^ t, 0, keepdims=False) for t in (0, 2))
    q_cols, piece_a = barrier((q_cols, piece_a))
    q_near = jnp.stack([piece] + q_cols)
    q_far = swap(q_near, 4)
    h_yc = swap(h_y, 1)
    a_cols = along_z(piece_a)
    a_cols, q_far, piece_b, h_c, h_yc = barrier((a_cols, q_far, piece_b, h_c, h_yc))
    a_near = jnp.stack([piece_a] + a_cols)
    a_far = swap(a_near, 4)
    y_near = swap(a_near[:, :96], 2)
    a_near_o = swap(a_near, 1)
    b_cols = along_z(piece_b)
    hids = [own, h_c, h_y, h_yc]
    att_0, att_1, att_23, q, k, v, lse, ot, normed, vec = attend(sc, hids, q_near, q_far, (a_near,))
    y_near, b_cols, piece_c, att_23, att_1 = barrier((y_near, b_cols, piece_c, att_23, att_1))
    c_cols = along_z(piece_c)
    att_y = swap(att_23, 2)
    b_near = jnp.stack([piece_b] + b_cols)
    a_far, b_near, att_y = barrier((a_far, b_near, att_y))
    b_far = swap(b_near, 4)
    y_far = swap(a_far[:, :96], 2)
    c_cols, b_far, y_far, a_near, a_far, y_near, b_near, att_1 = barrier(
        (c_cols, b_far, y_far, a_near, a_far, y_near, b_near, att_1))
    c_near = jnp.stack([piece_c] + c_cols)
    c_far = swap(c_near, 4)
    att_c = swap(jnp.stack([att_1, att_y[1]]), 1)
    a_near_o, a_far_o, y_near_o, y_far_o = (swap(t, 1) for t in (a_near, a_far, y_near, y_far))
    b_near_o, b_far_o, c_near_o = (swap(t, 1) for t in (b_near, b_far, c_near))
    got = [att_0, att_c, att_y]
    outs = [(t, part(48, 2)) for t in (a_near, a_far, a_near_o, a_far_o)]
    mixed, resid, ffn = call(
        mid_body, [sc, *got, own, vec, *outs], [(tall, BF), (tall, F32), (tall, BF)],
        [((768, 768), BF), ((4, 256, 192), BF)], us=3)
    ups = [(t, part(96, 0)) for t in (a_near, a_far, a_near_o, a_far_o)] + [y_near, y_far, y_near_o, y_far_o]
    four = (4, 256, 768)
    act, hat, slope, scale, nat = call(
        up_body, [sc, ffn, *ups] + [(t, part(8, 18)) for t in (a_near, a_far)],
        [(four, BF), (four, BF), (four, BF), ((256, 1), F32), ((4, 8, 768), F32)],
        [((4, 768, 768), BF), (four, F32), ((8, 8, 768), F32)], us=5)
    c_far, act = barrier((c_far, act))
    c_far_o = swap(c_far, 1)
    downs = [b_near, c_near, b_far, c_far, b_near_o, c_near_o, b_far_o, c_far_o]
    out, err, low, side_d = call(
        down_body, [sc, act, resid, teacher[0], vec, *downs],
        [(tall, BF), (tall, F32), (tall, BF), ((8, 768), F32)], [((3072, 768), BF)], us=5)
    halves_of = ((2, 8, 96, 768), BF)
    down_keep, down_send = call(
        down_grad_body, [sc, act, low], [halves_of] * 2, [((4, 8, 96, 768), BF)], us=3)
    down_got = swap(down_send, 1)
    up_low, mids = call(
        act_back_body, [sc, low, hat, slope, scale, nat, *downs], [(four, BF), ((16, 3072), F32)],
        [((3072, 768), BF), (four, F32)], us=5, deps=(down_keep,))
    slots = ((4, 96, 768), BF)
    d_near0, d_near1, d_far0, d_far1 = call(pair_body, [sc, down_keep, down_got], [slots] * 4, us=2, deps=(mids,))
    d_far0, up_low = barrier((d_far0, up_low))
    d_got0 = swap(d_far0, 4)
    up_keep, up_send = call(up_grad_body, [sc, ffn, up_low], [halves_of] * 2, [((4, 8, 96, 768), BF)], us=3, deps=(d_near0,))
    up_got = swap(up_send, 1)
    branch, d_res, *d_att, side_e = call(
        ffn_back_body, [sc, up_low, err, resid, *ups, *outs, vec, *got],
        [(tall, BF), (tall, F32)] + [((256, 192), BF)] * 4 + [((8, 768), F32)],
        [((4, 768, 768), BF), ((768, 768), BF), ((4, 256, 192), BF), ((4, 256, 192), BF)], us=6, deps=(up_keep,))
    u_near0, u_near1, u_far0, u_far1 = call(pair_body, [sc, up_keep, up_got], [slots] * 4, us=2, deps=(side_e,))
    d_got = [d_att[0]] + [swap(d_att[r], r) for r in (1, 2, 3)]
    out_keep, out_send = call(
        out_grad_body, [sc, mixed, branch], [((8, 48, 768), BF)] * 2, [((2, 8, 48, 768), BF)], us=1, deps=(u_near0,))
    out_got = swap(out_send, 1)
    own_part, sent = ((96, 768), F32), ((96, 768), BF)
    d_own0, *d_z0 = call(slots_body, [sc, d_near0, d_got0], [own_part] + [sent] * 3, us=1, deps=(out_keep,))

    def along_z_back(parts):
        return [swap(parts[step - 1], 8 * step) for step in (1, 2, 3)]

    d_z0, d_far1, u_far1, d_got, out_got = barrier((d_z0, d_far1, u_far1, d_got, out_got))
    d_z0 = along_z_back(d_z0)
    d_got1 = swap(d_far1, 4)
    uy_far = swap(u_far1, 2)
    dn_0, dn_1, dn_23, q_keep, q_send = attend_back(
        sc, d_got, (q, k, v, lse, ot, normed, vec), hids, q_near, q_far, side_e, side_d, mids, (d_own0, out_got))
    d_z0, d_got1, uy_far, u_near1, dn_0, dn_1, dn_23, q_keep, q_send = barrier(
        (d_z0, d_got1, uy_far, u_near1, dn_0, dn_1, dn_23, q_keep, q_send))
    near, far = (pl.BlockSpec((4, 48, 768), lambda i, at=at: (at, 0, 0), pipeline_mode=pl.Buffered(1)) for at in (0, 1))
    q_got = swap(q_send, 4)
    uy_near = swap(u_near1, 2)
    d_own1, *d_z1 = call(slots_body, [sc, d_near1, d_got1], [own_part] + [sent] * 3, us=1)
    d_z1 = along_z_back(d_z1)
    q_got, uy_far, d_own1 = barrier((q_got, uy_far, d_own1))
    u_x = call(join_far_body, [sc, u_far0, uy_far, (out_keep, far), (out_got, far)], [((4, 144, 768), BF)], us=1)[0]
    ux_got = swap(u_x, 4)
    d_z1, uy_near, dn_23, q_keep = barrier((d_z1, uy_near, dn_23, q_keep))
    q_own, *q_z = call(slots_body, [sc, q_keep, q_got], [((112, 576), F32)] + [((112, 576), BF)] * 3, us=1, deps=(u_x,))
    q_z = along_z_back(q_z)
    dn_y = swap(dn_23, 2)
    q_z, dn_y, d_own0 = barrier((q_z, dn_y, d_own0))
    one = [pl.BlockSpec((1, 256, 768), lambda i, at=at: (at, 0, 0), pipeline_mode=pl.Buffered(1)) for at in (0, 1)]
    q_sum, dn_1, early = call(
        middle_body, [sc, q_own, *q_z, dn_1, (dn_y, one[1]), d_own0, *d_z0, d_own1, *d_z1],
        [((112, 576), BF), (tall, BF), ((192, 768), BF)], us=1)
    q_y, q_c = swap(q_sum, 2), swap(q_sum, 1)
    q_yc = swap(q_y, 1)
    dn_c = swap(dn_1, 1)
    early_y = swap(early, 2)
    u_own, *u_z = call(
        join_near_body, [sc, u_near0, uy_near, (out_keep, near), (out_got, near), ux_got],
        [((144, 768), F32)] + [((144, 768), BF)] * 3, us=1, deps=(q_sum,))
    u_z = along_z_back(u_z)
    u_z, q_c, q_yc, q_y, dn_c, early_y = barrier((u_z, q_c, q_yc, q_y, dn_c, early_y))
    u_sum = call(total_body, [sc, u_own, *u_z], [((144, 768), BF)], us=1)[0]
    u_y = swap(u_sum, 2)
    hidden_grad = call(hidden_body, [sc, dn_0, (dn_y, one[0]), dn_c, own, vec, d_res], [(tall, F32)], us=1, deps=(u_sum,))[0]
    grad_qkv, gain, shift, bias, mid, loss = call(
        spread_qkv_body, [sc, q_sum, q_c, q_y, q_yc],
        [((96, 2304), F32), ((3, 96), F32), ((3, 96), F32), ((4, 96), F32), ((8, 384), F32), ((1, 1), F32)],
        [((4, 96, 576), BF)], us=2, deps=(hidden_grad,))
    five = call(fold_body, [sc, u_sum, u_y, early, early_y], [((432, 768), BF)], us=1, deps=(grad_qkv,))[0]
    more = swap(five, 1)
    grad_up, grad_out, grad_down = call(
        spread_body, [sc, five, more], [((96, 3072), F32), ((96, 768), F32), ((384, 768), F32)], [((4, 96, 768), F32)],
        us=2)
    return (out[None], loss[0, 0], hidden_grad[None], grad_qkv, grad_out, grad_up, grad_down,
            gain.T, shift.T, bias.T, mid[0], mid[1], mid[2])


def solution(mesh):
    step = fast if (mesh.shape["dp"], mesh.shape["ctx"]) == (8, 4) else shards
    placed = (
        P("dp", "ctx", None),
        P("dp", "ctx", None),
        P("dp"),
        P("dp", None),
        P("dp", None),
        P("dp", None),
        P("dp", None),
        P("dp", None),
        P("dp", None),
        P("dp", None),
        P("dp"),
        P("dp"),
        P("dp"),
    )
    return jax.shard_map(
        step,
        mesh=mesh,
        in_specs=placed,
        out_specs=(
            P("dp", "ctx", None),
            P(),
            P("dp", "ctx", None),
            P("dp", None),
            P("dp", None),
            P("dp", None),
            P("dp", None),
            P("dp", None),
            P("dp", None),
            P("dp", None),
            P("dp"),
            P("dp"),
            P("dp"),
        ),
        check_vma=False,
    )
```

```python
import math

import jax
import jax.numpy as jnp
from jax import lax
from jax.experimental import pallas as pl
from jax.experimental.pallas import tpu as pltpu
from jax.sharding import PartitionSpec as P

HEADS = 12
HEAD_DIM = 64


EPSILON = 1e-05
NEGATIVE = -1e30


def passed_along(value, axis, steps):
    count = lax.axis_size(axis)
    pairs = [(source, (source + steps) % count) for source in range(count)]
    return lax.ppermute(value, axis, pairs)


def passed_along_2(block, axis, distance):
    devices = range(lax.axis_size(axis))
    route = [(i - distance, i) for i in devices if i - distance in devices]
    return lax.ppermute(block, axis, route)


def layer_norm(values, gain_vec, shift_vec):
    average = jnp.mean(values, axis=-1, keepdims=True)
    centred = values - average
    variance = jnp.mean(centred * centred, axis=-1, keepdims=True)
    return centred * lax.rsqrt(variance + EPSILON) * gain_vec + shift_vec


def mid_norm(up_proj, gain_vec, shift_vec):
    return layer_norm(jax.nn.gelu(up_proj, approximate=False), gain_vec, shift_vec)


def split_heads(values):
    return values.reshape(values.shape[0], values.shape[1], HEADS, HEAD_DIM)


def key_mask(query_pos, key_start, key_count, lengths):
    key_pos = key_start + jnp.arange(key_count, dtype=jnp.int32)
    causal = key_pos[None, :] <= query_pos[:, None]
    inside = key_pos[None, :] < lengths[:, None]
    return causal[None, :, :] & inside[:, None, :]


def fold_keys(running, pieces, key_start, heads_q, query_pos, lengths):
    row_max, row_total, weighted = running
    key_piece, value_piece = pieces
    key_count = key_piece.shape[1]
    score_scale = 1.0 / math.sqrt(HEAD_DIM)
    scores = (
        jnp.einsum(
            "sqhd,skhd->shqk", heads_q, split_heads(key_piece), preferred_element_type=jnp.float32
        )
        * score_scale
    )
    allowed = key_mask(query_pos, key_start, key_count, lengths)[:, None]
    scores = jnp.where(allowed, scores, NEGATIVE)
    fresh_max = jnp.maximum(row_max, jnp.max(scores, axis=-1))
    exponent_vals = jnp.exp(scores - fresh_max[..., None])
    row_total = jnp.sum(exponent_vals, axis=-1)
    update = jnp.einsum(
        "shqk,skhd->sqhd",
        exponent_vals.astype(jnp.bfloat16),
        split_heads(value_piece),
        preferred_element_type=jnp.float32,
    )
    weighted = update
    return (fresh_max, row_total, weighted)


def grad_keys(
    heads_q, heads_do, log_total, dterm, key_piece, value_piece, key_start, query_pos, lengths
):
    seq_count, key_count = (key_piece.shape[0], key_piece.shape[1])
    heads_k = split_heads(key_piece)
    heads_v = split_heads(value_piece)
    score_scale = 1.0 / math.sqrt(HEAD_DIM)
    scores = (
        jnp.einsum("sqhd,skhd->shqk", heads_q, heads_k, preferred_element_type=jnp.float32)
        * score_scale
    )
    allowed = key_mask(query_pos, key_start, key_count, lengths)[:, None]
    probability = jnp.where(allowed, jnp.exp(scores - log_total[..., None]), 0.0)
    dprob = jnp.einsum("sqhd,skhd->shqk", heads_do, heads_v, preferred_element_type=jnp.float32)
    dscores = (probability * (dprob - dterm[..., None])).astype(jnp.bfloat16)
    dq_part = (
        jnp.einsum("shqk,skhd->sqhd", dscores, heads_k, preferred_element_type=jnp.float32)
        * score_scale
    )
    dk_part = (
        jnp.einsum("shqk,sqhd->skhd", dscores, heads_q, preferred_element_type=jnp.float32)
        * score_scale
    )
    dv_part = jnp.einsum(
        "shqk,sqhd->skhd",
        probability.astype(jnp.bfloat16),
        heads_do,
        preferred_element_type=jnp.float32,
    )
    return (
        dq_part,
        dk_part.reshape(seq_count, key_count, -1),
        dv_part.reshape(seq_count, key_count, -1),
    )


def shards(
    hidden,
    teacher,
    lengths,
    w_qkv,
    w_out,
    w_up,
    w_down,
    norm_gain,
    norm_shift,
    proj_bias,
    mid_gain,
    mid_shift,
    up_bias,
):
    (
        full_qkv,
        full_out,
        full_up,
        full_down,
        gain_full,
        shift_full,
        bias_full,
        mid_gain_full,
        mid_shift_full,
        up_bias_full,
    ) = (
        lax.all_gather(w_qkv, "dp", axis=0, tiled=True),
        lax.all_gather(w_out, "dp", axis=0, tiled=True),
        lax.all_gather(w_up, "dp", axis=0, tiled=True),
        lax.all_gather(w_down, "dp", axis=0, tiled=True),
        lax.all_gather(norm_gain, "dp", axis=0, tiled=True),
        lax.all_gather(norm_shift, "dp", axis=0, tiled=True),
        lax.all_gather(proj_bias, "dp", axis=0, tiled=True),
        lax.all_gather(mid_gain, "dp", axis=0, tiled=True),
        lax.all_gather(mid_shift, "dp", axis=0, tiled=True),
        lax.all_gather(up_bias, "dp", axis=0, tiled=True),
    )
    gain_f = gain_full.astype(jnp.float32)
    shift_f = shift_full.astype(jnp.float32)
    bias_f = bias_full.astype(jnp.float32)
    mid_gain_f = mid_gain_full.astype(jnp.float32)
    mid_shift_f = mid_shift_full.astype(jnp.float32)
    up_bias_f = up_bias_full.astype(jnp.float32)
    seq_count, local_rows, model_width = hidden.shape
    token_rows = seq_count * local_rows
    seq_shape = (seq_count, local_rows, model_width)
    ctx_place = lax.axis_index("ctx")
    ctx_parts = lax.axis_size("ctx")
    query_pos = ctx_place * local_rows + jnp.arange(local_rows, dtype=jnp.int32)
    last_query = ctx_place * local_rows + local_rows - 1
    valid_mask = (query_pos[None, :] < lengths[:, None]).astype(jnp.float32)
    valid_rows = valid_mask.reshape(token_rows, 1)
    hidden_rows = hidden.reshape(token_rows, model_width).astype(jnp.float32)
    normed, pull_in = jax.vjp(layer_norm, hidden_rows, gain_f[:, 0], shift_f[:, 0])
    normed_low = normed.astype(jnp.bfloat16)
    projected = jnp.dot(normed_low, full_qkv, preferred_element_type=jnp.float32)
    query_low = (projected[:, :model_width] + bias_f[:, 0]).astype(jnp.bfloat16).reshape(seq_shape)
    key_low = projected[:, model_width : 2 * model_width].astype(jnp.bfloat16).reshape(seq_shape)
    value_low = (
        (projected[:, 2 * model_width :] + bias_f[:, 1]).astype(jnp.bfloat16).reshape(seq_shape)
    )
    heads_q = split_heads(query_low)
    start_state = (
        jnp.full((seq_count, HEADS, local_rows), NEGATIVE, jnp.float32),
        jnp.zeros((seq_count, HEADS, local_rows), jnp.float32),
        jnp.zeros((seq_count, local_rows, HEADS, HEAD_DIM), jnp.float32),
    )
    pieces = (
        lax.all_gather(key_low, "ctx", axis=1, tiled=True),
        lax.all_gather(value_low, "ctx", axis=1, tiled=True),
    )
    key_start = jnp.int32(0)
    row_max, row_total, weighted = lax.cond(
        key_start <= last_query,
        lambda: fold_keys(start_state, pieces, key_start, heads_q, query_pos, lengths),
        lambda: start_state,
    )
    attended = weighted / jnp.transpose(row_total, (0, 2, 1))[..., None]
    log_total = row_max + jnp.log(row_total)
    attended_rows = attended.reshape(token_rows, model_width)
    mixed, pull_mix = jax.vjp(layer_norm, attended_rows, gain_f[:, 1], shift_f[:, 1])
    mixed_low = mixed.astype(jnp.bfloat16)
    residual = (
        hidden_rows
        + jnp.dot(mixed_low, full_out, preferred_element_type=jnp.float32)
        + bias_f[:, 2]
    )
    ffn_in, pull_ffn = jax.vjp(layer_norm, residual, gain_f[:, 2], shift_f[:, 2])
    ffn_low = ffn_in.astype(jnp.bfloat16)
    up_proj = jnp.dot(ffn_low, full_up, preferred_element_type=jnp.float32) + up_bias_f
    activated, pull_mid = jax.vjp(mid_norm, up_proj, mid_gain_f, mid_shift_f)
    act_low = activated.astype(jnp.bfloat16)
    result = (
        residual + jnp.dot(act_low, full_down, preferred_element_type=jnp.float32) + bias_f[:, 3]
    )
    layer_output = (result * valid_rows).astype(jnp.bfloat16).reshape(hidden.shape)
    error_rows = (
        result - teacher.reshape(token_rows, model_width).astype(jnp.float32)
    ) * valid_rows
    loss_total, valid_total = lax.psum(
        (0.5 * jnp.sum(error_rows * error_rows), jnp.sum(valid_mask)), ("dp", "ctx")
    )
    loss = loss_total / (valid_total * model_width)
    down_low = error_rows.astype(jnp.bfloat16)
    bias_down_grad = jnp.sum(down_low.astype(jnp.float32), axis=0)
    down_grad = jnp.einsum("rf,rd->fd", act_low, down_low, preferred_element_type=jnp.float32)
    d_act = jnp.einsum("rd,fd->rf", down_low, full_down, preferred_element_type=jnp.float32)
    d_up, mid_gain_grad, mid_shift_grad = pull_mid(d_act)
    up_low = d_up.astype(jnp.bfloat16)
    up_bias_grad = jnp.sum(up_low.astype(jnp.float32), axis=0)
    up_grad = jnp.einsum("rd,rf->df", ffn_low, up_low, preferred_element_type=jnp.float32)
    d_ffn = jnp.einsum("rf,df->rd", up_low, full_up, preferred_element_type=jnp.float32)
    d_res_norm, gain_two, shift_two = pull_ffn(d_ffn)
    d_residual = error_rows + d_res_norm
    branch_low = d_residual.astype(jnp.bfloat16)
    bias_out_grad = jnp.sum(branch_low.astype(jnp.float32), axis=0)
    out_grad = jnp.einsum("rd,re->de", mixed_low, branch_low, preferred_element_type=jnp.float32)
    d_mixed = jnp.einsum("re,de->rd", branch_low, full_out, preferred_element_type=jnp.float32)
    d_att, gain_one, shift_one = pull_mix(d_mixed)
    heads_do = split_heads(d_att.astype(jnp.bfloat16).reshape(seq_shape))
    dterm = jnp.einsum("sqhd,sqhd->shq", heads_do.astype(jnp.float32), attended)

    def grad_step(key_piece, value_piece, key_start):
        return grad_keys(
            heads_q,
            heads_do,
            log_total,
            dterm,
            key_piece,
            value_piece,
            key_start,
            query_pos,
            lengths,
        )

    dq_zero = jnp.zeros((seq_count, local_rows, HEADS, HEAD_DIM), jnp.float32)
    own_zero = jnp.zeros(seq_shape, jnp.float32)

    def pass_step(step_index, running):
        key_cur, value_cur, dk_run, dv_run, dq_sum = running
        owner = (ctx_place - step_index) % ctx_parts
        dq_part, dk_part, dv_part = lax.cond(
            owner <= ctx_place,
            lambda: grad_step(key_cur, value_cur, owner * local_rows),
            lambda: (dq_zero, own_zero, own_zero),
        )
        dk_run, dv_run = (
            passed_along((dk_run + dk_part).astype(jnp.bfloat16), "ctx", 1).astype(jnp.float32),
            passed_along((dv_run + dv_part).astype(jnp.bfloat16), "ctx", 1).astype(jnp.float32),
        )
        key_cur, value_cur = passed_along_2((key_cur, value_cur), "ctx", 1)
        return (key_cur, value_cur, dk_run, dv_run, dq_sum + dq_part)

    key_end, value_end, dk_own, dv_own, dq_sum = lax.fori_loop(
        0, ctx_parts, pass_step, (key_low, value_low, own_zero, own_zero, dq_zero)
    )
    dq_low = dq_sum.reshape(token_rows, model_width).astype(jnp.bfloat16)
    dk_low = dk_own.reshape(token_rows, model_width).astype(jnp.bfloat16)
    dv_low = dv_own.reshape(token_rows, model_width).astype(jnp.bfloat16)
    dqkv_low = jnp.concatenate([dq_low, dk_low, dv_low], axis=1)
    bias_q_grad = jnp.sum(dq_low.astype(jnp.float32), axis=0)
    bias_v_grad = jnp.sum(dv_low.astype(jnp.float32), axis=0)
    qkv_grad = jnp.einsum("rd,re->de", normed_low, dqkv_low, preferred_element_type=jnp.float32)
    d_normed = jnp.einsum("re,de->rd", dqkv_low, full_qkv, preferred_element_type=jnp.float32)
    d_in_norm, gain_zero, shift_zero = pull_in(d_normed)
    hidden_grad = (d_residual + d_in_norm).reshape(hidden.shape)
    gain_grad = jnp.stack([gain_zero, gain_one, gain_two], axis=1)
    shift_grad = jnp.stack([shift_zero, shift_one, shift_two], axis=1)
    bias_grad = jnp.stack([bias_q_grad, bias_v_grad, bias_out_grad, bias_down_grad], axis=1)
    shares = (
        lax.psum_scatter(
            qkv_grad.astype(jnp.bfloat16), "dp", scatter_dimension=0, tiled=True
        ).astype(jnp.float32),
        lax.psum_scatter(
            out_grad.astype(jnp.bfloat16), "dp", scatter_dimension=0, tiled=True
        ).astype(jnp.float32),
        lax.psum_scatter(
            up_grad.astype(jnp.bfloat16), "dp", scatter_dimension=0, tiled=True
        ).astype(jnp.float32),
        lax.psum_scatter(
            down_grad.astype(jnp.bfloat16), "dp", scatter_dimension=0, tiled=True
        ).astype(jnp.float32),
        lax.psum_scatter(
            gain_grad.astype(jnp.bfloat16), "dp", scatter_dimension=0, tiled=True
        ).astype(jnp.float32),
        lax.psum_scatter(
            shift_grad.astype(jnp.bfloat16), "dp", scatter_dimension=0, tiled=True
        ).astype(jnp.float32),
        lax.psum_scatter(
            bias_grad.astype(jnp.bfloat16), "dp", scatter_dimension=0, tiled=True
        ).astype(jnp.float32),
        lax.psum_scatter(
            mid_gain_grad.astype(jnp.bfloat16), "dp", scatter_dimension=0, tiled=True
        ).astype(jnp.float32),
        lax.psum_scatter(
            mid_shift_grad.astype(jnp.bfloat16), "dp", scatter_dimension=0, tiled=True
        ).astype(jnp.float32),
        lax.psum_scatter(
            up_bias_grad.astype(jnp.bfloat16), "dp", scatter_dimension=0, tiled=True
        ).astype(jnp.float32),
    )
    summed = (
        lax.psum(shares[0].astype(jnp.bfloat16), "ctx").astype(jnp.float32),
        lax.psum(shares[1].astype(jnp.bfloat16), "ctx").astype(jnp.float32),
        lax.psum(shares[2].astype(jnp.bfloat16), "ctx").astype(jnp.float32),
        lax.psum(shares[3].astype(jnp.bfloat16), "ctx").astype(jnp.float32),
        lax.psum(shares[4].astype(jnp.bfloat16), "ctx").astype(jnp.float32),
        lax.psum(shares[5].astype(jnp.bfloat16), "ctx").astype(jnp.float32),
        lax.psum(shares[6].astype(jnp.bfloat16), "ctx").astype(jnp.float32),
        lax.psum(shares[7].astype(jnp.bfloat16), "ctx").astype(jnp.float32),
        lax.psum(shares[8].astype(jnp.bfloat16), "ctx").astype(jnp.float32),
        lax.psum(shares[9].astype(jnp.bfloat16), "ctx").astype(jnp.float32),
    )
    return (
        layer_output,
        loss,
        hidden_grad,
        summed[0],
        summed[1],
        summed[2],
        summed[3],
        summed[4],
        summed[5],
        summed[6],
        summed[7],
        summed[8],
        summed[9],
    )


AXES = ("dp", "ctx")


def swap(value, mask):
    count = lax.axis_size("dp") * lax.axis_size("ctx")
    return lax.ppermute(value, AXES, [(i, i ^ mask) for i in range(count)])


def along_z(piece):
    return [swap(piece, 8 * step) for step in (1, 2, 3)]


def wide(value):
    return value.astype(jnp.float32)


def narrow(value):
    return value.astype(jnp.bfloat16)


VMEM_BYTES = 56 * 1024 * 1024


def whole(shape):
    return pl.BlockSpec(tuple(shape), lambda i: (0,) * len(shape), pipeline_mode=pl.Buffered(1))


def padded(shape, dtype):
    lead = math.prod(shape[:-2])
    size = jnp.dtype(dtype).itemsize
    rows = -(-shape[-2] // (32 // size)) * (32 // size) if len(shape) > 1 else 8
    return lead * rows * (-(-shape[-1] // 128) * 128) * size


def call(body, ins, outs, scratch=(), us=1, deps=(), room=6):
    pairs = [v if isinstance(v, tuple) else (v, whole(v.shape)) for v in ins[1:]]
    held = sum(padded(spec.block_shape, v.dtype) for v, spec in pairs)
    held += sum(padded(shape, dtype) for shape, dtype in (*outs, *scratch))
    count = len(pairs)

    def kernel(sc, *refs):
        body(sc, *refs[:count], *refs[count + len(deps):])

    return pl.pallas_call(
        kernel,
        grid=(1,),
        in_specs=[pl.BlockSpec(memory_space=pltpu.SMEM)] + [spec for _, spec in pairs]
        + [pl.BlockSpec(memory_space=pl.ANY)] * len(deps),
        out_specs=[whole(shape) for shape, _ in outs],
        out_shape=[jax.ShapeDtypeStruct(shape, dtype) for shape, dtype in outs],
        scratch_shapes=[pltpu.VMEM(shape, dtype) for shape, dtype in scratch],
        compiler_params=pltpu.CompilerParams(vmem_limit_bytes=held + room * 1024 * 1024),
        cost_estimate=pl.CostEstimate(flops=int(us * 2e7), bytes_accessed=0, transcendentals=0),
        name=body.__name__,
    )(ins[0], *[v for v, _ in pairs], *deps)


def after(value, *deps):
    return lax.optimization_barrier((value, *deps))[0]


BF, F32 = jnp.bfloat16, jnp.float32


def contract(a, b, da, db):
    return lax.dot_general(a, b, (((da,), (db,)), ((), ())), preferred_element_type=F32)


def block_of(sc, xr, zr):
    return 2 * ((sc[0] >> 1) ^ zr) + ((sc[0] & 1) ^ xr)


def slot_of(sc, block):
    return ((block & 1) ^ (sc[0] & 1)) * 4 + ((block >> 1) ^ (sc[0] >> 1))


def lay(sc, scr, near, far, rows, stride, offset=0):
    for xr, ref in ((0, near), (1, far)):
        for zr in range(4):
            at = pl.multiple_of(stride * block_of(sc, xr, zr) + offset, 16)
            scr[pl.ds(at, rows), :] = ref[zr]


def moments(value):
    average = jnp.mean(value, axis=-1, keepdims=True)
    centred = value - average
    scale = lax.rsqrt(jnp.mean(centred * centred, axis=-1, keepdims=True) + EPSILON)
    return centred * scale, scale


def norm_back(grad, hat, scale):
    return scale * (grad - jnp.mean(grad, axis=-1, keepdims=True) - hat * jnp.mean(grad * hat, axis=-1, keepdims=True))


def mine(ctx_at, row):
    out = row[:, :192]
    for j in range(1, 4):
        out = jnp.where(ctx_at == j, row[:, 192 * j:192 * j + 192], out)
    return out


def pack_body(sc, w, gain, shift, bias, out, scr):
    scr[...] = jnp.zeros((16, 128), F32)
    scr[0:3, :96] = gain[...].astype(F32)
    scr[3:6, :96] = shift[...].astype(F32)
    scr[6:10, :96] = bias[...].astype(F32)
    small = scr[...].T[:96].astype(BF)
    for j in range(4):
        @pl.when(sc[1] == j)
        def _():
            cols = [w[:, 768 * part + 192 * j:768 * part + 192 * j + 192] for part in range(3)]
            out[...] = jnp.concatenate(cols + [small, jnp.zeros((96, 48), BF)], axis=1)


def attend_body(sc, h0, h1, h2, h3, wa, wb, a0, a1, a23, q_o, k_o, v_o, lse_o, ot_o, n_o, vec_o, w_scr):
    ctx_at, length = sc[1], sc[2]
    lay(sc, w_scr, wa, wb, 96, 96)
    vec = w_scr[:, 512:640].astype(F32).T[64:80]
    vec_o[...] = vec
    bias_q, bias_v = mine(ctx_at, vec[6:7]), mine(ctx_at, vec[7:8])
    for r, ref in enumerate((h0, h1, h2, h3)):
        rows = pl.ds(pl.multiple_of((ctx_at ^ r) * 256, 256), 256)
        hat, _ = moments(ref[...].astype(F32))
        normed = (hat * vec[0:1] + vec[3:4]).astype(BF)
        n_o[rows, :] = normed
        p = jnp.dot(normed, w_scr[...], preferred_element_type=F32)
        for h in range(3):
            q_o[h, rows, :] = ((p[:, 64 * h:64 * h + 64] + bias_q[:, 64 * h:64 * h + 64]) * 0.125).astype(BF)
            k_o[h, rows, :] = p[:, 192 + 64 * h:256 + 64 * h].astype(BF)
            v_o[h, rows, :] = (p[:, 384 + 64 * h:448 + 64 * h] + bias_v[:, 64 * h:64 * h + 64]).astype(BF)

    def head(h, carry):
        for i in range(4):
            n = 256 * (i + 1)
            scores = contract(k_o[h, :n, :], q_o[h, 256 * i:256 * i + 256, :], 1, 1)
            limit = jnp.minimum(256 * i + lax.broadcasted_iota(jnp.int32, (1, 256), 1), length - 1)
            scores = jnp.where(lax.broadcasted_iota(jnp.int32, (n, 256), 0) <= limit, scores, NEGATIVE)
            top = jnp.max(scores, axis=0, keepdims=True)
            grown = jnp.exp(scores - top)
            total = jnp.sum(grown, axis=0, keepdims=True)
            out = contract(v_o[h, :n, :], grown.astype(BF), 0, 0) / total
            ot_o[i, pl.ds(pl.multiple_of(64 * h, 64), 64), :] = out
            lse_o[h, i:i + 1, :] = top + jnp.log(total)
        return carry

    lax.fori_loop(0, 3, head, 0)
    for r, ref in enumerate((a0, a1, a23.at[0], a23.at[1])):
        ref[...] = ot_o[ctx_at ^ r].T.astype(BF)


def attend(sc, hids, wa, wb, deps):
    rows = (256, 192)
    return call(
        attend_body, [sc, *hids, wa, wb],
        [(rows, BF)] * 2 + [((2, 256, 192), BF)] + [((3, 1024, 64), BF)] * 3
        + [((3, 8, 256), F32), ((4, 192, 256), F32), ((1024, 768), BF), ((16, 768), F32)],
        [((768, 640), BF)], us=13, deps=deps)


def attend_back_body(sc, d0, d1, d2, d3, q_i, k_i, v_i, lse_i, ot_i, n_i, h0, h1, h2, h3, wa, wb, vec_i, side_e, side_d, mids,
                     n0, n1, n23, keep, send, w_scr, do_scr, dq_s, dk_s, dv_s, dk_acc, dv_acc, all_scr, g_scr):
    ctx_at, length = sc[1], sc[2]
    lay(sc, w_scr, wa, wb, 96, 96)
    for r, ref in enumerate((d0, d1, d2, d3)):
        rows = pl.ds(pl.multiple_of((ctx_at ^ r) * 256, 256), 256)
        value = ref[...]
        for h in range(3):
            do_scr[h, rows, :] = value[:, 64 * h:64 * h + 64]

    def head(h, carry):
        for i in (3, 2, 1, 0):
            n = 256 * (i + 1)
            mine_rows = slice(256 * i, 256 * i + 256)
            q, do, k = q_i[h, mine_rows, :], do_scr[h, mine_rows, :], k_i[h, :n, :]
            out = ot_i[i, pl.ds(pl.multiple_of(64 * h, 64), 64), :]
            dterm = jnp.sum(do.astype(F32).T * out, axis=0, keepdims=True)
            limit = jnp.minimum(256 * i + lax.broadcasted_iota(jnp.int32, (1, 256), 1), length - 1)
            prob = jnp.exp(contract(k, q, 1, 1) - lse_i[h, i:i + 1, :])
            prob = jnp.where(lax.broadcasted_iota(jnp.int32, (n, 256), 0) <= limit, prob, 0.0)
            dscore = (prob * (contract(v_i[h, :n, :], do, 1, 1) - dterm)).astype(BF)
            dv = jnp.dot(prob.astype(BF), do, preferred_element_type=F32)
            dk = jnp.dot(dscore, q, preferred_element_type=F32)
            if i == 3:
                dv_acc[...] = dv
                dk_acc[...] = dk
            else:
                dv_acc[:n, :] += dv
                dk_acc[:n, :] += dk
            dq_s[h, mine_rows, :] = (contract(k, dscore, 0, 0) * 0.125).T.astype(BF)
        dk_s[h] = dk_acc[...].astype(BF)
        dv_s[h] = dv_acc[...].astype(BF)
        return carry

    lax.fori_loop(0, 3, head, 0)
    for i in range(4):
        rows = slice(256 * i, 256 * i + 256)
        all_scr[rows, :] = jnp.concatenate([s[h, rows, :] for s in (dq_s, dk_s, dv_s) for h in range(3)], axis=1)
    sums = jnp.sum(all_scr[...].astype(F32), axis=0, keepdims=True)
    bias_q = jnp.concatenate([jnp.where(ctx_at == j, sums[:, :192], 0.0) for j in range(4)], axis=1)
    bias_v = jnp.concatenate([jnp.where(ctx_at == j, sums[:, 384:], 0.0) for j in range(4)], axis=1)
    gain_sum, shift_sum = jnp.zeros((1, 768), F32), jnp.zeros((1, 768), F32)
    for r, (ref, out) in enumerate(((h0, n0), (h1, n1), (h2, n23.at[0]), (h3, n23.at[1]))):
        rows = pl.ds(pl.multiple_of((ctx_at ^ r) * 256, 256), 256)
        grad = contract(all_scr[rows, :], w_scr[:, :576], 1, 1)
        hat, _ = moments(ref[...].astype(F32))
        gain_sum += jnp.sum(grad * hat, axis=0, keepdims=True)
        shift_sum += jnp.sum(grad, axis=0, keepdims=True)
        out[...] = grad.astype(BF)
    rows16 = jnp.concatenate(
        [gain_sum, side_e[0:2], shift_sum, side_e[2:4], bias_q, bias_v, side_e[4:5], side_d[0:2], jnp.zeros((5, 768), F32)], axis=0)
    w_grad = contract(n_i[...], all_scr[...], 0, 0)
    for b in range(8):
        at = slot_of(sc, b)
        extra = jnp.concatenate([mids[:, 384 * b:384 * b + 384], rows16[:, 96 * b:96 * b + 96], jnp.zeros((16, 96), F32)], axis=1)
        g_scr[at, :96, :] = w_grad[96 * b:96 * b + 96].astype(BF)
        g_scr[at, 96:112, :] = extra.astype(BF)
    keep[...] = g_scr[:4]
    send[...] = g_scr[4:]


def attend_back(sc, douts, saved, hids, wa, wb, side_e, side_d, mids, deps):
    q, k, v, lse, ot, normed, vec = saved
    return call(
        attend_back_body, [sc, *douts, q, k, v, lse, ot, normed, *hids, wa, wb, vec, side_e, side_d, mids],
        [((256, 768), BF)] * 2 + [((2, 256, 768), BF)] + [((4, 112, 576), BF)] * 2,
        [((768, 640), BF), ((3, 1024, 64), BF), ((3, 1024, 64), BF), ((3, 1024, 64), BF), ((3, 1024, 64), BF),
         ((1024, 64), F32), ((1024, 64), F32), ((1024, 576), BF), ((8, 112, 576), BF)],
        us=12, deps=deps)


def part(rows, at):
    return pl.BlockSpec((4, rows, 768), lambda i: (0, at, 0), pipeline_mode=pl.Buffered(1))


def lay_out(sc, scr, own_near, own_far, other_near, other_far):
    core = sc[1] & 1
    lay(sc, scr, own_near, own_far, 48, 96, 48 * core)
    lay(sc, scr, other_near, other_far, 48, 96, 48 * (1 - core))


def lay_down(sc, scr, refs):
    for c in (0, 1):
        for xr in (0, 1):
            for y in (0, 1):
                lay_one(sc, scr, refs[4 * c + 2 * xr + y], xr, 96 * (sc[1] ^ (2 * y + c)))


def lay_one(sc, scr, ref, xr, offset):
    for zr in range(4):
        scr[pl.ds(pl.multiple_of(384 * block_of(sc, xr, zr) + offset, 32), 96), :] = ref[zr]


def join_heads(sc, scr, pieces):
    own, near, far = pieces
    for r, value in enumerate((own[...], near[0], far[0], near[1])):
        scr[r] = value
    return jnp.concatenate([scr[sc[1] ^ j] for j in range(4)], axis=1).astype(F32)


def mid_body(sc, g0, g1, g2, own, vec, on, of, tn, tf, mixed_o, resid_o, ffn_o, w_scr, a_scr):
    lay_out(sc, w_scr, on, of, tn, tf)
    hat, _ = moments(join_heads(sc, a_scr, (g0, g1, g2)))
    mixed = (hat * vec[1:2] + vec[4:5]).astype(BF)
    mixed_o[...] = mixed
    resid = own[...].astype(F32) + jnp.dot(mixed, w_scr[...], preferred_element_type=F32) + vec[8:9]
    resid_o[...] = resid
    hat, _ = moments(resid)
    ffn_o[...] = (hat * vec[2:3] + vec[5:6]).astype(BF)


def up_body(sc, ffn, w0n, w0f, w1n, w1f, w2n, w2f, w3n, w3f, mn, mf, act_o, hat_o, slope_o, scale_o, nat_o,
            w_scr, g_scr, m_scr):
    for xr, ref in ((0, mn), (1, mf)):
        for zr in range(4):
            m_scr[block_of(sc, xr, zr)] = ref[zr].astype(F32)
    flat = [m_scr[b] for b in range(8)]
    for j in range(4):
        two = flat[2 * j:2 * j + 2]
        nat_o[j, 0:1, :] = jnp.concatenate([m[0:1, :384] for m in two], axis=1)
        nat_o[j, 1:2, :] = jnp.concatenate([m[0:1, 384:] for m in two], axis=1)
        nat_o[j, 2:3, :] = jnp.concatenate([m[1:2, :384] for m in two], axis=1)
        nat_o[j, 3:8, :] = jnp.zeros((5, 768), F32)
    value = ffn[...]
    total = jnp.zeros((256, 1), F32)
    for t, (near, far) in enumerate(((w0n, w0f), (w1n, w1f), (w2n, w2f), (w3n, w3f))):
        j = sc[1] ^ t
        lay(sc, w_scr.at[t], near, far, 96, 96)
        up = jnp.dot(value, w_scr[t], preferred_element_type=F32) + nat_o[j, 2:3, :]
        chance = 0.5 * (1.0 + lax.erf(up * math.sqrt(0.5)))
        slope_o[j] = (chance + up * jnp.exp(-0.5 * up * up) * (1.0 / math.sqrt(2.0 * math.pi))).astype(BF)
        gelu = up * chance
        g_scr[j] = gelu
        total += jnp.sum(gelu, axis=-1, keepdims=True)
    average = total * (1.0 / 3072)
    square = jnp.zeros((256, 1), F32)
    for j in range(4):
        centred = g_scr[j] - average
        square += jnp.sum(centred * centred, axis=-1, keepdims=True)
    scale = lax.rsqrt(square * (1.0 / 3072) + EPSILON)
    scale_o[...] = scale
    for j in range(4):
        hat = (g_scr[j] - average) * scale
        hat_o[j] = hat.astype(BF)
        act_o[j] = (hat * nat_o[j, 0:1, :] + nat_o[j, 1:2, :]).astype(BF)


def down_body(sc, act, resid, teacher, vec, e0, e1, e2, e3, e4, e5, e6, e7, out_o, err_o, low_o, side_o, w_scr):
    lay_down(sc, w_scr, (e0, e1, e2, e3, e4, e5, e6, e7))
    result = resid[...] + vec[9:10]
    for j in range(4):
        result += jnp.dot(act[j], w_scr[768 * j:768 * j + 768, :], preferred_element_type=F32)
    pos = sc[1] * 256 + lax.broadcasted_iota(jnp.int32, (256, 1), 0)
    valid = jnp.where(pos < sc[2], 1.0, 0.0)
    out_o[...] = (result * valid).astype(BF)
    error = (result - teacher[...].astype(F32)) * valid
    err_o[...] = error
    low = error.astype(BF)
    low_o[...] = low
    side_o[0:1, :] = jnp.sum(low.astype(F32), axis=0, keepdims=True)
    loss = 0.5 * jnp.sum(jnp.sum(error * error, axis=0, keepdims=True), axis=1, keepdims=True)
    count = jnp.sum(valid, axis=0, keepdims=True)
    high = loss.astype(BF).astype(F32)
    lane = lax.broadcasted_iota(jnp.int32, (1, 768), 1) % 96
    side_o[1:2, :] = jnp.where(lane == 0, high, jnp.where(lane == 1, loss - high, jnp.where(lane == 2, count, 0.0)))
    side_o[2:8, :] = jnp.zeros((6, 768), F32)


def down_grad_body(sc, act, low, keep, send, g_scr):
    value = low[...]
    for j in range(4):
        grad = contract(act[j], value, 0, 0).astype(BF)
        for half in (0, 1):
            at = slot_of(sc, 2 * j + half)
            for q in range(4):
                g_scr[sc[1] ^ q, at] = grad[384 * half + 96 * q:384 * half + 96 * q + 96]
    for y in (0, 1):
        keep[y] = g_scr[2 * y]
        send[y] = g_scr[2 * y + 1]


def act_back_body(sc, low, hat_i, slope, scale, nat, e0, e1, e2, e3, e4, e5, e6, e7, up_o, mids_o, wd_scr, dh_scr):
    lay_down(sc, wd_scr, (e0, e1, e2, e3, e4, e5, e6, e7))
    value = low[...]
    first, second = jnp.zeros((256, 1), F32), jnp.zeros((256, 1), F32)
    for j in range(4):
        grad = contract(value, wd_scr[768 * j:768 * j + 768, :], 1, 1)
        hat = hat_i[j].astype(F32)
        cols = slice(768 * j, 768 * j + 768)
        mids_o[0:1, cols] = jnp.sum(grad * hat, axis=0, keepdims=True)
        mids_o[1:2, cols] = jnp.sum(grad, axis=0, keepdims=True)
        grad = grad * nat[j, 0:1, :]
        dh_scr[j] = grad
        first += jnp.sum(grad, axis=-1, keepdims=True)
        second += jnp.sum(grad * hat, axis=-1, keepdims=True)
    first, second = first * (1.0 / 3072), second * (1.0 / 3072)
    for j in range(4):
        hat = hat_i[j].astype(F32)
        grad = (scale[...] * (dh_scr[j] - first - hat * second) * slope[j].astype(F32)).astype(BF)
        up_o[j] = grad
        mids_o[2:3, 768 * j:768 * j + 768] = jnp.sum(grad.astype(F32), axis=0, keepdims=True)
    mids_o[3:16, :] = jnp.zeros((13, 3072), F32)


def ffn_back_body(sc, up_i, err, resid, w0n, w0f, w1n, w1f, w2n, w2f, w3n, w3f, on, of, tn, tf, vec, g0, g1, g2,
                  branch_o, dres_o, p0, p1, p2, p3, side_o, w_scr, o_scr, a_scr, b_scr):
    grad = jnp.zeros((256, 768), F32)
    for t, (near, far) in enumerate(((w0n, w0f), (w1n, w1f), (w2n, w2f), (w3n, w3f))):
        lay(sc, w_scr.at[t], near, far, 96, 96)
        grad += contract(up_i[sc[1] ^ t], w_scr[t], 1, 1)
    hat, factor = moments(resid[...])
    side_o[1:2, :] = jnp.sum(grad * hat, axis=0, keepdims=True)
    side_o[3:4, :] = jnp.sum(grad, axis=0, keepdims=True)
    dres = err[...] + norm_back(grad * vec[2:3], hat, factor)
    dres_o[...] = dres
    branch = dres.astype(BF)
    branch_o[...] = branch
    side_o[4:5, :] = jnp.sum(branch.astype(F32), axis=0, keepdims=True)
    lay_out(sc, o_scr, on, of, tn, tf)
    grad = contract(branch, o_scr[...], 1, 1)
    hat, factor = moments(join_heads(sc, a_scr, (g0, g1, g2)))
    side_o[0:1, :] = jnp.sum(grad * hat, axis=0, keepdims=True)
    side_o[2:3, :] = jnp.sum(grad, axis=0, keepdims=True)
    side_o[5:8, :] = jnp.zeros((3, 768), F32)
    grad = norm_back(grad * vec[1:2], hat, factor).astype(BF)
    for j in range(4):
        b_scr[j] = grad[:, 192 * j:192 * j + 192]
    for r, ref in enumerate((p0, p1, p2, p3)):
        ref[...] = b_scr[sc[1] ^ r]


def up_grad_body(sc, ffn, up, keep, send, g_scr):
    value = ffn[...]
    for j in range(4):
        grad = contract(value, up[j], 0, 0).astype(BF)
        for b in range(8):
            g_scr[sc[1] ^ j, slot_of(sc, b)] = grad[96 * b:96 * b + 96]
    for y in (0, 1):
        keep[y] = g_scr[2 * y]
        send[y] = g_scr[2 * y + 1]


def out_grad_body(sc, mixed, branch, out_keep, out_send, o_scr):
    grad = contract(mixed[...], branch[...], 0, 0).astype(BF)
    for b in range(8):
        for c in (0, 1):
            o_scr[(sc[1] & 1) ^ c, slot_of(sc, b)] = grad[96 * b + 48 * c:96 * b + 48 * c + 48]
    out_keep[...] = o_scr[0]
    out_send[...] = o_scr[1]


def added(a, b):
    return a.astype(F32) + b.astype(F32)


def pair_body(sc, keep, got, near0, near1, far0, far1):
    for y, near, far in ((0, near0, far0), (1, near1, far1)):
        near[...] = added(keep[y, :4], got[y, :4]).astype(BF)
        far[...] = added(keep[y, 4:], got[y, 4:]).astype(BF)


def slots_body(sc, near, got, own, s1, s2, s3):
    own[...] = added(near[0], got[0])
    for at, out in ((1, s1), (2, s2), (3, s3)):
        out[...] = added(near[at], got[at]).astype(BF)


def join_far_body(sc, mine, got, out_keep, out_got, far):
    far[:, :96, :] = added(mine[...], got[...]).astype(BF)
    far[:, 96:, :] = added(out_keep[...], out_got[...]).astype(BF)


def join_near_body(sc, mine, y_got, out_keep, out_got, x_got, own, s1, s2, s3):
    for at, out in ((0, own), (1, s1), (2, s2), (3, s3)):
        kind = out.dtype
        out[:96, :] = (added(mine[at], y_got[at]) + x_got[at, :96, :].astype(F32)).astype(kind)
        out[96:, :] = (added(out_keep[at], out_got[at]) + x_got[at, 96:, :].astype(F32)).astype(kind)


def total_of(own, parts):
    return (own[...] + sum(p[...].astype(F32) for p in parts)).astype(BF)


def middle_body(sc, q0, q1, q2, q3, dn, got, d0, d1, d2, d3, e0, e1, e2, e3, q_o, dn_o, early_o):
    q_o[...] = total_of(q0, (q1, q2, q3))
    dn_o[...] = added(dn[...], got[0]).astype(BF)
    early_o[0:96, :] = total_of(d0, (d1, d2, d3))
    early_o[96:192, :] = total_of(e0, (e1, e2, e3))


def fold_body(sc, own, other, early, early_got, out):
    out[0:96, :] = own[0:96, :]
    out[96:192, :] = other[0:96, :]
    out[192:240, :] = added(own[96:144, :], other[96:144, :]).astype(BF)
    out[240:336, :] = added(early[0:96, :], early_got[96:192, :]).astype(BF)
    out[336:432, :] = added(early[96:192, :], early_got[0:96, :]).astype(BF)


def spread_body(sc, mine, other, up_o, out_o, down_o, scr):
    core = sc[1] & 1
    for t, (ref, at) in enumerate(((mine, 0), (other, 0), (mine, 96), (other, 96))):
        scr[sc[1] ^ t] = ref[at:at + 96, :].astype(F32)
        rows = pl.multiple_of(96 * (sc[1] ^ t), 32)
        down_o[pl.ds(rows, 96), :] = ref[240 + at:336 + at, :].astype(F32)
    for j in range(4):
        up_o[:, 768 * j:768 * j + 768] = scr[j]
    out_o[pl.ds(pl.multiple_of(48 * core, 16), 48), :] = mine[192:240, :].astype(F32)
    out_o[pl.ds(pl.multiple_of(48 * (1 - core), 16), 48), :] = other[192:240, :].astype(F32)


def spread_qkv_body(sc, t0, t1, t2, t3, grad_o, gain_o, shift_o, bias_o, mid_o, loss_o, scr):
    rest = jnp.zeros((16, 576), F32)
    for r, ref in enumerate((t0, t1, t2, t3)):
        scr[sc[1] ^ r] = ref[:96, :]
        rest += ref[96:112, :].astype(F32)
    for p in range(3):
        cols = [scr[j, :, 192 * p:192 * p + 192] for j in range(4)]
        grad_o[:, 768 * p:768 * p + 768] = jnp.concatenate(cols, axis=1).astype(F32)
    gain_o[...] = rest[0:3, 384:480]
    shift_o[...] = rest[3:6, 384:480]
    bias_o[...] = rest[6:10, 384:480]
    mid_o[...] = rest[0:8, :384]
    row = rest[10:11, 384:480]
    lane = lax.broadcasted_iota(jnp.int32, (1, 96), 1)
    error = jnp.sum(jnp.where(lane < 2, row, 0.0), axis=1, keepdims=True)
    count = jnp.sum(jnp.where(lane == 2, row, 0.0), axis=1, keepdims=True)
    loss_o[...] = error / (count * 768.0)


def hidden_body(sc, a, b, c, own, vec, d_res, out):
    grad = (added(a[...], b[0]) + c[...].astype(F32)) * vec[0:1]
    hat, factor = moments(own[...].astype(F32))
    out[...] = d_res[...] + norm_back(grad, hat, factor)


def total_body(sc, own, s1, s2, s3, out):
    out[...] = total_of(own, (s1, s2, s3))


def fast(
    hidden, teacher, lengths, w_qkv, w_out, w_up, w_down, norm_gain, norm_shift, proj_bias,
    mid_gain, mid_shift, up_bias,
):
    dp_at, ctx_at = lax.axis_index("dp"), lax.axis_index("ctx")
    core = ctx_at & 1
    sc = jnp.stack([dp_at, ctx_at, lengths[0]]).astype(jnp.int32)
    own = hidden[0]
    tall = (256, 768)
    barrier = lax.optimization_barrier
    h_y, h_c = swap(own, 2), swap(own, 1)
    piece = call(pack_body, [sc, w_qkv, norm_gain.T, norm_shift.T, proj_bias.T], [((96, 640), BF)], [((16, 128), F32)], room=54)[0]
    q_cols = along_z(piece)
    mid_rows = jnp.concatenate([mid_gain, mid_shift, up_bias, jnp.zeros((13 * 384,), BF)]).reshape(8, 768)
    piece_a = jnp.concatenate([
        lax.dynamic_slice(w_up, (0, 768 * ctx_at), (96, 768)), lax.dynamic_slice(w_out, (48 * core, 0), (48, 768)), mid_rows])
    down4 = w_down.reshape(4, 96, 768)
    piece_b, piece_c = (lax.dynamic_index_in_dim(down4, ctx_at ^ t, 0, keepdims=False) for t in (0, 2))
    q_cols, piece_a = barrier((q_cols, piece_a))
    q_near = jnp.stack([piece] + q_cols)
    q_far = swap(q_near, 4)
    h_yc = swap(h_y, 1)
    a_cols = along_z(piece_a)
    a_cols, q_far, piece_b, h_c, h_yc = barrier((a_cols, q_far, piece_b, h_c, h_yc))
    a_near = jnp.stack([piece_a] + a_cols)
    a_far = swap(a_near, 4)
    y_near = swap(a_near[:, :96], 2)
    a_near_o = swap(a_near, 1)
    b_cols = along_z(piece_b)
    hids = [own, h_c, h_y, h_yc]
    att_0, att_1, att_23, q, k, v, lse, ot, normed, vec = attend(sc, hids, q_near, q_far, (a_near,))
    y_near, b_cols, piece_c, att_23, att_1 = barrier((y_near, b_cols, piece_c, att_23, att_1))
    c_cols = along_z(piece_c)
    att_y = swap(att_23, 2)
    b_near = jnp.stack([piece_b] + b_cols)
    a_far, b_near, att_y = barrier((a_far, b_near, att_y))
    b_far = swap(b_near, 4)
    y_far = swap(a_far[:, :96], 2)
    c_cols, b_far, y_far, a_near, a_far, y_near, b_near, att_1 = barrier(
        (c_cols, b_far, y_far, a_near, a_far, y_near, b_near, att_1))
    c_near = jnp.stack([piece_c] + c_cols)
    c_far = swap(c_near, 4)
    att_c = swap(jnp.stack([att_1, att_y[1]]), 1)
    a_near_o, a_far_o, y_near_o, y_far_o = (swap(t, 1) for t in (a_near, a_far, y_near, y_far))
    b_near_o, b_far_o, c_near_o = (swap(t, 1) for t in (b_near, b_far, c_near))
    got = [att_0, att_c, att_y]
    outs = [(t, part(48, 2)) for t in (a_near, a_far, a_near_o, a_far_o)]
    mixed, resid, ffn = call(
        mid_body, [sc, *got, own, vec, *outs], [(tall, BF), (tall, F32), (tall, BF)],
        [((768, 768), BF), ((4, 256, 192), BF)], us=3)
    ups = [(t, part(96, 0)) for t in (a_near, a_far, a_near_o, a_far_o)] + [y_near, y_far, y_near_o, y_far_o]
    four = (4, 256, 768)
    act, hat, slope, scale, nat = call(
        up_body, [sc, ffn, *ups] + [(t, part(8, 18)) for t in (a_near, a_far)],
        [(four, BF), (four, BF), (four, BF), ((256, 1), F32), ((4, 8, 768), F32)],
        [((4, 768, 768), BF), (four, F32), ((8, 8, 768), F32)], us=5)
    c_far, act = barrier((c_far, act))
    c_far_o = swap(c_far, 1)
    downs = [b_near, c_near, b_far, c_far, b_near_o, c_near_o, b_far_o, c_far_o]
    out, err, low, side_d = call(
        down_body, [sc, act, resid, teacher[0], vec, *downs],
        [(tall, BF), (tall, F32), (tall, BF), ((8, 768), F32)], [((3072, 768), BF)], us=5)
    halves_of = ((2, 8, 96, 768), BF)
    down_keep, down_send = call(
        down_grad_body, [sc, act, low], [halves_of] * 2, [((4, 8, 96, 768), BF)], us=3)
    down_got = swap(down_send, 1)
    up_low, mids = call(
        act_back_body, [sc, low, hat, slope, scale, nat, *downs], [(four, BF), ((16, 3072), F32)],
        [((3072, 768), BF), (four, F32)], us=5, deps=(down_keep,))
    slots = ((4, 96, 768), BF)
    d_near0, d_near1, d_far0, d_far1 = call(pair_body, [sc, down_keep, down_got], [slots] * 4, us=2, deps=(mids,))
    d_far0, up_low = barrier((d_far0, up_low))
    d_got0 = swap(d_far0, 4)
    up_keep, up_send = call(up_grad_body, [sc, ffn, up_low], [halves_of] * 2, [((4, 8, 96, 768), BF)], us=3, deps=(d_near0,))
    up_got = swap(up_send, 1)
    branch, d_res, *d_att, side_e = call(
        ffn_back_body, [sc, up_low, err, resid, *ups, *outs, vec, *got],
        [(tall, BF), (tall, F32)] + [((256, 192), BF)] * 4 + [((8, 768), F32)],
        [((4, 768, 768), BF), ((768, 768), BF), ((4, 256, 192), BF), ((4, 256, 192), BF)], us=6, deps=(up_keep,))
    u_near0, u_near1, u_far0, u_far1 = call(pair_body, [sc, up_keep, up_got], [slots] * 4, us=2, deps=(side_e,))
    d_got = [d_att[0]] + [swap(d_att[r], r) for r in (1, 2, 3)]
    out_keep, out_send = call(
        out_grad_body, [sc, mixed, branch], [((8, 48, 768), BF)] * 2, [((2, 8, 48, 768), BF)], us=1, deps=(u_near0,))
    out_got = swap(out_send, 1)
    own_part, sent = ((96, 768), F32), ((96, 768), BF)
    d_own0, *d_z0 = call(slots_body, [sc, d_near0, d_got0], [own_part] + [sent] * 3, us=1, deps=(out_keep,))

    def along_z_back(parts):
        return [swap(parts[step - 1], 8 * step) for step in (3, 2, 1)]

    d_z0, d_far1, u_far1, d_got, out_got = barrier((d_z0, d_far1, u_far1, d_got, out_got))
    d_z0 = along_z_back(d_z0)
    d_got1 = swap(d_far1, 4)
    uy_far = swap(u_far1, 2)
    dn_0, dn_1, dn_23, q_keep, q_send = attend_back(
        sc, d_got, (q, k, v, lse, ot, normed, vec), hids, q_near, q_far, side_e, side_d, mids, (d_own0, out_got))
    d_z0, d_got1, uy_far, u_near1, dn_0, dn_1, dn_23, q_keep, q_send = barrier(
        (d_z0, d_got1, uy_far, u_near1, dn_0, dn_1, dn_23, q_keep, q_send))
    near, far = (pl.BlockSpec((4, 48, 768), lambda i, at=at: (at, 0, 0), pipeline_mode=pl.Buffered(1)) for at in (0, 1))
    q_got = swap(q_send, 4)
    uy_near = swap(u_near1, 2)
    d_own1, *d_z1 = call(slots_body, [sc, d_near1, d_got1], [own_part] + [sent] * 3, us=1)
    d_z1 = along_z_back(d_z1)
    q_got, uy_far, d_own1 = barrier((q_got, uy_far, d_own1))
    u_x = call(join_far_body, [sc, u_far0, uy_far, (out_keep, far), (out_got, far)], [((4, 144, 768), BF)], us=1)[0]
    ux_got = swap(u_x, 4)
    d_z1, uy_near, dn_23, q_keep = barrier((d_z1, uy_near, dn_23, q_keep))
    q_own, *q_z = call(slots_body, [sc, q_keep, q_got], [((112, 576), F32)] + [((112, 576), BF)] * 3, us=1, deps=(u_x,))
    q_z = along_z_back(q_z)
    dn_y = swap(dn_23, 2)
    q_z, dn_y, d_own0 = barrier((q_z, dn_y, d_own0))
    one = [pl.BlockSpec((1, 256, 768), lambda i, at=at: (at, 0, 0), pipeline_mode=pl.Buffered(1)) for at in (0, 1)]
    q_sum, dn_1, early = call(
        middle_body, [sc, q_own, *q_z, dn_1, (dn_y, one[1]), d_own0, *d_z0, d_own1, *d_z1],
        [((112, 576), BF), (tall, BF), ((192, 768), BF)], us=1)
    q_y, q_c = swap(q_sum, 2), swap(q_sum, 1)
    q_yc = swap(q_y, 1)
    dn_c = swap(dn_1, 1)
    early_y = swap(early, 2)
    u_own, *u_z = call(
        join_near_body, [sc, u_near0, uy_near, (out_keep, near), (out_got, near), ux_got],
        [((144, 768), F32)] + [((144, 768), BF)] * 3, us=1, deps=(q_sum,))
    u_z = along_z_back(u_z)
    u_z, q_c, q_yc, q_y, dn_c, early_y = barrier((u_z, q_c, q_yc, q_y, dn_c, early_y))
    u_sum = call(total_body, [sc, u_own, *u_z], [((144, 768), BF)], us=1)[0]
    u_y = swap(u_sum, 2)
    hidden_grad = call(hidden_body, [sc, dn_0, (dn_y, one[0]), dn_c, own, vec, d_res], [(tall, F32)], us=1, deps=(u_sum,))[0]
    grad_qkv, gain, shift, bias, mid, loss = call(
        spread_qkv_body, [sc, q_sum, q_c, q_y, q_yc],
        [((96, 2304), F32), ((3, 96), F32), ((3, 96), F32), ((4, 96), F32), ((8, 384), F32), ((1, 1), F32)],
        [((4, 96, 576), BF)], us=2, deps=(hidden_grad,))
    five = call(fold_body, [sc, u_sum, u_y, early, early_y], [((432, 768), BF)], us=1, deps=(grad_qkv,))[0]
    more = swap(five, 1)
    grad_up, grad_out, grad_down = call(
        spread_body, [sc, five, more], [((96, 3072), F32), ((96, 768), F32), ((384, 768), F32)], [((4, 96, 768), F32)],
        us=2)
    return (out[None], loss[0, 0], hidden_grad[None], grad_qkv, grad_out, grad_up, grad_down,
            gain.T, shift.T, bias.T, mid[0], mid[1], mid[2])


def solution(mesh):
    step = fast if (mesh.shape["dp"], mesh.shape["ctx"]) == (8, 4) else shards
    placed = (
        P("dp", "ctx", None),
        P("dp", "ctx", None),
        P("dp"),
        P("dp", None),
        P("dp", None),
        P("dp", None),
        P("dp", None),
        P("dp", None),
        P("dp", None),
        P("dp", None),
        P("dp"),
        P("dp"),
        P("dp"),
    )
    return jax.shard_map(
        step,
        mesh=mesh,
        in_specs=placed,
        out_specs=(
            P("dp", "ctx", None),
            P(),
            P("dp", "ctx", None),
            P("dp", None),
            P("dp", None),
            P("dp", None),
            P("dp", None),
            P("dp", None),
            P("dp", None),
            P("dp", None),
            P("dp"),
            P("dp"),
            P("dp"),
        ),
        check_vma=False,
    )
```

```python
import math

import jax
import jax.numpy as jnp
from jax import lax
from jax.experimental import pallas as pl
from jax.experimental.pallas import tpu as pltpu
from jax.sharding import PartitionSpec as P

HEADS = 12
HEAD_DIM = 64


EPSILON = 1e-05
NEGATIVE = -1e30


def passed_along(value, axis, steps):
    count = lax.axis_size(axis)
    pairs = [(source, (source + steps) % count) for source in range(count)]
    return lax.ppermute(value, axis, pairs)


def passed_along_2(block, axis, distance):
    devices = range(lax.axis_size(axis))
    route = [(i - distance, i) for i in devices if i - distance in devices]
    return lax.ppermute(block, axis, route)


def layer_norm(values, gain_vec, shift_vec):
    average = jnp.mean(values, axis=-1, keepdims=True)
    centred = values - average
    variance = jnp.mean(centred * centred, axis=-1, keepdims=True)
    return centred * lax.rsqrt(variance + EPSILON) * gain_vec + shift_vec


def mid_norm(up_proj, gain_vec, shift_vec):
    return layer_norm(jax.nn.gelu(up_proj, approximate=False), gain_vec, shift_vec)


def split_heads(values):
    return values.reshape(values.shape[0], values.shape[1], HEADS, HEAD_DIM)


def key_mask(query_pos, key_start, key_count, lengths):
    key_pos = key_start + jnp.arange(key_count, dtype=jnp.int32)
    causal = key_pos[None, :] <= query_pos[:, None]
    inside = key_pos[None, :] < lengths[:, None]
    return causal[None, :, :] & inside[:, None, :]


def fold_keys(running, pieces, key_start, heads_q, query_pos, lengths):
    row_max, row_total, weighted = running
    key_piece, value_piece = pieces
    key_count = key_piece.shape[1]
    score_scale = 1.0 / math.sqrt(HEAD_DIM)
    scores = (
        jnp.einsum(
            "sqhd,skhd->shqk", heads_q, split_heads(key_piece), preferred_element_type=jnp.float32
        )
        * score_scale
    )
    allowed = key_mask(query_pos, key_start, key_count, lengths)[:, None]
    scores = jnp.where(allowed, scores, NEGATIVE)
    fresh_max = jnp.maximum(row_max, jnp.max(scores, axis=-1))
    exponent_vals = jnp.exp(scores - fresh_max[..., None])
    row_total = jnp.sum(exponent_vals, axis=-1)
    update = jnp.einsum(
        "shqk,skhd->sqhd",
        exponent_vals.astype(jnp.bfloat16),
        split_heads(value_piece),
        preferred_element_type=jnp.float32,
    )
    weighted = update
    return (fresh_max, row_total, weighted)


def grad_keys(
    heads_q, heads_do, log_total, dterm, key_piece, value_piece, key_start, query_pos, lengths
):
    seq_count, key_count = (key_piece.shape[0], key_piece.shape[1])
    heads_k = split_heads(key_piece)
    heads_v = split_heads(value_piece)
    score_scale = 1.0 / math.sqrt(HEAD_DIM)
    scores = (
        jnp.einsum("sqhd,skhd->shqk", heads_q, heads_k, preferred_element_type=jnp.float32)
        * score_scale
    )
    allowed = key_mask(query_pos, key_start, key_count, lengths)[:, None]
    probability = jnp.where(allowed, jnp.exp(scores - log_total[..., None]), 0.0)
    dprob = jnp.einsum("sqhd,skhd->shqk", heads_do, heads_v, preferred_element_type=jnp.float32)
    dscores = (probability * (dprob - dterm[..., None])).astype(jnp.bfloat16)
    dq_part = (
        jnp.einsum("shqk,skhd->sqhd", dscores, heads_k, preferred_element_type=jnp.float32)
        * score_scale
    )
    dk_part = (
        jnp.einsum("shqk,sqhd->skhd", dscores, heads_q, preferred_element_type=jnp.float32)
        * score_scale
    )
    dv_part = jnp.einsum(
        "shqk,sqhd->skhd",
        probability.astype(jnp.bfloat16),
        heads_do,
        preferred_element_type=jnp.float32,
    )
    return (
        dq_part,
        dk_part.reshape(seq_count, key_count, -1),
        dv_part.reshape(seq_count, key_count, -1),
    )


def shards(
    hidden,
    teacher,
    lengths,
    w_qkv,
    w_out,
    w_up,
    w_down,
    norm_gain,
    norm_shift,
    proj_bias,
    mid_gain,
    mid_shift,
    up_bias,
):
    (
        full_qkv,
        full_out,
        full_up,
        full_down,
        gain_full,
        shift_full,
        bias_full,
        mid_gain_full,
        mid_shift_full,
        up_bias_full,
    ) = (
        lax.all_gather(w_qkv, "dp", axis=0, tiled=True),
        lax.all_gather(w_out, "dp", axis=0, tiled=True),
        lax.all_gather(w_up, "dp", axis=0, tiled=True),
        lax.all_gather(w_down, "dp", axis=0, tiled=True),
        lax.all_gather(norm_gain, "dp", axis=0, tiled=True),
        lax.all_gather(norm_shift, "dp", axis=0, tiled=True),
        lax.all_gather(proj_bias, "dp", axis=0, tiled=True),
        lax.all_gather(mid_gain, "dp", axis=0, tiled=True),
        lax.all_gather(mid_shift, "dp", axis=0, tiled=True),
        lax.all_gather(up_bias, "dp", axis=0, tiled=True),
    )
    gain_f = gain_full.astype(jnp.float32)
    shift_f = shift_full.astype(jnp.float32)
    bias_f = bias_full.astype(jnp.float32)
    mid_gain_f = mid_gain_full.astype(jnp.float32)
    mid_shift_f = mid_shift_full.astype(jnp.float32)
    up_bias_f = up_bias_full.astype(jnp.float32)
    seq_count, local_rows, model_width = hidden.shape
    token_rows = seq_count * local_rows
    seq_shape = (seq_count, local_rows, model_width)
    ctx_place = lax.axis_index("ctx")
    ctx_parts = lax.axis_size("ctx")
    query_pos = ctx_place * local_rows + jnp.arange(local_rows, dtype=jnp.int32)
    last_query = ctx_place * local_rows + local_rows - 1
    valid_mask = (query_pos[None, :] < lengths[:, None]).astype(jnp.float32)
    valid_rows = valid_mask.reshape(token_rows, 1)
    hidden_rows = hidden.reshape(token_rows, model_width).astype(jnp.float32)
    normed, pull_in = jax.vjp(layer_norm, hidden_rows, gain_f[:, 0], shift_f[:, 0])
    normed_low = normed.astype(jnp.bfloat16)
    projected = jnp.dot(normed_low, full_qkv, preferred_element_type=jnp.float32)
    query_low = (projected[:, :model_width] + bias_f[:, 0]).astype(jnp.bfloat16).reshape(seq_shape)
    key_low = projected[:, model_width : 2 * model_width].astype(jnp.bfloat16).reshape(seq_shape)
    value_low = (
        (projected[:, 2 * model_width :] + bias_f[:, 1]).astype(jnp.bfloat16).reshape(seq_shape)
    )
    heads_q = split_heads(query_low)
    start_state = (
        jnp.full((seq_count, HEADS, local_rows), NEGATIVE, jnp.float32),
        jnp.zeros((seq_count, HEADS, local_rows), jnp.float32),
        jnp.zeros((seq_count, local_rows, HEADS, HEAD_DIM), jnp.float32),
    )
    pieces = (
        lax.all_gather(key_low, "ctx", axis=1, tiled=True),
        lax.all_gather(value_low, "ctx", axis=1, tiled=True),
    )
    key_start = jnp.int32(0)
    row_max, row_total, weighted = lax.cond(
        key_start <= last_query,
        lambda: fold_keys(start_state, pieces, key_start, heads_q, query_pos, lengths),
        lambda: start_state,
    )
    attended = weighted / jnp.transpose(row_total, (0, 2, 1))[..., None]
    log_total = row_max + jnp.log(row_total)
    attended_rows = attended.reshape(token_rows, model_width)
    mixed, pull_mix = jax.vjp(layer_norm, attended_rows, gain_f[:, 1], shift_f[:, 1])
    mixed_low = mixed.astype(jnp.bfloat16)
    residual = (
        hidden_rows
        + jnp.dot(mixed_low, full_out, preferred_element_type=jnp.float32)
        + bias_f[:, 2]
    )
    ffn_in, pull_ffn = jax.vjp(layer_norm, residual, gain_f[:, 2], shift_f[:, 2])
    ffn_low = ffn_in.astype(jnp.bfloat16)
    up_proj = jnp.dot(ffn_low, full_up, preferred_element_type=jnp.float32) + up_bias_f
    activated, pull_mid = jax.vjp(mid_norm, up_proj, mid_gain_f, mid_shift_f)
    act_low = activated.astype(jnp.bfloat16)
    result = (
        residual + jnp.dot(act_low, full_down, preferred_element_type=jnp.float32) + bias_f[:, 3]
    )
    layer_output = (result * valid_rows).astype(jnp.bfloat16).reshape(hidden.shape)
    error_rows = (
        result - teacher.reshape(token_rows, model_width).astype(jnp.float32)
    ) * valid_rows
    loss_total, valid_total = lax.psum(
        (0.5 * jnp.sum(error_rows * error_rows), jnp.sum(valid_mask)), ("dp", "ctx")
    )
    loss = loss_total / (valid_total * model_width)
    down_low = error_rows.astype(jnp.bfloat16)
    bias_down_grad = jnp.sum(down_low.astype(jnp.float32), axis=0)
    down_grad = jnp.einsum("rf,rd->fd", act_low, down_low, preferred_element_type=jnp.float32)
    d_act = jnp.einsum("rd,fd->rf", down_low, full_down, preferred_element_type=jnp.float32)
    d_up, mid_gain_grad, mid_shift_grad = pull_mid(d_act)
    up_low = d_up.astype(jnp.bfloat16)
    up_bias_grad = jnp.sum(up_low.astype(jnp.float32), axis=0)
    up_grad = jnp.einsum("rd,rf->df", ffn_low, up_low, preferred_element_type=jnp.float32)
    d_ffn = jnp.einsum("rf,df->rd", up_low, full_up, preferred_element_type=jnp.float32)
    d_res_norm, gain_two, shift_two = pull_ffn(d_ffn)
    d_residual = error_rows + d_res_norm
    branch_low = d_residual.astype(jnp.bfloat16)
    bias_out_grad = jnp.sum(branch_low.astype(jnp.float32), axis=0)
    out_grad = jnp.einsum("rd,re->de", mixed_low, branch_low, preferred_element_type=jnp.float32)
    d_mixed = jnp.einsum("re,de->rd", branch_low, full_out, preferred_element_type=jnp.float32)
    d_att, gain_one, shift_one = pull_mix(d_mixed)
    heads_do = split_heads(d_att.astype(jnp.bfloat16).reshape(seq_shape))
    dterm = jnp.einsum("sqhd,sqhd->shq", heads_do.astype(jnp.float32), attended)

    def grad_step(key_piece, value_piece, key_start):
        return grad_keys(
            heads_q,
            heads_do,
            log_total,
            dterm,
            key_piece,
            value_piece,
            key_start,
            query_pos,
            lengths,
        )

    dq_zero = jnp.zeros((seq_count, local_rows, HEADS, HEAD_DIM), jnp.float32)
    own_zero = jnp.zeros(seq_shape, jnp.float32)

    def pass_step(step_index, running):
        key_cur, value_cur, dk_run, dv_run, dq_sum = running
        owner = (ctx_place - step_index) % ctx_parts
        dq_part, dk_part, dv_part = lax.cond(
            owner <= ctx_place,
            lambda: grad_step(key_cur, value_cur, owner * local_rows),
            lambda: (dq_zero, own_zero, own_zero),
        )
        dk_run, dv_run = (
            passed_along((dk_run + dk_part).astype(jnp.bfloat16), "ctx", 1).astype(jnp.float32),
            passed_along((dv_run + dv_part).astype(jnp.bfloat16), "ctx", 1).astype(jnp.float32),
        )
        key_cur, value_cur = passed_along_2((key_cur, value_cur), "ctx", 1)
        return (key_cur, value_cur, dk_run, dv_run, dq_sum + dq_part)

    key_end, value_end, dk_own, dv_own, dq_sum = lax.fori_loop(
        0, ctx_parts, pass_step, (key_low, value_low, own_zero, own_zero, dq_zero)
    )
    dq_low = dq_sum.reshape(token_rows, model_width).astype(jnp.bfloat16)
    dk_low = dk_own.reshape(token_rows, model_width).astype(jnp.bfloat16)
    dv_low = dv_own.reshape(token_rows, model_width).astype(jnp.bfloat16)
    dqkv_low = jnp.concatenate([dq_low, dk_low, dv_low], axis=1)
    bias_q_grad = jnp.sum(dq_low.astype(jnp.float32), axis=0)
    bias_v_grad = jnp.sum(dv_low.astype(jnp.float32), axis=0)
    qkv_grad = jnp.einsum("rd,re->de", normed_low, dqkv_low, preferred_element_type=jnp.float32)
    d_normed = jnp.einsum("re,de->rd", dqkv_low, full_qkv, preferred_element_type=jnp.float32)
    d_in_norm, gain_zero, shift_zero = pull_in(d_normed)
    hidden_grad = (d_residual + d_in_norm).reshape(hidden.shape)
    gain_grad = jnp.stack([gain_zero, gain_one, gain_two], axis=1)
    shift_grad = jnp.stack([shift_zero, shift_one, shift_two], axis=1)
    bias_grad = jnp.stack([bias_q_grad, bias_v_grad, bias_out_grad, bias_down_grad], axis=1)
    shares = (
        lax.psum_scatter(
            qkv_grad.astype(jnp.bfloat16), "dp", scatter_dimension=0, tiled=True
        ).astype(jnp.float32),
        lax.psum_scatter(
            out_grad.astype(jnp.bfloat16), "dp", scatter_dimension=0, tiled=True
        ).astype(jnp.float32),
        lax.psum_scatter(
            up_grad.astype(jnp.bfloat16), "dp", scatter_dimension=0, tiled=True
        ).astype(jnp.float32),
        lax.psum_scatter(
            down_grad.astype(jnp.bfloat16), "dp", scatter_dimension=0, tiled=True
        ).astype(jnp.float32),
        lax.psum_scatter(
            gain_grad.astype(jnp.bfloat16), "dp", scatter_dimension=0, tiled=True
        ).astype(jnp.float32),
        lax.psum_scatter(
            shift_grad.astype(jnp.bfloat16), "dp", scatter_dimension=0, tiled=True
        ).astype(jnp.float32),
        lax.psum_scatter(
            bias_grad.astype(jnp.bfloat16), "dp", scatter_dimension=0, tiled=True
        ).astype(jnp.float32),
        lax.psum_scatter(
            mid_gain_grad.astype(jnp.bfloat16), "dp", scatter_dimension=0, tiled=True
        ).astype(jnp.float32),
        lax.psum_scatter(
            mid_shift_grad.astype(jnp.bfloat16), "dp", scatter_dimension=0, tiled=True
        ).astype(jnp.float32),
        lax.psum_scatter(
            up_bias_grad.astype(jnp.bfloat16), "dp", scatter_dimension=0, tiled=True
        ).astype(jnp.float32),
    )
    summed = (
        lax.psum(shares[0].astype(jnp.bfloat16), "ctx").astype(jnp.float32),
        lax.psum(shares[1].astype(jnp.bfloat16), "ctx").astype(jnp.float32),
        lax.psum(shares[2].astype(jnp.bfloat16), "ctx").astype(jnp.float32),
        lax.psum(shares[3].astype(jnp.bfloat16), "ctx").astype(jnp.float32),
        lax.psum(shares[4].astype(jnp.bfloat16), "ctx").astype(jnp.float32),
        lax.psum(shares[5].astype(jnp.bfloat16), "ctx").astype(jnp.float32),
        lax.psum(shares[6].astype(jnp.bfloat16), "ctx").astype(jnp.float32),
        lax.psum(shares[7].astype(jnp.bfloat16), "ctx").astype(jnp.float32),
        lax.psum(shares[8].astype(jnp.bfloat16), "ctx").astype(jnp.float32),
        lax.psum(shares[9].astype(jnp.bfloat16), "ctx").astype(jnp.float32),
    )
    return (
        layer_output,
        loss,
        hidden_grad,
        summed[0],
        summed[1],
        summed[2],
        summed[3],
        summed[4],
        summed[5],
        summed[6],
        summed[7],
        summed[8],
        summed[9],
    )


AXES = ("dp", "ctx")


def swap(value, mask):
    count = lax.axis_size("dp") * lax.axis_size("ctx")
    return lax.ppermute(value, AXES, [(i, i ^ mask) for i in range(count)])


def along_z(piece):
    return [swap(piece, 8 * step) for step in (1, 2, 3)]


def wide(value):
    return value.astype(jnp.float32)


def narrow(value):
    return value.astype(jnp.bfloat16)


VMEM_BYTES = 56 * 1024 * 1024


def whole(shape):
    return pl.BlockSpec(tuple(shape), lambda i: (0,) * len(shape), pipeline_mode=pl.Buffered(1))


def padded(shape, dtype):
    lead = math.prod(shape[:-2])
    size = jnp.dtype(dtype).itemsize
    rows = -(-shape[-2] // (32 // size)) * (32 // size) if len(shape) > 1 else 8
    return lead * rows * (-(-shape[-1] // 128) * 128) * size


def call(body, ins, outs, scratch=(), us=1, deps=(), room=6):
    pairs = [v if isinstance(v, tuple) else (v, whole(v.shape)) for v in ins[1:]]
    held = sum(padded(spec.block_shape, v.dtype) for v, spec in pairs)
    held += sum(padded(shape, dtype) for shape, dtype in (*outs, *scratch))
    count = len(pairs)

    def kernel(sc, *refs):
        body(sc, *refs[:count], *refs[count + len(deps):])

    return pl.pallas_call(
        kernel,
        grid=(1,),
        in_specs=[pl.BlockSpec(memory_space=pltpu.SMEM)] + [spec for _, spec in pairs]
        + [pl.BlockSpec(memory_space=pl.ANY)] * len(deps),
        out_specs=[whole(shape) for shape, _ in outs],
        out_shape=[jax.ShapeDtypeStruct(shape, dtype) for shape, dtype in outs],
        scratch_shapes=[pltpu.VMEM(shape, dtype) for shape, dtype in scratch],
        compiler_params=pltpu.CompilerParams(vmem_limit_bytes=held + room * 1024 * 1024),
        cost_estimate=pl.CostEstimate(flops=int(us * 2e7), bytes_accessed=0, transcendentals=0),
        name=body.__name__,
    )(ins[0], *[v for v, _ in pairs], *deps)


def after(value, *deps):
    return lax.optimization_barrier((value, *deps))[0]


BF, F32 = jnp.bfloat16, jnp.float32


def contract(a, b, da, db):
    return lax.dot_general(a, b, (((da,), (db,)), ((), ())), preferred_element_type=F32)


def block_of(sc, xr, zr):
    return 2 * ((sc[0] >> 1) ^ zr) + ((sc[0] & 1) ^ xr)


def slot_of(sc, block):
    return ((block & 1) ^ (sc[0] & 1)) * 4 + ((block >> 1) ^ (sc[0] >> 1))


def lay(sc, scr, near, far, rows, stride, offset=0):
    for xr, ref in ((0, near), (1, far)):
        for zr in range(4):
            at = pl.multiple_of(stride * block_of(sc, xr, zr) + offset, 16)
            scr[pl.ds(at, rows), :] = ref[zr]


def moments(value):
    average = jnp.mean(value, axis=-1, keepdims=True)
    centred = value - average
    scale = lax.rsqrt(jnp.mean(centred * centred, axis=-1, keepdims=True) + EPSILON)
    return centred * scale, scale


def norm_back(grad, hat, scale):
    return scale * (grad - jnp.mean(grad, axis=-1, keepdims=True) - hat * jnp.mean(grad * hat, axis=-1, keepdims=True))


def mine(ctx_at, row):
    out = row[:, :192]
    for j in range(1, 4):
        out = jnp.where(ctx_at == j, row[:, 192 * j:192 * j + 192], out)
    return out


def pack_body(sc, w, gain, shift, bias, out, scr):
    scr[...] = jnp.zeros((16, 128), F32)
    scr[0:3, :96] = gain[...].astype(F32)
    scr[3:6, :96] = shift[...].astype(F32)
    scr[6:10, :96] = bias[...].astype(F32)
    small = scr[...].T[:96].astype(BF)
    for j in range(4):
        @pl.when(sc[1] == j)
        def _():
            cols = [w[:, 768 * part + 192 * j:768 * part + 192 * j + 192] for part in range(3)]
            out[...] = jnp.concatenate(cols + [small, jnp.zeros((96, 48), BF)], axis=1)


def attend_body(sc, h0, h1, h2, h3, wa, wb, a0, a1, a23, q_o, k_o, v_o, lse_o, ot_o, n_o, vec_o, w_scr):
    ctx_at, length = sc[1], sc[2]
    lay(sc, w_scr, wa, wb, 96, 96)
    vec = w_scr[:, 512:640].astype(F32).T[64:80]
    vec_o[...] = vec
    bias_q, bias_v = mine(ctx_at, vec[6:7]), mine(ctx_at, vec[7:8])
    for r, ref in enumerate((h0, h1, h2, h3)):
        rows = pl.ds(pl.multiple_of((ctx_at ^ r) * 256, 256), 256)
        hat, _ = moments(ref[...].astype(F32))
        normed = (hat * vec[0:1] + vec[3:4]).astype(BF)
        n_o[rows, :] = normed
        p = jnp.dot(normed, w_scr[...], preferred_element_type=F32)
        for h in range(3):
            q_o[h, rows, :] = ((p[:, 64 * h:64 * h + 64] + bias_q[:, 64 * h:64 * h + 64]) * 0.125).astype(BF)
            k_o[h, rows, :] = p[:, 192 + 64 * h:256 + 64 * h].astype(BF)
            v_o[h, rows, :] = (p[:, 384 + 64 * h:448 + 64 * h] + bias_v[:, 64 * h:64 * h + 64]).astype(BF)

    def head(h, carry):
        for i in range(4):
            n = 256 * (i + 1)
            scores = contract(k_o[h, :n, :], q_o[h, 256 * i:256 * i + 256, :], 1, 1)
            limit = jnp.minimum(256 * i + lax.broadcasted_iota(jnp.int32, (1, 256), 1), length - 1)
            scores = jnp.where(lax.broadcasted_iota(jnp.int32, (n, 256), 0) <= limit, scores, NEGATIVE)
            top = jnp.max(scores, axis=0, keepdims=True)
            grown = jnp.exp(scores - top)
            total = jnp.sum(grown, axis=0, keepdims=True)
            out = contract(v_o[h, :n, :], grown.astype(BF), 0, 0) / total
            ot_o[i, pl.ds(pl.multiple_of(64 * h, 64), 64), :] = out
            lse_o[h, i:i + 1, :] = top + jnp.log(total)
        return carry

    lax.fori_loop(0, 3, head, 0)
    for r, ref in enumerate((a0, a1, a23.at[0], a23.at[1])):
        ref[...] = ot_o[ctx_at ^ r].T.astype(BF)


def attend(sc, hids, wa, wb, deps):
    rows = (256, 192)
    return call(
        attend_body, [sc, *hids, wa, wb],
        [(rows, BF)] * 2 + [((2, 256, 192), BF)] + [((3, 1024, 64), BF)] * 3
        + [((3, 8, 256), F32), ((4, 192, 256), F32), ((1024, 768), BF), ((16, 768), F32)],
        [((768, 640), BF)], us=13, deps=deps)


def attend_back_body(sc, d0, d1, d2, d3, q_i, k_i, v_i, lse_i, ot_i, n_i, h0, h1, h2, h3, wa, wb, vec_i, side_e, side_d, mids,
                     n0, n1, n23, keep, send, w_scr, do_scr, dq_s, dk_s, dv_s, dk_acc, dv_acc, all_scr, g_scr):
    ctx_at, length = sc[1], sc[2]
    lay(sc, w_scr, wa, wb, 96, 96)
    for r, ref in enumerate((d0, d1, d2, d3)):
        rows = pl.ds(pl.multiple_of((ctx_at ^ r) * 256, 256), 256)
        value = ref[...]
        for h in range(3):
            do_scr[h, rows, :] = value[:, 64 * h:64 * h + 64]

    def head(h, carry):
        for i in (3, 2, 1, 0):
            n = 256 * (i + 1)
            mine_rows = slice(256 * i, 256 * i + 256)
            q, do, k = q_i[h, mine_rows, :], do_scr[h, mine_rows, :], k_i[h, :n, :]
            out = ot_i[i, pl.ds(pl.multiple_of(64 * h, 64), 64), :]
            dterm = jnp.sum(do.astype(F32).T * out, axis=0, keepdims=True)
            limit = jnp.minimum(256 * i + lax.broadcasted_iota(jnp.int32, (1, 256), 1), length - 1)
            prob = jnp.exp(contract(k, q, 1, 1) - lse_i[h, i:i + 1, :])
            prob = jnp.where(lax.broadcasted_iota(jnp.int32, (n, 256), 0) <= limit, prob, 0.0)
            dscore = (prob * (contract(v_i[h, :n, :], do, 1, 1) - dterm)).astype(BF)
            dv = jnp.dot(prob.astype(BF), do, preferred_element_type=F32)
            dk = jnp.dot(dscore, q, preferred_element_type=F32)
            if i == 3:
                dv_acc[...] = dv
                dk_acc[...] = dk
            else:
                dv_acc[:n, :] += dv
                dk_acc[:n, :] += dk
            dq_s[h, mine_rows, :] = (contract(k, dscore, 0, 0) * 0.125).T.astype(BF)
        dk_s[h] = dk_acc[...].astype(BF)
        dv_s[h] = dv_acc[...].astype(BF)
        return carry

    lax.fori_loop(0, 3, head, 0)
    for i in range(4):
        rows = slice(256 * i, 256 * i + 256)
        all_scr[rows, :] = jnp.concatenate([s[h, rows, :] for s in (dq_s, dk_s, dv_s) for h in range(3)], axis=1)
    sums = jnp.sum(all_scr[...].astype(F32), axis=0, keepdims=True)
    bias_q = jnp.concatenate([jnp.where(ctx_at == j, sums[:, :192], 0.0) for j in range(4)], axis=1)
    bias_v = jnp.concatenate([jnp.where(ctx_at == j, sums[:, 384:], 0.0) for j in range(4)], axis=1)
    gain_sum, shift_sum = jnp.zeros((1, 768), F32), jnp.zeros((1, 768), F32)
    for r, (ref, out) in enumerate(((h0, n0), (h1, n1), (h2, n23.at[0]), (h3, n23.at[1]))):
        rows = pl.ds(pl.multiple_of((ctx_at ^ r) * 256, 256), 256)
        grad = contract(all_scr[rows, :], w_scr[:, :576], 1, 1)
        hat, _ = moments(ref[...].astype(F32))
        gain_sum += jnp.sum(grad * hat, axis=0, keepdims=True)
        shift_sum += jnp.sum(grad, axis=0, keepdims=True)
        out[...] = grad.astype(BF)
    rows16 = jnp.concatenate(
        [gain_sum, side_e[0:2], shift_sum, side_e[2:4], bias_q, bias_v, side_e[4:5], side_d[0:2], jnp.zeros((5, 768), F32)], axis=0)
    w_grad = contract(n_i[...], all_scr[...], 0, 0)
    for b in range(8):
        at = slot_of(sc, b)
        extra = jnp.concatenate([mids[:, 384 * b:384 * b + 384], rows16[:, 96 * b:96 * b + 96], jnp.zeros((16, 96), F32)], axis=1)
        g_scr[at, :96, :] = w_grad[96 * b:96 * b + 96].astype(BF)
        g_scr[at, 96:112, :] = extra.astype(BF)
    keep[...] = g_scr[:4]
    send[...] = g_scr[4:]


def attend_back(sc, douts, saved, hids, wa, wb, side_e, side_d, mids, deps):
    q, k, v, lse, ot, normed, vec = saved
    return call(
        attend_back_body, [sc, *douts, q, k, v, lse, ot, normed, *hids, wa, wb, vec, side_e, side_d, mids],
        [((256, 768), BF)] * 2 + [((2, 256, 768), BF)] + [((4, 112, 576), BF)] * 2,
        [((768, 640), BF), ((3, 1024, 64), BF), ((3, 1024, 64), BF), ((3, 1024, 64), BF), ((3, 1024, 64), BF),
         ((1024, 64), F32), ((1024, 64), F32), ((1024, 576), BF), ((8, 112, 576), BF)],
        us=12, deps=deps)


def part(rows, at):
    return pl.BlockSpec((4, rows, 768), lambda i: (0, at, 0), pipeline_mode=pl.Buffered(1))


def lay_out(sc, scr, own_near, own_far, other_near, other_far):
    core = sc[1] & 1
    lay(sc, scr, own_near, own_far, 48, 96, 48 * core)
    lay(sc, scr, other_near, other_far, 48, 96, 48 * (1 - core))


def lay_down(sc, scr, refs):
    for c in (0, 1):
        for xr in (0, 1):
            for y in (0, 1):
                lay_one(sc, scr, refs[4 * c + 2 * xr + y], xr, 96 * (sc[1] ^ (2 * y + c)))


def lay_one(sc, scr, ref, xr, offset):
    for zr in range(4):
        scr[pl.ds(pl.multiple_of(384 * block_of(sc, xr, zr) + offset, 32), 96), :] = ref[zr]


def join_heads(sc, scr, pieces):
    own, near, far = pieces
    for r, value in enumerate((own[...], near[0], far[0], near[1])):
        scr[r] = value
    return jnp.concatenate([scr[sc[1] ^ j] for j in range(4)], axis=1).astype(F32)


def mid_body(sc, g0, g1, g2, own, vec, on, of, tn, tf, mixed_o, resid_o, ffn_o, w_scr, a_scr):
    lay_out(sc, w_scr, on, of, tn, tf)
    hat, _ = moments(join_heads(sc, a_scr, (g0, g1, g2)))
    mixed = (hat * vec[1:2] + vec[4:5]).astype(BF)
    mixed_o[...] = mixed
    resid = own[...].astype(F32) + jnp.dot(mixed, w_scr[...], preferred_element_type=F32) + vec[8:9]
    resid_o[...] = resid
    hat, _ = moments(resid)
    ffn_o[...] = (hat * vec[2:3] + vec[5:6]).astype(BF)


def up_body(sc, ffn, w0n, w0f, w1n, w1f, w2n, w2f, w3n, w3f, mn, mf, act_o, hat_o, slope_o, scale_o, nat_o,
            w_scr, g_scr, m_scr):
    for xr, ref in ((0, mn), (1, mf)):
        for zr in range(4):
            m_scr[block_of(sc, xr, zr)] = ref[zr].astype(F32)
    flat = [m_scr[b] for b in range(8)]
    for j in range(4):
        two = flat[2 * j:2 * j + 2]
        nat_o[j, 0:1, :] = jnp.concatenate([m[0:1, :384] for m in two], axis=1)
        nat_o[j, 1:2, :] = jnp.concatenate([m[0:1, 384:] for m in two], axis=1)
        nat_o[j, 2:3, :] = jnp.concatenate([m[1:2, :384] for m in two], axis=1)
        nat_o[j, 3:8, :] = jnp.zeros((5, 768), F32)
    value = ffn[...]
    total = jnp.zeros((256, 1), F32)
    for t, (near, far) in enumerate(((w0n, w0f), (w1n, w1f), (w2n, w2f), (w3n, w3f))):
        j = sc[1] ^ t
        lay(sc, w_scr.at[t], near, far, 96, 96)
        up = jnp.dot(value, w_scr[t], preferred_element_type=F32) + nat_o[j, 2:3, :]
        chance = 0.5 * (1.0 + lax.erf(up * math.sqrt(0.5)))
        slope_o[j] = (chance + up * jnp.exp(-0.5 * up * up) * (1.0 / math.sqrt(2.0 * math.pi))).astype(BF)
        gelu = up * chance
        g_scr[j] = gelu
        total += jnp.sum(gelu, axis=-1, keepdims=True)
    average = total * (1.0 / 3072)
    square = jnp.zeros((256, 1), F32)
    for j in range(4):
        centred = g_scr[j] - average
        square += jnp.sum(centred * centred, axis=-1, keepdims=True)
    scale = lax.rsqrt(square * (1.0 / 3072) + EPSILON)
    scale_o[...] = scale
    for j in range(4):
        hat = (g_scr[j] - average) * scale
        hat_o[j] = hat.astype(BF)
        act_o[j] = (hat * nat_o[j, 0:1, :] + nat_o[j, 1:2, :]).astype(BF)


def down_body(sc, act, resid, teacher, vec, e0, e1, e2, e3, e4, e5, e6, e7, out_o, err_o, low_o, side_o, w_scr):
    lay_down(sc, w_scr, (e0, e1, e2, e3, e4, e5, e6, e7))
    result = resid[...] + vec[9:10]
    for j in range(4):
        result += jnp.dot(act[j], w_scr[768 * j:768 * j + 768, :], preferred_element_type=F32)
    pos = sc[1] * 256 + lax.broadcasted_iota(jnp.int32, (256, 1), 0)
    valid = jnp.where(pos < sc[2], 1.0, 0.0)
    out_o[...] = (result * valid).astype(BF)
    error = (result - teacher[...].astype(F32)) * valid
    err_o[...] = error
    low = error.astype(BF)
    low_o[...] = low
    side_o[0:1, :] = jnp.sum(low.astype(F32), axis=0, keepdims=True)
    loss = 0.5 * jnp.sum(jnp.sum(error * error, axis=0, keepdims=True), axis=1, keepdims=True)
    count = jnp.sum(valid, axis=0, keepdims=True)
    high = loss.astype(BF).astype(F32)
    lane = lax.broadcasted_iota(jnp.int32, (1, 768), 1) % 96
    side_o[1:2, :] = jnp.where(lane == 0, high, jnp.where(lane == 1, loss - high, jnp.where(lane == 2, count, 0.0)))
    side_o[2:8, :] = jnp.zeros((6, 768), F32)


def down_grad_body(sc, act, low, keep, send, g_scr):
    value = low[...]
    for j in range(4):
        grad = contract(act[j], value, 0, 0).astype(BF)
        for half in (0, 1):
            at = slot_of(sc, 2 * j + half)
            for q in range(4):
                g_scr[sc[1] ^ q, at] = grad[384 * half + 96 * q:384 * half + 96 * q + 96]
    for y in (0, 1):
        keep[y] = g_scr[2 * y]
        send[y] = g_scr[2 * y + 1]


def act_back_body(sc, low, hat_i, slope, scale, nat, e0, e1, e2, e3, e4, e5, e6, e7, up_o, mids_o, wd_scr, dh_scr):
    lay_down(sc, wd_scr, (e0, e1, e2, e3, e4, e5, e6, e7))
    value = low[...]
    first, second = jnp.zeros((256, 1), F32), jnp.zeros((256, 1), F32)
    for j in range(4):
        grad = contract(value, wd_scr[768 * j:768 * j + 768, :], 1, 1)
        hat = hat_i[j].astype(F32)
        cols = slice(768 * j, 768 * j + 768)
        mids_o[0:1, cols] = jnp.sum(grad * hat, axis=0, keepdims=True)
        mids_o[1:2, cols] = jnp.sum(grad, axis=0, keepdims=True)
        grad = grad * nat[j, 0:1, :]
        dh_scr[j] = grad
        first += jnp.sum(grad, axis=-1, keepdims=True)
        second += jnp.sum(grad * hat, axis=-1, keepdims=True)
    first, second = first * (1.0 / 3072), second * (1.0 / 3072)
    for j in range(4):
        hat = hat_i[j].astype(F32)
        grad = (scale[...] * (dh_scr[j] - first - hat * second) * slope[j].astype(F32)).astype(BF)
        up_o[j] = grad
        mids_o[2:3, 768 * j:768 * j + 768] = jnp.sum(grad.astype(F32), axis=0, keepdims=True)
    mids_o[3:16, :] = jnp.zeros((13, 3072), F32)


def ffn_back_body(sc, up_i, err, resid, w0n, w0f, w1n, w1f, w2n, w2f, w3n, w3f, on, of, tn, tf, vec, g0, g1, g2,
                  branch_o, dres_o, p0, p1, p2, p3, side_o, w_scr, o_scr, a_scr, b_scr):
    grad = jnp.zeros((256, 768), F32)
    for t, (near, far) in enumerate(((w0n, w0f), (w1n, w1f), (w2n, w2f), (w3n, w3f))):
        lay(sc, w_scr.at[t], near, far, 96, 96)
        grad += contract(up_i[sc[1] ^ t], w_scr[t], 1, 1)
    hat, factor = moments(resid[...])
    side_o[1:2, :] = jnp.sum(grad * hat, axis=0, keepdims=True)
    side_o[3:4, :] = jnp.sum(grad, axis=0, keepdims=True)
    dres = err[...] + norm_back(grad * vec[2:3], hat, factor)
    dres_o[...] = dres
    branch = dres.astype(BF)
    branch_o[...] = branch
    side_o[4:5, :] = jnp.sum(branch.astype(F32), axis=0, keepdims=True)
    lay_out(sc, o_scr, on, of, tn, tf)
    grad = contract(branch, o_scr[...], 1, 1)
    hat, factor = moments(join_heads(sc, a_scr, (g0, g1, g2)))
    side_o[0:1, :] = jnp.sum(grad * hat, axis=0, keepdims=True)
    side_o[2:3, :] = jnp.sum(grad, axis=0, keepdims=True)
    side_o[5:8, :] = jnp.zeros((3, 768), F32)
    grad = norm_back(grad * vec[1:2], hat, factor).astype(BF)
    for j in range(4):
        b_scr[j] = grad[:, 192 * j:192 * j + 192]
    for r, ref in enumerate((p0, p1, p2, p3)):
        ref[...] = b_scr[sc[1] ^ r]


def up_grad_body(sc, ffn, up, keep, send, g_scr):
    value = ffn[...]
    for j in range(4):
        grad = contract(value, up[j], 0, 0).astype(BF)
        for b in range(8):
            g_scr[sc[1] ^ j, slot_of(sc, b)] = grad[96 * b:96 * b + 96]
    for y in (0, 1):
        keep[y] = g_scr[2 * y]
        send[y] = g_scr[2 * y + 1]


def out_grad_body(sc, mixed, branch, out_keep, out_send, o_scr):
    grad = contract(mixed[...], branch[...], 0, 0).astype(BF)
    for b in range(8):
        for c in (0, 1):
            o_scr[(sc[1] & 1) ^ c, slot_of(sc, b)] = grad[96 * b + 48 * c:96 * b + 48 * c + 48]
    out_keep[...] = o_scr[0]
    out_send[...] = o_scr[1]


def added(a, b):
    return a.astype(F32) + b.astype(F32)


def pair_body(sc, keep, got, near0, near1, far0, far1):
    for y, near, far in ((0, near0, far0), (1, near1, far1)):
        near[...] = added(keep[y, :4], got[y, :4]).astype(BF)
        far[...] = added(keep[y, 4:], got[y, 4:]).astype(BF)


def slots_body(sc, near, got, own, s1, s2, s3):
    own[...] = added(near[0], got[0])
    for at, out in ((1, s1), (2, s2), (3, s3)):
        out[...] = added(near[at], got[at]).astype(BF)


def join_far_body(sc, mine, got, out_keep, out_got, far):
    far[:, :96, :] = added(mine[...], got[...]).astype(BF)
    far[:, 96:, :] = added(out_keep[...], out_got[...]).astype(BF)


def join_near_body(sc, mine, y_got, out_keep, out_got, x_got, own, s1, s2, s3):
    for at, out in ((0, own), (1, s1), (2, s2), (3, s3)):
        kind = out.dtype
        out[:96, :] = (added(mine[at], y_got[at]) + x_got[at, :96, :].astype(F32)).astype(kind)
        out[96:, :] = (added(out_keep[at], out_got[at]) + x_got[at, 96:, :].astype(F32)).astype(kind)


def total_of(own, parts):
    return (own[...] + sum(p[...].astype(F32) for p in parts)).astype(BF)


def middle_body(sc, q0, q1, q2, q3, dn, got, d0, d1, d2, d3, e0, e1, e2, e3, q_o, dn_o, early_o):
    q_o[...] = total_of(q0, (q1, q2, q3))
    dn_o[...] = added(dn[...], got[0]).astype(BF)
    early_o[0:96, :] = total_of(d0, (d1, d2, d3))
    early_o[96:192, :] = total_of(e0, (e1, e2, e3))


def fold_body(sc, own, other, early, early_got, out):
    out[0:96, :] = own[0:96, :]
    out[96:192, :] = other[0:96, :]
    out[192:240, :] = added(own[96:144, :], other[96:144, :]).astype(BF)
    out[240:336, :] = added(early[0:96, :], early_got[96:192, :]).astype(BF)
    out[336:432, :] = added(early[96:192, :], early_got[0:96, :]).astype(BF)


def spread_body(sc, mine, other, up_o, out_o, down_o, scr):
    core = sc[1] & 1
    for t, (ref, at) in enumerate(((mine, 0), (other, 0), (mine, 96), (other, 96))):
        scr[sc[1] ^ t] = ref[at:at + 96, :].astype(F32)
        rows = pl.multiple_of(96 * (sc[1] ^ t), 32)
        down_o[pl.ds(rows, 96), :] = ref[240 + at:336 + at, :].astype(F32)
    for j in range(4):
        up_o[:, 768 * j:768 * j + 768] = scr[j]
    out_o[pl.ds(pl.multiple_of(48 * core, 16), 48), :] = mine[192:240, :].astype(F32)
    out_o[pl.ds(pl.multiple_of(48 * (1 - core), 16), 48), :] = other[192:240, :].astype(F32)


def spread_qkv_body(sc, t0, t1, t2, t3, grad_o, gain_o, shift_o, bias_o, mid_o, loss_o, scr):
    rest = jnp.zeros((16, 576), F32)
    for r, ref in enumerate((t0, t1, t2, t3)):
        scr[sc[1] ^ r] = ref[:96, :]
        rest += ref[96:112, :].astype(F32)
    for p in range(3):
        cols = [scr[j, :, 192 * p:192 * p + 192] for j in range(4)]
        grad_o[:, 768 * p:768 * p + 768] = jnp.concatenate(cols, axis=1).astype(F32)
    gain_o[...] = rest[0:3, 384:480]
    shift_o[...] = rest[3:6, 384:480]
    bias_o[...] = rest[6:10, 384:480]
    mid_o[...] = rest[0:8, :384]
    row = rest[10:11, 384:480]
    lane = lax.broadcasted_iota(jnp.int32, (1, 96), 1)
    error = jnp.sum(jnp.where(lane < 2, row, 0.0), axis=1, keepdims=True)
    count = jnp.sum(jnp.where(lane == 2, row, 0.0), axis=1, keepdims=True)
    loss_o[...] = error / (count * 768.0)


def hidden_body(sc, a, b, c, own, vec, d_res, out, mark):
    mark[...] = jnp.zeros((8, 128), F32)
    grad = (added(a[...], b[0]) + c[...].astype(F32)) * vec[0:1]
    hat, factor = moments(own[...].astype(F32))
    out[...] = d_res[...] + norm_back(grad, hat, factor)


def total_body(sc, own, s1, s2, s3, out):
    out[...] = total_of(own, (s1, s2, s3))


def fast(
    hidden, teacher, lengths, w_qkv, w_out, w_up, w_down, norm_gain, norm_shift, proj_bias,
    mid_gain, mid_shift, up_bias,
):
    dp_at, ctx_at = lax.axis_index("dp"), lax.axis_index("ctx")
    core = ctx_at & 1
    sc = jnp.stack([dp_at, ctx_at, lengths[0]]).astype(jnp.int32)
    own = hidden[0]
    tall = (256, 768)
    barrier = lax.optimization_barrier
    h_y, h_c = swap(own, 2), swap(own, 1)
    piece = call(pack_body, [sc, w_qkv, norm_gain.T, norm_shift.T, proj_bias.T], [((96, 640), BF)], [((16, 128), F32)], room=54)[0]
    q_cols = along_z(piece)
    mid_rows = jnp.concatenate([mid_gain, mid_shift, up_bias, jnp.zeros((13 * 384,), BF)]).reshape(8, 768)
    piece_a = jnp.concatenate([
        lax.dynamic_slice(w_up, (0, 768 * ctx_at), (96, 768)), lax.dynamic_slice(w_out, (48 * core, 0), (48, 768)), mid_rows])
    down4 = w_down.reshape(4, 96, 768)
    piece_b, piece_c = (lax.dynamic_index_in_dim(down4, ctx_at ^ t, 0, keepdims=False) for t in (0, 2))
    q_cols, piece_a = barrier((q_cols, piece_a))
    q_near = jnp.stack([piece] + q_cols)
    q_far = swap(q_near, 4)
    h_yc = swap(h_y, 1)
    a_cols = along_z(piece_a)
    a_cols, q_far, piece_b, h_c, h_yc = barrier((a_cols, q_far, piece_b, h_c, h_yc))
    a_near = jnp.stack([piece_a] + a_cols)
    a_far = swap(a_near, 4)
    y_near = swap(a_near[:, :96], 2)
    a_near_o = swap(a_near, 1)
    b_cols = along_z(piece_b)
    hids = [own, h_c, h_y, h_yc]
    att_0, att_1, att_23, q, k, v, lse, ot, normed, vec = attend(sc, hids, q_near, q_far, (a_near,))
    y_near, b_cols, piece_c, att_23, att_1 = barrier((y_near, b_cols, piece_c, att_23, att_1))
    c_cols = along_z(piece_c)
    att_y = swap(att_23, 2)
    b_near = jnp.stack([piece_b] + b_cols)
    a_far, b_near, att_y = barrier((a_far, b_near, att_y))
    b_far = swap(b_near, 4)
    y_far = swap(a_far[:, :96], 2)
    c_near = jnp.stack([piece_c] + c_cols)
    c_near, b_far, y_far, a_near, a_far, y_near, b_near, att_1 = barrier(
        (c_near, b_far, y_far, a_near, a_far, y_near, b_near, att_1))
    c_far = swap(b_far, 2)
    att_c = swap(jnp.stack([att_1, att_y[1]]), 1)
    a_near_o, a_far_o, y_near_o, y_far_o = (swap(t, 1) for t in (a_near, a_far, y_near, y_far))
    b_near_o, b_far_o, c_near_o = (swap(t, 1) for t in (b_near, b_far, c_near))
    got = [att_0, att_c, att_y]
    outs = [(t, part(48, 2)) for t in (a_near, a_far, a_near_o, a_far_o)]
    mixed, resid, ffn = call(
        mid_body, [sc, *got, own, vec, *outs], [(tall, BF), (tall, F32), (tall, BF)],
        [((768, 768), BF), ((4, 256, 192), BF)], us=3)
    ups = [(t, part(96, 0)) for t in (a_near, a_far, a_near_o, a_far_o)] + [y_near, y_far, y_near_o, y_far_o]
    four = (4, 256, 768)
    act, hat, slope, scale, nat = call(
        up_body, [sc, ffn, *ups] + [(t, part(8, 18)) for t in (a_near, a_far)],
        [(four, BF), (four, BF), (four, BF), ((256, 1), F32), ((4, 8, 768), F32)],
        [((4, 768, 768), BF), (four, F32), ((8, 8, 768), F32)], us=5)
    c_far, act = barrier((c_far, act))
    c_far_o = swap(c_far, 1)
    downs = [b_near, c_near, b_far, c_far, b_near_o, c_near_o, b_far_o, c_far_o]
    out, err, low, side_d = call(
        down_body, [sc, act, resid, teacher[0], vec, *downs],
        [(tall, BF), (tall, F32), (tall, BF), ((8, 768), F32)], [((3072, 768), BF)], us=5)
    halves_of = ((2, 8, 96, 768), BF)
    down_keep, down_send = call(
        down_grad_body, [sc, act, low], [halves_of] * 2, [((4, 8, 96, 768), BF)], us=3)
    down_got = swap(down_send, 1)
    up_low, mids = call(
        act_back_body, [sc, low, hat, slope, scale, nat, *downs], [(four, BF), ((16, 3072), F32)],
        [((3072, 768), BF), (four, F32)], us=5, deps=(down_keep,))
    slots = ((4, 96, 768), BF)
    d_near0, d_near1, d_far0, d_far1 = call(pair_body, [sc, down_keep, down_got], [slots] * 4, us=2, deps=(mids,))
    d_far0, up_low = barrier((d_far0, up_low))
    d_got0 = swap(d_far0, 4)
    up_keep, up_send = call(up_grad_body, [sc, ffn, up_low], [halves_of] * 2, [((4, 8, 96, 768), BF)], us=3, deps=(d_near0,))
    up_got = swap(up_send, 1)
    branch, d_res, *d_att, side_e = call(
        ffn_back_body, [sc, up_low, err, resid, *ups, *outs, vec, *got],
        [(tall, BF), (tall, F32)] + [((256, 192), BF)] * 4 + [((8, 768), F32)],
        [((4, 768, 768), BF), ((768, 768), BF), ((4, 256, 192), BF), ((4, 256, 192), BF)], us=6, deps=(up_keep,))
    u_near0, u_near1, u_far0, u_far1 = call(pair_body, [sc, up_keep, up_got], [slots] * 4, us=2, deps=(side_e,))
    d_got = [d_att[0]] + [swap(d_att[r], r) for r in (1, 2, 3)]
    out_keep, out_send = call(
        out_grad_body, [sc, mixed, branch], [((8, 48, 768), BF)] * 2, [((2, 8, 48, 768), BF)], us=1, deps=(u_near0,))
    out_got = swap(out_send, 1)
    own_part, sent = ((96, 768), F32), ((96, 768), BF)
    d_own0, *d_z0 = call(slots_body, [sc, d_near0, d_got0], [own_part] + [sent] * 3, us=1, deps=(out_keep,))

    def along_z_back(parts):
        return [swap(parts[step - 1], 8 * step) for step in (3, 2, 1)]

    d_z0, d_far1, u_far1, d_got, out_got = barrier((d_z0, d_far1, u_far1, d_got, out_got))
    d_z0 = along_z_back(d_z0)
    d_got1 = swap(d_far1, 4)
    uy_far = swap(u_far1, 2)
    dn_0, dn_1, dn_23, q_keep, q_send = attend_back(
        sc, d_got, (q, k, v, lse, ot, normed, vec), hids, q_near, q_far, side_e, side_d, mids, (d_own0, out_got))
    d_z0, d_got1, uy_far, u_near1, dn_0, dn_1, dn_23, q_keep, q_send = barrier(
        (d_z0, d_got1, uy_far, u_near1, dn_0, dn_1, dn_23, q_keep, q_send))
    near, far = (pl.BlockSpec((4, 48, 768), lambda i, at=at: (at, 0, 0), pipeline_mode=pl.Buffered(1)) for at in (0, 1))
    q_got = swap(q_send, 4)
    uy_near = swap(u_near1, 2)
    d_own1, *d_z1 = call(slots_body, [sc, d_near1, d_got1], [own_part] + [sent] * 3, us=1)
    d_z1 = along_z_back(d_z1)
    q_got, uy_far, d_own1 = barrier((q_got, uy_far, d_own1))
    u_x = call(join_far_body, [sc, u_far0, uy_far, (out_keep, far), (out_got, far)], [((4, 144, 768), BF)], us=1)[0]
    ux_got = swap(u_x, 4)
    d_z1, uy_near, dn_23, q_keep = barrier((d_z1, uy_near, dn_23, q_keep))
    q_own, *q_z = call(slots_body, [sc, q_keep, q_got], [((112, 576), F32)] + [((112, 576), BF)] * 3, us=1, deps=(u_x,))
    q_z = along_z_back(q_z)
    dn_y = swap(dn_23, 2)
    q_z, dn_y, d_own0 = barrier((q_z, dn_y, d_own0))
    one = [pl.BlockSpec((1, 256, 768), lambda i, at=at: (at, 0, 0), pipeline_mode=pl.Buffered(1)) for at in (0, 1)]
    q_sum, dn_1, early = call(
        middle_body, [sc, q_own, *q_z, dn_1, (dn_y, one[1]), d_own0, *d_z0, d_own1, *d_z1],
        [((112, 576), BF), (tall, BF), ((192, 768), BF)], us=1)
    q_y, q_c = swap(q_sum, 2), swap(q_sum, 1)
    q_yc = swap(q_y, 1)
    dn_c = swap(dn_1, 1)
    early_y = swap(early, 2)
    u_own, *u_z = call(
        join_near_body, [sc, u_near0, uy_near, (out_keep, near), (out_got, near), ux_got],
        [((144, 768), F32)] + [((144, 768), BF)] * 3, us=1, deps=(q_sum,))
    u_z = along_z_back(u_z)
    u_z, q_c, q_yc, q_y, dn_c, early_y = barrier((u_z, q_c, q_yc, q_y, dn_c, early_y))
    u_sum = call(total_body, [sc, u_own, *u_z], [((144, 768), BF)], us=1)[0]
    u_y = swap(u_sum, 2)
    hidden_grad, mark = call(hidden_body, [sc, dn_0, (dn_y, one[0]), dn_c, own, vec, d_res], [(tall, F32), ((8, 128), F32)], us=1, deps=(u_sum,))
    grad_qkv, gain, shift, bias, mid, loss = call(
        spread_qkv_body, [sc, q_sum, q_c, q_y, q_yc],
        [((96, 2304), F32), ((3, 96), F32), ((3, 96), F32), ((4, 96), F32), ((8, 384), F32), ((1, 1), F32)],
        [((4, 96, 576), BF)], us=2, deps=(mark,))
    five = call(fold_body, [sc, u_sum, u_y, early, early_y], [((432, 768), BF)], us=1, deps=(loss,))[0]
    more = swap(five, 1)
    grad_up, grad_out, grad_down = call(
        spread_body, [sc, five, more], [((96, 3072), F32), ((96, 768), F32), ((384, 768), F32)], [((4, 96, 768), F32)],
        us=2)
    return (out[None], loss[0, 0], hidden_grad[None], grad_qkv, grad_out, grad_up, grad_down,
            gain.T, shift.T, bias.T, mid[0], mid[1], mid[2])


def solution(mesh):
    step = fast if (mesh.shape["dp"], mesh.shape["ctx"]) == (8, 4) else shards
    placed = (
        P("dp", "ctx", None),
        P("dp", "ctx", None),
        P("dp"),
        P("dp", None),
        P("dp", None),
        P("dp", None),
        P("dp", None),
        P("dp", None),
        P("dp", None),
        P("dp", None),
        P("dp"),
        P("dp"),
        P("dp"),
    )
    return jax.shard_map(
        step,
        mesh=mesh,
        in_specs=placed,
        out_specs=(
            P("dp", "ctx", None),
            P(),
            P("dp", "ctx", None),
            P("dp", None),
            P("dp", None),
            P("dp", None),
            P("dp", None),
            P("dp", None),
            P("dp", None),
            P("dp", None),
            P("dp"),
            P("dp"),
            P("dp"),
        ),
        check_vma=False,
    )
```

```python
import math

import jax
import jax.numpy as jnp
from jax import lax
from jax.experimental import pallas as pl
from jax.experimental.pallas import tpu as pltpu
from jax.sharding import PartitionSpec as P

HEADS = 12
HEAD_DIM = 64


EPSILON = 1e-05
NEGATIVE = -1e30


def passed_along(value, axis, steps):
    count = lax.axis_size(axis)
    pairs = [(source, (source + steps) % count) for source in range(count)]
    return lax.ppermute(value, axis, pairs)


def passed_along_2(block, axis, distance):
    devices = range(lax.axis_size(axis))
    route = [(i - distance, i) for i in devices if i - distance in devices]
    return lax.ppermute(block, axis, route)


def layer_norm(values, gain_vec, shift_vec):
    average = jnp.mean(values, axis=-1, keepdims=True)
    centred = values - average
    variance = jnp.mean(centred * centred, axis=-1, keepdims=True)
    return centred * lax.rsqrt(variance + EPSILON) * gain_vec + shift_vec


def mid_norm(up_proj, gain_vec, shift_vec):
    return layer_norm(jax.nn.gelu(up_proj, approximate=False), gain_vec, shift_vec)


def split_heads(values):
    return values.reshape(values.shape[0], values.shape[1], HEADS, HEAD_DIM)


def key_mask(query_pos, key_start, key_count, lengths):
    key_pos = key_start + jnp.arange(key_count, dtype=jnp.int32)
    causal = key_pos[None, :] <= query_pos[:, None]
    inside = key_pos[None, :] < lengths[:, None]
    return causal[None, :, :] & inside[:, None, :]


def fold_keys(running, pieces, key_start, heads_q, query_pos, lengths):
    row_max, row_total, weighted = running
    key_piece, value_piece = pieces
    key_count = key_piece.shape[1]
    score_scale = 1.0 / math.sqrt(HEAD_DIM)
    scores = (
        jnp.einsum(
            "sqhd,skhd->shqk", heads_q, split_heads(key_piece), preferred_element_type=jnp.float32
        )
        * score_scale
    )
    allowed = key_mask(query_pos, key_start, key_count, lengths)[:, None]
    scores = jnp.where(allowed, scores, NEGATIVE)
    fresh_max = jnp.maximum(row_max, jnp.max(scores, axis=-1))
    exponent_vals = jnp.exp(scores - fresh_max[..., None])
    row_total = jnp.sum(exponent_vals, axis=-1)
    update = jnp.einsum(
        "shqk,skhd->sqhd",
        exponent_vals.astype(jnp.bfloat16),
        split_heads(value_piece),
        preferred_element_type=jnp.float32,
    )
    weighted = update
    return (fresh_max, row_total, weighted)


def grad_keys(
    heads_q, heads_do, log_total, dterm, key_piece, value_piece, key_start, query_pos, lengths
):
    seq_count, key_count = (key_piece.shape[0], key_piece.shape[1])
    heads_k = split_heads(key_piece)
    heads_v = split_heads(value_piece)
    score_scale = 1.0 / math.sqrt(HEAD_DIM)
    scores = (
        jnp.einsum("sqhd,skhd->shqk", heads_q, heads_k, preferred_element_type=jnp.float32)
        * score_scale
    )
    allowed = key_mask(query_pos, key_start, key_count, lengths)[:, None]
    probability = jnp.where(allowed, jnp.exp(scores - log_total[..., None]), 0.0)
    dprob = jnp.einsum("sqhd,skhd->shqk", heads_do, heads_v, preferred_element_type=jnp.float32)
    dscores = (probability * (dprob - dterm[..., None])).astype(jnp.bfloat16)
    dq_part = (
        jnp.einsum("shqk,skhd->sqhd", dscores, heads_k, preferred_element_type=jnp.float32)
        * score_scale
    )
    dk_part = (
        jnp.einsum("shqk,sqhd->skhd", dscores, heads_q, preferred_element_type=jnp.float32)
        * score_scale
    )
    dv_part = jnp.einsum(
        "shqk,sqhd->skhd",
        probability.astype(jnp.bfloat16),
        heads_do,
        preferred_element_type=jnp.float32,
    )
    return (
        dq_part,
        dk_part.reshape(seq_count, key_count, -1),
        dv_part.reshape(seq_count, key_count, -1),
    )


def shards(
    hidden,
    teacher,
    lengths,
    w_qkv,
    w_out,
    w_up,
    w_down,
    norm_gain,
    norm_shift,
    proj_bias,
    mid_gain,
    mid_shift,
    up_bias,
):
    (
        full_qkv,
        full_out,
        full_up,
        full_down,
        gain_full,
        shift_full,
        bias_full,
        mid_gain_full,
        mid_shift_full,
        up_bias_full,
    ) = (
        lax.all_gather(w_qkv, "dp", axis=0, tiled=True),
        lax.all_gather(w_out, "dp", axis=0, tiled=True),
        lax.all_gather(w_up, "dp", axis=0, tiled=True),
        lax.all_gather(w_down, "dp", axis=0, tiled=True),
        lax.all_gather(norm_gain, "dp", axis=0, tiled=True),
        lax.all_gather(norm_shift, "dp", axis=0, tiled=True),
        lax.all_gather(proj_bias, "dp", axis=0, tiled=True),
        lax.all_gather(mid_gain, "dp", axis=0, tiled=True),
        lax.all_gather(mid_shift, "dp", axis=0, tiled=True),
        lax.all_gather(up_bias, "dp", axis=0, tiled=True),
    )
    gain_f = gain_full.astype(jnp.float32)
    shift_f = shift_full.astype(jnp.float32)
    bias_f = bias_full.astype(jnp.float32)
    mid_gain_f = mid_gain_full.astype(jnp.float32)
    mid_shift_f = mid_shift_full.astype(jnp.float32)
    up_bias_f = up_bias_full.astype(jnp.float32)
    seq_count, local_rows, model_width = hidden.shape
    token_rows = seq_count * local_rows
    seq_shape = (seq_count, local_rows, model_width)
    ctx_place = lax.axis_index("ctx")
    ctx_parts = lax.axis_size("ctx")
    query_pos = ctx_place * local_rows + jnp.arange(local_rows, dtype=jnp.int32)
    last_query = ctx_place * local_rows + local_rows - 1
    valid_mask = (query_pos[None, :] < lengths[:, None]).astype(jnp.float32)
    valid_rows = valid_mask.reshape(token_rows, 1)
    hidden_rows = hidden.reshape(token_rows, model_width).astype(jnp.float32)
    normed, pull_in = jax.vjp(layer_norm, hidden_rows, gain_f[:, 0], shift_f[:, 0])
    normed_low = normed.astype(jnp.bfloat16)
    projected = jnp.dot(normed_low, full_qkv, preferred_element_type=jnp.float32)
    query_low = (projected[:, :model_width] + bias_f[:, 0]).astype(jnp.bfloat16).reshape(seq_shape)
    key_low = projected[:, model_width : 2 * model_width].astype(jnp.bfloat16).reshape(seq_shape)
    value_low = (
        (projected[:, 2 * model_width :] + bias_f[:, 1]).astype(jnp.bfloat16).reshape(seq_shape)
    )
    heads_q = split_heads(query_low)
    start_state = (
        jnp.full((seq_count, HEADS, local_rows), NEGATIVE, jnp.float32),
        jnp.zeros((seq_count, HEADS, local_rows), jnp.float32),
        jnp.zeros((seq_count, local_rows, HEADS, HEAD_DIM), jnp.float32),
    )
    pieces = (
        lax.all_gather(key_low, "ctx", axis=1, tiled=True),
        lax.all_gather(value_low, "ctx", axis=1, tiled=True),
    )
    key_start = jnp.int32(0)
    row_max, row_total, weighted = lax.cond(
        key_start <= last_query,
        lambda: fold_keys(start_state, pieces, key_start, heads_q, query_pos, lengths),
        lambda: start_state,
    )
    attended = weighted / jnp.transpose(row_total, (0, 2, 1))[..., None]
    log_total = row_max + jnp.log(row_total)
    attended_rows = attended.reshape(token_rows, model_width)
    mixed, pull_mix = jax.vjp(layer_norm, attended_rows, gain_f[:, 1], shift_f[:, 1])
    mixed_low = mixed.astype(jnp.bfloat16)
    residual = (
        hidden_rows
        + jnp.dot(mixed_low, full_out, preferred_element_type=jnp.float32)
        + bias_f[:, 2]
    )
    ffn_in, pull_ffn = jax.vjp(layer_norm, residual, gain_f[:, 2], shift_f[:, 2])
    ffn_low = ffn_in.astype(jnp.bfloat16)
    up_proj = jnp.dot(ffn_low, full_up, preferred_element_type=jnp.float32) + up_bias_f
    activated, pull_mid = jax.vjp(mid_norm, up_proj, mid_gain_f, mid_shift_f)
    act_low = activated.astype(jnp.bfloat16)
    result = (
        residual + jnp.dot(act_low, full_down, preferred_element_type=jnp.float32) + bias_f[:, 3]
    )
    layer_output = (result * valid_rows).astype(jnp.bfloat16).reshape(hidden.shape)
    error_rows = (
        result - teacher.reshape(token_rows, model_width).astype(jnp.float32)
    ) * valid_rows
    loss_total, valid_total = lax.psum(
        (0.5 * jnp.sum(error_rows * error_rows), jnp.sum(valid_mask)), ("dp", "ctx")
    )
    loss = loss_total / (valid_total * model_width)
    down_low = error_rows.astype(jnp.bfloat16)
    bias_down_grad = jnp.sum(down_low.astype(jnp.float32), axis=0)
    down_grad = jnp.einsum("rf,rd->fd", act_low, down_low, preferred_element_type=jnp.float32)
    d_act = jnp.einsum("rd,fd->rf", down_low, full_down, preferred_element_type=jnp.float32)
    d_up, mid_gain_grad, mid_shift_grad = pull_mid(d_act)
    up_low = d_up.astype(jnp.bfloat16)
    up_bias_grad = jnp.sum(up_low.astype(jnp.float32), axis=0)
    up_grad = jnp.einsum("rd,rf->df", ffn_low, up_low, preferred_element_type=jnp.float32)
    d_ffn = jnp.einsum("rf,df->rd", up_low, full_up, preferred_element_type=jnp.float32)
    d_res_norm, gain_two, shift_two = pull_ffn(d_ffn)
    d_residual = error_rows + d_res_norm
    branch_low = d_residual.astype(jnp.bfloat16)
    bias_out_grad = jnp.sum(branch_low.astype(jnp.float32), axis=0)
    out_grad = jnp.einsum("rd,re->de", mixed_low, branch_low, preferred_element_type=jnp.float32)
    d_mixed = jnp.einsum("re,de->rd", branch_low, full_out, preferred_element_type=jnp.float32)
    d_att, gain_one, shift_one = pull_mix(d_mixed)
    heads_do = split_heads(d_att.astype(jnp.bfloat16).reshape(seq_shape))
    dterm = jnp.einsum("sqhd,sqhd->shq", heads_do.astype(jnp.float32), attended)

    def grad_step(key_piece, value_piece, key_start):
        return grad_keys(
            heads_q,
            heads_do,
            log_total,
            dterm,
            key_piece,
            value_piece,
            key_start,
            query_pos,
            lengths,
        )

    dq_zero = jnp.zeros((seq_count, local_rows, HEADS, HEAD_DIM), jnp.float32)
    own_zero = jnp.zeros(seq_shape, jnp.float32)

    def pass_step(step_index, running):
        key_cur, value_cur, dk_run, dv_run, dq_sum = running
        owner = (ctx_place - step_index) % ctx_parts
        dq_part, dk_part, dv_part = lax.cond(
            owner <= ctx_place,
            lambda: grad_step(key_cur, value_cur, owner * local_rows),
            lambda: (dq_zero, own_zero, own_zero),
        )
        dk_run, dv_run = (
            passed_along((dk_run + dk_part).astype(jnp.bfloat16), "ctx", 1).astype(jnp.float32),
            passed_along((dv_run + dv_part).astype(jnp.bfloat16), "ctx", 1).astype(jnp.float32),
        )
        key_cur, value_cur = passed_along_2((key_cur, value_cur), "ctx", 1)
        return (key_cur, value_cur, dk_run, dv_run, dq_sum + dq_part)

    key_end, value_end, dk_own, dv_own, dq_sum = lax.fori_loop(
        0, ctx_parts, pass_step, (key_low, value_low, own_zero, own_zero, dq_zero)
    )
    dq_low = dq_sum.reshape(token_rows, model_width).astype(jnp.bfloat16)
    dk_low = dk_own.reshape(token_rows, model_width).astype(jnp.bfloat16)
    dv_low = dv_own.reshape(token_rows, model_width).astype(jnp.bfloat16)
    dqkv_low = jnp.concatenate([dq_low, dk_low, dv_low], axis=1)
    bias_q_grad = jnp.sum(dq_low.astype(jnp.float32), axis=0)
    bias_v_grad = jnp.sum(dv_low.astype(jnp.float32), axis=0)
    qkv_grad = jnp.einsum("rd,re->de", normed_low, dqkv_low, preferred_element_type=jnp.float32)
    d_normed = jnp.einsum("re,de->rd", dqkv_low, full_qkv, preferred_element_type=jnp.float32)
    d_in_norm, gain_zero, shift_zero = pull_in(d_normed)
    hidden_grad = (d_residual + d_in_norm).reshape(hidden.shape)
    gain_grad = jnp.stack([gain_zero, gain_one, gain_two], axis=1)
    shift_grad = jnp.stack([shift_zero, shift_one, shift_two], axis=1)
    bias_grad = jnp.stack([bias_q_grad, bias_v_grad, bias_out_grad, bias_down_grad], axis=1)
    shares = (
        lax.psum_scatter(
            qkv_grad.astype(jnp.bfloat16), "dp", scatter_dimension=0, tiled=True
        ).astype(jnp.float32),
        lax.psum_scatter(
            out_grad.astype(jnp.bfloat16), "dp", scatter_dimension=0, tiled=True
        ).astype(jnp.float32),
        lax.psum_scatter(
            up_grad.astype(jnp.bfloat16), "dp", scatter_dimension=0, tiled=True
        ).astype(jnp.float32),
        lax.psum_scatter(
            down_grad.astype(jnp.bfloat16), "dp", scatter_dimension=0, tiled=True
        ).astype(jnp.float32),
        lax.psum_scatter(
            gain_grad.astype(jnp.bfloat16), "dp", scatter_dimension=0, tiled=True
        ).astype(jnp.float32),
        lax.psum_scatter(
            shift_grad.astype(jnp.bfloat16), "dp", scatter_dimension=0, tiled=True
        ).astype(jnp.float32),
        lax.psum_scatter(
            bias_grad.astype(jnp.bfloat16), "dp", scatter_dimension=0, tiled=True
        ).astype(jnp.float32),
        lax.psum_scatter(
            mid_gain_grad.astype(jnp.bfloat16), "dp", scatter_dimension=0, tiled=True
        ).astype(jnp.float32),
        lax.psum_scatter(
            mid_shift_grad.astype(jnp.bfloat16), "dp", scatter_dimension=0, tiled=True
        ).astype(jnp.float32),
        lax.psum_scatter(
            up_bias_grad.astype(jnp.bfloat16), "dp", scatter_dimension=0, tiled=True
        ).astype(jnp.float32),
    )
    summed = (
        lax.psum(shares[0].astype(jnp.bfloat16), "ctx").astype(jnp.float32),
        lax.psum(shares[1].astype(jnp.bfloat16), "ctx").astype(jnp.float32),
        lax.psum(shares[2].astype(jnp.bfloat16), "ctx").astype(jnp.float32),
        lax.psum(shares[3].astype(jnp.bfloat16), "ctx").astype(jnp.float32),
        lax.psum(shares[4].astype(jnp.bfloat16), "ctx").astype(jnp.float32),
        lax.psum(shares[5].astype(jnp.bfloat16), "ctx").astype(jnp.float32),
        lax.psum(shares[6].astype(jnp.bfloat16), "ctx").astype(jnp.float32),
        lax.psum(shares[7].astype(jnp.bfloat16), "ctx").astype(jnp.float32),
        lax.psum(shares[8].astype(jnp.bfloat16), "ctx").astype(jnp.float32),
        lax.psum(shares[9].astype(jnp.bfloat16), "ctx").astype(jnp.float32),
    )
    return (
        layer_output,
        loss,
        hidden_grad,
        summed[0],
        summed[1],
        summed[2],
        summed[3],
        summed[4],
        summed[5],
        summed[6],
        summed[7],
        summed[8],
        summed[9],
    )


AXES = ("dp", "ctx")


def swap(value, mask):
    count = lax.axis_size("dp") * lax.axis_size("ctx")
    return lax.ppermute(value, AXES, [(i, i ^ mask) for i in range(count)])


def along_z(piece):
    return [swap(piece, 8 * step) for step in (1, 2, 3)]


def wide(value):
    return value.astype(jnp.float32)


def narrow(value):
    return value.astype(jnp.bfloat16)


VMEM_BYTES = 56 * 1024 * 1024


def whole(shape):
    return pl.BlockSpec(tuple(shape), lambda i: (0,) * len(shape), pipeline_mode=pl.Buffered(1))


def padded(shape, dtype):
    lead = math.prod(shape[:-2])
    size = jnp.dtype(dtype).itemsize
    rows = -(-shape[-2] // (32 // size)) * (32 // size) if len(shape) > 1 else 8
    return lead * rows * (-(-shape[-1] // 128) * 128) * size


def call(body, ins, outs, scratch=(), us=1, deps=(), room=6):
    pairs = [v if isinstance(v, tuple) else (v, whole(v.shape)) for v in ins[1:]]
    held = sum(padded(spec.block_shape, v.dtype) for v, spec in pairs)
    held += sum(padded(shape, dtype) for shape, dtype in (*outs, *scratch))
    count = len(pairs)

    def kernel(sc, *refs):
        body(sc, *refs[:count], *refs[count + len(deps):])

    return pl.pallas_call(
        kernel,
        grid=(1,),
        in_specs=[pl.BlockSpec(memory_space=pltpu.SMEM)] + [spec for _, spec in pairs]
        + [pl.BlockSpec(memory_space=pl.ANY)] * len(deps),
        out_specs=[whole(shape) for shape, _ in outs],
        out_shape=[jax.ShapeDtypeStruct(shape, dtype) for shape, dtype in outs],
        scratch_shapes=[pltpu.VMEM(shape, dtype) for shape, dtype in scratch],
        compiler_params=pltpu.CompilerParams(vmem_limit_bytes=held + room * 1024 * 1024),
        cost_estimate=pl.CostEstimate(flops=int(us * 2e7), bytes_accessed=0, transcendentals=0),
        name=body.__name__,
    )(ins[0], *[v for v, _ in pairs], *deps)


def after(value, *deps):
    return lax.optimization_barrier((value, *deps))[0]


BF, F32 = jnp.bfloat16, jnp.float32


def contract(a, b, da, db):
    return lax.dot_general(a, b, (((da,), (db,)), ((), ())), preferred_element_type=F32)


def block_of(sc, xr, zr):
    return 2 * ((sc[0] >> 1) ^ zr) + ((sc[0] & 1) ^ xr)


def slot_of(sc, block):
    return ((block & 1) ^ (sc[0] & 1)) * 4 + ((block >> 1) ^ (sc[0] >> 1))


def lay(sc, scr, near, far, rows, stride, offset=0):
    for xr, ref in ((0, near), (1, far)):
        for zr in range(4):
            at = pl.multiple_of(stride * block_of(sc, xr, zr) + offset, 16)
            scr[pl.ds(at, rows), :] = ref[zr]


def moments(value):
    average = jnp.mean(value, axis=-1, keepdims=True)
    centred = value - average
    scale = lax.rsqrt(jnp.mean(centred * centred, axis=-1, keepdims=True) + EPSILON)
    return centred * scale, scale


def norm_back(grad, hat, scale):
    return scale * (grad - jnp.mean(grad, axis=-1, keepdims=True) - hat * jnp.mean(grad * hat, axis=-1, keepdims=True))


def mine(ctx_at, row):
    out = row[:, :192]
    for j in range(1, 4):
        out = jnp.where(ctx_at == j, row[:, 192 * j:192 * j + 192], out)
    return out


def pack_body(sc, w, gain, shift, bias, out, scr):
    scr[...] = jnp.zeros((16, 128), F32)
    scr[0:3, :96] = gain[...].astype(F32)
    scr[3:6, :96] = shift[...].astype(F32)
    scr[6:10, :96] = bias[...].astype(F32)
    small = scr[...].T[:96].astype(BF)
    for j in range(4):
        @pl.when(sc[1] == j)
        def _():
            cols = [w[:, 768 * part + 192 * j:768 * part + 192 * j + 192] for part in range(3)]
            out[...] = jnp.concatenate(cols + [small, jnp.zeros((96, 48), BF)], axis=1)


def attend_body(sc, h0, h1, h2, h3, wa, wb, a0, a1, a23, q_o, k_o, v_o, lse_o, ot_o, n_o, vec_o, w_scr):
    ctx_at, length = sc[1], sc[2]
    lay(sc, w_scr, wa, wb, 96, 96)
    vec = w_scr[:, 512:640].astype(F32).T[64:80]
    vec_o[...] = vec
    bias_q, bias_v = mine(ctx_at, vec[6:7]), mine(ctx_at, vec[7:8])
    for r, ref in enumerate((h0, h1, h2, h3)):
        rows = pl.ds(pl.multiple_of((ctx_at ^ r) * 256, 256), 256)
        hat, _ = moments(ref[...].astype(F32))
        normed = (hat * vec[0:1] + vec[3:4]).astype(BF)
        n_o[rows, :] = normed
        p = jnp.dot(normed, w_scr[...], preferred_element_type=F32)
        for h in range(3):
            q_o[h, rows, :] = ((p[:, 64 * h:64 * h + 64] + bias_q[:, 64 * h:64 * h + 64]) * 0.125).astype(BF)
            k_o[h, rows, :] = p[:, 192 + 64 * h:256 + 64 * h].astype(BF)
            v_o[h, rows, :] = (p[:, 384 + 64 * h:448 + 64 * h] + bias_v[:, 64 * h:64 * h + 64]).astype(BF)

    def head(h, carry):
        for i in range(4):
            n = 256 * (i + 1)
            scores = contract(k_o[h, :n, :], q_o[h, 256 * i:256 * i + 256, :], 1, 1)
            limit = jnp.minimum(256 * i + lax.broadcasted_iota(jnp.int32, (1, 256), 1), length - 1)
            scores = jnp.where(lax.broadcasted_iota(jnp.int32, (n, 256), 0) <= limit, scores, NEGATIVE)
            top = jnp.max(scores, axis=0, keepdims=True)
            grown = jnp.exp(scores - top)
            total = jnp.sum(grown, axis=0, keepdims=True)
            out = contract(v_o[h, :n, :], grown.astype(BF), 0, 0) / total
            ot_o[i, pl.ds(pl.multiple_of(64 * h, 64), 64), :] = out
            lse_o[h, i:i + 1, :] = top + jnp.log(total)
        return carry

    lax.fori_loop(0, 3, head, 0)
    for r, ref in enumerate((a0, a1, a23.at[0], a23.at[1])):
        ref[...] = ot_o[ctx_at ^ r].T.astype(BF)


def attend(sc, hids, wa, wb, deps):
    rows = (256, 192)
    return call(
        attend_body, [sc, *hids, wa, wb],
        [(rows, BF)] * 2 + [((2, 256, 192), BF)] + [((3, 1024, 64), BF)] * 3
        + [((3, 8, 256), F32), ((4, 192, 256), F32), ((1024, 768), BF), ((16, 768), F32)],
        [((768, 640), BF)], us=13, deps=deps)


def attend_back_body(sc, d0, d1, d2, d3, q_i, k_i, v_i, lse_i, ot_i, n_i, h0, h1, h2, h3, wa, wb, vec_i, side_e, side_d, mids,
                     n0, n1, n23, keep, send, w_scr, do_scr, dq_s, dk_s, dv_s, dk_acc, dv_acc, all_scr, g_scr):
    ctx_at, length = sc[1], sc[2]
    lay(sc, w_scr, wa, wb, 96, 96)
    for r, ref in enumerate((d0, d1, d2, d3)):
        rows = pl.ds(pl.multiple_of((ctx_at ^ r) * 256, 256), 256)
        value = ref[...]
        for h in range(3):
            do_scr[h, rows, :] = value[:, 64 * h:64 * h + 64]

    def head(h, carry):
        for i in (3, 2, 1, 0):
            n = 256 * (i + 1)
            mine_rows = slice(256 * i, 256 * i + 256)
            q, do, k = q_i[h, mine_rows, :], do_scr[h, mine_rows, :], k_i[h, :n, :]
            out = ot_i[i, pl.ds(pl.multiple_of(64 * h, 64), 64), :]
            dterm = jnp.sum(do.astype(F32).T * out, axis=0, keepdims=True)
            limit = jnp.minimum(256 * i + lax.broadcasted_iota(jnp.int32, (1, 256), 1), length - 1)
            prob = jnp.exp(contract(k, q, 1, 1) - lse_i[h, i:i + 1, :])
            prob = jnp.where(lax.broadcasted_iota(jnp.int32, (n, 256), 0) <= limit, prob, 0.0)
            dscore = (prob * (contract(v_i[h, :n, :], do, 1, 1) - dterm)).astype(BF)
            dv = jnp.dot(prob.astype(BF), do, preferred_element_type=F32)
            dk = jnp.dot(dscore, q, preferred_element_type=F32)
            if i == 3:
                dv_acc[...] = dv
                dk_acc[...] = dk
            else:
                dv_acc[:n, :] += dv
                dk_acc[:n, :] += dk
            dq_s[h, mine_rows, :] = (contract(k, dscore, 0, 0) * 0.125).T.astype(BF)
        dk_s[h] = dk_acc[...].astype(BF)
        dv_s[h] = dv_acc[...].astype(BF)
        return carry

    lax.fori_loop(0, 3, head, 0)
    for i in range(4):
        rows = slice(256 * i, 256 * i + 256)
        all_scr[rows, :] = jnp.concatenate([s[h, rows, :] for s in (dq_s, dk_s, dv_s) for h in range(3)], axis=1)
    sums = jnp.sum(all_scr[...].astype(F32), axis=0, keepdims=True)
    bias_q = jnp.concatenate([jnp.where(ctx_at == j, sums[:, :192], 0.0) for j in range(4)], axis=1)
    bias_v = jnp.concatenate([jnp.where(ctx_at == j, sums[:, 384:], 0.0) for j in range(4)], axis=1)
    gain_sum, shift_sum = jnp.zeros((1, 768), F32), jnp.zeros((1, 768), F32)
    for r, (ref, out) in enumerate(((h0, n0), (h1, n1), (h2, n23.at[0]), (h3, n23.at[1]))):
        rows = pl.ds(pl.multiple_of((ctx_at ^ r) * 256, 256), 256)
        grad = contract(all_scr[rows, :], w_scr[:, :576], 1, 1)
        hat, _ = moments(ref[...].astype(F32))
        gain_sum += jnp.sum(grad * hat, axis=0, keepdims=True)
        shift_sum += jnp.sum(grad, axis=0, keepdims=True)
        out[...] = grad.astype(BF)
    rows16 = jnp.concatenate(
        [gain_sum, side_e[0:2], shift_sum, side_e[2:4], bias_q, bias_v, side_e[4:5], side_d[0:2], jnp.zeros((5, 768), F32)], axis=0)
    w_grad = contract(n_i[...], all_scr[...], 0, 0)
    for b in range(8):
        at = slot_of(sc, b)
        extra = jnp.concatenate([mids[:, 384 * b:384 * b + 384], rows16[:, 96 * b:96 * b + 96], jnp.zeros((16, 96), F32)], axis=1)
        g_scr[at, :96, :] = w_grad[96 * b:96 * b + 96].astype(BF)
        g_scr[at, 96:112, :] = extra.astype(BF)
    keep[...] = g_scr[:4]
    send[...] = g_scr[4:]


def attend_back(sc, douts, saved, hids, wa, wb, side_e, side_d, mids, deps):
    q, k, v, lse, ot, normed, vec = saved
    return call(
        attend_back_body, [sc, *douts, q, k, v, lse, ot, normed, *hids, wa, wb, vec, side_e, side_d, mids],
        [((256, 768), BF)] * 2 + [((2, 256, 768), BF)] + [((4, 112, 576), BF)] * 2,
        [((768, 640), BF), ((3, 1024, 64), BF), ((3, 1024, 64), BF), ((3, 1024, 64), BF), ((3, 1024, 64), BF),
         ((1024, 64), F32), ((1024, 64), F32), ((1024, 576), BF), ((8, 112, 576), BF)],
        us=12, deps=deps)


def part(rows, at):
    return pl.BlockSpec((4, rows, 768), lambda i: (0, at, 0), pipeline_mode=pl.Buffered(1))


def lay_out(sc, scr, own_near, own_far, other_near, other_far):
    core = sc[1] & 1
    lay(sc, scr, own_near, own_far, 48, 96, 48 * core)
    lay(sc, scr, other_near, other_far, 48, 96, 48 * (1 - core))


def lay_down(sc, scr, refs):
    for c in (0, 1):
        for xr in (0, 1):
            for y in (0, 1):
                lay_one(sc, scr, refs[4 * c + 2 * xr + y], xr, 96 * (sc[1] ^ (2 * y + c)))


def lay_one(sc, scr, ref, xr, offset):
    for zr in range(4):
        scr[pl.ds(pl.multiple_of(384 * block_of(sc, xr, zr) + offset, 32), 96), :] = ref[zr]


def join_heads(sc, scr, pieces):
    own, near, far = pieces
    for r, value in enumerate((own[...], near[0], far[0], near[1])):
        scr[r] = value
    return jnp.concatenate([scr[sc[1] ^ j] for j in range(4)], axis=1).astype(F32)


def mid_body(sc, g0, g1, g2, own, vec, on, of, tn, tf, mixed_o, resid_o, ffn_o, w_scr, a_scr):
    lay_out(sc, w_scr, on, of, tn, tf)
    hat, _ = moments(join_heads(sc, a_scr, (g0, g1, g2)))
    mixed = (hat * vec[1:2] + vec[4:5]).astype(BF)
    mixed_o[...] = mixed
    resid = own[...].astype(F32) + jnp.dot(mixed, w_scr[...], preferred_element_type=F32) + vec[8:9]
    resid_o[...] = resid
    hat, _ = moments(resid)
    ffn_o[...] = (hat * vec[2:3] + vec[5:6]).astype(BF)


def up_body(sc, ffn, w0n, w0f, w1n, w1f, w2n, w2f, w3n, w3f, mn, mf, act_o, hat_o, slope_o, scale_o, nat_o,
            w_scr, g_scr, m_scr):
    for xr, ref in ((0, mn), (1, mf)):
        for zr in range(4):
            m_scr[block_of(sc, xr, zr)] = ref[zr].astype(F32)
    flat = [m_scr[b] for b in range(8)]
    for j in range(4):
        two = flat[2 * j:2 * j + 2]
        nat_o[j, 0:1, :] = jnp.concatenate([m[0:1, :384] for m in two], axis=1)
        nat_o[j, 1:2, :] = jnp.concatenate([m[0:1, 384:] for m in two], axis=1)
        nat_o[j, 2:3, :] = jnp.concatenate([m[1:2, :384] for m in two], axis=1)
        nat_o[j, 3:8, :] = jnp.zeros((5, 768), F32)
    value = ffn[...]
    total = jnp.zeros((256, 1), F32)
    for t, (near, far) in enumerate(((w0n, w0f), (w1n, w1f), (w2n, w2f), (w3n, w3f))):
        j = sc[1] ^ t
        lay(sc, w_scr.at[t], near, far, 96, 96)
        up = jnp.dot(value, w_scr[t], preferred_element_type=F32) + nat_o[j, 2:3, :]
        chance = 0.5 * (1.0 + lax.erf(up * math.sqrt(0.5)))
        slope_o[j] = (chance + up * jnp.exp(-0.5 * up * up) * (1.0 / math.sqrt(2.0 * math.pi))).astype(BF)
        gelu = up * chance
        g_scr[j] = gelu
        total += jnp.sum(gelu, axis=-1, keepdims=True)
    average = total * (1.0 / 3072)
    square = jnp.zeros((256, 1), F32)
    for j in range(4):
        centred = g_scr[j] - average
        square += jnp.sum(centred * centred, axis=-1, keepdims=True)
    scale = lax.rsqrt(square * (1.0 / 3072) + EPSILON)
    scale_o[...] = scale
    for j in range(4):
        hat = (g_scr[j] - average) * scale
        hat_o[j] = hat.astype(BF)
        act_o[j] = (hat * nat_o[j, 0:1, :] + nat_o[j, 1:2, :]).astype(BF)


def down_body(sc, act, resid, teacher, vec, e0, e1, e2, e3, e4, e5, e6, e7, out_o, err_o, low_o, side_o, w_scr):
    lay_down(sc, w_scr, (e0, e1, e2, e3, e4, e5, e6, e7))
    result = resid[...] + vec[9:10]
    for j in range(4):
        result += jnp.dot(act[j], w_scr[768 * j:768 * j + 768, :], preferred_element_type=F32)
    pos = sc[1] * 256 + lax.broadcasted_iota(jnp.int32, (256, 1), 0)
    valid = jnp.where(pos < sc[2], 1.0, 0.0)
    out_o[...] = (result * valid).astype(BF)
    error = (result - teacher[...].astype(F32)) * valid
    err_o[...] = error
    low = error.astype(BF)
    low_o[...] = low
    side_o[0:1, :] = jnp.sum(low.astype(F32), axis=0, keepdims=True)
    loss = 0.5 * jnp.sum(jnp.sum(error * error, axis=0, keepdims=True), axis=1, keepdims=True)
    count = jnp.sum(valid, axis=0, keepdims=True)
    high = loss.astype(BF).astype(F32)
    lane = lax.broadcasted_iota(jnp.int32, (1, 768), 1) % 96
    side_o[1:2, :] = jnp.where(lane == 0, high, jnp.where(lane == 1, loss - high, jnp.where(lane == 2, count, 0.0)))
    side_o[2:8, :] = jnp.zeros((6, 768), F32)


def down_grad_body(sc, act, low, keep, send, g_scr):
    value = low[...]
    for j in range(4):
        grad = contract(act[j], value, 0, 0).astype(BF)
        for half in (0, 1):
            at = slot_of(sc, 2 * j + half)
            for q in range(4):
                g_scr[sc[1] ^ q, at] = grad[384 * half + 96 * q:384 * half + 96 * q + 96]
    for y in (0, 1):
        keep[y] = g_scr[2 * y]
        send[y] = g_scr[2 * y + 1]


def act_back_body(sc, low, hat_i, slope, scale, nat, e0, e1, e2, e3, e4, e5, e6, e7, up_o, mids_o, wd_scr, dh_scr):
    lay_down(sc, wd_scr, (e0, e1, e2, e3, e4, e5, e6, e7))
    value = low[...]
    first, second = jnp.zeros((256, 1), F32), jnp.zeros((256, 1), F32)
    for j in range(4):
        grad = contract(value, wd_scr[768 * j:768 * j + 768, :], 1, 1)
        hat = hat_i[j].astype(F32)
        cols = slice(768 * j, 768 * j + 768)
        mids_o[0:1, cols] = jnp.sum(grad * hat, axis=0, keepdims=True)
        mids_o[1:2, cols] = jnp.sum(grad, axis=0, keepdims=True)
        grad = grad * nat[j, 0:1, :]
        dh_scr[j] = grad
        first += jnp.sum(grad, axis=-1, keepdims=True)
        second += jnp.sum(grad * hat, axis=-1, keepdims=True)
    first, second = first * (1.0 / 3072), second * (1.0 / 3072)
    for j in range(4):
        hat = hat_i[j].astype(F32)
        grad = (scale[...] * (dh_scr[j] - first - hat * second) * slope[j].astype(F32)).astype(BF)
        up_o[j] = grad
        mids_o[2:3, 768 * j:768 * j + 768] = jnp.sum(grad.astype(F32), axis=0, keepdims=True)
    mids_o[3:16, :] = jnp.zeros((13, 3072), F32)


def ffn_back_body(sc, up_i, err, resid, w0n, w0f, w1n, w1f, w2n, w2f, w3n, w3f, on, of, tn, tf, vec, g0, g1, g2,
                  branch_o, dres_o, p0, p1, p2, p3, side_o, w_scr, o_scr, a_scr, b_scr):
    grad = jnp.zeros((256, 768), F32)
    for t, (near, far) in enumerate(((w0n, w0f), (w1n, w1f), (w2n, w2f), (w3n, w3f))):
        lay(sc, w_scr.at[t], near, far, 96, 96)
        grad += contract(up_i[sc[1] ^ t], w_scr[t], 1, 1)
    hat, factor = moments(resid[...])
    side_o[1:2, :] = jnp.sum(grad * hat, axis=0, keepdims=True)
    side_o[3:4, :] = jnp.sum(grad, axis=0, keepdims=True)
    dres = err[...] + norm_back(grad * vec[2:3], hat, factor)
    dres_o[...] = dres
    branch = dres.astype(BF)
    branch_o[...] = branch
    side_o[4:5, :] = jnp.sum(branch.astype(F32), axis=0, keepdims=True)
    lay_out(sc, o_scr, on, of, tn, tf)
    grad = contract(branch, o_scr[...], 1, 1)
    hat, factor = moments(join_heads(sc, a_scr, (g0, g1, g2)))
    side_o[0:1, :] = jnp.sum(grad * hat, axis=0, keepdims=True)
    side_o[2:3, :] = jnp.sum(grad, axis=0, keepdims=True)
    side_o[5:8, :] = jnp.zeros((3, 768), F32)
    grad = norm_back(grad * vec[1:2], hat, factor).astype(BF)
    for j in range(4):
        b_scr[j] = grad[:, 192 * j:192 * j + 192]
    for r, ref in enumerate((p0, p1, p2, p3)):
        ref[...] = b_scr[sc[1] ^ r]


def up_grad_body(sc, ffn, up, keep, send, g_scr):
    value = ffn[...]
    for j in range(4):
        grad = contract(value, up[j], 0, 0).astype(BF)
        for b in range(8):
            g_scr[sc[1] ^ j, slot_of(sc, b)] = grad[96 * b:96 * b + 96]
    for y in (0, 1):
        keep[y] = g_scr[2 * y]
        send[y] = g_scr[2 * y + 1]


def out_grad_body(sc, mixed, branch, out_keep, out_send, o_scr):
    grad = contract(mixed[...], branch[...], 0, 0).astype(BF)
    for b in range(8):
        for c in (0, 1):
            o_scr[(sc[1] & 1) ^ c, slot_of(sc, b)] = grad[96 * b + 48 * c:96 * b + 48 * c + 48]
    out_keep[...] = o_scr[0]
    out_send[...] = o_scr[1]


def added(a, b):
    return a.astype(F32) + b.astype(F32)


def pair_body(sc, keep, got, near0, near1, far0, far1):
    for y, near, far in ((0, near0, far0), (1, near1, far1)):
        near[...] = added(keep[y, :4], got[y, :4]).astype(BF)
        far[...] = added(keep[y, 4:], got[y, 4:]).astype(BF)


def slots_body(sc, near, got, own, s1, s2, s3):
    own[...] = added(near[0], got[0])
    for at, out in ((1, s1), (2, s2), (3, s3)):
        out[...] = added(near[at], got[at]).astype(BF)


def join_far_body(sc, mine, got, out_keep, out_got, far):
    far[:, :96, :] = added(mine[...], got[...]).astype(BF)
    far[:, 96:, :] = added(out_keep[...], out_got[...]).astype(BF)


def join_near_body(sc, mine, y_got, out_keep, out_got, x_got, own, s1, s2, s3):
    for at, out in ((0, own), (1, s1), (2, s2), (3, s3)):
        kind = out.dtype
        out[:96, :] = (added(mine[at], y_got[at]) + x_got[at, :96, :].astype(F32)).astype(kind)
        out[96:, :] = (added(out_keep[at], out_got[at]) + x_got[at, 96:, :].astype(F32)).astype(kind)


def total_of(own, parts):
    return (own[...] + sum(p[...].astype(F32) for p in parts)).astype(BF)


def middle_body(sc, q0, q1, q2, q3, dn, got, d0, d1, d2, d3, e0, e1, e2, e3, q_o, dn_o, early_o):
    q_o[...] = total_of(q0, (q1, q2, q3))
    dn_o[...] = added(dn[...], got[0]).astype(BF)
    early_o[0:96, :] = total_of(d0, (d1, d2, d3))
    early_o[96:192, :] = total_of(e0, (e1, e2, e3))


def fold_body(sc, own, other, out):
    out[0:96, :] = added(own[0:96, :], other[96:192, :]).astype(BF)
    out[96:192, :] = added(own[96:192, :], other[0:96, :]).astype(BF)


def spread_down_body(sc, mine, other, down_o):
    for t, (ref, at) in enumerate(((mine, 0), (other, 0), (mine, 96), (other, 96))):
        rows = pl.multiple_of(96 * (sc[1] ^ t), 32)
        down_o[pl.ds(rows, 96), :] = ref[at:at + 96, :].astype(F32)


def spread_body(sc, t0, t1, t2, t3, up_o, out_o, scr):
    core = sc[1] & 1
    for t, ref in enumerate((t0, t1, t2, t3)):
        scr[sc[1] ^ t] = ref[:96, :]
    for j in range(4):
        up_o[:, 768 * j:768 * j + 768] = scr[j].astype(F32)
    out_o[pl.ds(pl.multiple_of(48 * core, 16), 48), :] = added(t0[96:144, :], t2[96:144, :])
    out_o[pl.ds(pl.multiple_of(48 * (1 - core), 16), 48), :] = added(t1[96:144, :], t3[96:144, :])


def spread_qkv_body(sc, t0, t1, t2, t3, grad_o, gain_o, shift_o, bias_o, mid_o, loss_o, scr):
    rest = jnp.zeros((16, 576), F32)
    for r, ref in enumerate((t0, t1, t2, t3)):
        scr[sc[1] ^ r] = ref[:96, :]
        rest += ref[96:112, :].astype(F32)
    for p in range(3):
        cols = [scr[j, :, 192 * p:192 * p + 192] for j in range(4)]
        grad_o[:, 768 * p:768 * p + 768] = jnp.concatenate(cols, axis=1).astype(F32)
    gain_o[...] = rest[0:3, 384:480]
    shift_o[...] = rest[3:6, 384:480]
    bias_o[...] = rest[6:10, 384:480]
    mid_o[...] = rest[0:8, :384]
    row = rest[10:11, 384:480]
    lane = lax.broadcasted_iota(jnp.int32, (1, 96), 1)
    error = jnp.sum(jnp.where(lane < 2, row, 0.0), axis=1, keepdims=True)
    count = jnp.sum(jnp.where(lane == 2, row, 0.0), axis=1, keepdims=True)
    loss_o[...] = error / (count * 768.0)


def hidden_body(sc, a, b, c, own, vec, d_res, out, mark):
    mark[...] = jnp.zeros((8, 128), F32)
    grad = (added(a[...], b[0]) + c[...].astype(F32)) * vec[0:1]
    hat, factor = moments(own[...].astype(F32))
    out[...] = d_res[...] + norm_back(grad, hat, factor)


def total_body(sc, own, s1, s2, s3, out):
    out[...] = total_of(own, (s1, s2, s3))


def fast(
    hidden, teacher, lengths, w_qkv, w_out, w_up, w_down, norm_gain, norm_shift, proj_bias,
    mid_gain, mid_shift, up_bias,
):
    dp_at, ctx_at = lax.axis_index("dp"), lax.axis_index("ctx")
    core = ctx_at & 1
    sc = jnp.stack([dp_at, ctx_at, lengths[0]]).astype(jnp.int32)
    own = hidden[0]
    tall = (256, 768)
    barrier = lax.optimization_barrier
    h_y, h_c = swap(own, 2), swap(own, 1)
    piece = call(pack_body, [sc, w_qkv, norm_gain.T, norm_shift.T, proj_bias.T], [((96, 640), BF)], [((16, 128), F32)], room=54)[0]
    q_cols = along_z(piece)
    mid_rows = jnp.concatenate([mid_gain, mid_shift, up_bias, jnp.zeros((13 * 384,), BF)]).reshape(8, 768)
    piece_a = jnp.concatenate([
        lax.dynamic_slice(w_up, (0, 768 * ctx_at), (96, 768)), lax.dynamic_slice(w_out, (48 * core, 0), (48, 768)), mid_rows])
    down4 = w_down.reshape(4, 96, 768)
    piece_b, piece_c = (lax.dynamic_index_in_dim(down4, ctx_at ^ t, 0, keepdims=False) for t in (0, 2))
    q_cols, piece_a = barrier((q_cols, piece_a))
    q_near = jnp.stack([piece] + q_cols)
    q_far = swap(q_near, 4)
    h_yc = swap(h_y, 1)
    a_cols = along_z(piece_a)
    a_cols, q_far, piece_b, h_c, h_yc = barrier((a_cols, q_far, piece_b, h_c, h_yc))
    a_near = jnp.stack([piece_a] + a_cols)
    a_far = swap(a_near, 4)
    y_near = swap(a_near[:, :96], 2)
    a_near_o = swap(a_near, 1)
    b_cols = along_z(piece_b)
    hids = [own, h_c, h_y, h_yc]
    att_0, att_1, att_23, q, k, v, lse, ot, normed, vec = attend(sc, hids, q_near, q_far, (a_near,))
    y_near, b_cols, piece_c, att_23, att_1 = barrier((y_near, b_cols, piece_c, att_23, att_1))
    c_cols = along_z(piece_c)
    att_y = swap(att_23, 2)
    b_near = jnp.stack([piece_b] + b_cols)
    a_far, b_near, att_y = barrier((a_far, b_near, att_y))
    b_far = swap(b_near, 4)
    y_far = swap(a_far[:, :96], 2)
    c_near = jnp.stack([piece_c] + c_cols)
    c_near, b_far, y_far, a_near, a_far, y_near, b_near, att_1 = barrier(
        (c_near, b_far, y_far, a_near, a_far, y_near, b_near, att_1))
    c_far = swap(b_far, 2)
    att_c = swap(jnp.stack([att_1, att_y[1]]), 1)
    a_near_o, a_far_o, y_near_o, y_far_o = (swap(t, 1) for t in (a_near, a_far, y_near, y_far))
    b_near_o, b_far_o, c_near_o = (swap(t, 1) for t in (b_near, b_far, c_near))
    got = [att_0, att_c, att_y]
    outs = [(t, part(48, 2)) for t in (a_near, a_far, a_near_o, a_far_o)]
    mixed, resid, ffn = call(
        mid_body, [sc, *got, own, vec, *outs], [(tall, BF), (tall, F32), (tall, BF)],
        [((768, 768), BF), ((4, 256, 192), BF)], us=3)
    ups = [(t, part(96, 0)) for t in (a_near, a_far, a_near_o, a_far_o)] + [y_near, y_far, y_near_o, y_far_o]
    four = (4, 256, 768)
    act, hat, slope, scale, nat = call(
        up_body, [sc, ffn, *ups] + [(t, part(8, 18)) for t in (a_near, a_far)],
        [(four, BF), (four, BF), (four, BF), ((256, 1), F32), ((4, 8, 768), F32)],
        [((4, 768, 768), BF), (four, F32), ((8, 8, 768), F32)], us=5)
    c_far, act = barrier((c_far, act))
    c_far_o = swap(c_far, 1)
    downs = [b_near, c_near, b_far, c_far, b_near_o, c_near_o, b_far_o, c_far_o]
    out, err, low, side_d = call(
        down_body, [sc, act, resid, teacher[0], vec, *downs],
        [(tall, BF), (tall, F32), (tall, BF), ((8, 768), F32)], [((3072, 768), BF)], us=5)
    halves_of = ((2, 8, 96, 768), BF)
    down_keep, down_send = call(
        down_grad_body, [sc, act, low], [halves_of] * 2, [((4, 8, 96, 768), BF)], us=3)
    down_got = swap(down_send, 1)
    up_low, mids = call(
        act_back_body, [sc, low, hat, slope, scale, nat, *downs], [(four, BF), ((16, 3072), F32)],
        [((3072, 768), BF), (four, F32)], us=5, deps=(down_keep,))
    slots = ((4, 96, 768), BF)
    d_near0, d_near1, d_far0, d_far1 = call(pair_body, [sc, down_keep, down_got], [slots] * 4, us=2, deps=(mids,))
    d_far0, up_low = barrier((d_far0, up_low))
    d_got0 = swap(d_far0, 4)
    up_keep, up_send = call(up_grad_body, [sc, ffn, up_low], [halves_of] * 2, [((4, 8, 96, 768), BF)], us=3, deps=(d_near0,))
    up_got = swap(up_send, 1)
    branch, d_res, *d_att, side_e = call(
        ffn_back_body, [sc, up_low, err, resid, *ups, *outs, vec, *got],
        [(tall, BF), (tall, F32)] + [((256, 192), BF)] * 4 + [((8, 768), F32)],
        [((4, 768, 768), BF), ((768, 768), BF), ((4, 256, 192), BF), ((4, 256, 192), BF)], us=6, deps=(up_keep,))
    u_near0, u_near1, u_far0, u_far1 = call(pair_body, [sc, up_keep, up_got], [slots] * 4, us=2, deps=(side_e,))
    d_got = [d_att[0]] + [swap(d_att[r], r) for r in (1, 2, 3)]
    out_keep, out_send = call(
        out_grad_body, [sc, mixed, branch], [((8, 48, 768), BF)] * 2, [((2, 8, 48, 768), BF)], us=1, deps=(u_near0,))
    out_got = swap(out_send, 1)
    own_part, sent = ((96, 768), F32), ((96, 768), BF)
    d_own0, *d_z0 = call(slots_body, [sc, d_near0, d_got0], [own_part] + [sent] * 3, us=1, deps=(out_keep,))

    def along_z_back(parts):
        return [swap(parts[step - 1], 8 * step) for step in (3, 2, 1)]

    d_z0, d_far1, u_far1, d_got, out_got = barrier((d_z0, d_far1, u_far1, d_got, out_got))
    d_z0 = along_z_back(d_z0)
    d_got1 = swap(d_far1, 4)
    uy_far = swap(u_far1, 2)
    dn_0, dn_1, dn_23, q_keep, q_send = attend_back(
        sc, d_got, (q, k, v, lse, ot, normed, vec), hids, q_near, q_far, side_e, side_d, mids, (d_own0, out_got))
    d_z0, d_got1, uy_far, u_near1, dn_0, dn_1, dn_23, q_keep, q_send = barrier(
        (d_z0, d_got1, uy_far, u_near1, dn_0, dn_1, dn_23, q_keep, q_send))
    near, far = (pl.BlockSpec((4, 48, 768), lambda i, at=at: (at, 0, 0), pipeline_mode=pl.Buffered(1)) for at in (0, 1))
    q_got = swap(q_send, 4)
    uy_near = swap(u_near1, 2)
    d_own1, *d_z1 = call(slots_body, [sc, d_near1, d_got1], [own_part] + [sent] * 3, us=1)
    d_z1 = along_z_back(d_z1)
    q_got, uy_far, d_own1 = barrier((q_got, uy_far, d_own1))
    u_x = call(join_far_body, [sc, u_far0, uy_far, (out_keep, far), (out_got, far)], [((4, 144, 768), BF)], us=1)[0]
    ux_got = swap(u_x, 4)
    d_z1, uy_near, dn_23, q_keep = barrier((d_z1, uy_near, dn_23, q_keep))
    q_own, *q_z = call(slots_body, [sc, q_keep, q_got], [((112, 576), F32)] + [((112, 576), BF)] * 3, us=1, deps=(u_x,))
    q_z = along_z_back(q_z)
    dn_y = swap(dn_23, 2)
    q_z, dn_y, d_own0 = barrier((q_z, dn_y, d_own0))
    one = [pl.BlockSpec((1, 256, 768), lambda i, at=at: (at, 0, 0), pipeline_mode=pl.Buffered(1)) for at in (0, 1)]
    q_sum, dn_1, early = call(
        middle_body, [sc, q_own, *q_z, dn_1, (dn_y, one[1]), d_own0, *d_z0, d_own1, *d_z1],
        [((112, 576), BF), (tall, BF), ((192, 768), BF)], us=1)
    q_y, q_c = swap(q_sum, 2), swap(q_sum, 1)
    q_yc = swap(q_y, 1)
    dn_c = swap(dn_1, 1)
    early_y = swap(early, 2)
    u_own, *u_z = call(
        join_near_body, [sc, u_near0, uy_near, (out_keep, near), (out_got, near), ux_got],
        [((144, 768), F32)] + [((144, 768), BF)] * 3, us=1, deps=(q_sum,))
    u_z = along_z_back(u_z)
    u_z, q_c, q_yc, q_y, dn_c, early_y = barrier((u_z, q_c, q_yc, q_y, dn_c, early_y))
    u_sum = call(total_body, [sc, u_own, *u_z], [((144, 768), BF)], us=1)[0]
    u_y = swap(u_sum, 2)
    hidden_grad, mark = call(hidden_body, [sc, dn_0, (dn_y, one[0]), dn_c, own, vec, d_res], [(tall, F32), ((8, 128), F32)], us=1, deps=(u_sum,))
    grad_qkv, gain, shift, bias, mid, loss = call(
        spread_qkv_body, [sc, q_sum, q_c, q_y, q_yc],
        [((96, 2304), F32), ((3, 96), F32), ((3, 96), F32), ((4, 96), F32), ((8, 384), F32), ((1, 1), F32)],
        [((4, 96, 576), BF)], us=2, deps=(mark,))
    two = call(fold_body, [sc, early, early_y], [((192, 768), BF)], us=1, deps=(loss,))[0]
    two, u_sum, u_y = lax.optimization_barrier((two, u_sum, u_y))
    u_c, u_yc, more = swap(u_sum, 1), swap(u_y, 1), swap(two, 1)
    grad_down = call(spread_down_body, [sc, two, more], [((384, 768), F32)], us=1)[0]
    grad_up, grad_out = call(
        spread_body, [sc, u_sum, u_c, u_y, u_yc], [((96, 3072), F32), ((96, 768), F32)], [((4, 96, 768), BF)], us=2)
    return (out[None], loss[0, 0], hidden_grad[None], grad_qkv, grad_out, grad_up, grad_down,
            gain.T, shift.T, bias.T, mid[0], mid[1], mid[2])


def solution(mesh):
    step = fast if (mesh.shape["dp"], mesh.shape["ctx"]) == (8, 4) else shards
    placed = (
        P("dp", "ctx", None),
        P("dp", "ctx", None),
        P("dp"),
        P("dp", None),
        P("dp", None),
        P("dp", None),
        P("dp", None),
        P("dp", None),
        P("dp", None),
        P("dp", None),
        P("dp"),
        P("dp"),
        P("dp"),
    )
    return jax.shard_map(
        step,
        mesh=mesh,
        in_specs=placed,
        out_specs=(
            P("dp", "ctx", None),
            P(),
            P("dp", "ctx", None),
            P("dp", None),
            P("dp", None),
            P("dp", None),
            P("dp", None),
            P("dp", None),
            P("dp", None),
            P("dp", None),
            P("dp"),
            P("dp"),
            P("dp"),
        ),
        check_vma=False,
    )
```
